512 devices in a mesh: dom: 128 (over z, y, core), pipe: 4 (over x).
Axes of the slice: x: 4, y: 4, z: 16, core: 2. Of those that a mesh axis runs over, the one named last changes fastest.
Arguments:
- inputs: bfloat16 [2, 32768, 512], P(None, 'dom'), may hold values from -6 to 6
- cotangent: bfloat16 [2, 32768, 512], P(None, 'dom'), may hold values from -6 to 6
- w_send: bfloat16 [4, 512, 512], P('pipe'), may hold values from -0.25 to 0.25
- w_recv: bfloat16 [4, 512, 512], P('pipe'), may hold values from -0.25 to 0.25
- w_message: bfloat16 [4, 512, 512], P('pipe'), may hold values from -0.25 to 0.25
- w_node: bfloat16 [4, 512, 512], P('pipe'), may hold values from -0.25 to 0.25
- w_aggregate: bfloat16 [4, 512, 512], P('pipe'), may hold values from -0.25 to 0.25
- gains: float32 [4, 512], P('pipe'), may hold values from 0.1 to 1.9
- edge_send: int32 [256, 128], P('dom'), may hold values from 0 to 511, as said below
- edge_recv: int32 [256, 128], P('dom'), may hold values from 0 to 255, as said below
- edge_count: int32 [256], P('dom'), may hold values from 1 to 128, as said below
- halo_send: int32 [128, 2, 1], P('dom'), may hold values from 0 to 1, as said below
Outputs:
- section_out: bfloat16 [4, 2, 32768, 512], P('pipe', None, 'dom')
- input_grad: bfloat16 [4, 2, 32768, 512], P('pipe', None, 'dom')
The draws below stay inside these ranges and needn't reach their ends.
Inputs may be any that keep to these rules, and one draw needn't show every extreme that they name: `edge_send`: rows 0 to 255 are the partition's own rows, the next 128 the blocks received from the previous partition in list order, the last 128 those from the next partition. The largest and smallest values are reached. `edge_recv`: both ends are reached. `edge_count`: the live slots of a block are its first ones; one block is full and one has a single live slot. `halo_send`: each list names 1 distinct own blocks. Lists wrap around the partitions.
All inputs are finite; a program needn't handle non-finite values.
Results may differ from the reference program's by a relative error of at most 0.015.
Values may be sent and summed in bfloat16 or wider, within the bound.
A program may use at most 64 MiB of HBM per device.

```python
import jax
import jax.numpy as jnp
from jax import lax

D = 512
BLOCK = 128
NB = 2
HB = 1
EB = 2
MICRO = 2
PARTITIONS = 128
SECTIONS = 4
NODES = 32768


def draw_halo_send(key, part):
    scores = jax.random.randint(jax.random.fold_in(key, 11), (PARTITIONS, 2, NB), 0, 1 << 20) * NB + jnp.arange(NB)
    orders = jnp.argsort(scores, axis=-1, stable=True).astype(jnp.int32)
    return orders[:, :, :HB].astype(jnp.int32)


def draw_edge_send(key, part):
    own_rows = NB * BLOCK
    halo_span = HB * BLOCK
    kinds = jax.random.randint(jax.random.fold_in(key, 13), (PARTITIONS * EB, BLOCK), 0, 8)
    lower = jnp.where(kinds < 6, 0, jnp.where(kinds == 6, own_rows, own_rows + halo_span))
    upper = jnp.where(kinds < 6, own_rows, jnp.where(kinds == 6, own_rows + halo_span, own_rows + 2 * halo_span))
    drawn = jax.random.randint(jax.random.fold_in(key, 17), (PARTITIONS * EB, BLOCK), lower, upper)
    row_ids = jnp.arange(PARTITIONS * EB)[:, None]
    column_ids = jnp.arange(BLOCK)[None, :]
    drawn = jnp.where((row_ids == 0) & (column_ids == 0), own_rows + 2 * halo_span - 1, drawn)
    drawn = jnp.where((row_ids == 0) & (column_ids == 1), 0, drawn)
    return drawn.astype(jnp.int32)


def draw_edge_recv(key, part):
    own_rows = NB * BLOCK
    drawn = jax.random.randint(jax.random.fold_in(key, 19), (PARTITIONS * EB, BLOCK), 0, own_rows)
    row_ids = jnp.arange(PARTITIONS * EB)[:, None]
    column_ids = jnp.arange(BLOCK)[None, :]
    drawn = jnp.where((row_ids == 0) & (column_ids == 0), own_rows - 1, drawn)
    drawn = jnp.where((row_ids == 0) & (column_ids == 1), 0, drawn)
    return drawn.astype(jnp.int32)


def draw_edge_count(key, part):
    heavy = jax.random.randint(jax.random.fold_in(key, 23), (PARTITIONS,), 0, 4) == 0
    device = jnp.arange(PARTITIONS * EB) // EB
    lower = jnp.where(heavy, BLOCK // 2, BLOCK // 4)[device]
    upper = jnp.where(heavy, BLOCK + 1, 3 * BLOCK // 4 + 1)[device]
    drawn = jax.random.randint(jax.random.fold_in(key, 29), (PARTITIONS * EB,), lower, upper)
    positions = jnp.arange(PARTITIONS * EB)
    drawn = jnp.where(positions == 0, BLOCK, drawn)
    drawn = jnp.where(positions == 1, 1, drawn)
    return drawn.astype(jnp.int32)


def block_scale(own_key, extent, pieces, smallest, top_value):
    level, own = 1.0, jax.random.fold_in(own_key, 6)
    for dim, blocks in pieces:
        steps = jnp.exp(jax.random.uniform(jax.random.fold_in(own, dim), (blocks,), jnp.float32, smallest / len(pieces), top_value / len(pieces)))
        level = level * jnp.repeat(steps, extent[dim] // blocks).reshape([-1 if axis == dim else 1 for axis in range(len(extent))])
    return level


def bell_draw(rng, shape, deviation, bound, cuts=(), kind=jnp.bfloat16):
    result = deviation * jax.random.normal(rng, shape, jnp.float32)
    if cuts:
        result = result * block_scale(rng, shape, cuts, -0.22, 0.18)
    return jnp.clip(result, -bound, bound).astype(kind)


def setup_inputs(seed: int = 0) -> dict:
    arg_keys = jax.random.split(jax.random.key(seed), 13)
    inputs = bell_draw(arg_keys[0], (MICRO, NODES, D), 1.0, 6.0, ((1, 128),))
    cotangent = bell_draw(arg_keys[1], (MICRO, NODES, D), 1.0, 6.0, ((1, 128),))
    w_send = bell_draw(arg_keys[2], (SECTIONS, D, D), D ** -0.5, 0.25, ((0, 4),))
    w_recv = bell_draw(arg_keys[3], (SECTIONS, D, D), D ** -0.5, 0.25, ((0, 4),))
    w_message = bell_draw(arg_keys[4], (SECTIONS, D, D), D ** -0.5, 0.25, ((0, 4),))
    w_node = bell_draw(arg_keys[5], (SECTIONS, D, D), D ** -0.5, 0.25, ((0, 4),))
    w_aggregate = bell_draw(arg_keys[6], (SECTIONS, D, D), D ** -0.5, 0.25, ((0, 4),))
    gains = jnp.clip(1.0 + 0.18 * jax.random.normal(arg_keys[7], (SECTIONS, D), jnp.float32), 0.1, 1.9)
    edge_send = draw_edge_send(jax.random.fold_in(arg_keys[12], 71), 0)
    edge_recv = draw_edge_recv(jax.random.fold_in(arg_keys[12], 71), 0)
    edge_count = draw_edge_count(jax.random.fold_in(arg_keys[12], 71), 0)
    halo_send = draw_halo_send(jax.random.fold_in(arg_keys[12], 71), 0)
    return dict(inputs=inputs, cotangent=cotangent, w_send=w_send, w_recv=w_recv, w_message=w_message, w_node=w_node, w_aggregate=w_aggregate, gains=gains, edge_send=edge_send, edge_recv=edge_recv, edge_count=edge_count, halo_send=halo_send)


EPSILON = 1e-05

def dot_plain(operand, matrix):
    return jnp.dot(operand, matrix, preferred_element_type=jnp.float32)

def dot_transposed(operand, matrix):
    return lax.dot_general(operand, matrix, (((1,), (1,)), ((), ())), preferred_element_type=jnp.float32)

def silu_slope(values):
    sigmoid_value = jax.nn.sigmoid(values)
    return sigmoid_value * (1.0 + values * (1.0 - sigmoid_value))

def normalize(activated):
    mean_value = lax.optimization_barrier(jnp.mean(activated, axis=-1, keepdims=True))
    centred = activated - mean_value
    variance = lax.optimization_barrier(jnp.mean(centred * centred, axis=-1, keepdims=True))
    scale_inverse = lax.rsqrt(variance + EPSILON)
    return (centred * scale_inverse, scale_inverse)

def edge_rows(edge_send, edge_recv, edge_count, halo_send):
    own_rows = NB * BLOCK
    halo_span = HB * BLOCK
    block_total = edge_send.shape[0]
    device = (jnp.arange(block_total, dtype=jnp.int32) // EB)[:, None]
    is_own = edge_send < own_rows
    is_prev = (edge_send >= own_rows) & (edge_send < own_rows + halo_span)
    offset = jnp.where(is_prev, edge_send - own_rows, edge_send - own_rows - halo_span)
    offset = jnp.clip(offset, 0, halo_span - 1)
    which_block = offset // BLOCK
    row_offset = offset % BLOCK
    prev_device = (device - 1) % PARTITIONS
    next_device = (device + 1) % PARTITIONS
    prev_block = halo_send[prev_device, 0, which_block]
    next_block = halo_send[next_device, 1, which_block]
    from_prev = prev_device * own_rows + prev_block * BLOCK + row_offset
    from_next = next_device * own_rows + next_block * BLOCK + row_offset
    senders = jnp.where(is_own, device * own_rows + edge_send, jnp.where(is_prev, from_prev, from_next))
    receivers = device * own_rows + edge_recv
    live_mask = jnp.arange(BLOCK, dtype=jnp.int32)[None, :] < edge_count[:, None]
    return (senders.reshape(-1).astype(jnp.int32), receivers.reshape(-1).astype(jnp.int32), live_mask.reshape(-1))

def layer_forward(hidden, matrices, senders, receivers, live_float):
    send_matrix, recv_matrix, message_matrix, node_matrix, aggregate_matrix = matrices
    projected = dot_plain(hidden, send_matrix).astype(jnp.bfloat16)
    recv_part = dot_plain(hidden, recv_matrix)
    pre_edge = jnp.take(projected, senders, axis=0).astype(jnp.float32) + jnp.take(recv_part, receivers, axis=0)
    edge_hidden = jax.nn.silu(pre_edge).astype(jnp.bfloat16)
    messages = dot_plain(edge_hidden, message_matrix) * live_float
    aggregate = jax.ops.segment_sum(messages, receivers, num_segments=hidden.shape[0]).astype(jnp.bfloat16)
    node_pre = dot_plain(hidden, node_matrix) + dot_plain(aggregate, aggregate_matrix)
    return (pre_edge, node_pre)

def layer_backward(upstream, pre_edge, node_pre, matrices, gain_row, senders, receivers, live_float):
    send_matrix, recv_matrix, message_matrix, node_matrix, aggregate_matrix = matrices
    row_total = node_pre.shape[0]
    unit, scale_inverse = normalize(jax.nn.silu(node_pre))
    upstream_float = upstream.astype(jnp.float32)
    grad_unit = upstream_float * gain_row
    grad_activated = scale_inverse * (grad_unit - lax.optimization_barrier(jnp.mean(grad_unit, axis=-1, keepdims=True)) - unit * lax.optimization_barrier(jnp.mean(grad_unit * unit, axis=-1, keepdims=True)))
    grad_node_pre = (grad_activated * silu_slope(node_pre)).astype(jnp.bfloat16)
    grad_aggregate = dot_transposed(grad_node_pre, aggregate_matrix).astype(jnp.bfloat16)
    grad_rows = upstream_float + dot_transposed(grad_node_pre, node_matrix)
    grad_message = jnp.take(grad_aggregate, receivers, axis=0) * live_float.astype(jnp.bfloat16)
    grad_edge = (dot_transposed(grad_message, message_matrix) * silu_slope(pre_edge)).astype(jnp.bfloat16)
    grad_rows = grad_rows + jax.ops.segment_sum(dot_transposed(grad_edge, recv_matrix), receivers, num_segments=row_total)
    grad_rows = grad_rows + jax.ops.segment_sum(dot_transposed(grad_edge, send_matrix), senders, num_segments=row_total)
    return grad_rows.astype(jnp.bfloat16)

def reference(inputs, cotangent, w_send, w_recv, w_message, w_node, w_aggregate, gains, edge_send, edge_recv, edge_count, halo_send):
    senders, receivers, live_mask = edge_rows(edge_send, edge_recv, edge_count, halo_send)
    live_float = live_mask.astype(jnp.float32)[:, None]
    phase_inputs = []
    outputs = []
    current = [inputs[position] for position in range(MICRO)]
    for section in range(SECTIONS):
        matrices = (w_send[section], w_recv[section], w_message[section], w_node[section], w_aggregate[section])
        phase_inputs.append(current)
        produced = []
        for micro_index in range(MICRO):
            hidden = current[micro_index]
            pre_edge, node_pre = layer_forward(hidden, matrices, senders, receivers, live_float)
            unit, scale_inverse = normalize(jax.nn.silu(node_pre))
            produced.append((hidden.astype(jnp.float32) + unit * gains[section]).astype(jnp.bfloat16))
        outputs.append(jnp.stack(produced))
        current = produced
    gradients = [None] * SECTIONS
    upstream_list = [cotangent[position] for position in range(MICRO)]
    for section in range(SECTIONS - 1, -1, -1):
        matrices = (w_send[section], w_recv[section], w_message[section], w_node[section], w_aggregate[section])
        results = []
        for micro_index in range(MICRO):
            hidden = phase_inputs[section][micro_index]
            pre_edge, node_pre = layer_forward(hidden, matrices, senders, receivers, live_float)
            results.append(layer_backward(upstream_list[micro_index], pre_edge, node_pre, matrices, gains[section], senders, receivers, live_float))
        gradients[section] = jnp.stack(results)
        upstream_list = results
    return (jnp.stack(outputs), jnp.stack(gradients))
```

```python
import functools

import jax
import jax.numpy as jnp
from jax import lax
from jax.experimental import pallas as pl
from jax.experimental.pallas import tpu as pltpu
from jax.sharding import PartitionSpec as P

EPSILON = 1e-05
F32 = jnp.float32
BF16 = jnp.bfloat16


def mm(x, w):
    return jnp.dot(x, w, preferred_element_type=F32)


def mm_t(x, w):
    return lax.dot_general(x, w, (((1,), (1,)), ((), ())), preferred_element_type=F32)


def sigmoid(v):
    return 1.0 / (1.0 + jnp.exp(-v))


def split_sum(onehot, values):
    hi = values.astype(BF16)
    lo = (values - hi.astype(F32)).astype(BF16)
    return mm(onehot, hi) + mm(onehot, lo)


def fwd_kernel(hs_ref, h_ref, fp_ref, fn_ref, osnd_ref, orcv_ref, orcvt_ref,
               ws_ref, wr_ref, wm_ref, wn_ref, wa_ref, g_ref,
               out_ref, a_ref, u_ref, hn_ref, hp_ref):
    own = h_ref.shape[1]
    span = fp_ref.shape[1]
    block = span
    gain = g_ref[...]
    osnd = osnd_ref[...]
    for m in range(h_ref.shape[0]):
        h = h_ref[m]
        gathered = (mm(osnd[:, :own], h) + mm(osnd[:, own:own + span], fp_ref[m])
                    + mm(osnd[:, own + span:], fn_ref[m])).astype(BF16)
        send_part = mm(gathered, ws_ref[...]).astype(BF16).astype(F32)
        recv_rows = mm(orcv_ref[...], h).astype(BF16)
        pre = send_part + mm(recv_rows, wr_ref[...])
        a_ref[m] = pre
        edge_hidden = (pre * sigmoid(pre)).astype(BF16)
        messages = mm(edge_hidden, wm_ref[...])
        agg = split_sum(orcvt_ref[...], messages).astype(BF16)
        node_pre = mm(h, wn_ref[...]) + mm(agg, wa_ref[...])
        u_ref[m] = node_pre
        act = node_pre * sigmoid(node_pre)
        mean = jnp.mean(act, axis=-1, keepdims=True)
        cen = act - mean
        var = jnp.mean(cen * cen, axis=-1, keepdims=True)
        unit = cen * lax.rsqrt(var + EPSILON)
        out = (h.astype(F32) + unit * gain).astype(BF16)
        out_ref[m] = out
        hs0 = hs_ref[0]
        hs1 = hs_ref[1]
        nblocks = own // block
        sel_n = out[0:block]
        sel_p = out[0:block]
        for b in range(1, nblocks):
            piece = out[b * block:(b + 1) * block]
            sel_n = jnp.where(hs0 == b, piece, sel_n)
            sel_p = jnp.where(hs1 == b, piece, sel_p)
        hn_ref[m] = sel_n
        hp_ref[m] = sel_p


def bwd_kernel(hs_ref, pin_ref, gn_ref, gp_ref, a_ref, u_ref, osndt_ref, orcvl_ref, orcvt_ref,
               ws_ref, wr_ref, wm_ref, wn_ref, wa_ref, g_ref,
               p32_ref, p16_ref, hg_ref):
    own = pin_ref.shape[1]
    span = gn_ref.shape[1]
    block = span
    nblocks = own // block
    gain = g_ref[...]
    hs0 = hs_ref[0]
    hs1 = hs_ref[1]
    osndt = osndt_ref[...]
    for m in range(pin_ref.shape[0]):
        pieces = []
        gn = gn_ref[m].astype(F32)
        gp = gp_ref[m].astype(F32)
        for b in range(nblocks):
            piece = pin_ref[m, b * block:(b + 1) * block].astype(F32)
            piece = piece + jnp.where(hs0 == b, gn, 0.0) + jnp.where(hs1 == b, gp, 0.0)
            pieces.append(piece)
        c = jnp.concatenate(pieces, axis=0).astype(BF16).astype(F32)
        node_pre = u_ref[m]
        sig_u = sigmoid(node_pre)
        act = node_pre * sig_u
        mean = jnp.mean(act, axis=-1, keepdims=True)
        cen = act - mean
        var = jnp.mean(cen * cen, axis=-1, keepdims=True)
        rs = lax.rsqrt(var + EPSILON)
        unit = cen * rs
        gu = c * gain
        gact = rs * (gu - jnp.mean(gu, axis=-1, keepdims=True)
                     - unit * jnp.mean(gu * unit, axis=-1, keepdims=True))
        du = (gact * (sig_u * (1.0 + node_pre * (1.0 - sig_u)))).astype(BF16)
        dagg = mm_t(du, wa_ref[...]).astype(BF16)
        rows = c + mm_t(du, wn_ref[...])
        gmsg = mm(orcvl_ref[...], dagg).astype(BF16)
        pre = a_ref[m]
        sig_a = sigmoid(pre)
        dedge = (mm_t(gmsg, wm_ref[...]) * (sig_a * (1.0 + pre * (1.0 - sig_a)))).astype(BF16)
        rows = rows + split_sum(orcvt_ref[...], mm_t(dedge, wr_ref[...]))
        send_rows = split_sum(osndt, mm_t(dedge, ws_ref[...]))
        total = rows + send_rows[:own]
        p32_ref[m] = total
        p16_ref[m] = total.astype(BF16)
        hg_ref[m] = send_rows[own:].astype(BF16)


def vmem_call(kernel, out_shapes, n_in, smem_first=True):
    in_specs = [pl.BlockSpec(memory_space=pltpu.SMEM)] + [pl.BlockSpec(memory_space=pltpu.VMEM)] * (n_in - 1)
    return pl.pallas_call(
        kernel,
        out_shape=out_shapes,
        in_specs=in_specs,
        out_specs=tuple(pl.BlockSpec(memory_space=pltpu.VMEM) for _ in out_shapes),
        compiler_params=pltpu.CompilerParams(vmem_limit_bytes=48 * 1024 * 1024),
    )


def shards(inputs, cotangent, w_send, w_recv, w_message, w_node, w_aggregate, gains,
           edge_send, edge_recv, edge_count, halo_send):
    sections = lax.axis_size("pipe")
    parts = lax.axis_size("dom")
    p_idx = lax.axis_index("pipe")
    micro, own, latent = inputs.shape
    block = edge_send.shape[1]
    span = halo_send.shape[2] * block
    ext_rows = own + 2 * span
    weights = (w_send[0], w_recv[0], w_message[0], w_node[0], w_aggregate[0])
    gain = gains[0].reshape(1, latent)
    hs = halo_send[0].reshape(-1).astype(jnp.int32)

    snd = edge_send.reshape(-1)
    rcv = edge_recv.reshape(-1)
    live = (jnp.arange(block)[None, :] < edge_count[:, None]).reshape(-1)
    osnd = (snd[:, None] == jnp.arange(ext_rows)[None, :]).astype(BF16)
    orcv_b = rcv[:, None] == jnp.arange(own)[None, :]
    orcv = orcv_b.astype(BF16)
    orcvl_b = orcv_b & live[:, None]
    orcvl = orcvl_b.astype(BF16)
    orcvt = orcvl_b.T.astype(BF16)
    osndt = osnd.T

    def blocks_of(x):
        shaped = x.reshape(micro, own // block, block, latent)
        nxt = jnp.take(shaped, hs[0], axis=1)
        prv = jnp.take(shaped, hs[1], axis=1)
        return nxt, prv

    S, D = sections, parts

    def perm_pipe(shift):
        return [(i, (i + shift) % S) for i in range(S)]

    def perm_both(dshift, pshift):
        return [(d * S + p, ((d + dshift) % D) * S + (p + pshift) % S)
                for d in range(D) for p in range(S)]

    both = ("dom", "pipe")

    fwd = vmem_call(
        fwd_kernel,
        (jax.ShapeDtypeStruct((micro, own, latent), BF16),
         jax.ShapeDtypeStruct((micro, own, latent), F32),
         jax.ShapeDtypeStruct((micro, own, latent), F32),
         jax.ShapeDtypeStruct((micro, span, latent), BF16),
         jax.ShapeDtypeStruct((micro, span, latent), BF16)),
        13)
    bwd = vmem_call(
        bwd_kernel,
        (jax.ShapeDtypeStruct((micro, own, latent), F32),
         jax.ShapeDtypeStruct((micro, own, latent), BF16),
         jax.ShapeDtypeStruct((micro, 2 * span, latent), BF16)),
        15)

    nxt0, prv0 = blocks_of(inputs)
    from_prev = lax.ppermute(nxt0, "dom", [(i, (i + 1) % D) for i in range(D)])
    from_next = lax.ppermute(prv0, "dom", [(i, (i - 1) % D) for i in range(D)])
    h = inputs
    out_rec = a_rec = u_rec = None
    for t in range(S):
        out, a, u, hn, hp = fwd(hs, h, from_prev, from_next, osnd, orcv, orcvt, *weights, gain)
        here = p_idx == t
        if t == 0:
            out_rec, a_rec, u_rec = out, a, u
        else:
            out_rec = jnp.where(here, out, out_rec)
            a_rec = jnp.where(here, a, a_rec)
            u_rec = jnp.where(here, u, u_rec)
        if t < S - 1:
            h = lax.ppermute(out, "pipe", perm_pipe(1))
            from_prev = lax.ppermute(hn, both, perm_both(1, 1))
            from_next = lax.ppermute(hp, both, perm_both(-1, 1))

    pin = cotangent
    zeros = jnp.zeros((micro, span, latent), BF16)
    g_next = g_prev = zeros
    grad_rec = None
    for t in range(S - 1, -1, -1):
        p32, p16, hg = bwd(hs, pin, g_next, g_prev, a_rec, u_rec, osndt, orcvl, orcvt, *weights, gain)
        to_prev = hg[:, :span]
        to_next = hg[:, span:]
        sn = lax.ppermute(to_prev, "dom", [(i, (i - 1) % D) for i in range(D)])
        sp = lax.ppermute(to_next, "dom", [(i, (i + 1) % D) for i in range(D)])
        shaped = p32.reshape(micro, own // block, block, latent)
        sel = jnp.arange(own // block)[None, :, None, None]
        summed = (shaped + jnp.where(sel == hs[0], sn.astype(F32)[:, None], 0.0)
                  + jnp.where(sel == hs[1], sp.astype(F32)[:, None], 0.0))
        grad = summed.reshape(micro, own, latent).astype(BF16)
        here = p_idx == t
        grad_rec = grad if t == S - 1 else jnp.where(here, grad, grad_rec)
        if t > 0:
            pin = lax.ppermute(p16, "pipe", perm_pipe(-1))
            g_next = lax.ppermute(to_prev, both, perm_both(-1, -1))
            g_prev = lax.ppermute(to_next, both, perm_both(1, -1))
    return (out_rec[None], grad_rec[None])


def solution(mesh):
    in_specs = (
        P(None, "dom", None),
        P(None, "dom", None),
        P("pipe", None, None),
        P("pipe", None, None),
        P("pipe", None, None),
        P("pipe", None, None),
        P("pipe", None, None),
        P("pipe", None),
        P("dom", None),
        P("dom", None),
        P("dom"),
        P("dom", None, None),
    )
    out_specs = (P("pipe", None, "dom", None), P("pipe", None, "dom", None))
    return jax.shard_map(shards, mesh=mesh, in_specs=in_specs, out_specs=out_specs, check_vma=False)
```

```python
import functools

import jax
import jax.numpy as jnp
from jax import lax
from jax.experimental import pallas as pl
from jax.experimental.pallas import tpu as pltpu
from jax.sharding import PartitionSpec as P

EPSILON = 1e-05
F32 = jnp.float32
BF16 = jnp.bfloat16


def mm(x, w):
    return jnp.dot(x, w, preferred_element_type=F32)


def mm_t(x, w):
    return lax.dot_general(x, w, (((1,), (1,)), ((), ())), preferred_element_type=F32)


def sigmoid(v):
    return 1.0 / (1.0 + jnp.exp(-v))


def split_sum(onehot, values):
    hi = values.astype(BF16)
    lo = (values - hi.astype(F32)).astype(BF16)
    return mm(onehot, hi) + mm(onehot, lo)


def fwd_kernel(hs_ref, h_ref, fp_ref, fn_ref, osnd_ref, orcv_ref, orcvt_ref,
               ws_ref, wr_ref, wm_ref, wn_ref, wa_ref, g_ref,
               out_ref, a_ref, u_ref, hn_ref, hp_ref):
    own = h_ref.shape[1]
    span = fp_ref.shape[1]
    block = span
    gain = g_ref[...]
    osnd = osnd_ref[...]
    for m in range(h_ref.shape[0]):
        h = h_ref[m]
        gathered = (mm(osnd[:, :own], h) + mm(osnd[:, own:own + span], fp_ref[m])
                    + mm(osnd[:, own + span:], fn_ref[m])).astype(BF16)
        send_part = mm(gathered, ws_ref[...]).astype(BF16).astype(F32)
        recv_rows = mm(orcv_ref[...], h).astype(BF16)
        pre = send_part + mm(recv_rows, wr_ref[...])
        a_ref[m] = pre
        edge_hidden = (pre * sigmoid(pre)).astype(BF16)
        messages = mm(edge_hidden, wm_ref[...])
        agg = split_sum(orcvt_ref[...], messages).astype(BF16)
        node_pre = mm(h, wn_ref[...]) + mm(agg, wa_ref[...])
        u_ref[m] = node_pre
        act = node_pre * sigmoid(node_pre)
        mean = jnp.mean(act, axis=-1, keepdims=True)
        cen = act - mean
        var = jnp.mean(cen * cen, axis=-1, keepdims=True)
        unit = cen * lax.rsqrt(var + EPSILON)
        out = (h.astype(F32) + unit * gain).astype(BF16)
        out_ref[m] = out
        hs0 = hs_ref[0]
        hs1 = hs_ref[1]
        nblocks = own // block
        sel_n = out[0:block]
        sel_p = out[0:block]
        for b in range(1, nblocks):
            piece = out[b * block:(b + 1) * block]
            sel_n = jnp.where(hs0 == b, piece, sel_n)
            sel_p = jnp.where(hs1 == b, piece, sel_p)
        hn_ref[m] = sel_n
        hp_ref[m] = sel_p


def bwd_kernel(hs_ref, pin_ref, gn_ref, gp_ref, a_ref, u_ref, osndt_ref, orcvl_ref, orcvt_ref,
               ws_ref, wr_ref, wm_ref, wn_ref, wa_ref, g_ref,
               p32_ref, p16_ref, hg_ref):
    own = pin_ref.shape[1]
    span = gn_ref.shape[1]
    block = span
    nblocks = own // block
    gain = g_ref[...]
    hs0 = hs_ref[0]
    hs1 = hs_ref[1]
    osndt = osndt_ref[...]
    for m in range(pin_ref.shape[0]):
        pieces = []
        gn = gn_ref[m].astype(F32)
        gp = gp_ref[m].astype(F32)
        for b in range(nblocks):
            piece = pin_ref[m, b * block:(b + 1) * block].astype(F32)
            piece = piece + jnp.where(hs0 == b, gn, 0.0) + jnp.where(hs1 == b, gp, 0.0)
            pieces.append(piece)
        c = jnp.concatenate(pieces, axis=0).astype(BF16).astype(F32)
        node_pre = u_ref[m]
        sig_u = sigmoid(node_pre)
        act = node_pre * sig_u
        mean = jnp.mean(act, axis=-1, keepdims=True)
        cen = act - mean
        var = jnp.mean(cen * cen, axis=-1, keepdims=True)
        rs = lax.rsqrt(var + EPSILON)
        unit = cen * rs
        gu = c * gain
        gact = rs * (gu - jnp.mean(gu, axis=-1, keepdims=True)
                     - unit * jnp.mean(gu * unit, axis=-1, keepdims=True))
        du = (gact * (sig_u * (1.0 + node_pre * (1.0 - sig_u)))).astype(BF16)
        dagg = mm_t(du, wa_ref[...]).astype(BF16)
        rows = c + mm_t(du, wn_ref[...])
        gmsg = mm(orcvl_ref[...], dagg).astype(BF16)
        pre = a_ref[m]
        sig_a = sigmoid(pre)
        dedge = (mm_t(gmsg, wm_ref[...]) * (sig_a * (1.0 + pre * (1.0 - sig_a)))).astype(BF16)
        rows = rows + split_sum(orcvt_ref[...], mm_t(dedge, wr_ref[...]))
        send_rows = split_sum(osndt, mm_t(dedge, ws_ref[...]))
        total = rows + send_rows[:own]
        p32_ref[m] = total
        p16_ref[m] = total.astype(BF16)
        hg_ref[m] = send_rows[own:].astype(BF16)


MESH_ID = pl.DeviceIdType.MESH


def comm_kernel(sends, n_in, parts, sections, *refs):
    ins = refs[:n_in]
    outs = refs[n_in:n_in + len(sends)]
    send_sem, recv_sem = refs[n_in + len(sends):]
    d = lax.axis_index("dom")
    p = lax.axis_index("pipe")
    barrier = pltpu.get_barrier_semaphore()
    for _, _, _, dd, dp in sends:
        src = (lax.rem(d - dd + parts, parts), lax.rem(p - dp + sections, sections))
        pl.semaphore_signal(barrier, 1, device_id=src, device_id_type=MESH_ID)
    pl.semaphore_wait(barrier, len(sends))
    copies = []
    for i, (k, start, rows, dd, dp) in enumerate(sends):
        dst = (lax.rem(d + dd + parts, parts), lax.rem(p + dp + sections, sections))
        source = ins[k] if start is None else ins[k].at[:, pl.ds(start, rows)]
        copy = pltpu.make_async_remote_copy(
            src_ref=source, dst_ref=outs[i], send_sem=send_sem.at[i], recv_sem=recv_sem.at[i],
            device_id=dst, device_id_type=MESH_ID)
        copy.start()
        copies.append(copy)
    for copy in copies:
        copy.wait()


def exchange(sends, payloads, parts, sections, cid):
    out_shapes = []
    for k, start, rows, _, _ in sends:
        shape = payloads[k].shape
        if start is not None:
            shape = (shape[0], rows) + shape[2:]
        out_shapes.append(jax.ShapeDtypeStruct(shape, payloads[k].dtype))
    n = len(sends)
    return pl.pallas_call(
        functools.partial(comm_kernel, tuple(sends), len(payloads), parts, sections),
        out_shape=tuple(out_shapes),
        in_specs=[pl.BlockSpec(memory_space=pl.ANY)] * len(payloads),
        out_specs=tuple(pl.BlockSpec(memory_space=pl.ANY) for _ in sends),
        scratch_shapes=[pltpu.SemaphoreType.DMA((n,)), pltpu.SemaphoreType.DMA((n,))],
        compiler_params=pltpu.CompilerParams(collective_id=cid, has_side_effects=True),
    )(*payloads)


def vmem_call(kernel, out_shapes, n_in, smem_first=True):
    in_specs = [pl.BlockSpec(memory_space=pltpu.SMEM)] + [pl.BlockSpec(memory_space=pltpu.VMEM)] * (n_in - 1)
    return pl.pallas_call(
        kernel,
        out_shape=out_shapes,
        in_specs=in_specs,
        out_specs=tuple(pl.BlockSpec(memory_space=pltpu.VMEM) for _ in out_shapes),
        compiler_params=pltpu.CompilerParams(vmem_limit_bytes=48 * 1024 * 1024),
    )


def shards(inputs, cotangent, w_send, w_recv, w_message, w_node, w_aggregate, gains,
           edge_send, edge_recv, edge_count, halo_send):
    sections = lax.axis_size("pipe")
    parts = lax.axis_size("dom")
    p_idx = lax.axis_index("pipe")
    micro, own, latent = inputs.shape
    block = edge_send.shape[1]
    span = halo_send.shape[2] * block
    ext_rows = own + 2 * span
    weights = (w_send[0], w_recv[0], w_message[0], w_node[0], w_aggregate[0])
    gain = gains[0].reshape(1, latent)
    hs = halo_send[0].reshape(-1).astype(jnp.int32)

    snd = edge_send.reshape(-1)
    rcv = edge_recv.reshape(-1)
    live = (jnp.arange(block)[None, :] < edge_count[:, None]).reshape(-1)
    osnd = (snd[:, None] == jnp.arange(ext_rows)[None, :]).astype(BF16)
    orcv_b = rcv[:, None] == jnp.arange(own)[None, :]
    orcv = orcv_b.astype(BF16)
    orcvl_b = orcv_b & live[:, None]
    orcvl = orcvl_b.astype(BF16)
    orcvt = orcvl_b.T.astype(BF16)
    osndt = osnd.T

    def blocks_of(x):
        shaped = x.reshape(micro, own // block, block, latent)
        nxt = jnp.take(shaped, hs[0], axis=1)
        prv = jnp.take(shaped, hs[1], axis=1)
        return nxt, prv

    S, D = sections, parts

    def perm_pipe(shift):
        return [(i, (i + shift) % S) for i in range(S)]

    def perm_both(dshift, pshift):
        return [(d * S + p, ((d + dshift) % D) * S + (p + pshift) % S)
                for d in range(D) for p in range(S)]

    both = ("dom", "pipe")

    fwd = vmem_call(
        fwd_kernel,
        (jax.ShapeDtypeStruct((micro, own, latent), BF16),
         jax.ShapeDtypeStruct((micro, own, latent), F32),
         jax.ShapeDtypeStruct((micro, own, latent), F32),
         jax.ShapeDtypeStruct((micro, span, latent), BF16),
         jax.ShapeDtypeStruct((micro, span, latent), BF16)),
        13)
    bwd = vmem_call(
        bwd_kernel,
        (jax.ShapeDtypeStruct((micro, own, latent), F32),
         jax.ShapeDtypeStruct((micro, own, latent), BF16),
         jax.ShapeDtypeStruct((micro, 2 * span, latent), BF16)),
        15)

    nxt0, prv0 = blocks_of(inputs)
    from_prev, from_next = exchange(
        [(0, None, span, 1, 0), (1, None, span, -1, 0)], (nxt0, prv0), D, S, 0)
    h = inputs
    out_rec = a_rec = u_rec = None
    for t in range(S):
        out, a, u, hn, hp = fwd(hs, h, from_prev, from_next, osnd, orcv, orcvt, *weights, gain)
        here = p_idx == t
        if t == 0:
            out_rec, a_rec, u_rec = out, a, u
        else:
            out_rec = jnp.where(here, out, out_rec)
            a_rec = jnp.where(here, a, a_rec)
            u_rec = jnp.where(here, u, u_rec)
        if t < S - 1:
            h, from_prev, from_next = exchange(
                [(0, None, own, 0, 1), (1, None, span, 1, 1), (2, None, span, -1, 1)],
                (out, hn, hp), D, S, 1)

    pin = cotangent
    zeros = jnp.zeros((micro, span, latent), BF16)
    g_next = g_prev = zeros
    grad_rec = None
    for t in range(S - 1, -1, -1):
        p32, p16, hg = bwd(hs, pin, g_next, g_prev, a_rec, u_rec, osndt, orcvl, orcvt, *weights, gain)
        if t > 0:
            sn, sp, pin, g_next, g_prev = exchange(
                [(1, 0, span, -1, 0), (1, span, span, 1, 0), (0, None, own, 0, -1),
                 (1, 0, span, -1, -1), (1, span, span, 1, -1)],
                (p16, hg), D, S, 2)
        else:
            sn, sp = exchange([(0, 0, span, -1, 0), (0, span, span, 1, 0)], (hg,), D, S, 3)
        shaped = p32.reshape(micro, own // block, block, latent)
        sel = jnp.arange(own // block)[None, :, None, None]
        summed = (shaped + jnp.where(sel == hs[0], sn.astype(F32)[:, None], 0.0)
                  + jnp.where(sel == hs[1], sp.astype(F32)[:, None], 0.0))
        grad = summed.reshape(micro, own, latent).astype(BF16)
        here = p_idx == t
        grad_rec = grad if t == S - 1 else jnp.where(here, grad, grad_rec)
    return (out_rec[None], grad_rec[None])


def solution(mesh):
    in_specs = (
        P(None, "dom", None),
        P(None, "dom", None),
        P("pipe", None, None),
        P("pipe", None, None),
        P("pipe", None, None),
        P("pipe", None, None),
        P("pipe", None, None),
        P("pipe", None),
        P("dom", None),
        P("dom", None),
        P("dom"),
        P("dom", None, None),
    )
    out_specs = (P("pipe", None, "dom", None), P("pipe", None, "dom", None))
    return jax.shard_map(shards, mesh=mesh, in_specs=in_specs, out_specs=out_specs, check_vma=False)
```

```python
import functools

import jax
import jax.numpy as jnp
from jax import lax
from jax.experimental import pallas as pl
from jax.experimental.pallas import tpu as pltpu
from jax.sharding import PartitionSpec as P

EPSILON = 1e-05
F32 = jnp.float32
BF16 = jnp.bfloat16


def mm(x, w):
    return jnp.dot(x, w, preferred_element_type=F32)


def mm_t(x, w):
    return lax.dot_general(x, w, (((1,), (1,)), ((), ())), preferred_element_type=F32)


def sigmoid(v):
    return 1.0 / (1.0 + jnp.exp(-v))


def split_sum(onehot, values):
    hi = values.astype(BF16)
    lo = (values - hi.astype(F32)).astype(BF16)
    return mm(onehot, hi) + mm(onehot, lo)


def fwd_kernel(hs_ref, h_ref, fp_ref, fn_ref, osnd_ref, orcv_ref, orcvt_ref,
               ws_ref, wr_ref, wm_ref, wn_ref, wa_ref, g_ref,
               out_ref, a_ref, u_ref, hn_ref, hp_ref):
    own = h_ref.shape[1]
    span = fp_ref.shape[1]
    block = span
    gain = g_ref[...]
    osnd = osnd_ref[...]
    for m in range(h_ref.shape[0]):
        h = h_ref[m]
        gathered = (mm(osnd[:, :own], h) + mm(osnd[:, own:own + span], fp_ref[m])
                    + mm(osnd[:, own + span:], fn_ref[m])).astype(BF16)
        send_part = mm(gathered, ws_ref[...]).astype(BF16).astype(F32)
        recv_rows = mm(orcv_ref[...], h).astype(BF16)
        pre = send_part + mm(recv_rows, wr_ref[...])
        a_ref[m] = pre
        edge_hidden = (pre * sigmoid(pre)).astype(BF16)
        messages = mm(edge_hidden, wm_ref[...])
        agg = split_sum(orcvt_ref[...], messages).astype(BF16)
        node_pre = mm(h, wn_ref[...]) + mm(agg, wa_ref[...])
        u_ref[m] = node_pre
        act = node_pre * sigmoid(node_pre)
        mean = jnp.mean(act, axis=-1, keepdims=True)
        cen = act - mean
        var = jnp.mean(cen * cen, axis=-1, keepdims=True)
        unit = cen * lax.rsqrt(var + EPSILON)
        out = (h.astype(F32) + unit * gain).astype(BF16)
        out_ref[m] = out
        hs0 = hs_ref[0]
        hs1 = hs_ref[1]
        nblocks = own // block
        sel_n = out[0:block]
        sel_p = out[0:block]
        for b in range(1, nblocks):
            piece = out[b * block:(b + 1) * block]
            sel_n = jnp.where(hs0 == b, piece, sel_n)
            sel_p = jnp.where(hs1 == b, piece, sel_p)
        hn_ref[m] = sel_n
        hp_ref[m] = sel_p


def bwd_kernel(hs_ref, pin_ref, a_ref, u_ref, osndt_ref, orcvl_ref, orcvt_ref,
               ws_ref, wr_ref, wm_ref, wn_ref, wa_ref, g_ref,
               p32_ref, hg_ref):
    own = pin_ref.shape[1]
    gain = g_ref[...]
    osndt = osndt_ref[...]
    for m in range(pin_ref.shape[0]):
        c = pin_ref[m].astype(F32)
        node_pre = u_ref[m]
        sig_u = sigmoid(node_pre)
        act = node_pre * sig_u
        mean = jnp.mean(act, axis=-1, keepdims=True)
        cen = act - mean
        var = jnp.mean(cen * cen, axis=-1, keepdims=True)
        rs = lax.rsqrt(var + EPSILON)
        unit = cen * rs
        gu = c * gain
        gact = rs * (gu - jnp.mean(gu, axis=-1, keepdims=True)
                     - unit * jnp.mean(gu * unit, axis=-1, keepdims=True))
        du = (gact * (sig_u * (1.0 + node_pre * (1.0 - sig_u)))).astype(BF16)
        dagg = mm_t(du, wa_ref[...]).astype(BF16)
        rows = c + mm_t(du, wn_ref[...])
        gmsg = mm(orcvl_ref[...], dagg).astype(BF16)
        pre = a_ref[m]
        sig_a = sigmoid(pre)
        dedge = (mm_t(gmsg, wm_ref[...]) * (sig_a * (1.0 + pre * (1.0 - sig_a)))).astype(BF16)
        rows = rows + split_sum(orcvt_ref[...], mm_t(dedge, wr_ref[...]))
        send_rows = split_sum(osndt, mm_t(dedge, ws_ref[...]))
        total = rows + send_rows[:own]
        p32_ref[m] = total
        hg_ref[m] = send_rows[own:].astype(BF16)


MESH_ID = pl.DeviceIdType.MESH


def comm_kernel(sends, n_in, parts, sections, *refs):
    ins = refs[:n_in]
    outs = refs[n_in:n_in + len(sends)]
    send_sem, recv_sem = refs[n_in + len(sends):]
    d = lax.axis_index("dom")
    p = lax.axis_index("pipe")
    barrier = pltpu.get_barrier_semaphore()
    for _, _, _, dd, dp in sends:
        src = (lax.rem(d - dd + parts, parts), lax.rem(p - dp + sections, sections))
        pl.semaphore_signal(barrier, 1, device_id=src, device_id_type=MESH_ID)
    pl.semaphore_wait(barrier, len(sends))
    copies = []
    for i, (k, start, rows, dd, dp) in enumerate(sends):
        dst = (lax.rem(d + dd + parts, parts), lax.rem(p + dp + sections, sections))
        source = ins[k] if start is None else ins[k].at[:, pl.ds(start, rows)]
        copy = pltpu.make_async_remote_copy(
            src_ref=source, dst_ref=outs[i], send_sem=send_sem.at[i], recv_sem=recv_sem.at[i],
            device_id=dst, device_id_type=MESH_ID)
        copy.start()
        copies.append(copy)
    for copy in copies:
        copy.wait()


def exchange(sends, payloads, parts, sections, cid):
    out_shapes = []
    for k, start, rows, _, _ in sends:
        shape = payloads[k].shape
        if start is not None:
            shape = (shape[0], rows) + shape[2:]
        out_shapes.append(jax.ShapeDtypeStruct(shape, payloads[k].dtype))
    n = len(sends)
    return pl.pallas_call(
        functools.partial(comm_kernel, tuple(sends), len(payloads), parts, sections),
        out_shape=tuple(out_shapes),
        in_specs=[pl.BlockSpec(memory_space=pl.ANY)] * len(payloads),
        out_specs=tuple(pl.BlockSpec(memory_space=pl.ANY) for _ in sends),
        scratch_shapes=[pltpu.SemaphoreType.DMA((n,)), pltpu.SemaphoreType.DMA((n,))],
        compiler_params=pltpu.CompilerParams(collective_id=cid, has_side_effects=True),
    )(*payloads)


def vmem_call(kernel, out_shapes, n_in, smem_first=True):
    in_specs = [pl.BlockSpec(memory_space=pltpu.SMEM)] + [pl.BlockSpec(memory_space=pltpu.VMEM)] * (n_in - 1)
    return pl.pallas_call(
        kernel,
        out_shape=out_shapes,
        in_specs=in_specs,
        out_specs=tuple(pl.BlockSpec(memory_space=pltpu.VMEM) for _ in out_shapes),
        compiler_params=pltpu.CompilerParams(vmem_limit_bytes=48 * 1024 * 1024),
    )


def shards(inputs, cotangent, w_send, w_recv, w_message, w_node, w_aggregate, gains,
           edge_send, edge_recv, edge_count, halo_send):
    sections = lax.axis_size("pipe")
    parts = lax.axis_size("dom")
    p_idx = lax.axis_index("pipe")
    micro, own, latent = inputs.shape
    block = edge_send.shape[1]
    span = halo_send.shape[2] * block
    ext_rows = own + 2 * span
    weights = (w_send[0], w_recv[0], w_message[0], w_node[0], w_aggregate[0])
    gain = gains[0].reshape(1, latent)
    hs = halo_send[0].reshape(-1).astype(jnp.int32)

    snd = edge_send.reshape(-1)
    rcv = edge_recv.reshape(-1)
    live = (jnp.arange(block)[None, :] < edge_count[:, None]).reshape(-1)
    osnd = (snd[:, None] == jnp.arange(ext_rows)[None, :]).astype(BF16)
    orcv_b = rcv[:, None] == jnp.arange(own)[None, :]
    orcv = orcv_b.astype(BF16)
    orcvl_b = orcv_b & live[:, None]
    orcvl = orcvl_b.astype(BF16)
    orcvt = orcvl_b.T.astype(BF16)
    osndt = osnd.T

    def blocks_of(x):
        shaped = x.reshape(micro, own // block, block, latent)
        nxt = jnp.take(shaped, hs[0], axis=1)
        prv = jnp.take(shaped, hs[1], axis=1)
        return nxt, prv

    S, D = sections, parts

    def perm_pipe(shift):
        return [(i, (i + shift) % S) for i in range(S)]

    def perm_both(dshift, pshift):
        return [(d * S + p, ((d + dshift) % D) * S + (p + pshift) % S)
                for d in range(D) for p in range(S)]

    both = ("dom", "pipe")

    fwd = vmem_call(
        fwd_kernel,
        (jax.ShapeDtypeStruct((micro, own, latent), BF16),
         jax.ShapeDtypeStruct((micro, own, latent), F32),
         jax.ShapeDtypeStruct((micro, own, latent), F32),
         jax.ShapeDtypeStruct((micro, span, latent), BF16),
         jax.ShapeDtypeStruct((micro, span, latent), BF16)),
        13)
    bwd = vmem_call(
        bwd_kernel,
        (jax.ShapeDtypeStruct((micro, own, latent), F32),
         jax.ShapeDtypeStruct((micro, 2 * span, latent), BF16)),
        13)

    nxt0, prv0 = blocks_of(inputs)
    halo_fwd = [(0, None, span, 1, 0), (1, None, span, -1, 0)]
    from_prev, from_next = exchange(halo_fwd, (nxt0, prv0), D, S, 0)
    h = inputs
    out_rec = a_rec = u_rec = None
    for t in range(S):
        out, a, u, hn, hp = fwd(hs, h, from_prev, from_next, osnd, orcv, orcvt, *weights, gain)
        here = p_idx == t
        if t == 0:
            out_rec, a_rec, u_rec = out, a, u
        else:
            out_rec = jnp.where(here, out, out_rec)
            a_rec = jnp.where(here, a, a_rec)
            u_rec = jnp.where(here, u, u_rec)
        if t < S - 1:
            (h,) = exchange([(0, None, own, 0, 1)], (out,), D, S, 1)
            nxt, prv = blocks_of(h)
            from_prev, from_next = exchange(halo_fwd, (nxt, prv), D, S, 0)

    pin = cotangent
    grad_rec = None
    for t in range(S - 1, -1, -1):
        p32, hg = bwd(hs, pin, a_rec, u_rec, osndt, orcvl, orcvt, *weights, gain)
        sn, sp = exchange([(0, 0, span, -1, 0), (0, span, span, 1, 0)], (hg,), D, S, 2)
        shaped = p32.reshape(micro, own // block, block, latent)
        sel = jnp.arange(own // block)[None, :, None, None]
        summed = (shaped + jnp.where(sel == hs[0], sn.astype(F32)[:, None], 0.0)
                  + jnp.where(sel == hs[1], sp.astype(F32)[:, None], 0.0))
        grad = summed.reshape(micro, own, latent).astype(BF16)
        here = p_idx == t
        grad_rec = grad if t == S - 1 else jnp.where(here, grad, grad_rec)
        if t > 0:
            (pin,) = exchange([(0, None, own, 0, -1)], (grad,), D, S, 3)
    return (out_rec[None], grad_rec[None])


def solution(mesh):
    in_specs = (
        P(None, "dom", None),
        P(None, "dom", None),
        P("pipe", None, None),
        P("pipe", None, None),
        P("pipe", None, None),
        P("pipe", None, None),
        P("pipe", None, None),
        P("pipe", None),
        P("dom", None),
        P("dom", None),
        P("dom"),
        P("dom", None, None),
    )
    out_specs = (P("pipe", None, "dom", None), P("pipe", None, "dom", None))
    return jax.shard_map(shards, mesh=mesh, in_specs=in_specs, out_specs=out_specs, check_vma=False)
```

```python
import functools

import jax
import jax.numpy as jnp
from jax import lax
from jax.experimental import pallas as pl
from jax.experimental.pallas import tpu as pltpu
from jax.sharding import PartitionSpec as P

EPSILON = 1e-05
F32 = jnp.float32
BF16 = jnp.bfloat16


def mm(x, w):
    return jnp.dot(x, w, preferred_element_type=F32)


def mm_t(x, w):
    return lax.dot_general(x, w, (((1,), (1,)), ((), ())), preferred_element_type=F32)


def sigmoid(v):
    return 1.0 / (1.0 + jnp.exp(-v))


def split_sum(onehot, values):
    hi = values.astype(BF16)
    lo = (values - hi.astype(F32)).astype(BF16)
    return mm(onehot, hi) + mm(onehot, lo)


def fwd_kernel(hs_ref, h_ref, fp_ref, fn_ref, osnd_ref, orcv_ref, orcvt_ref,
               ws_ref, wr_ref, wm_ref, wn_ref, wa_ref, g_ref,
               out_ref, a_ref, u_ref, hn_ref, hp_ref):
    own = h_ref.shape[1]
    span = fp_ref.shape[1]
    block = span
    gain = g_ref[...]
    osnd = osnd_ref[...]
    for m in range(h_ref.shape[0]):
        h = h_ref[m]
        gathered = (mm(osnd[:, :own], h) + mm(osnd[:, own:own + span], fp_ref[m])
                    + mm(osnd[:, own + span:], fn_ref[m])).astype(BF16)
        send_part = mm(gathered, ws_ref[...]).astype(BF16).astype(F32)
        recv_rows = mm(orcv_ref[...], h).astype(BF16)
        pre = send_part + mm(recv_rows, wr_ref[...])
        a_ref[m] = pre
        edge_hidden = (pre * sigmoid(pre)).astype(BF16)
        messages = mm(edge_hidden, wm_ref[...])
        agg = split_sum(orcvt_ref[...], messages).astype(BF16)
        node_pre = mm(h, wn_ref[...]) + mm(agg, wa_ref[...])
        u_ref[m] = node_pre
        act = node_pre * sigmoid(node_pre)
        mean = jnp.mean(act, axis=-1, keepdims=True)
        cen = act - mean
        var = jnp.mean(cen * cen, axis=-1, keepdims=True)
        unit = cen * lax.rsqrt(var + EPSILON)
        out = (h.astype(F32) + unit * gain).astype(BF16)
        out_ref[m] = out
        hs0 = hs_ref[0]
        hs1 = hs_ref[1]
        nblocks = own // block
        sel_n = out[0:block]
        sel_p = out[0:block]
        for b in range(1, nblocks):
            piece = out[b * block:(b + 1) * block]
            sel_n = jnp.where(hs0 == b, piece, sel_n)
            sel_p = jnp.where(hs1 == b, piece, sel_p)
        hn_ref[m] = sel_n
        hp_ref[m] = sel_p


def bwd_kernel(hs_ref, pin_ref, a_ref, u_ref, osndt_ref, orcvl_ref, orcvt_ref,
               ws_ref, wr_ref, wm_ref, wn_ref, wa_ref, g_ref,
               p32_ref, hg_ref):
    own = pin_ref.shape[1]
    gain = g_ref[...]
    osndt = osndt_ref[...]
    for m in range(pin_ref.shape[0]):
        c = pin_ref[m].astype(F32)
        node_pre = u_ref[m]
        sig_u = sigmoid(node_pre)
        act = node_pre * sig_u
        mean = jnp.mean(act, axis=-1, keepdims=True)
        cen = act - mean
        var = jnp.mean(cen * cen, axis=-1, keepdims=True)
        rs = lax.rsqrt(var + EPSILON)
        unit = cen * rs
        gu = c * gain
        gact = rs * (gu - jnp.mean(gu, axis=-1, keepdims=True)
                     - unit * jnp.mean(gu * unit, axis=-1, keepdims=True))
        du = (gact * (sig_u * (1.0 + node_pre * (1.0 - sig_u)))).astype(BF16)
        dagg = mm_t(du, wa_ref[...]).astype(BF16)
        rows = c + mm_t(du, wn_ref[...])
        gmsg = mm(orcvl_ref[...], dagg).astype(BF16)
        pre = a_ref[m]
        sig_a = sigmoid(pre)
        dedge = (mm_t(gmsg, wm_ref[...]) * (sig_a * (1.0 + pre * (1.0 - sig_a)))).astype(BF16)
        rows = rows + split_sum(orcvt_ref[...], mm_t(dedge, wr_ref[...]))
        send_rows = split_sum(osndt, mm_t(dedge, ws_ref[...]))
        total = rows + send_rows[:own]
        p32_ref[m] = total
        hg_ref[m] = send_rows[own:].astype(BF16)


MESH_ID = pl.DeviceIdType.MESH


def comm_kernel(sends, n_in, parts, sections, *refs):
    ins = refs[:n_in]
    outs = refs[n_in:n_in + len(sends)]
    send_sem, recv_sem = refs[n_in + len(sends):]
    d = lax.axis_index("dom")
    p = lax.axis_index("pipe")
    barrier = pltpu.get_barrier_semaphore()
    for _, _, _, dd, dp in sends:
        src = (lax.rem(d - dd + parts, parts), lax.rem(p - dp + sections, sections))
        pl.semaphore_signal(barrier, 1, device_id=src, device_id_type=MESH_ID)
    pl.semaphore_wait(barrier, len(sends))
    copies = []
    for i, (k, start, rows, dd, dp) in enumerate(sends):
        dst = (lax.rem(d + dd + parts, parts), lax.rem(p + dp + sections, sections))
        source = ins[k] if start is None else ins[k].at[:, pl.ds(start, rows)]
        copy = pltpu.make_async_remote_copy(
            src_ref=source, dst_ref=outs[i], send_sem=send_sem.at[i], recv_sem=recv_sem.at[i],
            device_id=dst, device_id_type=MESH_ID)
        copy.start()
        copies.append(copy)
    for copy in copies:
        copy.wait()


def exchange(sends, payloads, parts, sections, cid):
    out_shapes = []
    for k, start, rows, _, _ in sends:
        shape = payloads[k].shape
        if start is not None:
            shape = (shape[0], rows) + shape[2:]
        out_shapes.append(jax.ShapeDtypeStruct(shape, payloads[k].dtype))
    n = len(sends)
    return pl.pallas_call(
        functools.partial(comm_kernel, tuple(sends), len(payloads), parts, sections),
        out_shape=tuple(out_shapes),
        in_specs=[pl.BlockSpec(memory_space=pl.ANY)] * len(payloads),
        out_specs=tuple(pl.BlockSpec(memory_space=pl.ANY) for _ in sends),
        scratch_shapes=[pltpu.SemaphoreType.DMA((n,)), pltpu.SemaphoreType.DMA((n,))],
        compiler_params=pltpu.CompilerParams(collective_id=cid, has_side_effects=True),
    )(*payloads)


def fwd_comm_kernel(parts, sections, hs_ref, out_ref, h_ref, fp_ref, fn_ref,
                    hbuf, fpbuf, fnbuf, stage_n, stage_p, send_sem, recv_sem):
    micro, own, _ = out_ref.shape
    block = fp_ref.shape[1]
    d = lax.axis_index("dom")
    p = lax.axis_index("pipe")
    pipe_next = (d, lax.rem(p + 1, sections))
    pipe_prev = (d, lax.rem(p - 1 + sections, sections))
    dom_next = (lax.rem(d + 1, parts), p)
    dom_prev = (lax.rem(d - 1 + parts, parts), p)
    barrier = pltpu.get_barrier_semaphore()
    for src in (pipe_prev, dom_prev, dom_next):
        pl.semaphore_signal(barrier, 1, device_id=src, device_id_type=MESH_ID)
    pl.semaphore_wait(barrier, 3)
    pipe_copies = []
    for m in range(micro):
        copy = pltpu.make_async_remote_copy(
            src_ref=out_ref.at[m], dst_ref=hbuf.at[m], send_sem=send_sem.at[0, m],
            recv_sem=recv_sem.at[0, m], device_id=pipe_next, device_id_type=MESH_ID)
        copy.start()
        pipe_copies.append(copy)
    hs0 = hs_ref[0]
    hs1 = hs_ref[1]
    halo_copies = []
    for m in range(micro):
        pipe_copies[m].wait_recv()
        h = hbuf[m]
        sel_n = h[0:block]
        sel_p = h[0:block]
        for b in range(1, own // block):
            piece = h[b * block:(b + 1) * block]
            sel_n = jnp.where(hs0 == b, piece, sel_n)
            sel_p = jnp.where(hs1 == b, piece, sel_p)
        stage_n[m] = sel_n
        stage_p[m] = sel_p
        for j, (stage, buf, dst) in enumerate(((stage_n, fpbuf, dom_next), (stage_p, fnbuf, dom_prev))):
            copy = pltpu.make_async_remote_copy(
                src_ref=stage.at[m], dst_ref=buf.at[m], send_sem=send_sem.at[1 + j, m],
                recv_sem=recv_sem.at[1 + j, m], device_id=dst, device_id_type=MESH_ID)
            copy.start()
            halo_copies.append(copy)
    for copy in pipe_copies:
        copy.wait_send()
    for copy in halo_copies:
        copy.wait()
    h_ref[...] = hbuf[...]
    fp_ref[...] = fpbuf[...]
    fn_ref[...] = fnbuf[...]


def fwd_comm(hs, out, span, parts, sections):
    micro, own, latent = out.shape
    vm = pl.BlockSpec(memory_space=pltpu.VMEM)
    return pl.pallas_call(
        functools.partial(fwd_comm_kernel, parts, sections),
        out_shape=(jax.ShapeDtypeStruct((micro, own, latent), out.dtype),
                   jax.ShapeDtypeStruct((micro, span, latent), out.dtype),
                   jax.ShapeDtypeStruct((micro, span, latent), out.dtype)),
        in_specs=[pl.BlockSpec(memory_space=pltpu.SMEM), vm],
        out_specs=(vm, vm, vm),
        scratch_shapes=[pltpu.VMEM((micro, own, latent), out.dtype),
                        pltpu.VMEM((micro, span, latent), out.dtype),
                        pltpu.VMEM((micro, span, latent), out.dtype),
                        pltpu.VMEM((micro, span, latent), out.dtype),
                        pltpu.VMEM((micro, span, latent), out.dtype),
                        pltpu.SemaphoreType.DMA((3, micro)),
                        pltpu.SemaphoreType.DMA((3, micro))],
        compiler_params=pltpu.CompilerParams(collective_id=4, has_side_effects=True,
                                             vmem_limit_bytes=48 * 1024 * 1024),
    )(hs, out)


def bwd_comm_kernel(parts, sections, send_pipe, hs_ref, p32_ref, hg_ref, *refs):
    if send_pipe:
        grad_ref, pin_ref, snbuf, spbuf, gbuf, pinbuf, send_sem, recv_sem = refs
    else:
        grad_ref, snbuf, spbuf, gbuf, send_sem, recv_sem = refs
    micro, own, _ = p32_ref.shape
    block = snbuf.shape[1]
    d = lax.axis_index("dom")
    p = lax.axis_index("pipe")
    pipe_prev = (d, lax.rem(p - 1 + sections, sections))
    pipe_next = (d, lax.rem(p + 1, sections))
    dom_next = (lax.rem(d + 1, parts), p)
    dom_prev = (lax.rem(d - 1 + parts, parts), p)
    barrier = pltpu.get_barrier_semaphore()
    sources = [dom_next, dom_prev] + ([pipe_next] if send_pipe else [])
    for src in sources:
        pl.semaphore_signal(barrier, 1, device_id=src, device_id_type=MESH_ID)
    pl.semaphore_wait(barrier, len(sources))
    halo_copies = []
    for m in range(micro):
        pair = []
        for j, (lo, buf, dst) in enumerate(((0, snbuf, dom_prev), (block, spbuf, dom_next))):
            copy = pltpu.make_async_remote_copy(
                src_ref=hg_ref.at[m, pl.ds(lo, block)], dst_ref=buf.at[m],
                send_sem=send_sem.at[j, m], recv_sem=recv_sem.at[j, m],
                device_id=dst, device_id_type=MESH_ID)
            copy.start()
            pair.append(copy)
        halo_copies.append(pair)
    hs0 = hs_ref[0]
    hs1 = hs_ref[1]
    pipe_copies = []
    for m in range(micro):
        for copy in halo_copies[m]:
            copy.wait_recv()
        sn = snbuf[m].astype(F32)
        sp = spbuf[m].astype(F32)
        for b in range(own // block):
            piece = p32_ref[m, b * block:(b + 1) * block]
            piece = piece + jnp.where(hs0 == b, sn, 0.0) + jnp.where(hs1 == b, sp, 0.0)
            gbuf[m, b * block:(b + 1) * block] = piece.astype(gbuf.dtype)
        if send_pipe:
            copy = pltpu.make_async_remote_copy(
                src_ref=gbuf.at[m], dst_ref=pinbuf.at[m], send_sem=send_sem.at[2, m],
                recv_sem=recv_sem.at[2, m], device_id=pipe_prev, device_id_type=MESH_ID)
            copy.start()
            pipe_copies.append(copy)
    for pair in halo_copies:
        for copy in pair:
            copy.wait_send()
    for copy in pipe_copies:
        copy.wait()
    grad_ref[...] = gbuf[...]
    if send_pipe:
        pin_ref[...] = pinbuf[...]


def bwd_comm(hs, p32, hg, span, parts, sections, send_pipe):
    micro, own, latent = p32.shape
    vm = pl.BlockSpec(memory_space=pltpu.VMEM)
    grad = jax.ShapeDtypeStruct((micro, own, latent), BF16)
    scratch = [pltpu.VMEM((micro, span, latent), BF16), pltpu.VMEM((micro, span, latent), BF16),
               pltpu.VMEM((micro, own, latent), BF16)]
    if send_pipe:
        scratch.append(pltpu.VMEM((micro, own, latent), BF16))
    scratch += [pltpu.SemaphoreType.DMA((3, micro)), pltpu.SemaphoreType.DMA((3, micro))]
    outs = (grad, grad) if send_pipe else (grad,)
    return pl.pallas_call(
        functools.partial(bwd_comm_kernel, parts, sections, send_pipe),
        out_shape=outs,
        in_specs=[pl.BlockSpec(memory_space=pltpu.SMEM), vm, vm],
        out_specs=tuple(vm for _ in outs),
        scratch_shapes=scratch,
        compiler_params=pltpu.CompilerParams(collective_id=5 if send_pipe else 6, has_side_effects=True,
                                             vmem_limit_bytes=48 * 1024 * 1024),
    )(hs, p32, hg)


def vmem_call(kernel, out_shapes, n_in, smem_first=True):
    in_specs = [pl.BlockSpec(memory_space=pltpu.SMEM)] + [pl.BlockSpec(memory_space=pltpu.VMEM)] * (n_in - 1)
    return pl.pallas_call(
        kernel,
        out_shape=out_shapes,
        in_specs=in_specs,
        out_specs=tuple(pl.BlockSpec(memory_space=pltpu.VMEM) for _ in out_shapes),
        compiler_params=pltpu.CompilerParams(vmem_limit_bytes=48 * 1024 * 1024),
    )


def shards(inputs, cotangent, w_send, w_recv, w_message, w_node, w_aggregate, gains,
           edge_send, edge_recv, edge_count, halo_send):
    sections = lax.axis_size("pipe")
    parts = lax.axis_size("dom")
    p_idx = lax.axis_index("pipe")
    micro, own, latent = inputs.shape
    block = edge_send.shape[1]
    span = halo_send.shape[2] * block
    ext_rows = own + 2 * span
    weights = (w_send[0], w_recv[0], w_message[0], w_node[0], w_aggregate[0])
    gain = gains[0].reshape(1, latent)
    hs = halo_send[0].reshape(-1).astype(jnp.int32)

    snd = edge_send.reshape(-1)
    rcv = edge_recv.reshape(-1)
    live = (jnp.arange(block)[None, :] < edge_count[:, None]).reshape(-1)
    osnd = (snd[:, None] == jnp.arange(ext_rows)[None, :]).astype(BF16)
    orcv_b = rcv[:, None] == jnp.arange(own)[None, :]
    orcv = orcv_b.astype(BF16)
    orcvl_b = orcv_b & live[:, None]
    orcvl = orcvl_b.astype(BF16)
    orcvt = orcvl_b.T.astype(BF16)
    osndt = osnd.T

    def blocks_of(x):
        shaped = x.reshape(micro, own // block, block, latent)
        nxt = jnp.take(shaped, hs[0], axis=1)
        prv = jnp.take(shaped, hs[1], axis=1)
        return nxt, prv

    S, D = sections, parts

    def perm_pipe(shift):
        return [(i, (i + shift) % S) for i in range(S)]

    def perm_both(dshift, pshift):
        return [(d * S + p, ((d + dshift) % D) * S + (p + pshift) % S)
                for d in range(D) for p in range(S)]

    both = ("dom", "pipe")

    fwd = vmem_call(
        fwd_kernel,
        (jax.ShapeDtypeStruct((micro, own, latent), BF16),
         jax.ShapeDtypeStruct((micro, own, latent), F32),
         jax.ShapeDtypeStruct((micro, own, latent), F32),
         jax.ShapeDtypeStruct((micro, span, latent), BF16),
         jax.ShapeDtypeStruct((micro, span, latent), BF16)),
        13)
    bwd = vmem_call(
        bwd_kernel,
        (jax.ShapeDtypeStruct((micro, own, latent), F32),
         jax.ShapeDtypeStruct((micro, 2 * span, latent), BF16)),
        13)

    nxt0, prv0 = blocks_of(inputs)
    halo_fwd = [(0, None, span, 1, 0), (1, None, span, -1, 0)]
    from_prev, from_next = exchange(halo_fwd, (nxt0, prv0), D, S, 0)
    h = inputs
    out_rec = a_rec = u_rec = None
    for t in range(S):
        out, a, u, hn, hp = fwd(hs, h, from_prev, from_next, osnd, orcv, orcvt, *weights, gain)
        here = p_idx == t
        if t == 0:
            out_rec, a_rec, u_rec = out, a, u
        else:
            out_rec = jnp.where(here, out, out_rec)
            a_rec = jnp.where(here, a, a_rec)
            u_rec = jnp.where(here, u, u_rec)
        if t < S - 1:
            h, from_prev, from_next = fwd_comm(hs, out, span, D, S)

    pin = cotangent
    grad_rec = None
    for t in range(S - 1, -1, -1):
        p32, hg = bwd(hs, pin, a_rec, u_rec, osndt, orcvl, orcvt, *weights, gain)
        if t > 0:
            grad, pin = bwd_comm(hs, p32, hg, span, D, S, True)
        else:
            (grad,) = bwd_comm(hs, p32, hg, span, D, S, False)
        here = p_idx == t
        grad_rec = grad if t == S - 1 else jnp.where(here, grad, grad_rec)
    return (out_rec[None], grad_rec[None])


def solution(mesh):
    in_specs = (
        P(None, "dom", None),
        P(None, "dom", None),
        P("pipe", None, None),
        P("pipe", None, None),
        P("pipe", None, None),
        P("pipe", None, None),
        P("pipe", None, None),
        P("pipe", None),
        P("dom", None),
        P("dom", None),
        P("dom"),
        P("dom", None, None),
    )
    out_specs = (P("pipe", None, "dom", None), P("pipe", None, "dom", None))
    return jax.shard_map(shards, mesh=mesh, in_specs=in_specs, out_specs=out_specs, check_vma=False)
```

```python
import functools

import jax
import jax.numpy as jnp
from jax import lax
from jax.experimental import pallas as pl
from jax.experimental.pallas import tpu as pltpu
from jax.sharding import PartitionSpec as P

EPSILON = 1e-05
F32 = jnp.float32
BF16 = jnp.bfloat16


def mm(x, w):
    return jnp.dot(x, w, preferred_element_type=F32)


def mm_t(x, w):
    return lax.dot_general(x, w, (((1,), (1,)), ((), ())), preferred_element_type=F32)


def sigmoid(v):
    return 1.0 / (1.0 + jnp.exp(-v))


def split_sum(onehot, values):
    hi = values.astype(BF16)
    lo = (values - hi.astype(F32)).astype(BF16)
    return mm(onehot, hi) + mm(onehot, lo)


def fwd_micro(m, hs_ref, h_ref, fp_ref, fn_ref, osnd_ref, orcv_ref, orcvt_ref,
              ws_ref, wr_ref, wm_ref, wn_ref, wa_ref, g_ref, out_ref, a_ref, u_ref):
    own = h_ref.shape[1]
    span = fp_ref.shape[1]
    osnd = osnd_ref[...]
    h = h_ref[m]
    gathered = (mm(osnd[:, :own], h) + mm(osnd[:, own:own + span], fp_ref[m])
                + mm(osnd[:, own + span:], fn_ref[m])).astype(BF16)
    send_part = mm(gathered, ws_ref[...]).astype(BF16).astype(F32)
    recv_rows = mm(orcv_ref[...], h).astype(BF16)
    pre = send_part + mm(recv_rows, wr_ref[...])
    a_ref[m] = pre
    edge_hidden = (pre * sigmoid(pre)).astype(BF16)
    messages = mm(edge_hidden, wm_ref[...])
    agg = split_sum(orcvt_ref[...], messages).astype(BF16)
    node_pre = mm(h, wn_ref[...]) + mm(agg, wa_ref[...])
    u_ref[m] = node_pre
    act = node_pre * sigmoid(node_pre)
    mean = jnp.mean(act, axis=-1, keepdims=True)
    cen = act - mean
    var = jnp.mean(cen * cen, axis=-1, keepdims=True)
    unit = cen * lax.rsqrt(var + EPSILON)
    out_ref[m] = (h.astype(F32) + unit * g_ref[...]).astype(BF16)


def fwd_kernel(*refs):
    for m in range(refs[1].shape[0]):
        fwd_micro(m, *refs)


def bwd_micro(m, pin_ref, a_ref, u_ref, osndt_ref, orcvl_ref, orcvt_ref,
              ws_ref, wr_ref, wm_ref, wn_ref, wa_ref, g_ref, p32_ref, hg_ref):
    own = pin_ref.shape[1]
    gain = g_ref[...]
    c = pin_ref[m].astype(F32)
    node_pre = u_ref[m]
    sig_u = sigmoid(node_pre)
    act = node_pre * sig_u
    mean = jnp.mean(act, axis=-1, keepdims=True)
    cen = act - mean
    var = jnp.mean(cen * cen, axis=-1, keepdims=True)
    rs = lax.rsqrt(var + EPSILON)
    unit = cen * rs
    gu = c * gain
    gact = rs * (gu - jnp.mean(gu, axis=-1, keepdims=True)
                 - unit * jnp.mean(gu * unit, axis=-1, keepdims=True))
    du = (gact * (sig_u * (1.0 + node_pre * (1.0 - sig_u)))).astype(BF16)
    dagg = mm_t(du, wa_ref[...]).astype(BF16)
    rows = c + mm_t(du, wn_ref[...])
    gmsg = mm(orcvl_ref[...], dagg).astype(BF16)
    pre = a_ref[m]
    sig_a = sigmoid(pre)
    dedge = (mm_t(gmsg, wm_ref[...]) * (sig_a * (1.0 + pre * (1.0 - sig_a)))).astype(BF16)
    rows = rows + split_sum(orcvt_ref[...], mm_t(dedge, wr_ref[...]))
    send_rows = split_sum(osndt_ref[...], mm_t(dedge, ws_ref[...]))
    p32_ref[m] = rows + send_rows[:own]
    hg_ref[m] = send_rows[own:].astype(BF16)


MESH_ID = pl.DeviceIdType.MESH


def comm_kernel(sends, n_in, parts, sections, *refs):
    ins = refs[:n_in]
    outs = refs[n_in:n_in + len(sends)]
    send_sem, recv_sem = refs[n_in + len(sends):]
    d = lax.axis_index("dom")
    p = lax.axis_index("pipe")
    barrier = pltpu.get_barrier_semaphore()
    for _, _, _, dd, dp in sends:
        src = (lax.rem(d - dd + parts, parts), lax.rem(p - dp + sections, sections))
        pl.semaphore_signal(barrier, 1, device_id=src, device_id_type=MESH_ID)
    pl.semaphore_wait(barrier, len(sends))
    copies = []
    for i, (k, start, rows, dd, dp) in enumerate(sends):
        dst = (lax.rem(d + dd + parts, parts), lax.rem(p + dp + sections, sections))
        source = ins[k] if start is None else ins[k].at[:, pl.ds(start, rows)]
        copy = pltpu.make_async_remote_copy(
            src_ref=source, dst_ref=outs[i], send_sem=send_sem.at[i], recv_sem=recv_sem.at[i],
            device_id=dst, device_id_type=MESH_ID)
        copy.start()
        copies.append(copy)
    for copy in copies:
        copy.wait()


def exchange(sends, payloads, parts, sections, cid):
    out_shapes = []
    for k, start, rows, _, _ in sends:
        shape = payloads[k].shape
        if start is not None:
            shape = (shape[0], rows) + shape[2:]
        out_shapes.append(jax.ShapeDtypeStruct(shape, payloads[k].dtype))
    n = len(sends)
    return pl.pallas_call(
        functools.partial(comm_kernel, tuple(sends), len(payloads), parts, sections),
        out_shape=tuple(out_shapes),
        in_specs=[pl.BlockSpec(memory_space=pl.ANY)] * len(payloads),
        out_specs=tuple(pl.BlockSpec(memory_space=pl.ANY) for _ in sends),
        scratch_shapes=[pltpu.SemaphoreType.DMA((n,)), pltpu.SemaphoreType.DMA((n,))],
        compiler_params=pltpu.CompilerParams(collective_id=cid, has_side_effects=True),
    )(*payloads)


def fwd_tick_kernel(parts, sections, hs_ref, h_ref, fp_ref, fn_ref, osnd_ref, orcv_ref, orcvt_ref,
                    ws_ref, wr_ref, wm_ref, wn_ref, wa_ref, g_ref,
                    out_ref, a_ref, u_ref, hn_ref, fpn_ref, fnn_ref,
                    hbuf, fpbuf, fnbuf, stage_n, stage_p, send_sem, recv_sem):
    micro, own, _ = h_ref.shape
    block = fp_ref.shape[1]
    d = lax.axis_index("dom")
    p = lax.axis_index("pipe")
    pipe_next = (d, lax.rem(p + 1, sections))
    pipe_prev = (d, lax.rem(p - 1 + sections, sections))
    dom_next = (lax.rem(d + 1, parts), p)
    dom_prev = (lax.rem(d - 1 + parts, parts), p)
    barrier = pltpu.get_barrier_semaphore()
    for src in (pipe_prev, dom_prev, dom_next):
        pl.semaphore_signal(barrier, 1, device_id=src, device_id_type=MESH_ID)
    compute_refs = (hs_ref, h_ref, fp_ref, fn_ref, osnd_ref, orcv_ref, orcvt_ref,
                    ws_ref, wr_ref, wm_ref, wn_ref, wa_ref, g_ref, out_ref, a_ref, u_ref)
    pipe_copies = []
    for m in range(micro):
        fwd_micro(m, *compute_refs)
        if m == 0:
            pl.semaphore_wait(barrier, 3)
        copy = pltpu.make_async_remote_copy(
            src_ref=out_ref.at[m], dst_ref=hbuf.at[m], send_sem=send_sem.at[0, m],
            recv_sem=recv_sem.at[0, m], device_id=pipe_next, device_id_type=MESH_ID)
        copy.start()
        pipe_copies.append(copy)
    hs0 = hs_ref[0]
    hs1 = hs_ref[1]
    halo_copies = []
    for m in range(micro):
        pipe_copies[m].wait_recv()
        h = hbuf[m]
        sel_n = h[0:block]
        sel_p = h[0:block]
        for b in range(1, own // block):
            piece = h[b * block:(b + 1) * block]
            sel_n = jnp.where(hs0 == b, piece, sel_n)
            sel_p = jnp.where(hs1 == b, piece, sel_p)
        stage_n[m] = sel_n
        stage_p[m] = sel_p
        for j, (stage, buf, dst) in enumerate(((stage_n, fpbuf, dom_next), (stage_p, fnbuf, dom_prev))):
            copy = pltpu.make_async_remote_copy(
                src_ref=stage.at[m], dst_ref=buf.at[m], send_sem=send_sem.at[1 + j, m],
                recv_sem=recv_sem.at[1 + j, m], device_id=dst, device_id_type=MESH_ID)
            copy.start()
            halo_copies.append(copy)
    for copy in pipe_copies:
        copy.wait_send()
    for copy in halo_copies:
        copy.wait()
    hn_ref[...] = hbuf[...]
    fpn_ref[...] = fpbuf[...]
    fnn_ref[...] = fnbuf[...]


def fwd_tick(operands, span, parts, sections):
    h = operands[1]
    micro, own, latent = h.shape
    vm = pl.BlockSpec(memory_space=pltpu.VMEM)
    bf = lambda rows: jax.ShapeDtypeStruct((micro, rows, latent), BF16)
    f32 = jax.ShapeDtypeStruct((micro, own, latent), F32)
    return pl.pallas_call(
        functools.partial(fwd_tick_kernel, parts, sections),
        out_shape=(bf(own), f32, f32, bf(own), bf(span), bf(span)),
        in_specs=[pl.BlockSpec(memory_space=pltpu.SMEM)] + [vm] * (len(operands) - 1),
        out_specs=tuple(vm for _ in range(6)),
        scratch_shapes=[pltpu.VMEM((micro, own, latent), BF16),
                        pltpu.VMEM((micro, span, latent), BF16),
                        pltpu.VMEM((micro, span, latent), BF16),
                        pltpu.VMEM((micro, span, latent), BF16),
                        pltpu.VMEM((micro, span, latent), BF16),
                        pltpu.SemaphoreType.DMA((3, micro)),
                        pltpu.SemaphoreType.DMA((3, micro))],
        compiler_params=pltpu.CompilerParams(collective_id=4, has_side_effects=True,
                                             vmem_limit_bytes=48 * 1024 * 1024),
    )(*operands)


def bwd_tick_kernel(parts, sections, send_pipe, hs_ref, pin_ref, a_ref, u_ref, osndt_ref, orcvl_ref,
                    orcvt_ref, ws_ref, wr_ref, wm_ref, wn_ref, wa_ref, g_ref, *refs):
    if send_pipe:
        grad_ref, pinn_ref, p32, hg, snbuf, spbuf, gbuf, pinbuf, send_sem, recv_sem = refs
    else:
        grad_ref, p32, hg, snbuf, spbuf, gbuf, send_sem, recv_sem = refs
    micro, own, _ = pin_ref.shape
    block = snbuf.shape[1]
    d = lax.axis_index("dom")
    p = lax.axis_index("pipe")
    pipe_prev = (d, lax.rem(p - 1 + sections, sections))
    pipe_next = (d, lax.rem(p + 1, sections))
    dom_next = (lax.rem(d + 1, parts), p)
    dom_prev = (lax.rem(d - 1 + parts, parts), p)
    barrier = pltpu.get_barrier_semaphore()
    sources = [dom_next, dom_prev] + ([pipe_next] if send_pipe else [])
    for src in sources:
        pl.semaphore_signal(barrier, 1, device_id=src, device_id_type=MESH_ID)
    compute_refs = (pin_ref, a_ref, u_ref, osndt_ref, orcvl_ref, orcvt_ref,
                    ws_ref, wr_ref, wm_ref, wn_ref, wa_ref, g_ref, p32, hg)
    halo_copies = []
    for m in range(micro):
        bwd_micro(m, *compute_refs)
        if m == 0:
            pl.semaphore_wait(barrier, len(sources))
        pair = []
        for j, (lo, buf, dst) in enumerate(((0, snbuf, dom_prev), (block, spbuf, dom_next))):
            copy = pltpu.make_async_remote_copy(
                src_ref=hg.at[m, pl.ds(lo, block)], dst_ref=buf.at[m],
                send_sem=send_sem.at[j, m], recv_sem=recv_sem.at[j, m],
                device_id=dst, device_id_type=MESH_ID)
            copy.start()
            pair.append(copy)
        halo_copies.append(pair)
    hs0 = hs_ref[0]
    hs1 = hs_ref[1]
    pipe_copies = []
    for m in range(micro):
        for copy in halo_copies[m]:
            copy.wait_recv()
        sn = snbuf[m].astype(F32)
        sp = spbuf[m].astype(F32)
        for b in range(own // block):
            piece = p32[m, b * block:(b + 1) * block]
            piece = piece + jnp.where(hs0 == b, sn, 0.0) + jnp.where(hs1 == b, sp, 0.0)
            gbuf[m, b * block:(b + 1) * block] = piece.astype(gbuf.dtype)
        if send_pipe:
            copy = pltpu.make_async_remote_copy(
                src_ref=gbuf.at[m], dst_ref=pinbuf.at[m], send_sem=send_sem.at[2, m],
                recv_sem=recv_sem.at[2, m], device_id=pipe_prev, device_id_type=MESH_ID)
            copy.start()
            pipe_copies.append(copy)
    for pair in halo_copies:
        for copy in pair:
            copy.wait_send()
    for copy in pipe_copies:
        copy.wait()
    grad_ref[...] = gbuf[...]
    if send_pipe:
        pinn_ref[...] = pinbuf[...]


def bwd_tick(operands, span, parts, sections, send_pipe):
    pin = operands[1]
    micro, own, latent = pin.shape
    vm = pl.BlockSpec(memory_space=pltpu.VMEM)
    grad = jax.ShapeDtypeStruct((micro, own, latent), BF16)
    scratch = [pltpu.VMEM((micro, own, latent), F32), pltpu.VMEM((micro, 2 * span, latent), BF16),
               pltpu.VMEM((micro, span, latent), BF16), pltpu.VMEM((micro, span, latent), BF16),
               pltpu.VMEM((micro, own, latent), BF16)]
    if send_pipe:
        scratch.append(pltpu.VMEM((micro, own, latent), BF16))
    scratch += [pltpu.SemaphoreType.DMA((3, micro)), pltpu.SemaphoreType.DMA((3, micro))]
    outs = (grad, grad) if send_pipe else (grad,)
    return pl.pallas_call(
        functools.partial(bwd_tick_kernel, parts, sections, send_pipe),
        out_shape=outs,
        in_specs=[pl.BlockSpec(memory_space=pltpu.SMEM)] + [vm] * (len(operands) - 1),
        out_specs=tuple(vm for _ in outs),
        scratch_shapes=scratch,
        compiler_params=pltpu.CompilerParams(collective_id=5 if send_pipe else 6, has_side_effects=True,
                                             vmem_limit_bytes=48 * 1024 * 1024),
    )(*operands)


def vmem_call(kernel, out_shapes, n_in, smem_first=True):
    in_specs = [pl.BlockSpec(memory_space=pltpu.SMEM)] + [pl.BlockSpec(memory_space=pltpu.VMEM)] * (n_in - 1)
    return pl.pallas_call(
        kernel,
        out_shape=out_shapes,
        in_specs=in_specs,
        out_specs=tuple(pl.BlockSpec(memory_space=pltpu.VMEM) for _ in out_shapes),
        compiler_params=pltpu.CompilerParams(vmem_limit_bytes=48 * 1024 * 1024),
    )


def shards(inputs, cotangent, w_send, w_recv, w_message, w_node, w_aggregate, gains,
           edge_send, edge_recv, edge_count, halo_send):
    sections = lax.axis_size("pipe")
    parts = lax.axis_size("dom")
    p_idx = lax.axis_index("pipe")
    micro, own, latent = inputs.shape
    block = edge_send.shape[1]
    span = halo_send.shape[2] * block
    ext_rows = own + 2 * span
    weights = (w_send[0], w_recv[0], w_message[0], w_node[0], w_aggregate[0])
    gain = gains[0].reshape(1, latent)
    hs = halo_send[0].reshape(-1).astype(jnp.int32)

    snd = edge_send.reshape(-1)
    rcv = edge_recv.reshape(-1)
    live = (jnp.arange(block)[None, :] < edge_count[:, None]).reshape(-1)
    osnd = (snd[:, None] == jnp.arange(ext_rows)[None, :]).astype(BF16)
    orcv_b = rcv[:, None] == jnp.arange(own)[None, :]
    orcv = orcv_b.astype(BF16)
    orcvl_b = orcv_b & live[:, None]
    orcvl = orcvl_b.astype(BF16)
    orcvt = orcvl_b.T.astype(BF16)
    osndt = osnd.T

    def blocks_of(x):
        shaped = x.reshape(micro, own // block, block, latent)
        nxt = jnp.take(shaped, hs[0], axis=1)
        prv = jnp.take(shaped, hs[1], axis=1)
        return nxt, prv

    S, D = sections, parts

    def perm_pipe(shift):
        return [(i, (i + shift) % S) for i in range(S)]

    def perm_both(dshift, pshift):
        return [(d * S + p, ((d + dshift) % D) * S + (p + pshift) % S)
                for d in range(D) for p in range(S)]

    both = ("dom", "pipe")

    fwd = vmem_call(
        fwd_kernel,
        (jax.ShapeDtypeStruct((micro, own, latent), BF16),
         jax.ShapeDtypeStruct((micro, own, latent), F32),
         jax.ShapeDtypeStruct((micro, own, latent), F32)),
        13)

    nxt0, prv0 = blocks_of(inputs)
    halo_fwd = [(0, None, span, 1, 0), (1, None, span, -1, 0)]
    from_prev, from_next = exchange(halo_fwd, (nxt0, prv0), D, S, 0)
    h = inputs
    out_rec = a_rec = u_rec = None
    for t in range(S):
        operands = (hs, h, from_prev, from_next, osnd, orcv, orcvt, *weights, gain)
        if t < S - 1:
            out, a, u, h, from_prev, from_next = fwd_tick(operands, span, D, S)
        else:
            out, a, u = fwd(*operands)
        here = p_idx == t
        if t == 0:
            out_rec, a_rec, u_rec = out, a, u
        else:
            out_rec = jnp.where(here, out, out_rec)
            a_rec = jnp.where(here, a, a_rec)
            u_rec = jnp.where(here, u, u_rec)

    pin = cotangent
    grad_rec = None
    for t in range(S - 1, -1, -1):
        operands = (hs, pin, a_rec, u_rec, osndt, orcvl, orcvt, *weights, gain)
        if t > 0:
            grad, pin = bwd_tick(operands, span, D, S, True)
        else:
            (grad,) = bwd_tick(operands, span, D, S, False)
        here = p_idx == t
        grad_rec = grad if t == S - 1 else jnp.where(here, grad, grad_rec)
    return (out_rec[None], grad_rec[None])


def solution(mesh):
    in_specs = (
        P(None, "dom", None),
        P(None, "dom", None),
        P("pipe", None, None),
        P("pipe", None, None),
        P("pipe", None, None),
        P("pipe", None, None),
        P("pipe", None, None),
        P("pipe", None),
        P("dom", None),
        P("dom", None),
        P("dom"),
        P("dom", None, None),
    )
    out_specs = (P("pipe", None, "dom", None), P("pipe", None, "dom", None))
    return jax.shard_map(shards, mesh=mesh, in_specs=in_specs, out_specs=out_specs, check_vma=False)
```

```python
import functools

import jax
import jax.numpy as jnp
from jax import lax
from jax.experimental import pallas as pl
from jax.experimental.pallas import tpu as pltpu
from jax.sharding import PartitionSpec as P

EPSILON = 1e-05
F32 = jnp.float32
BF16 = jnp.bfloat16


def mm(x, w):
    return jnp.dot(x, w, preferred_element_type=F32)


def mm_t(x, w):
    return lax.dot_general(x, w, (((1,), (1,)), ((), ())), preferred_element_type=F32)


def sigmoid(v):
    return 1.0 / (1.0 + jnp.exp(-v))


def split_sum(onehot, values):
    hi = values.astype(BF16)
    lo = (values - hi.astype(F32)).astype(BF16)
    return mm(onehot, hi) + mm(onehot, lo)


def fwd_micro(m, hs_ref, h_ref, fp_ref, fn_ref, osnd_ref, orcv_ref, orcvt_ref,
              ws_ref, wr_ref, wm_ref, wn_ref, wa_ref, g_ref, out_ref, a_ref, u_ref):
    own = h_ref.shape[1]
    span = fp_ref.shape[1]
    osnd = osnd_ref[...]
    h = h_ref[m]
    gathered = (mm(osnd[:, :own], h) + mm(osnd[:, own:own + span], fp_ref[m])
                + mm(osnd[:, own + span:], fn_ref[m])).astype(BF16)
    send_part = mm(gathered, ws_ref[...]).astype(BF16).astype(F32)
    recv_rows = mm(orcv_ref[...], h).astype(BF16)
    pre = send_part + mm(recv_rows, wr_ref[...])
    a_ref[m] = pre
    edge_hidden = (pre * sigmoid(pre)).astype(BF16)
    messages = mm(edge_hidden, wm_ref[...])
    agg = split_sum(orcvt_ref[...], messages).astype(BF16)
    node_pre = mm(h, wn_ref[...]) + mm(agg, wa_ref[...])
    u_ref[m] = node_pre
    act = node_pre * sigmoid(node_pre)
    mean = jnp.mean(act, axis=-1, keepdims=True)
    cen = act - mean
    var = jnp.mean(cen * cen, axis=-1, keepdims=True)
    unit = cen * lax.rsqrt(var + EPSILON)
    out_ref[m] = (h.astype(F32) + unit * g_ref[...]).astype(BF16)


def fwd_kernel(*refs):
    for m in range(refs[1].shape[0]):
        fwd_micro(m, *refs)


def bwd_micro(m, pin_ref, a_ref, u_ref, osndt_ref, orcvl_ref, orcvt_ref,
              ws_ref, wr_ref, wm_ref, wn_ref, wa_ref, g_ref, p32_ref, hg_ref):
    own = pin_ref.shape[1]
    gain = g_ref[...]
    c = pin_ref[m].astype(F32)
    node_pre = u_ref[m]
    sig_u = sigmoid(node_pre)
    act = node_pre * sig_u
    mean = jnp.mean(act, axis=-1, keepdims=True)
    cen = act - mean
    var = jnp.mean(cen * cen, axis=-1, keepdims=True)
    rs = lax.rsqrt(var + EPSILON)
    unit = cen * rs
    gu = c * gain
    gact = rs * (gu - jnp.mean(gu, axis=-1, keepdims=True)
                 - unit * jnp.mean(gu * unit, axis=-1, keepdims=True))
    du = (gact * (sig_u * (1.0 + node_pre * (1.0 - sig_u)))).astype(BF16)
    dagg = mm_t(du, wa_ref[...]).astype(BF16)
    rows = c + mm_t(du, wn_ref[...])
    gmsg = mm(orcvl_ref[...], dagg).astype(BF16)
    pre = a_ref[m]
    sig_a = sigmoid(pre)
    dedge = (mm_t(gmsg, wm_ref[...]) * (sig_a * (1.0 + pre * (1.0 - sig_a)))).astype(BF16)
    rows = rows + split_sum(orcvt_ref[...], mm_t(dedge, wr_ref[...]))
    send_rows = split_sum(osndt_ref[...], mm_t(dedge, ws_ref[...]))
    p32_ref[m] = rows + send_rows[:own]
    hg_ref[m] = send_rows[own:].astype(BF16)


MESH_ID = pl.DeviceIdType.MESH


def comm_kernel(sends, n_in, parts, sections, *refs):
    ins = refs[:n_in]
    outs = refs[n_in:n_in + len(sends)]
    send_sem, recv_sem = refs[n_in + len(sends):]
    d = lax.axis_index("dom")
    p = lax.axis_index("pipe")
    barrier = pltpu.get_barrier_semaphore()
    for _, _, _, dd, dp in sends:
        src = (lax.rem(d - dd + parts, parts), lax.rem(p - dp + sections, sections))
        pl.semaphore_signal(barrier, 1, device_id=src, device_id_type=MESH_ID)
    pl.semaphore_wait(barrier, len(sends))
    copies = []
    for i, (k, start, rows, dd, dp) in enumerate(sends):
        dst = (lax.rem(d + dd + parts, parts), lax.rem(p + dp + sections, sections))
        source = ins[k] if start is None else ins[k].at[:, pl.ds(start, rows)]
        copy = pltpu.make_async_remote_copy(
            src_ref=source, dst_ref=outs[i], send_sem=send_sem.at[i], recv_sem=recv_sem.at[i],
            device_id=dst, device_id_type=MESH_ID)
        copy.start()
        copies.append(copy)
    for copy in copies:
        copy.wait()


def exchange(sends, payloads, parts, sections, cid):
    out_shapes = []
    for k, start, rows, _, _ in sends:
        shape = payloads[k].shape
        if start is not None:
            shape = (shape[0], rows) + shape[2:]
        out_shapes.append(jax.ShapeDtypeStruct(shape, payloads[k].dtype))
    n = len(sends)
    return pl.pallas_call(
        functools.partial(comm_kernel, tuple(sends), len(payloads), parts, sections),
        out_shape=tuple(out_shapes),
        in_specs=[pl.BlockSpec(memory_space=pl.ANY)] * len(payloads),
        out_specs=tuple(pl.BlockSpec(memory_space=pl.ANY) for _ in sends),
        scratch_shapes=[pltpu.SemaphoreType.DMA((n,)), pltpu.SemaphoreType.DMA((n,))],
        compiler_params=pltpu.CompilerParams(collective_id=cid, has_side_effects=True),
    )(*payloads)


def record_copies(pairs, sem, active):
    def run():
        copies = [pltpu.make_async_copy(buf, rec, sem.at[i]) for i, (buf, rec) in enumerate(pairs)]
        for copy in copies:
            copy.start()
        for copy in copies:
            copy.wait()
    if active is None:
        run()
    else:
        pl.when(active)(run)


def fwd_tick_kernel(parts, sections, tick, hs_ref, h_ref, fp_ref, fn_ref, osnd_ref, orcv_ref, orcvt_ref,
                    ws_ref, wr_ref, wm_ref, wn_ref, wa_ref, g_ref, *refs):
    if tick > 0:
        refs = refs[3:]
    (orec, arec, urec, hn_ref, fpn_ref, fnn_ref, obuf, abuf, ubuf,
     hbuf, fpbuf, fnbuf, stage_n, stage_p, send_sem, recv_sem, rec_sem) = refs
    micro, own, _ = h_ref.shape
    block = fp_ref.shape[1]
    d = lax.axis_index("dom")
    p = lax.axis_index("pipe")
    pipe_next = (d, lax.rem(p + 1, sections))
    pipe_prev = (d, lax.rem(p - 1 + sections, sections))
    dom_next = (lax.rem(d + 1, parts), p)
    dom_prev = (lax.rem(d - 1 + parts, parts), p)
    barrier = pltpu.get_barrier_semaphore()
    for src in (pipe_prev, dom_prev, dom_next):
        pl.semaphore_signal(barrier, 1, device_id=src, device_id_type=MESH_ID)
    compute_refs = (hs_ref, h_ref, fp_ref, fn_ref, osnd_ref, orcv_ref, orcvt_ref,
                    ws_ref, wr_ref, wm_ref, wn_ref, wa_ref, g_ref, obuf, abuf, ubuf)
    pipe_copies = []
    for m in range(micro):
        fwd_micro(m, *compute_refs)
        if m == 0:
            pl.semaphore_wait(barrier, 3)
        copy = pltpu.make_async_remote_copy(
            src_ref=obuf.at[m], dst_ref=hbuf.at[m], send_sem=send_sem.at[0, m],
            recv_sem=recv_sem.at[0, m], device_id=pipe_next, device_id_type=MESH_ID)
        copy.start()
        pipe_copies.append(copy)
    record_copies(((obuf, orec), (abuf, arec), (ubuf, urec)), rec_sem,
                  None if tick == 0 else p == tick)
    hs0 = hs_ref[0]
    hs1 = hs_ref[1]
    halo_copies = []
    for m in range(micro):
        pipe_copies[m].wait_recv()
        h = hbuf[m]
        sel_n = h[0:block]
        sel_p = h[0:block]
        for b in range(1, own // block):
            piece = h[b * block:(b + 1) * block]
            sel_n = jnp.where(hs0 == b, piece, sel_n)
            sel_p = jnp.where(hs1 == b, piece, sel_p)
        stage_n[m] = sel_n
        stage_p[m] = sel_p
        for j, (stage, buf, dst) in enumerate(((stage_n, fpbuf, dom_next), (stage_p, fnbuf, dom_prev))):
            copy = pltpu.make_async_remote_copy(
                src_ref=stage.at[m], dst_ref=buf.at[m], send_sem=send_sem.at[1 + j, m],
                recv_sem=recv_sem.at[1 + j, m], device_id=dst, device_id_type=MESH_ID)
            copy.start()
            halo_copies.append(copy)
    for copy in pipe_copies:
        copy.wait_send()
    for copy in halo_copies:
        copy.wait()
    hn_ref[...] = hbuf[...]
    fpn_ref[...] = fpbuf[...]
    fnn_ref[...] = fnbuf[...]


def fwd_tick(operands, records, tick, span, parts, sections):
    h = operands[1]
    micro, own, latent = h.shape
    vm = pl.BlockSpec(memory_space=pltpu.VMEM)
    anyspec = pl.BlockSpec(memory_space=pl.ANY)
    bf = lambda rows: jax.ShapeDtypeStruct((micro, rows, latent), BF16)
    f32 = jax.ShapeDtypeStruct((micro, own, latent), F32)
    n = len(operands)
    extra = () if tick == 0 else tuple(records)
    return pl.pallas_call(
        functools.partial(fwd_tick_kernel, parts, sections, tick),
        out_shape=(bf(own), f32, f32, bf(own), bf(span), bf(span)),
        in_specs=[pl.BlockSpec(memory_space=pltpu.SMEM)] + [vm] * (n - 1) + [anyspec] * len(extra),
        out_specs=(anyspec, anyspec, anyspec, vm, vm, vm),
        scratch_shapes=[pltpu.VMEM((micro, own, latent), BF16),
                        pltpu.VMEM((micro, own, latent), F32),
                        pltpu.VMEM((micro, own, latent), F32),
                        pltpu.VMEM((micro, own, latent), BF16),
                        pltpu.VMEM((micro, span, latent), BF16),
                        pltpu.VMEM((micro, span, latent), BF16),
                        pltpu.VMEM((micro, span, latent), BF16),
                        pltpu.VMEM((micro, span, latent), BF16),
                        pltpu.SemaphoreType.DMA((3, micro)),
                        pltpu.SemaphoreType.DMA((3, micro)),
                        pltpu.SemaphoreType.DMA((3,))],
        input_output_aliases={} if tick == 0 else {n: 0, n + 1: 1, n + 2: 2},
        compiler_params=pltpu.CompilerParams(collective_id=10 + tick,
                                             has_side_effects=True,
                                             vmem_limit_bytes=48 * 1024 * 1024),
    )(*operands, *extra)


def fwd_last_kernel(tick, hs_ref, h_ref, fp_ref, fn_ref, osnd_ref, orcv_ref, orcvt_ref,
                    ws_ref, wr_ref, wm_ref, wn_ref, wa_ref, g_ref, orec_in, arec_in, urec_in,
                    orec, arec, urec, obuf, abuf, ubuf, rec_sem):
    compute_refs = (hs_ref, h_ref, fp_ref, fn_ref, osnd_ref, orcv_ref, orcvt_ref,
                    ws_ref, wr_ref, wm_ref, wn_ref, wa_ref, g_ref, obuf, abuf, ubuf)
    for m in range(h_ref.shape[0]):
        fwd_micro(m, *compute_refs)
    record_copies(((obuf, orec), (abuf, arec), (ubuf, urec)), rec_sem,
                  lax.axis_index("pipe") == tick)


def fwd_last(operands, records, tick):
    h = operands[1]
    micro, own, latent = h.shape
    vm = pl.BlockSpec(memory_space=pltpu.VMEM)
    anyspec = pl.BlockSpec(memory_space=pl.ANY)
    n = len(operands)
    return pl.pallas_call(
        functools.partial(fwd_last_kernel, tick),
        out_shape=tuple(jax.ShapeDtypeStruct(r.shape, r.dtype) for r in records),
        in_specs=[pl.BlockSpec(memory_space=pltpu.SMEM)] + [vm] * (n - 1) + [anyspec] * 3,
        out_specs=(anyspec, anyspec, anyspec),
        scratch_shapes=[pltpu.VMEM((micro, own, latent), BF16),
                        pltpu.VMEM((micro, own, latent), F32),
                        pltpu.VMEM((micro, own, latent), F32),
                        pltpu.SemaphoreType.DMA((3,))],
        input_output_aliases={n: 0, n + 1: 1, n + 2: 2},
        compiler_params=pltpu.CompilerParams(vmem_limit_bytes=48 * 1024 * 1024),
    )(*operands, *records)


def bwd_tick_kernel(parts, sections, tick, first, hs_ref, pin_ref, a_ref, u_ref, osndt_ref, orcvl_ref,
                    orcvt_ref, ws_ref, wr_ref, wm_ref, wn_ref, wa_ref, g_ref, *refs):
    send_pipe = tick > 0
    if not first:
        refs = refs[1:]
    if send_pipe:
        grec, pinn_ref, p32, hg, snbuf, spbuf, gbuf, pinbuf, send_sem, recv_sem, rec_sem = refs
    else:
        grec, p32, hg, snbuf, spbuf, gbuf, send_sem, recv_sem, rec_sem = refs
    micro, own, _ = pin_ref.shape
    block = snbuf.shape[1]
    d = lax.axis_index("dom")
    p = lax.axis_index("pipe")
    pipe_prev = (d, lax.rem(p - 1 + sections, sections))
    pipe_next = (d, lax.rem(p + 1, sections))
    dom_next = (lax.rem(d + 1, parts), p)
    dom_prev = (lax.rem(d - 1 + parts, parts), p)
    barrier = pltpu.get_barrier_semaphore()
    sources = [dom_next, dom_prev] + ([pipe_next] if send_pipe else [])
    for src in sources:
        pl.semaphore_signal(barrier, 1, device_id=src, device_id_type=MESH_ID)
    compute_refs = (pin_ref, a_ref, u_ref, osndt_ref, orcvl_ref, orcvt_ref,
                    ws_ref, wr_ref, wm_ref, wn_ref, wa_ref, g_ref, p32, hg)
    halo_copies = []
    for m in range(micro):
        bwd_micro(m, *compute_refs)
        if m == 0:
            pl.semaphore_wait(barrier, len(sources))
        pair = []
        for j, (lo, buf, dst) in enumerate(((0, snbuf, dom_prev), (block, spbuf, dom_next))):
            copy = pltpu.make_async_remote_copy(
                src_ref=hg.at[m, pl.ds(lo, block)], dst_ref=buf.at[m],
                send_sem=send_sem.at[j, m], recv_sem=recv_sem.at[j, m],
                device_id=dst, device_id_type=MESH_ID)
            copy.start()
            pair.append(copy)
        halo_copies.append(pair)
    hs0 = hs_ref[0]
    hs1 = hs_ref[1]
    pipe_copies = []
    for m in range(micro):
        for copy in halo_copies[m]:
            copy.wait_recv()
        sn = snbuf[m].astype(F32)
        sp = spbuf[m].astype(F32)
        for b in range(own // block):
            piece = p32[m, b * block:(b + 1) * block]
            piece = piece + jnp.where(hs0 == b, sn, 0.0) + jnp.where(hs1 == b, sp, 0.0)
            gbuf[m, b * block:(b + 1) * block] = piece.astype(gbuf.dtype)
        if send_pipe:
            copy = pltpu.make_async_remote_copy(
                src_ref=gbuf.at[m], dst_ref=pinbuf.at[m], send_sem=send_sem.at[2, m],
                recv_sem=recv_sem.at[2, m], device_id=pipe_prev, device_id_type=MESH_ID)
            copy.start()
            pipe_copies.append(copy)
    record_copies(((gbuf, grec),), rec_sem, None if first else p == tick)
    for pair in halo_copies:
        for copy in pair:
            copy.wait_send()
    for copy in pipe_copies:
        copy.wait()
    if send_pipe:
        pinn_ref[...] = pinbuf[...]


def bwd_tick(operands, grad_rec, tick, span, parts, sections):
    pin = operands[1]
    micro, own, latent = pin.shape
    send_pipe = tick > 0
    first = grad_rec is None
    vm = pl.BlockSpec(memory_space=pltpu.VMEM)
    anyspec = pl.BlockSpec(memory_space=pl.ANY)
    grad = jax.ShapeDtypeStruct((micro, own, latent), BF16)
    scratch = [pltpu.VMEM((micro, own, latent), F32), pltpu.VMEM((micro, 2 * span, latent), BF16),
               pltpu.VMEM((micro, span, latent), BF16), pltpu.VMEM((micro, span, latent), BF16),
               pltpu.VMEM((micro, own, latent), BF16)]
    if send_pipe:
        scratch.append(pltpu.VMEM((micro, own, latent), BF16))
    scratch += [pltpu.SemaphoreType.DMA((3, micro)), pltpu.SemaphoreType.DMA((3, micro)),
                pltpu.SemaphoreType.DMA((1,))]
    outs = (grad, grad) if send_pipe else (grad,)
    n = len(operands)
    extra = () if first else (grad_rec,)
    return pl.pallas_call(
        functools.partial(bwd_tick_kernel, parts, sections, tick, first),
        out_shape=outs,
        in_specs=[pl.BlockSpec(memory_space=pltpu.SMEM)] + [vm] * (n - 1) + [anyspec] * len(extra),
        out_specs=(anyspec,) + ((vm,) if send_pipe else ()),
        scratch_shapes=scratch,
        input_output_aliases={} if first else {n: 0},
        compiler_params=pltpu.CompilerParams(collective_id=20 + tick, has_side_effects=True,
                                             vmem_limit_bytes=48 * 1024 * 1024),
    )(*operands, *extra)


def vmem_call(kernel, out_shapes, n_in, smem_first=True):
    in_specs = [pl.BlockSpec(memory_space=pltpu.SMEM)] + [pl.BlockSpec(memory_space=pltpu.VMEM)] * (n_in - 1)
    return pl.pallas_call(
        kernel,
        out_shape=out_shapes,
        in_specs=in_specs,
        out_specs=tuple(pl.BlockSpec(memory_space=pltpu.VMEM) for _ in out_shapes),
        compiler_params=pltpu.CompilerParams(vmem_limit_bytes=48 * 1024 * 1024),
    )


def shards(inputs, cotangent, w_send, w_recv, w_message, w_node, w_aggregate, gains,
           edge_send, edge_recv, edge_count, halo_send):
    sections = lax.axis_size("pipe")
    parts = lax.axis_size("dom")
    p_idx = lax.axis_index("pipe")
    micro, own, latent = inputs.shape
    block = edge_send.shape[1]
    span = halo_send.shape[2] * block
    ext_rows = own + 2 * span
    weights = (w_send[0], w_recv[0], w_message[0], w_node[0], w_aggregate[0])
    gain = gains[0].reshape(1, latent)
    hs = halo_send[0].reshape(-1).astype(jnp.int32)

    snd = edge_send.reshape(-1)
    rcv = edge_recv.reshape(-1)
    live = (jnp.arange(block)[None, :] < edge_count[:, None]).reshape(-1)
    osnd = (snd[:, None] == jnp.arange(ext_rows)[None, :]).astype(BF16)
    orcv_b = rcv[:, None] == jnp.arange(own)[None, :]
    orcv = orcv_b.astype(BF16)
    orcvl_b = orcv_b & live[:, None]
    orcvl = orcvl_b.astype(BF16)
    orcvt = orcvl_b.T.astype(BF16)
    osndt = osnd.T

    def blocks_of(x):
        shaped = x.reshape(micro, own // block, block, latent)
        nxt = jnp.take(shaped, hs[0], axis=1)
        prv = jnp.take(shaped, hs[1], axis=1)
        return nxt, prv

    S, D = sections, parts

    def perm_pipe(shift):
        return [(i, (i + shift) % S) for i in range(S)]

    def perm_both(dshift, pshift):
        return [(d * S + p, ((d + dshift) % D) * S + (p + pshift) % S)
                for d in range(D) for p in range(S)]

    both = ("dom", "pipe")

    fwd = vmem_call(
        fwd_kernel,
        (jax.ShapeDtypeStruct((micro, own, latent), BF16),
         jax.ShapeDtypeStruct((micro, own, latent), F32),
         jax.ShapeDtypeStruct((micro, own, latent), F32)),
        13)

    nxt0, prv0 = blocks_of(inputs)
    halo_fwd = [(0, None, span, 1, 0), (1, None, span, -1, 0)]
    from_prev, from_next = exchange(halo_fwd, (nxt0, prv0), D, S, 0)
    h = inputs
    records = None
    for t in range(S):
        operands = (hs, h, from_prev, from_next, osnd, orcv, orcvt, *weights, gain)
        if t < S - 1:
            out_rec, a_rec, u_rec, h, from_prev, from_next = fwd_tick(operands, records, t, span, D, S)
        else:
            out_rec, a_rec, u_rec = fwd_last(operands, records, t)
        records = (out_rec, a_rec, u_rec)

    pin = cotangent
    grad_rec = None
    for t in range(S - 1, -1, -1):
        operands = (hs, pin, a_rec, u_rec, osndt, orcvl, orcvt, *weights, gain)
        if t > 0:
            grad_rec, pin = bwd_tick(operands, grad_rec, t, span, D, S)
        else:
            (grad_rec,) = bwd_tick(operands, grad_rec, t, span, D, S)
    return (out_rec[None], grad_rec[None])


def solution(mesh):
    in_specs = (
        P(None, "dom", None),
        P(None, "dom", None),
        P("pipe", None, None),
        P("pipe", None, None),
        P("pipe", None, None),
        P("pipe", None, None),
        P("pipe", None, None),
        P("pipe", None),
        P("dom", None),
        P("dom", None),
        P("dom"),
        P("dom", None, None),
    )
    out_specs = (P("pipe", None, "dom", None), P("pipe", None, "dom", None))
    return jax.shard_map(shards, mesh=mesh, in_specs=in_specs, out_specs=out_specs, check_vma=False)
```

```python
import functools

import jax
import jax.numpy as jnp
from jax import lax
from jax.experimental import pallas as pl
from jax.experimental.pallas import tpu as pltpu
from jax.sharding import PartitionSpec as P

EPSILON = 1e-05
F32 = jnp.float32
BF16 = jnp.bfloat16


def mm(x, w):
    return jnp.dot(x, w, preferred_element_type=F32)


def mm_t(x, w):
    return lax.dot_general(x, w, (((1,), (1,)), ((), ())), preferred_element_type=F32)


def sigmoid(v):
    return 1.0 / (1.0 + jnp.exp(-v))


def split_sum(onehot, values):
    hi = values.astype(BF16)
    lo = (values - hi.astype(F32)).astype(BF16)
    return mm(onehot, hi) + mm(onehot, lo)


def fwd_micro(m, hs_ref, h_ref, fp_ref, fn_ref, osnd_ref, orcv_ref, orcvt_ref,
              ws_ref, wr_ref, wm_ref, wn_ref, wa_ref, g_ref, out_ref, a_ref, u_ref):
    own = h_ref.shape[1]
    span = fp_ref.shape[1]
    osnd = osnd_ref[...]
    h = h_ref[m]
    gathered = (mm(osnd[:, :own], h) + mm(osnd[:, own:own + span], fp_ref[m])
                + mm(osnd[:, own + span:], fn_ref[m])).astype(BF16)
    send_part = mm(gathered, ws_ref[...]).astype(BF16).astype(F32)
    recv_rows = mm(orcv_ref[...], h).astype(BF16)
    pre = send_part + mm(recv_rows, wr_ref[...])
    a_ref[m] = pre
    edge_hidden = (pre * sigmoid(pre)).astype(BF16)
    messages = mm(edge_hidden, wm_ref[...])
    agg = split_sum(orcvt_ref[...], messages).astype(BF16)
    node_pre = mm(h, wn_ref[...]) + mm(agg, wa_ref[...])
    u_ref[m] = node_pre
    act = node_pre * sigmoid(node_pre)
    mean = jnp.mean(act, axis=-1, keepdims=True)
    cen = act - mean
    var = jnp.mean(cen * cen, axis=-1, keepdims=True)
    unit = cen * lax.rsqrt(var + EPSILON)
    out_ref[m] = (h.astype(F32) + unit * g_ref[...]).astype(BF16)


def fwd_kernel(*refs):
    for m in range(refs[1].shape[0]):
        fwd_micro(m, *refs)


def bwd_micro(m, pin_ref, a_ref, u_ref, osndt_ref, orcvl_ref, orcvt_ref,
              ws_ref, wr_ref, wm_ref, wn_ref, wa_ref, g_ref, p32_ref, hg_ref):
    own = pin_ref.shape[1]
    gain = g_ref[...]
    c = pin_ref[m].astype(F32)
    node_pre = u_ref[m]
    sig_u = sigmoid(node_pre)
    act = node_pre * sig_u
    mean = jnp.mean(act, axis=-1, keepdims=True)
    cen = act - mean
    var = jnp.mean(cen * cen, axis=-1, keepdims=True)
    rs = lax.rsqrt(var + EPSILON)
    unit = cen * rs
    gu = c * gain
    gact = rs * (gu - jnp.mean(gu, axis=-1, keepdims=True)
                 - unit * jnp.mean(gu * unit, axis=-1, keepdims=True))
    du = (gact * (sig_u * (1.0 + node_pre * (1.0 - sig_u)))).astype(BF16)
    dagg = mm_t(du, wa_ref[...]).astype(BF16)
    rows = c + mm_t(du, wn_ref[...])
    gmsg = mm(orcvl_ref[...], dagg).astype(BF16)
    pre = a_ref[m]
    sig_a = sigmoid(pre)
    dedge = (mm_t(gmsg, wm_ref[...]) * (sig_a * (1.0 + pre * (1.0 - sig_a)))).astype(BF16)
    rows = rows + split_sum(orcvt_ref[...], mm_t(dedge, wr_ref[...]))
    send_rows = split_sum(osndt_ref[...], mm_t(dedge, ws_ref[...]))
    p32_ref[m] = rows + send_rows[:own]
    hg_ref[m] = send_rows[own:].astype(BF16)


MESH_ID = pl.DeviceIdType.MESH


def comm_kernel(sends, n_in, parts, sections, *refs):
    ins = refs[:n_in]
    outs = refs[n_in:n_in + len(sends)]
    send_sem, recv_sem = refs[n_in + len(sends):]
    d = lax.axis_index("dom")
    p = lax.axis_index("pipe")
    barrier = pltpu.get_barrier_semaphore()
    for _, _, _, dd, dp in sends:
        src = (lax.rem(d - dd + parts, parts), lax.rem(p - dp + sections, sections))
        pl.semaphore_signal(barrier, 1, device_id=src, device_id_type=MESH_ID)
    pl.semaphore_wait(barrier, len(sends))
    copies = []
    for i, (k, start, rows, dd, dp) in enumerate(sends):
        dst = (lax.rem(d + dd + parts, parts), lax.rem(p + dp + sections, sections))
        source = ins[k] if start is None else ins[k].at[:, pl.ds(start, rows)]
        copy = pltpu.make_async_remote_copy(
            src_ref=source, dst_ref=outs[i], send_sem=send_sem.at[i], recv_sem=recv_sem.at[i],
            device_id=dst, device_id_type=MESH_ID)
        copy.start()
        copies.append(copy)
    for copy in copies:
        copy.wait()


def exchange(sends, payloads, parts, sections, cid):
    out_shapes = []
    for k, start, rows, _, _ in sends:
        shape = payloads[k].shape
        if start is not None:
            shape = (shape[0], rows) + shape[2:]
        out_shapes.append(jax.ShapeDtypeStruct(shape, payloads[k].dtype))
    n = len(sends)
    return pl.pallas_call(
        functools.partial(comm_kernel, tuple(sends), len(payloads), parts, sections),
        out_shape=tuple(out_shapes),
        in_specs=[pl.BlockSpec(memory_space=pl.ANY)] * len(payloads),
        out_specs=tuple(pl.BlockSpec(memory_space=pl.ANY) for _ in sends),
        scratch_shapes=[pltpu.SemaphoreType.DMA((n,)), pltpu.SemaphoreType.DMA((n,))],
        compiler_params=pltpu.CompilerParams(collective_id=cid, has_side_effects=True),
    )(*payloads)


def record_copies(pairs, sem, active):
    def run():
        copies = [pltpu.make_async_copy(buf, rec, sem.at[i]) for i, (buf, rec) in enumerate(pairs)]
        for copy in copies:
            copy.start()
        for copy in copies:
            copy.wait()
    if active is None:
        run()
    else:
        pl.when(active)(run)


def fwd_tick_kernel(parts, sections, tick, hs_ref, h_ref, fp_ref, fn_ref, osnd_ref, orcv_ref, orcvt_ref,
                    ws_ref, wr_ref, wm_ref, wn_ref, wa_ref, g_ref, *refs):
    if tick > 0:
        refs = refs[3:]
    (orec, arec, urec, hn_ref, fpn_ref, fnn_ref, obuf, abuf, ubuf,
     hbuf, fpbuf, fnbuf, stage_n, stage_p, send_sem, recv_sem, rec_sem) = refs
    micro, own, _ = h_ref.shape
    block = fp_ref.shape[1]
    d = lax.axis_index("dom")
    p = lax.axis_index("pipe")
    pipe_next = (d, lax.rem(p + 1, sections))
    pipe_prev = (d, lax.rem(p - 1 + sections, sections))
    dom_next = (lax.rem(d + 1, parts), p)
    dom_prev = (lax.rem(d - 1 + parts, parts), p)
    barrier = pltpu.get_barrier_semaphore()
    for src in (pipe_prev, dom_prev, dom_next):
        pl.semaphore_signal(barrier, 1, device_id=src, device_id_type=MESH_ID)
    compute_refs = (hs_ref, h_ref, fp_ref, fn_ref, osnd_ref, orcv_ref, orcvt_ref,
                    ws_ref, wr_ref, wm_ref, wn_ref, wa_ref, g_ref, obuf, abuf, ubuf)
    pipe_copies = []
    for m in range(micro):
        fwd_micro(m, *compute_refs)
        if m == 0:
            pl.semaphore_wait(barrier, 3)
        copy = pltpu.make_async_remote_copy(
            src_ref=obuf.at[m], dst_ref=hbuf.at[m], send_sem=send_sem.at[0, m],
            recv_sem=recv_sem.at[0, m], device_id=pipe_next, device_id_type=MESH_ID)
        copy.start()
        pipe_copies.append(copy)
    record_copies(((obuf, orec), (abuf, arec), (ubuf, urec)), rec_sem,
                  None if tick == 0 else p == tick)
    hs0 = hs_ref[0]
    hs1 = hs_ref[1]
    halo_copies = []
    for m in range(micro):
        pipe_copies[m].wait_recv()
        h = hbuf[m]
        sel_n = h[0:block]
        sel_p = h[0:block]
        for b in range(1, own // block):
            piece = h[b * block:(b + 1) * block]
            sel_n = jnp.where(hs0 == b, piece, sel_n)
            sel_p = jnp.where(hs1 == b, piece, sel_p)
        stage_n[m] = sel_n
        stage_p[m] = sel_p
        for j, (stage, buf, dst) in enumerate(((stage_n, fpbuf, dom_next), (stage_p, fnbuf, dom_prev))):
            copy = pltpu.make_async_remote_copy(
                src_ref=stage.at[m], dst_ref=buf.at[m], send_sem=send_sem.at[1 + j, m],
                recv_sem=recv_sem.at[1 + j, m], device_id=dst, device_id_type=MESH_ID)
            copy.start()
            halo_copies.append(copy)
    for copy in pipe_copies:
        copy.wait_send()
    for copy in halo_copies:
        copy.wait()
    hn_ref[...] = hbuf[...]
    fpn_ref[...] = fpbuf[...]
    fnn_ref[...] = fnbuf[...]


def fwd_tick(operands, records, tick, span, parts, sections):
    h = operands[1]
    micro, own, latent = h.shape
    vm = pl.BlockSpec(memory_space=pltpu.VMEM)
    anyspec = pl.BlockSpec(memory_space=pl.ANY)
    bf = lambda rows: jax.ShapeDtypeStruct((micro, rows, latent), BF16)
    f32 = jax.ShapeDtypeStruct((micro, own, latent), F32)
    n = len(operands)
    extra = () if tick == 0 else tuple(records)
    return pl.pallas_call(
        functools.partial(fwd_tick_kernel, parts, sections, tick),
        out_shape=(bf(own), f32, f32, bf(own), bf(span), bf(span)),
        in_specs=[pl.BlockSpec(memory_space=pltpu.SMEM)] + [vm] * (n - 1) + [anyspec] * len(extra),
        out_specs=(anyspec, anyspec, anyspec, vm, vm, vm),
        scratch_shapes=[pltpu.VMEM((micro, own, latent), BF16),
                        pltpu.VMEM((micro, own, latent), F32),
                        pltpu.VMEM((micro, own, latent), F32),
                        pltpu.VMEM((micro, own, latent), BF16),
                        pltpu.VMEM((micro, span, latent), BF16),
                        pltpu.VMEM((micro, span, latent), BF16),
                        pltpu.VMEM((micro, span, latent), BF16),
                        pltpu.VMEM((micro, span, latent), BF16),
                        pltpu.SemaphoreType.DMA((3, micro)),
                        pltpu.SemaphoreType.DMA((3, micro)),
                        pltpu.SemaphoreType.DMA((3,))],
        input_output_aliases={} if tick == 0 else {n: 0, n + 1: 1, n + 2: 2},
        compiler_params=pltpu.CompilerParams(collective_id=10 + tick,
                                             has_side_effects=True,
                                             vmem_limit_bytes=48 * 1024 * 1024),
    )(*operands, *extra)


def fwd_last_kernel(tick, hs_ref, h_ref, fp_ref, fn_ref, osnd_ref, orcv_ref, orcvt_ref,
                    ws_ref, wr_ref, wm_ref, wn_ref, wa_ref, g_ref, orec_in, arec_in, urec_in,
                    orec, arec, urec, obuf, abuf, ubuf, rec_sem):
    compute_refs = (hs_ref, h_ref, fp_ref, fn_ref, osnd_ref, orcv_ref, orcvt_ref,
                    ws_ref, wr_ref, wm_ref, wn_ref, wa_ref, g_ref, obuf, abuf, ubuf)
    for m in range(h_ref.shape[0]):
        fwd_micro(m, *compute_refs)
    record_copies(((obuf, orec), (abuf, arec), (ubuf, urec)), rec_sem,
                  lax.axis_index("pipe") == tick)


def fwd_last(operands, records, tick):
    h = operands[1]
    micro, own, latent = h.shape
    vm = pl.BlockSpec(memory_space=pltpu.VMEM)
    anyspec = pl.BlockSpec(memory_space=pl.ANY)
    n = len(operands)
    return pl.pallas_call(
        functools.partial(fwd_last_kernel, tick),
        out_shape=tuple(jax.ShapeDtypeStruct(r.shape, r.dtype) for r in records),
        in_specs=[pl.BlockSpec(memory_space=pltpu.SMEM)] + [vm] * (n - 1) + [anyspec] * 3,
        out_specs=(anyspec, anyspec, anyspec),
        scratch_shapes=[pltpu.VMEM((micro, own, latent), BF16),
                        pltpu.VMEM((micro, own, latent), F32),
                        pltpu.VMEM((micro, own, latent), F32),
                        pltpu.SemaphoreType.DMA((3,))],
        input_output_aliases={n: 0, n + 1: 1, n + 2: 2},
        compiler_params=pltpu.CompilerParams(vmem_limit_bytes=48 * 1024 * 1024),
    )(*operands, *records)


def bwd_tick_kernel(parts, sections, tick, first, hs_ref, pin_ref, a_ref, u_ref, osndt_ref, orcvl_ref,
                    orcvt_ref, ws_ref, wr_ref, wm_ref, wn_ref, wa_ref, g_ref, *refs):
    send_pipe = tick > 0
    if not first:
        refs = refs[1:]
    if send_pipe:
        grec, pinn_ref, p32, hg, snbuf, spbuf, gbuf, pinbuf, send_sem, recv_sem, rec_sem = refs
    else:
        grec, p32, hg, snbuf, spbuf, gbuf, send_sem, recv_sem, rec_sem = refs
    micro, own, _ = pin_ref.shape
    block = snbuf.shape[1]
    d = lax.axis_index("dom")
    p = lax.axis_index("pipe")
    pipe_prev = (d, lax.rem(p - 1 + sections, sections))
    pipe_next = (d, lax.rem(p + 1, sections))
    dom_next = (lax.rem(d + 1, parts), p)
    dom_prev = (lax.rem(d - 1 + parts, parts), p)
    barrier = pltpu.get_barrier_semaphore()
    sources = [dom_next, dom_prev] + ([pipe_next] if send_pipe else [])
    for src in sources:
        pl.semaphore_signal(barrier, 1, device_id=src, device_id_type=MESH_ID)
    compute_refs = (pin_ref, a_ref, u_ref, osndt_ref, orcvl_ref, orcvt_ref,
                    ws_ref, wr_ref, wm_ref, wn_ref, wa_ref, g_ref, p32, hg)
    halo_copies = []
    for m in range(micro):
        bwd_micro(m, *compute_refs)
        if m == 0:
            pl.semaphore_wait(barrier, len(sources))
        pair = []
        for j, (lo, buf, dst) in enumerate(((0, snbuf, dom_prev), (block, spbuf, dom_next))):
            copy = pltpu.make_async_remote_copy(
                src_ref=hg.at[m, pl.ds(lo, block)], dst_ref=buf.at[m],
                send_sem=send_sem.at[j, m], recv_sem=recv_sem.at[j, m],
                device_id=dst, device_id_type=MESH_ID)
            copy.start()
            pair.append(copy)
        halo_copies.append(pair)
    hs0 = hs_ref[0]
    hs1 = hs_ref[1]
    pipe_copies = []
    for m in range(micro):
        for copy in halo_copies[m]:
            copy.wait_recv()
        sn = snbuf[m].astype(F32)
        sp = spbuf[m].astype(F32)
        for b in range(own // block):
            piece = p32[m, b * block:(b + 1) * block]
            piece = piece + jnp.where(hs0 == b, sn, 0.0) + jnp.where(hs1 == b, sp, 0.0)
            gbuf[m, b * block:(b + 1) * block] = piece.astype(gbuf.dtype)
        if send_pipe:
            copy = pltpu.make_async_remote_copy(
                src_ref=gbuf.at[m], dst_ref=pinbuf.at[m], send_sem=send_sem.at[2, m],
                recv_sem=recv_sem.at[2, m], device_id=pipe_prev, device_id_type=MESH_ID)
            copy.start()
            pipe_copies.append(copy)
    record_copies(((gbuf, grec),), rec_sem, None if first else p == tick)
    for pair in halo_copies:
        for copy in pair:
            copy.wait_send()
    for copy in pipe_copies:
        copy.wait()
    if send_pipe:
        pinn_ref[...] = pinbuf[...]


def bwd_tick(operands, grad_rec, tick, span, parts, sections):
    pin = operands[1]
    micro, own, latent = pin.shape
    send_pipe = tick > 0
    first = grad_rec is None
    vm = pl.BlockSpec(memory_space=pltpu.VMEM)
    anyspec = pl.BlockSpec(memory_space=pl.ANY)
    grad = jax.ShapeDtypeStruct((micro, own, latent), BF16)
    scratch = [pltpu.VMEM((micro, own, latent), F32), pltpu.VMEM((micro, 2 * span, latent), BF16),
               pltpu.VMEM((micro, span, latent), BF16), pltpu.VMEM((micro, span, latent), BF16),
               pltpu.VMEM((micro, own, latent), BF16)]
    if send_pipe:
        scratch.append(pltpu.VMEM((micro, own, latent), BF16))
    scratch += [pltpu.SemaphoreType.DMA((3, micro)), pltpu.SemaphoreType.DMA((3, micro)),
                pltpu.SemaphoreType.DMA((1,))]
    outs = (grad, grad) if send_pipe else (grad,)
    n = len(operands)
    extra = () if first else (grad_rec,)
    return pl.pallas_call(
        functools.partial(bwd_tick_kernel, parts, sections, tick, first),
        out_shape=outs,
        in_specs=[pl.BlockSpec(memory_space=pltpu.SMEM)] + [vm] * (n - 1) + [anyspec] * len(extra),
        out_specs=(anyspec,) + ((vm,) if send_pipe else ()),
        scratch_shapes=scratch,
        input_output_aliases={} if first else {n: 0},
        compiler_params=pltpu.CompilerParams(collective_id=20 + tick, has_side_effects=True,
                                             vmem_limit_bytes=48 * 1024 * 1024),
    )(*operands, *extra)


def vmem_call(kernel, out_shapes, n_in, smem_first=True):
    in_specs = [pl.BlockSpec(memory_space=pltpu.SMEM)] + [pl.BlockSpec(memory_space=pltpu.VMEM)] * (n_in - 1)
    return pl.pallas_call(
        kernel,
        out_shape=out_shapes,
        in_specs=in_specs,
        out_specs=tuple(pl.BlockSpec(memory_space=pltpu.VMEM) for _ in out_shapes),
        compiler_params=pltpu.CompilerParams(vmem_limit_bytes=48 * 1024 * 1024),
    )


def whole_kernel(parts, sections, hs_ref, x_ref, cot_ref, osnd_ref, orcv_ref, orcvt_ref, osndt_ref,
                 orcvl_ref, ws_ref, wr_ref, wm_ref, wn_ref, wa_ref, g_ref,
                 out_ref, grad_ref,
                 hbuf, fpbuf, fnbuf, stage_n, stage_p, abuf, ubuf, cbuf, p32, hg, snbuf, spbuf,
                 fsend, frecv, bsend, brecv):
    micro, own, _ = x_ref.shape
    block = fpbuf.shape[1]
    d = lax.axis_index("dom")
    p = lax.axis_index("pipe")
    pipe_next = (d, lax.rem(p + 1, sections))
    pipe_prev = (d, lax.rem(p - 1 + sections, sections))
    dom_next = (lax.rem(d + 1, parts), p)
    dom_prev = (lax.rem(d - 1 + parts, parts), p)
    barrier = pltpu.get_barrier_semaphore()
    for nb in (pipe_prev, pipe_next, dom_prev, dom_next):
        pl.semaphore_signal(barrier, 1, device_id=nb, device_id_type=MESH_ID)
    pl.semaphore_wait(barrier, 4)
    hs0 = hs_ref[0]
    hs1 = hs_ref[1]
    has_prev = p > 0
    has_next = p < sections - 1

    def remote(src, dst, sems, idx, target):
        send_sem, recv_sem = sems
        return pltpu.make_async_remote_copy(
            src_ref=src, dst_ref=dst, send_sem=send_sem.at[idx], recv_sem=recv_sem.at[idx],
            device_id=target, device_id_type=MESH_ID)

    fwd_refs = (hs_ref, hbuf, fpbuf, fnbuf, osnd_ref, orcv_ref, orcvt_ref,
                ws_ref, wr_ref, wm_ref, wn_ref, wa_ref, g_ref, out_ref, abuf, ubuf)
    fwd_pipe = []
    fwd_halo = []
    for m in range(micro):
        pipe_in = remote(out_ref.at[m], hbuf.at[m], (fsend, frecv), m, pipe_next)
        pl.when(has_prev)(pipe_in.wait_recv)

        @pl.when(p == 0)
        def _():
            hbuf[m] = x_ref[m]

        h = hbuf[m]
        sel_n = h[0:block]
        sel_p = h[0:block]
        for b in range(1, own // block):
            piece = h[b * block:(b + 1) * block]
            sel_n = jnp.where(hs0 == b, piece, sel_n)
            sel_p = jnp.where(hs1 == b, piece, sel_p)
        stage_n[m] = sel_n
        stage_p[m] = sel_p
        pair = [remote(stage_n.at[m], fpbuf.at[m], (fsend, frecv), micro + 2 * m, dom_next),
                remote(stage_p.at[m], fnbuf.at[m], (fsend, frecv), micro + 2 * m + 1, dom_prev)]
        for copy in pair:
            copy.start()
        for copy in pair:
            copy.wait_recv()
        fwd_halo.extend(pair)
        fwd_micro(m, *fwd_refs)
        pl.when(has_next)(pipe_in.start)
        fwd_pipe.append(pipe_in)

    bwd_refs = (cbuf, abuf, ubuf, osndt_ref, orcvl_ref, orcvt_ref,
                ws_ref, wr_ref, wm_ref, wn_ref, wa_ref, g_ref, p32, hg)
    bwd_pipe = []
    bwd_halo = []
    for m in range(micro):
        pipe_in = remote(grad_ref.at[m], cbuf.at[m], (bsend, brecv), m, pipe_prev)
        pl.when(has_next)(pipe_in.wait_recv)

        @pl.when(p == sections - 1)
        def _():
            cbuf[m] = cot_ref[m]

        bwd_micro(m, *bwd_refs)
        pair = [remote(hg.at[m, pl.ds(0, block)], snbuf.at[m], (bsend, brecv), micro + 2 * m, dom_prev),
                remote(hg.at[m, pl.ds(block, block)], spbuf.at[m], (bsend, brecv), micro + 2 * m + 1,
                       dom_next)]
        for copy in pair:
            copy.start()
        for copy in pair:
            copy.wait_recv()
        bwd_halo.extend(pair)
        sn = snbuf[m].astype(F32)
        sp = spbuf[m].astype(F32)
        for b in range(own // block):
            piece = p32[m, b * block:(b + 1) * block]
            piece = piece + jnp.where(hs0 == b, sn, 0.0) + jnp.where(hs1 == b, sp, 0.0)
            grad_ref[m, b * block:(b + 1) * block] = piece.astype(grad_ref.dtype)
        pl.when(has_prev)(pipe_in.start)
        bwd_pipe.append(pipe_in)

    for copy in fwd_pipe:
        pl.when(has_next)(copy.wait_send)
    for copy in bwd_pipe:
        pl.when(has_prev)(copy.wait_send)
    for copy in fwd_halo + bwd_halo:
        copy.wait_send()


def whole(operands, span, parts, sections):
    x = operands[1]
    micro, own, latent = x.shape
    vm = pl.BlockSpec(memory_space=pltpu.VMEM)
    bf = lambda rows: pltpu.VMEM((micro, rows, latent), BF16)
    f32 = pltpu.VMEM((micro, own, latent), F32)
    n = 2 * micro + micro * 2
    return pl.pallas_call(
        functools.partial(whole_kernel, parts, sections),
        out_shape=(jax.ShapeDtypeStruct((micro, own, latent), BF16),
                   jax.ShapeDtypeStruct((micro, own, latent), BF16)),
        in_specs=[pl.BlockSpec(memory_space=pltpu.SMEM)] + [vm] * (len(operands) - 1),
        out_specs=(vm, vm),
        scratch_shapes=[bf(own), bf(span), bf(span), bf(span), bf(span), f32, f32, bf(own), f32,
                        bf(2 * span), bf(span), bf(span),
                        pltpu.SemaphoreType.DMA((3 * micro,)), pltpu.SemaphoreType.DMA((3 * micro,)),
                        pltpu.SemaphoreType.DMA((3 * micro,)), pltpu.SemaphoreType.DMA((3 * micro,))],
        compiler_params=pltpu.CompilerParams(collective_id=0, has_side_effects=True,
                                             vmem_limit_bytes=48 * 1024 * 1024),
    )(*operands)


def shards(inputs, cotangent, w_send, w_recv, w_message, w_node, w_aggregate, gains,
           edge_send, edge_recv, edge_count, halo_send):
    sections = lax.axis_size("pipe")
    parts = lax.axis_size("dom")
    p_idx = lax.axis_index("pipe")
    micro, own, latent = inputs.shape
    block = edge_send.shape[1]
    span = halo_send.shape[2] * block
    ext_rows = own + 2 * span
    weights = (w_send[0], w_recv[0], w_message[0], w_node[0], w_aggregate[0])
    gain = gains[0].reshape(1, latent)
    hs = halo_send[0].reshape(-1).astype(jnp.int32)

    snd = edge_send.reshape(-1)
    rcv = edge_recv.reshape(-1)
    live = (jnp.arange(block)[None, :] < edge_count[:, None]).reshape(-1)
    osnd = (snd[:, None] == jnp.arange(ext_rows)[None, :]).astype(BF16)
    orcv_b = rcv[:, None] == jnp.arange(own)[None, :]
    orcv = orcv_b.astype(BF16)
    orcvl_b = orcv_b & live[:, None]
    orcvl = orcvl_b.astype(BF16)
    orcvt = orcvl_b.T.astype(BF16)
    osndt = osnd.T

    def blocks_of(x):
        shaped = x.reshape(micro, own // block, block, latent)
        nxt = jnp.take(shaped, hs[0], axis=1)
        prv = jnp.take(shaped, hs[1], axis=1)
        return nxt, prv

    S, D = sections, parts

    def perm_pipe(shift):
        return [(i, (i + shift) % S) for i in range(S)]

    def perm_both(dshift, pshift):
        return [(d * S + p, ((d + dshift) % D) * S + (p + pshift) % S)
                for d in range(D) for p in range(S)]

    both = ("dom", "pipe")

    fwd = vmem_call(
        fwd_kernel,
        (jax.ShapeDtypeStruct((micro, own, latent), BF16),
         jax.ShapeDtypeStruct((micro, own, latent), F32),
         jax.ShapeDtypeStruct((micro, own, latent), F32)),
        13)

    out_rec, grad_rec = whole(
        (hs, inputs, cotangent, osnd, orcv, orcvt, osndt, orcvl, *weights, gain), span, D, S)
    return (out_rec[None], grad_rec[None])


def solution(mesh):
    in_specs = (
        P(None, "dom", None),
        P(None, "dom", None),
        P("pipe", None, None),
        P("pipe", None, None),
        P("pipe", None, None),
        P("pipe", None, None),
        P("pipe", None, None),
        P("pipe", None),
        P("dom", None),
        P("dom", None),
        P("dom"),
        P("dom", None, None),
    )
    out_specs = (P("pipe", None, "dom", None), P("pipe", None, "dom", None))
    return jax.shard_map(shards, mesh=mesh, in_specs=in_specs, out_specs=out_specs, check_vma=False)
```

```python
import functools

import jax
import jax.numpy as jnp
from jax import lax
from jax.experimental import pallas as pl
from jax.experimental.pallas import tpu as pltpu
from jax.sharding import PartitionSpec as P

EPSILON = 1e-05
F32 = jnp.float32
BF16 = jnp.bfloat16


def mm(x, w):
    return jnp.dot(x, w, preferred_element_type=F32)


def mm_t(x, w):
    return lax.dot_general(x, w, (((1,), (1,)), ((), ())), preferred_element_type=F32)


def sigmoid(v):
    return 1.0 / (1.0 + jnp.exp(-v))


def split_sum(onehot, values):
    hi = values.astype(BF16)
    lo = (values - hi.astype(F32)).astype(BF16)
    return mm(onehot, hi) + mm(onehot, lo)


def fwd_micro(m, hs_ref, h_ref, fp_ref, fn_ref, osnd_ref, orcv_ref, orcvt_ref,
              ws_ref, wr_ref, wm_ref, wn_ref, wa_ref, g_ref, out_ref, a_ref, u_ref):
    own = h_ref.shape[1]
    span = fp_ref.shape[1]
    osnd = osnd_ref[...]
    h = h_ref[m]
    gathered = (mm(osnd[:, :own], h) + mm(osnd[:, own:own + span], fp_ref[m])
                + mm(osnd[:, own + span:], fn_ref[m])).astype(BF16)
    send_part = mm(gathered, ws_ref[...]).astype(BF16).astype(F32)
    recv_rows = mm(orcv_ref[...], h).astype(BF16)
    pre = send_part + mm(recv_rows, wr_ref[...])
    a_ref[m] = pre
    edge_hidden = (pre * sigmoid(pre)).astype(BF16)
    messages = mm(edge_hidden, wm_ref[...])
    agg = split_sum(orcvt_ref[...], messages).astype(BF16)
    node_pre = mm(h, wn_ref[...]) + mm(agg, wa_ref[...])
    u_ref[m] = node_pre
    act = node_pre * sigmoid(node_pre)
    mean = jnp.mean(act, axis=-1, keepdims=True)
    cen = act - mean
    var = jnp.mean(cen * cen, axis=-1, keepdims=True)
    unit = cen * lax.rsqrt(var + EPSILON)
    out_ref[m] = (h.astype(F32) + unit * g_ref[...]).astype(BF16)


def fwd_kernel(*refs):
    for m in range(refs[1].shape[0]):
        fwd_micro(m, *refs)


def bwd_micro(m, pin_ref, a_ref, u_ref, osndt_ref, orcvl_ref, orcvt_ref,
              ws_ref, wr_ref, wm_ref, wn_ref, wa_ref, g_ref, p32_ref, hg_ref):
    own = pin_ref.shape[1]
    gain = g_ref[...]
    c = pin_ref[m].astype(F32)
    node_pre = u_ref[m]
    sig_u = sigmoid(node_pre)
    act = node_pre * sig_u
    mean = jnp.mean(act, axis=-1, keepdims=True)
    cen = act - mean
    var = jnp.mean(cen * cen, axis=-1, keepdims=True)
    rs = lax.rsqrt(var + EPSILON)
    unit = cen * rs
    gu = c * gain
    gact = rs * (gu - jnp.mean(gu, axis=-1, keepdims=True)
                 - unit * jnp.mean(gu * unit, axis=-1, keepdims=True))
    du = (gact * (sig_u * (1.0 + node_pre * (1.0 - sig_u)))).astype(BF16)
    dagg = mm_t(du, wa_ref[...]).astype(BF16)
    rows = c + mm_t(du, wn_ref[...])
    gmsg = mm(orcvl_ref[...], dagg).astype(BF16)
    pre = a_ref[m]
    sig_a = sigmoid(pre)
    dedge = (mm_t(gmsg, wm_ref[...]) * (sig_a * (1.0 + pre * (1.0 - sig_a)))).astype(BF16)
    rows = rows + split_sum(orcvt_ref[...], mm_t(dedge, wr_ref[...]))
    send_rows = split_sum(osndt_ref[...], mm_t(dedge, ws_ref[...]))
    p32_ref[m] = rows + send_rows[:own]
    hg_ref[m] = send_rows[own:].astype(BF16)


MESH_ID = pl.DeviceIdType.MESH


def comm_kernel(sends, n_in, parts, sections, *refs):
    ins = refs[:n_in]
    outs = refs[n_in:n_in + len(sends)]
    send_sem, recv_sem = refs[n_in + len(sends):]
    d = lax.axis_index("dom")
    p = lax.axis_index("pipe")
    barrier = pltpu.get_barrier_semaphore()
    for _, _, _, dd, dp in sends:
        src = (lax.rem(d - dd + parts, parts), lax.rem(p - dp + sections, sections))
        pl.semaphore_signal(barrier, 1, device_id=src, device_id_type=MESH_ID)
    pl.semaphore_wait(barrier, len(sends))
    copies = []
    for i, (k, start, rows, dd, dp) in enumerate(sends):
        dst = (lax.rem(d + dd + parts, parts), lax.rem(p + dp + sections, sections))
        source = ins[k] if start is None else ins[k].at[:, pl.ds(start, rows)]
        copy = pltpu.make_async_remote_copy(
            src_ref=source, dst_ref=outs[i], send_sem=send_sem.at[i], recv_sem=recv_sem.at[i],
            device_id=dst, device_id_type=MESH_ID)
        copy.start()
        copies.append(copy)
    for copy in copies:
        copy.wait()


def exchange(sends, payloads, parts, sections, cid):
    out_shapes = []
    for k, start, rows, _, _ in sends:
        shape = payloads[k].shape
        if start is not None:
            shape = (shape[0], rows) + shape[2:]
        out_shapes.append(jax.ShapeDtypeStruct(shape, payloads[k].dtype))
    n = len(sends)
    return pl.pallas_call(
        functools.partial(comm_kernel, tuple(sends), len(payloads), parts, sections),
        out_shape=tuple(out_shapes),
        in_specs=[pl.BlockSpec(memory_space=pl.ANY)] * len(payloads),
        out_specs=tuple(pl.BlockSpec(memory_space=pl.ANY) for _ in sends),
        scratch_shapes=[pltpu.SemaphoreType.DMA((n,)), pltpu.SemaphoreType.DMA((n,))],
        compiler_params=pltpu.CompilerParams(collective_id=cid, has_side_effects=True),
    )(*payloads)


def record_copies(pairs, sem, active):
    def run():
        copies = [pltpu.make_async_copy(buf, rec, sem.at[i]) for i, (buf, rec) in enumerate(pairs)]
        for copy in copies:
            copy.start()
        for copy in copies:
            copy.wait()
    if active is None:
        run()
    else:
        pl.when(active)(run)


def fwd_tick_kernel(parts, sections, tick, hs_ref, h_ref, fp_ref, fn_ref, osnd_ref, orcv_ref, orcvt_ref,
                    ws_ref, wr_ref, wm_ref, wn_ref, wa_ref, g_ref, *refs):
    if tick > 0:
        refs = refs[3:]
    (orec, arec, urec, hn_ref, fpn_ref, fnn_ref, obuf, abuf, ubuf,
     hbuf, fpbuf, fnbuf, stage_n, stage_p, send_sem, recv_sem, rec_sem) = refs
    micro, own, _ = h_ref.shape
    block = fp_ref.shape[1]
    d = lax.axis_index("dom")
    p = lax.axis_index("pipe")
    pipe_next = (d, lax.rem(p + 1, sections))
    pipe_prev = (d, lax.rem(p - 1 + sections, sections))
    dom_next = (lax.rem(d + 1, parts), p)
    dom_prev = (lax.rem(d - 1 + parts, parts), p)
    barrier = pltpu.get_barrier_semaphore()
    for src in (pipe_prev, dom_prev, dom_next):
        pl.semaphore_signal(barrier, 1, device_id=src, device_id_type=MESH_ID)
    compute_refs = (hs_ref, h_ref, fp_ref, fn_ref, osnd_ref, orcv_ref, orcvt_ref,
                    ws_ref, wr_ref, wm_ref, wn_ref, wa_ref, g_ref, obuf, abuf, ubuf)
    pipe_copies = []
    for m in range(micro):
        fwd_micro(m, *compute_refs)
        if m == 0:
            pl.semaphore_wait(barrier, 3)
        copy = pltpu.make_async_remote_copy(
            src_ref=obuf.at[m], dst_ref=hbuf.at[m], send_sem=send_sem.at[0, m],
            recv_sem=recv_sem.at[0, m], device_id=pipe_next, device_id_type=MESH_ID)
        copy.start()
        pipe_copies.append(copy)
    record_copies(((obuf, orec), (abuf, arec), (ubuf, urec)), rec_sem,
                  None if tick == 0 else p == tick)
    hs0 = hs_ref[0]
    hs1 = hs_ref[1]
    halo_copies = []
    for m in range(micro):
        pipe_copies[m].wait_recv()
        h = hbuf[m]
        sel_n = h[0:block]
        sel_p = h[0:block]
        for b in range(1, own // block):
            piece = h[b * block:(b + 1) * block]
            sel_n = jnp.where(hs0 == b, piece, sel_n)
            sel_p = jnp.where(hs1 == b, piece, sel_p)
        stage_n[m] = sel_n
        stage_p[m] = sel_p
        for j, (stage, buf, dst) in enumerate(((stage_n, fpbuf, dom_next), (stage_p, fnbuf, dom_prev))):
            copy = pltpu.make_async_remote_copy(
                src_ref=stage.at[m], dst_ref=buf.at[m], send_sem=send_sem.at[1 + j, m],
                recv_sem=recv_sem.at[1 + j, m], device_id=dst, device_id_type=MESH_ID)
            copy.start()
            halo_copies.append(copy)
    for copy in pipe_copies:
        copy.wait_send()
    for copy in halo_copies:
        copy.wait()
    hn_ref[...] = hbuf[...]
    fpn_ref[...] = fpbuf[...]
    fnn_ref[...] = fnbuf[...]


def fwd_tick(operands, records, tick, span, parts, sections):
    h = operands[1]
    micro, own, latent = h.shape
    vm = pl.BlockSpec(memory_space=pltpu.VMEM)
    anyspec = pl.BlockSpec(memory_space=pl.ANY)
    bf = lambda rows: jax.ShapeDtypeStruct((micro, rows, latent), BF16)
    f32 = jax.ShapeDtypeStruct((micro, own, latent), F32)
    n = len(operands)
    extra = () if tick == 0 else tuple(records)
    return pl.pallas_call(
        functools.partial(fwd_tick_kernel, parts, sections, tick),
        out_shape=(bf(own), f32, f32, bf(own), bf(span), bf(span)),
        in_specs=[pl.BlockSpec(memory_space=pltpu.SMEM)] + [vm] * (n - 1) + [anyspec] * len(extra),
        out_specs=(anyspec, anyspec, anyspec, vm, vm, vm),
        scratch_shapes=[pltpu.VMEM((micro, own, latent), BF16),
                        pltpu.VMEM((micro, own, latent), F32),
                        pltpu.VMEM((micro, own, latent), F32),
                        pltpu.VMEM((micro, own, latent), BF16),
                        pltpu.VMEM((micro, span, latent), BF16),
                        pltpu.VMEM((micro, span, latent), BF16),
                        pltpu.VMEM((micro, span, latent), BF16),
                        pltpu.VMEM((micro, span, latent), BF16),
                        pltpu.SemaphoreType.DMA((3, micro)),
                        pltpu.SemaphoreType.DMA((3, micro)),
                        pltpu.SemaphoreType.DMA((3,))],
        input_output_aliases={} if tick == 0 else {n: 0, n + 1: 1, n + 2: 2},
        compiler_params=pltpu.CompilerParams(collective_id=10 + tick,
                                             has_side_effects=True,
                                             vmem_limit_bytes=48 * 1024 * 1024),
    )(*operands, *extra)


def fwd_last_kernel(tick, hs_ref, h_ref, fp_ref, fn_ref, osnd_ref, orcv_ref, orcvt_ref,
                    ws_ref, wr_ref, wm_ref, wn_ref, wa_ref, g_ref, orec_in, arec_in, urec_in,
                    orec, arec, urec, obuf, abuf, ubuf, rec_sem):
    compute_refs = (hs_ref, h_ref, fp_ref, fn_ref, osnd_ref, orcv_ref, orcvt_ref,
                    ws_ref, wr_ref, wm_ref, wn_ref, wa_ref, g_ref, obuf, abuf, ubuf)
    for m in range(h_ref.shape[0]):
        fwd_micro(m, *compute_refs)
    record_copies(((obuf, orec), (abuf, arec), (ubuf, urec)), rec_sem,
                  lax.axis_index("pipe") == tick)


def fwd_last(operands, records, tick):
    h = operands[1]
    micro, own, latent = h.shape
    vm = pl.BlockSpec(memory_space=pltpu.VMEM)
    anyspec = pl.BlockSpec(memory_space=pl.ANY)
    n = len(operands)
    return pl.pallas_call(
        functools.partial(fwd_last_kernel, tick),
        out_shape=tuple(jax.ShapeDtypeStruct(r.shape, r.dtype) for r in records),
        in_specs=[pl.BlockSpec(memory_space=pltpu.SMEM)] + [vm] * (n - 1) + [anyspec] * 3,
        out_specs=(anyspec, anyspec, anyspec),
        scratch_shapes=[pltpu.VMEM((micro, own, latent), BF16),
                        pltpu.VMEM((micro, own, latent), F32),
                        pltpu.VMEM((micro, own, latent), F32),
                        pltpu.SemaphoreType.DMA((3,))],
        input_output_aliases={n: 0, n + 1: 1, n + 2: 2},
        compiler_params=pltpu.CompilerParams(vmem_limit_bytes=48 * 1024 * 1024),
    )(*operands, *records)


def bwd_tick_kernel(parts, sections, tick, first, hs_ref, pin_ref, a_ref, u_ref, osndt_ref, orcvl_ref,
                    orcvt_ref, ws_ref, wr_ref, wm_ref, wn_ref, wa_ref, g_ref, *refs):
    send_pipe = tick > 0
    if not first:
        refs = refs[1:]
    if send_pipe:
        grec, pinn_ref, p32, hg, snbuf, spbuf, gbuf, pinbuf, send_sem, recv_sem, rec_sem = refs
    else:
        grec, p32, hg, snbuf, spbuf, gbuf, send_sem, recv_sem, rec_sem = refs
    micro, own, _ = pin_ref.shape
    block = snbuf.shape[1]
    d = lax.axis_index("dom")
    p = lax.axis_index("pipe")
    pipe_prev = (d, lax.rem(p - 1 + sections, sections))
    pipe_next = (d, lax.rem(p + 1, sections))
    dom_next = (lax.rem(d + 1, parts), p)
    dom_prev = (lax.rem(d - 1 + parts, parts), p)
    barrier = pltpu.get_barrier_semaphore()
    sources = [dom_next, dom_prev] + ([pipe_next] if send_pipe else [])
    for src in sources:
        pl.semaphore_signal(barrier, 1, device_id=src, device_id_type=MESH_ID)
    compute_refs = (pin_ref, a_ref, u_ref, osndt_ref, orcvl_ref, orcvt_ref,
                    ws_ref, wr_ref, wm_ref, wn_ref, wa_ref, g_ref, p32, hg)
    halo_copies = []
    for m in range(micro):
        bwd_micro(m, *compute_refs)
        if m == 0:
            pl.semaphore_wait(barrier, len(sources))
        pair = []
        for j, (lo, buf, dst) in enumerate(((0, snbuf, dom_prev), (block, spbuf, dom_next))):
            copy = pltpu.make_async_remote_copy(
                src_ref=hg.at[m, pl.ds(lo, block)], dst_ref=buf.at[m],
                send_sem=send_sem.at[j, m], recv_sem=recv_sem.at[j, m],
                device_id=dst, device_id_type=MESH_ID)
            copy.start()
            pair.append(copy)
        halo_copies.append(pair)
    hs0 = hs_ref[0]
    hs1 = hs_ref[1]
    pipe_copies = []
    for m in range(micro):
        for copy in halo_copies[m]:
            copy.wait_recv()
        sn = snbuf[m].astype(F32)
        sp = spbuf[m].astype(F32)
        for b in range(own // block):
            piece = p32[m, b * block:(b + 1) * block]
            piece = piece + jnp.where(hs0 == b, sn, 0.0) + jnp.where(hs1 == b, sp, 0.0)
            gbuf[m, b * block:(b + 1) * block] = piece.astype(gbuf.dtype)
        if send_pipe:
            copy = pltpu.make_async_remote_copy(
                src_ref=gbuf.at[m], dst_ref=pinbuf.at[m], send_sem=send_sem.at[2, m],
                recv_sem=recv_sem.at[2, m], device_id=pipe_prev, device_id_type=MESH_ID)
            copy.start()
            pipe_copies.append(copy)
    record_copies(((gbuf, grec),), rec_sem, None if first else p == tick)
    for pair in halo_copies:
        for copy in pair:
            copy.wait_send()
    for copy in pipe_copies:
        copy.wait()
    if send_pipe:
        pinn_ref[...] = pinbuf[...]


def bwd_tick(operands, grad_rec, tick, span, parts, sections):
    pin = operands[1]
    micro, own, latent = pin.shape
    send_pipe = tick > 0
    first = grad_rec is None
    vm = pl.BlockSpec(memory_space=pltpu.VMEM)
    anyspec = pl.BlockSpec(memory_space=pl.ANY)
    grad = jax.ShapeDtypeStruct((micro, own, latent), BF16)
    scratch = [pltpu.VMEM((micro, own, latent), F32), pltpu.VMEM((micro, 2 * span, latent), BF16),
               pltpu.VMEM((micro, span, latent), BF16), pltpu.VMEM((micro, span, latent), BF16),
               pltpu.VMEM((micro, own, latent), BF16)]
    if send_pipe:
        scratch.append(pltpu.VMEM((micro, own, latent), BF16))
    scratch += [pltpu.SemaphoreType.DMA((3, micro)), pltpu.SemaphoreType.DMA((3, micro)),
                pltpu.SemaphoreType.DMA((1,))]
    outs = (grad, grad) if send_pipe else (grad,)
    n = len(operands)
    extra = () if first else (grad_rec,)
    return pl.pallas_call(
        functools.partial(bwd_tick_kernel, parts, sections, tick, first),
        out_shape=outs,
        in_specs=[pl.BlockSpec(memory_space=pltpu.SMEM)] + [vm] * (n - 1) + [anyspec] * len(extra),
        out_specs=(anyspec,) + ((vm,) if send_pipe else ()),
        scratch_shapes=scratch,
        input_output_aliases={} if first else {n: 0},
        compiler_params=pltpu.CompilerParams(collective_id=20 + tick, has_side_effects=True,
                                             vmem_limit_bytes=48 * 1024 * 1024),
    )(*operands, *extra)


def vmem_call(kernel, out_shapes, n_in, smem_first=True):
    in_specs = [pl.BlockSpec(memory_space=pltpu.SMEM)] + [pl.BlockSpec(memory_space=pltpu.VMEM)] * (n_in - 1)
    return pl.pallas_call(
        kernel,
        out_shape=out_shapes,
        in_specs=in_specs,
        out_specs=tuple(pl.BlockSpec(memory_space=pltpu.VMEM) for _ in out_shapes),
        compiler_params=pltpu.CompilerParams(vmem_limit_bytes=48 * 1024 * 1024),
    )


def whole_kernel(parts, sections, hs_ref, x_hbm, cot_hbm, osnd_ref, orcv_ref, orcvt_ref, osndt_ref,
                 orcvl_ref, ws_hbm, wr_hbm, wm_hbm, wn_hbm, wa_hbm, g_ref,
                 out_ref, grad_ref,
                 xbuf, cotbuf, wbuf,
                 hbuf, fpbuf, fnbuf, stage_n, stage_p, abuf, ubuf, cbuf, p32, hg, snbuf, spbuf,
                 fsend, frecv, bsend, brecv, lsem):
    micro, own, latent = xbuf.shape
    block = fpbuf.shape[1]
    span = block
    loads = [pltpu.make_async_copy(x_hbm, xbuf, lsem.at[0])]
    for i, w in enumerate((ws_hbm, wr_hbm, wm_hbm, wn_hbm, wa_hbm)):
        loads.append(pltpu.make_async_copy(w, wbuf.at[i], lsem.at[1 + i]))
    loads.append(pltpu.make_async_copy(cot_hbm, cotbuf, lsem.at[6]))
    for copy in loads:
        copy.start()
    d = lax.axis_index("dom")
    p = lax.axis_index("pipe")
    pipe_next = (d, lax.rem(p + 1, sections))
    pipe_prev = (d, lax.rem(p - 1 + sections, sections))
    dom_next = (lax.rem(d + 1, parts), p)
    dom_prev = (lax.rem(d - 1 + parts, parts), p)
    barrier = pltpu.get_barrier_semaphore()
    for nb in (pipe_prev, pipe_next, dom_prev, dom_next):
        pl.semaphore_signal(barrier, 1, device_id=nb, device_id_type=MESH_ID)
    pl.semaphore_wait(barrier, 4)
    hs0 = hs_ref[0]
    hs1 = hs_ref[1]
    has_prev = p > 0
    has_next = p < sections - 1
    gain = g_ref[...]
    ws, wr, wm, wn, wa = (wbuf.at[i] for i in range(5))

    def remote(src, dst, sems, idx, target):
        send_sem, recv_sem = sems
        return pltpu.make_async_remote_copy(
            src_ref=src, dst_ref=dst, send_sem=send_sem.at[idx], recv_sem=recv_sem.at[idx],
            device_id=target, device_id_type=MESH_ID)

    loads[0].wait()
    fwd_pipe = []
    fwd_halo = []
    for m in range(micro):
        pipe_in = remote(out_ref.at[m], hbuf.at[m], (fsend, frecv), m, pipe_next)
        pl.when(has_prev)(pipe_in.wait_recv)

        @pl.when(p == 0)
        def _():
            hbuf[m] = xbuf[m]

        h = hbuf[m]
        sel_n = h[0:block]
        sel_p = h[0:block]
        for b in range(1, own // block):
            piece = h[b * block:(b + 1) * block]
            sel_n = jnp.where(hs0 == b, piece, sel_n)
            sel_p = jnp.where(hs1 == b, piece, sel_p)
        stage_n[m] = sel_n
        stage_p[m] = sel_p
        pair = [remote(stage_n.at[m], fpbuf.at[m], (fsend, frecv), micro + 2 * m, dom_next),
                remote(stage_p.at[m], fnbuf.at[m], (fsend, frecv), micro + 2 * m + 1, dom_prev)]
        for copy in pair:
            copy.start()
        if m == 0:
            for copy in loads[1:6]:
                copy.wait()
        osnd = osnd_ref[...]
        own_gather = mm(osnd[:, :own], h)
        recv_rows = mm(orcv_ref[...], h).astype(BF16)
        recv_part = mm(recv_rows, wr[...])
        node_part = mm(h, wn[...])
        for copy in pair:
            copy.wait_recv()
        fwd_halo.extend(pair)
        gathered = (own_gather + mm(osnd[:, own:own + span], fpbuf[m])
                    + mm(osnd[:, own + span:], fnbuf[m])).astype(BF16)
        send_part = mm(gathered, ws[...]).astype(BF16).astype(F32)
        pre = send_part + recv_part
        abuf[m] = pre
        edge_hidden = (pre * sigmoid(pre)).astype(BF16)
        messages = mm(edge_hidden, wm[...])
        agg = split_sum(orcvt_ref[...], messages).astype(BF16)
        node_pre = node_part + mm(agg, wa[...])
        ubuf[m] = node_pre
        act = node_pre * sigmoid(node_pre)
        mean = jnp.mean(act, axis=-1, keepdims=True)
        cen = act - mean
        var = jnp.mean(cen * cen, axis=-1, keepdims=True)
        unit = cen * lax.rsqrt(var + EPSILON)
        out_ref[m] = (h.astype(F32) + unit * gain).astype(BF16)
        pl.when(has_next)(pipe_in.start)
        fwd_pipe.append(pipe_in)

    loads[6].wait()
    bwd_pipe = []
    bwd_halo = []
    for m in range(micro):
        pipe_in = remote(grad_ref.at[m], cbuf.at[m], (bsend, brecv), m, pipe_prev)
        pl.when(has_next)(pipe_in.wait_recv)

        @pl.when(p == sections - 1)
        def _():
            cbuf[m] = cotbuf[m]

        c = cbuf[m].astype(F32)
        node_pre = ubuf[m]
        sig_u = sigmoid(node_pre)
        act = node_pre * sig_u
        mean = jnp.mean(act, axis=-1, keepdims=True)
        cen = act - mean
        var = jnp.mean(cen * cen, axis=-1, keepdims=True)
        rs = lax.rsqrt(var + EPSILON)
        unit = cen * rs
        gu = c * gain
        gact = rs * (gu - jnp.mean(gu, axis=-1, keepdims=True)
                     - unit * jnp.mean(gu * unit, axis=-1, keepdims=True))
        du = (gact * (sig_u * (1.0 + node_pre * (1.0 - sig_u)))).astype(BF16)
        dagg = mm_t(du, wa[...]).astype(BF16)
        gmsg = mm(orcvl_ref[...], dagg).astype(BF16)
        pre = abuf[m]
        sig_a = sigmoid(pre)
        dedge = (mm_t(gmsg, wm[...]) * (sig_a * (1.0 + pre * (1.0 - sig_a)))).astype(BF16)
        send_x = mm_t(dedge, ws[...])
        osndt = osndt_ref[...]
        hg[m] = split_sum(osndt[own:], send_x).astype(BF16)
        pair = [remote(hg.at[m, pl.ds(0, block)], snbuf.at[m], (bsend, brecv), micro + 2 * m, dom_prev),
                remote(hg.at[m, pl.ds(block, block)], spbuf.at[m], (bsend, brecv), micro + 2 * m + 1,
                       dom_next)]
        for copy in pair:
            copy.start()
        rows = c + mm_t(du, wn[...])
        rows = rows + split_sum(orcvt_ref[...], mm_t(dedge, wr[...]))
        p32[m] = rows + split_sum(osndt[:own], send_x)
        for copy in pair:
            copy.wait_recv()
        bwd_halo.extend(pair)
        sn = snbuf[m].astype(F32)
        sp = spbuf[m].astype(F32)
        for b in range(own // block):
            piece = p32[m, b * block:(b + 1) * block]
            piece = piece + jnp.where(hs0 == b, sn, 0.0) + jnp.where(hs1 == b, sp, 0.0)
            grad_ref[m, b * block:(b + 1) * block] = piece.astype(grad_ref.dtype)
        pl.when(has_prev)(pipe_in.start)
        bwd_pipe.append(pipe_in)

    for copy in fwd_pipe:
        pl.when(has_next)(copy.wait_send)
    for copy in bwd_pipe:
        pl.when(has_prev)(copy.wait_send)
    for copy in fwd_halo + bwd_halo:
        copy.wait_send()


def whole(operands, span, parts, sections):
    x = operands[1]
    micro, own, latent = x.shape
    vm = pl.BlockSpec(memory_space=pltpu.VMEM)
    anyspec = pl.BlockSpec(memory_space=pl.ANY)
    bf = lambda rows: pltpu.VMEM((micro, rows, latent), BF16)
    f32 = pltpu.VMEM((micro, own, latent), F32)
    in_specs = [pl.BlockSpec(memory_space=pltpu.SMEM), anyspec, anyspec] + [vm] * 5 + [anyspec] * 5 + [vm]
    return pl.pallas_call(
        functools.partial(whole_kernel, parts, sections),
        out_shape=(jax.ShapeDtypeStruct((micro, own, latent), BF16),
                   jax.ShapeDtypeStruct((micro, own, latent), BF16)),
        in_specs=in_specs,
        out_specs=(vm, vm),
        scratch_shapes=[bf(own), bf(own), pltpu.VMEM((5, latent, latent), BF16),
                        bf(own), bf(span), bf(span), bf(span), bf(span), f32, f32, bf(own), f32,
                        bf(2 * span), bf(span), bf(span),
                        pltpu.SemaphoreType.DMA((3 * micro,)), pltpu.SemaphoreType.DMA((3 * micro,)),
                        pltpu.SemaphoreType.DMA((3 * micro,)), pltpu.SemaphoreType.DMA((3 * micro,)),
                        pltpu.SemaphoreType.DMA((7,))],
        compiler_params=pltpu.CompilerParams(collective_id=0, has_side_effects=True,
                                             vmem_limit_bytes=48 * 1024 * 1024),
    )(*operands)


def shards(inputs, cotangent, w_send, w_recv, w_message, w_node, w_aggregate, gains,
           edge_send, edge_recv, edge_count, halo_send):
    sections = lax.axis_size("pipe")
    parts = lax.axis_size("dom")
    p_idx = lax.axis_index("pipe")
    micro, own, latent = inputs.shape
    block = edge_send.shape[1]
    span = halo_send.shape[2] * block
    ext_rows = own + 2 * span
    weights = (w_send[0], w_recv[0], w_message[0], w_node[0], w_aggregate[0])
    gain = gains[0].reshape(1, latent)
    hs = halo_send[0].reshape(-1).astype(jnp.int32)

    snd = edge_send.reshape(-1)
    rcv = edge_recv.reshape(-1)
    live = (jnp.arange(block)[None, :] < edge_count[:, None]).reshape(-1)
    osnd = (snd[:, None] == jnp.arange(ext_rows)[None, :]).astype(BF16)
    orcv_b = rcv[:, None] == jnp.arange(own)[None, :]
    orcv = orcv_b.astype(BF16)
    orcvl_b = orcv_b & live[:, None]
    orcvl = orcvl_b.astype(BF16)
    orcvt = orcvl_b.T.astype(BF16)
    osndt = osnd.T

    def blocks_of(x):
        shaped = x.reshape(micro, own // block, block, latent)
        nxt = jnp.take(shaped, hs[0], axis=1)
        prv = jnp.take(shaped, hs[1], axis=1)
        return nxt, prv

    S, D = sections, parts

    def perm_pipe(shift):
        return [(i, (i + shift) % S) for i in range(S)]

    def perm_both(dshift, pshift):
        return [(d * S + p, ((d + dshift) % D) * S + (p + pshift) % S)
                for d in range(D) for p in range(S)]

    both = ("dom", "pipe")

    fwd = vmem_call(
        fwd_kernel,
        (jax.ShapeDtypeStruct((micro, own, latent), BF16),
         jax.ShapeDtypeStruct((micro, own, latent), F32),
         jax.ShapeDtypeStruct((micro, own, latent), F32)),
        13)

    out_rec, grad_rec = whole(
        (hs, inputs, cotangent, osnd, orcv, orcvt, osndt, orcvl, *weights, gain), span, D, S)
    return (out_rec[None], grad_rec[None])


def solution(mesh):
    in_specs = (
        P(None, "dom", None),
        P(None, "dom", None),
        P("pipe", None, None),
        P("pipe", None, None),
        P("pipe", None, None),
        P("pipe", None, None),
        P("pipe", None, None),
        P("pipe", None),
        P("dom", None),
        P("dom", None),
        P("dom"),
        P("dom", None, None),
    )
    out_specs = (P("pipe", None, "dom", None), P("pipe", None, "dom", None))
    return jax.shard_map(shards, mesh=mesh, in_specs=in_specs, out_specs=out_specs, check_vma=False)
```

```python
import functools

import jax
import jax.numpy as jnp
from jax import lax
from jax.experimental import pallas as pl
from jax.experimental.pallas import tpu as pltpu
from jax.sharding import PartitionSpec as P

EPSILON = 1e-05
F32 = jnp.float32
BF16 = jnp.bfloat16


def mm(x, w):
    return jnp.dot(x, w, preferred_element_type=F32)


def mm_t(x, w):
    return lax.dot_general(x, w, (((1,), (1,)), ((), ())), preferred_element_type=F32)


def sigmoid(v):
    return 1.0 / (1.0 + jnp.exp(-v))


def split_sum(onehot, values):
    hi = values.astype(BF16)
    lo = (values - hi.astype(F32)).astype(BF16)
    return mm(onehot, hi) + mm(onehot, lo)


def fwd_micro(m, hs_ref, h_ref, fp_ref, fn_ref, osnd_ref, orcv_ref, orcvt_ref,
              ws_ref, wr_ref, wm_ref, wn_ref, wa_ref, g_ref, out_ref, a_ref, u_ref):
    own = h_ref.shape[1]
    span = fp_ref.shape[1]
    osnd = osnd_ref[...]
    h = h_ref[m]
    gathered = (mm(osnd[:, :own], h) + mm(osnd[:, own:own + span], fp_ref[m])
                + mm(osnd[:, own + span:], fn_ref[m])).astype(BF16)
    send_part = mm(gathered, ws_ref[...]).astype(BF16).astype(F32)
    recv_rows = mm(orcv_ref[...], h).astype(BF16)
    pre = send_part + mm(recv_rows, wr_ref[...])
    a_ref[m] = pre
    edge_hidden = (pre * sigmoid(pre)).astype(BF16)
    messages = mm(edge_hidden, wm_ref[...])
    agg = split_sum(orcvt_ref[...], messages).astype(BF16)
    node_pre = mm(h, wn_ref[...]) + mm(agg, wa_ref[...])
    u_ref[m] = node_pre
    act = node_pre * sigmoid(node_pre)
    mean = jnp.mean(act, axis=-1, keepdims=True)
    cen = act - mean
    var = jnp.mean(cen * cen, axis=-1, keepdims=True)
    unit = cen * lax.rsqrt(var + EPSILON)
    out_ref[m] = (h.astype(F32) + unit * g_ref[...]).astype(BF16)


def fwd_kernel(*refs):
    for m in range(refs[1].shape[0]):
        fwd_micro(m, *refs)


def bwd_micro(m, pin_ref, a_ref, u_ref, osndt_ref, orcvl_ref, orcvt_ref,
              ws_ref, wr_ref, wm_ref, wn_ref, wa_ref, g_ref, p32_ref, hg_ref):
    own = pin_ref.shape[1]
    gain = g_ref[...]
    c = pin_ref[m].astype(F32)
    node_pre = u_ref[m]
    sig_u = sigmoid(node_pre)
    act = node_pre * sig_u
    mean = jnp.mean(act, axis=-1, keepdims=True)
    cen = act - mean
    var = jnp.mean(cen * cen, axis=-1, keepdims=True)
    rs = lax.rsqrt(var + EPSILON)
    unit = cen * rs
    gu = c * gain
    gact = rs * (gu - jnp.mean(gu, axis=-1, keepdims=True)
                 - unit * jnp.mean(gu * unit, axis=-1, keepdims=True))
    du = (gact * (sig_u * (1.0 + node_pre * (1.0 - sig_u)))).astype(BF16)
    dagg = mm_t(du, wa_ref[...]).astype(BF16)
    rows = c + mm_t(du, wn_ref[...])
    gmsg = mm(orcvl_ref[...], dagg).astype(BF16)
    pre = a_ref[m]
    sig_a = sigmoid(pre)
    dedge = (mm_t(gmsg, wm_ref[...]) * (sig_a * (1.0 + pre * (1.0 - sig_a)))).astype(BF16)
    rows = rows + split_sum(orcvt_ref[...], mm_t(dedge, wr_ref[...]))
    send_rows = split_sum(osndt_ref[...], mm_t(dedge, ws_ref[...]))
    p32_ref[m] = rows + send_rows[:own]
    hg_ref[m] = send_rows[own:].astype(BF16)


MESH_ID = pl.DeviceIdType.MESH


def comm_kernel(sends, n_in, parts, sections, *refs):
    ins = refs[:n_in]
    outs = refs[n_in:n_in + len(sends)]
    send_sem, recv_sem = refs[n_in + len(sends):]
    d = lax.axis_index("dom")
    p = lax.axis_index("pipe")
    barrier = pltpu.get_barrier_semaphore()
    for _, _, _, dd, dp in sends:
        src = (lax.rem(d - dd + parts, parts), lax.rem(p - dp + sections, sections))
        pl.semaphore_signal(barrier, 1, device_id=src, device_id_type=MESH_ID)
    pl.semaphore_wait(barrier, len(sends))
    copies = []
    for i, (k, start, rows, dd, dp) in enumerate(sends):
        dst = (lax.rem(d + dd + parts, parts), lax.rem(p + dp + sections, sections))
        source = ins[k] if start is None else ins[k].at[:, pl.ds(start, rows)]
        copy = pltpu.make_async_remote_copy(
            src_ref=source, dst_ref=outs[i], send_sem=send_sem.at[i], recv_sem=recv_sem.at[i],
            device_id=dst, device_id_type=MESH_ID)
        copy.start()
        copies.append(copy)
    for copy in copies:
        copy.wait()


def exchange(sends, payloads, parts, sections, cid):
    out_shapes = []
    for k, start, rows, _, _ in sends:
        shape = payloads[k].shape
        if start is not None:
            shape = (shape[0], rows) + shape[2:]
        out_shapes.append(jax.ShapeDtypeStruct(shape, payloads[k].dtype))
    n = len(sends)
    return pl.pallas_call(
        functools.partial(comm_kernel, tuple(sends), len(payloads), parts, sections),
        out_shape=tuple(out_shapes),
        in_specs=[pl.BlockSpec(memory_space=pl.ANY)] * len(payloads),
        out_specs=tuple(pl.BlockSpec(memory_space=pl.ANY) for _ in sends),
        scratch_shapes=[pltpu.SemaphoreType.DMA((n,)), pltpu.SemaphoreType.DMA((n,))],
        compiler_params=pltpu.CompilerParams(collective_id=cid, has_side_effects=True),
    )(*payloads)


def record_copies(pairs, sem, active):
    def run():
        copies = [pltpu.make_async_copy(buf, rec, sem.at[i]) for i, (buf, rec) in enumerate(pairs)]
        for copy in copies:
            copy.start()
        for copy in copies:
            copy.wait()
    if active is None:
        run()
    else:
        pl.when(active)(run)


def fwd_tick_kernel(parts, sections, tick, hs_ref, h_ref, fp_ref, fn_ref, osnd_ref, orcv_ref, orcvt_ref,
                    ws_ref, wr_ref, wm_ref, wn_ref, wa_ref, g_ref, *refs):
    if tick > 0:
        refs = refs[3:]
    (orec, arec, urec, hn_ref, fpn_ref, fnn_ref, obuf, abuf, ubuf,
     hbuf, fpbuf, fnbuf, stage_n, stage_p, send_sem, recv_sem, rec_sem) = refs
    micro, own, _ = h_ref.shape
    block = fp_ref.shape[1]
    d = lax.axis_index("dom")
    p = lax.axis_index("pipe")
    pipe_next = (d, lax.rem(p + 1, sections))
    pipe_prev = (d, lax.rem(p - 1 + sections, sections))
    dom_next = (lax.rem(d + 1, parts), p)
    dom_prev = (lax.rem(d - 1 + parts, parts), p)
    barrier = pltpu.get_barrier_semaphore()
    for src in (pipe_prev, dom_prev, dom_next):
        pl.semaphore_signal(barrier, 1, device_id=src, device_id_type=MESH_ID)
    compute_refs = (hs_ref, h_ref, fp_ref, fn_ref, osnd_ref, orcv_ref, orcvt_ref,
                    ws_ref, wr_ref, wm_ref, wn_ref, wa_ref, g_ref, obuf, abuf, ubuf)
    pipe_copies = []
    for m in range(micro):
        fwd_micro(m, *compute_refs)
        if m == 0:
            pl.semaphore_wait(barrier, 3)
        copy = pltpu.make_async_remote_copy(
            src_ref=obuf.at[m], dst_ref=hbuf.at[m], send_sem=send_sem.at[0, m],
            recv_sem=recv_sem.at[0, m], device_id=pipe_next, device_id_type=MESH_ID)
        copy.start()
        pipe_copies.append(copy)
    record_copies(((obuf, orec), (abuf, arec), (ubuf, urec)), rec_sem,
                  None if tick == 0 else p == tick)
    hs0 = hs_ref[0]
    hs1 = hs_ref[1]
    halo_copies = []
    for m in range(micro):
        pipe_copies[m].wait_recv()
        h = hbuf[m]
        sel_n = h[0:block]
        sel_p = h[0:block]
        for b in range(1, own // block):
            piece = h[b * block:(b + 1) * block]
            sel_n = jnp.where(hs0 == b, piece, sel_n)
            sel_p = jnp.where(hs1 == b, piece, sel_p)
        stage_n[m] = sel_n
        stage_p[m] = sel_p
        for j, (stage, buf, dst) in enumerate(((stage_n, fpbuf, dom_next), (stage_p, fnbuf, dom_prev))):
            copy = pltpu.make_async_remote_copy(
                src_ref=stage.at[m], dst_ref=buf.at[m], send_sem=send_sem.at[1 + j, m],
                recv_sem=recv_sem.at[1 + j, m], device_id=dst, device_id_type=MESH_ID)
            copy.start()
            halo_copies.append(copy)
    for copy in pipe_copies:
        copy.wait_send()
    for copy in halo_copies:
        copy.wait()
    hn_ref[...] = hbuf[...]
    fpn_ref[...] = fpbuf[...]
    fnn_ref[...] = fnbuf[...]


def fwd_tick(operands, records, tick, span, parts, sections):
    h = operands[1]
    micro, own, latent = h.shape
    vm = pl.BlockSpec(memory_space=pltpu.VMEM)
    anyspec = pl.BlockSpec(memory_space=pl.ANY)
    bf = lambda rows: jax.ShapeDtypeStruct((micro, rows, latent), BF16)
    f32 = jax.ShapeDtypeStruct((micro, own, latent), F32)
    n = len(operands)
    extra = () if tick == 0 else tuple(records)
    return pl.pallas_call(
        functools.partial(fwd_tick_kernel, parts, sections, tick),
        out_shape=(bf(own), f32, f32, bf(own), bf(span), bf(span)),
        in_specs=[pl.BlockSpec(memory_space=pltpu.SMEM)] + [vm] * (n - 1) + [anyspec] * len(extra),
        out_specs=(anyspec, anyspec, anyspec, vm, vm, vm),
        scratch_shapes=[pltpu.VMEM((micro, own, latent), BF16),
                        pltpu.VMEM((micro, own, latent), F32),
                        pltpu.VMEM((micro, own, latent), F32),
                        pltpu.VMEM((micro, own, latent), BF16),
                        pltpu.VMEM((micro, span, latent), BF16),
                        pltpu.VMEM((micro, span, latent), BF16),
                        pltpu.VMEM((micro, span, latent), BF16),
                        pltpu.VMEM((micro, span, latent), BF16),
                        pltpu.SemaphoreType.DMA((3, micro)),
                        pltpu.SemaphoreType.DMA((3, micro)),
                        pltpu.SemaphoreType.DMA((3,))],
        input_output_aliases={} if tick == 0 else {n: 0, n + 1: 1, n + 2: 2},
        compiler_params=pltpu.CompilerParams(collective_id=10 + tick,
                                             has_side_effects=True,
                                             vmem_limit_bytes=48 * 1024 * 1024),
    )(*operands, *extra)


def fwd_last_kernel(tick, hs_ref, h_ref, fp_ref, fn_ref, osnd_ref, orcv_ref, orcvt_ref,
                    ws_ref, wr_ref, wm_ref, wn_ref, wa_ref, g_ref, orec_in, arec_in, urec_in,
                    orec, arec, urec, obuf, abuf, ubuf, rec_sem):
    compute_refs = (hs_ref, h_ref, fp_ref, fn_ref, osnd_ref, orcv_ref, orcvt_ref,
                    ws_ref, wr_ref, wm_ref, wn_ref, wa_ref, g_ref, obuf, abuf, ubuf)
    for m in range(h_ref.shape[0]):
        fwd_micro(m, *compute_refs)
    record_copies(((obuf, orec), (abuf, arec), (ubuf, urec)), rec_sem,
                  lax.axis_index("pipe") == tick)


def fwd_last(operands, records, tick):
    h = operands[1]
    micro, own, latent = h.shape
    vm = pl.BlockSpec(memory_space=pltpu.VMEM)
    anyspec = pl.BlockSpec(memory_space=pl.ANY)
    n = len(operands)
    return pl.pallas_call(
        functools.partial(fwd_last_kernel, tick),
        out_shape=tuple(jax.ShapeDtypeStruct(r.shape, r.dtype) for r in records),
        in_specs=[pl.BlockSpec(memory_space=pltpu.SMEM)] + [vm] * (n - 1) + [anyspec] * 3,
        out_specs=(anyspec, anyspec, anyspec),
        scratch_shapes=[pltpu.VMEM((micro, own, latent), BF16),
                        pltpu.VMEM((micro, own, latent), F32),
                        pltpu.VMEM((micro, own, latent), F32),
                        pltpu.SemaphoreType.DMA((3,))],
        input_output_aliases={n: 0, n + 1: 1, n + 2: 2},
        compiler_params=pltpu.CompilerParams(vmem_limit_bytes=48 * 1024 * 1024),
    )(*operands, *records)


def bwd_tick_kernel(parts, sections, tick, first, hs_ref, pin_ref, a_ref, u_ref, osndt_ref, orcvl_ref,
                    orcvt_ref, ws_ref, wr_ref, wm_ref, wn_ref, wa_ref, g_ref, *refs):
    send_pipe = tick > 0
    if not first:
        refs = refs[1:]
    if send_pipe:
        grec, pinn_ref, p32, hg, snbuf, spbuf, gbuf, pinbuf, send_sem, recv_sem, rec_sem = refs
    else:
        grec, p32, hg, snbuf, spbuf, gbuf, send_sem, recv_sem, rec_sem = refs
    micro, own, _ = pin_ref.shape
    block = snbuf.shape[1]
    d = lax.axis_index("dom")
    p = lax.axis_index("pipe")
    pipe_prev = (d, lax.rem(p - 1 + sections, sections))
    pipe_next = (d, lax.rem(p + 1, sections))
    dom_next = (lax.rem(d + 1, parts), p)
    dom_prev = (lax.rem(d - 1 + parts, parts), p)
    barrier = pltpu.get_barrier_semaphore()
    sources = [dom_next, dom_prev] + ([pipe_next] if send_pipe else [])
    for src in sources:
        pl.semaphore_signal(barrier, 1, device_id=src, device_id_type=MESH_ID)
    compute_refs = (pin_ref, a_ref, u_ref, osndt_ref, orcvl_ref, orcvt_ref,
                    ws_ref, wr_ref, wm_ref, wn_ref, wa_ref, g_ref, p32, hg)
    halo_copies = []
    for m in range(micro):
        bwd_micro(m, *compute_refs)
        if m == 0:
            pl.semaphore_wait(barrier, len(sources))
        pair = []
        for j, (lo, buf, dst) in enumerate(((0, snbuf, dom_prev), (block, spbuf, dom_next))):
            copy = pltpu.make_async_remote_copy(
                src_ref=hg.at[m, pl.ds(lo, block)], dst_ref=buf.at[m],
                send_sem=send_sem.at[j, m], recv_sem=recv_sem.at[j, m],
                device_id=dst, device_id_type=MESH_ID)
            copy.start()
            pair.append(copy)
        halo_copies.append(pair)
    hs0 = hs_ref[0]
    hs1 = hs_ref[1]
    pipe_copies = []
    for m in range(micro):
        for copy in halo_copies[m]:
            copy.wait_recv()
        sn = snbuf[m].astype(F32)
        sp = spbuf[m].astype(F32)
        for b in range(own // block):
            piece = p32[m, b * block:(b + 1) * block]
            piece = piece + jnp.where(hs0 == b, sn, 0.0) + jnp.where(hs1 == b, sp, 0.0)
            gbuf[m, b * block:(b + 1) * block] = piece.astype(gbuf.dtype)
        if send_pipe:
            copy = pltpu.make_async_remote_copy(
                src_ref=gbuf.at[m], dst_ref=pinbuf.at[m], send_sem=send_sem.at[2, m],
                recv_sem=recv_sem.at[2, m], device_id=pipe_prev, device_id_type=MESH_ID)
            copy.start()
            pipe_copies.append(copy)
    record_copies(((gbuf, grec),), rec_sem, None if first else p == tick)
    for pair in halo_copies:
        for copy in pair:
            copy.wait_send()
    for copy in pipe_copies:
        copy.wait()
    if send_pipe:
        pinn_ref[...] = pinbuf[...]


def bwd_tick(operands, grad_rec, tick, span, parts, sections):
    pin = operands[1]
    micro, own, latent = pin.shape
    send_pipe = tick > 0
    first = grad_rec is None
    vm = pl.BlockSpec(memory_space=pltpu.VMEM)
    anyspec = pl.BlockSpec(memory_space=pl.ANY)
    grad = jax.ShapeDtypeStruct((micro, own, latent), BF16)
    scratch = [pltpu.VMEM((micro, own, latent), F32), pltpu.VMEM((micro, 2 * span, latent), BF16),
               pltpu.VMEM((micro, span, latent), BF16), pltpu.VMEM((micro, span, latent), BF16),
               pltpu.VMEM((micro, own, latent), BF16)]
    if send_pipe:
        scratch.append(pltpu.VMEM((micro, own, latent), BF16))
    scratch += [pltpu.SemaphoreType.DMA((3, micro)), pltpu.SemaphoreType.DMA((3, micro)),
                pltpu.SemaphoreType.DMA((1,))]
    outs = (grad, grad) if send_pipe else (grad,)
    n = len(operands)
    extra = () if first else (grad_rec,)
    return pl.pallas_call(
        functools.partial(bwd_tick_kernel, parts, sections, tick, first),
        out_shape=outs,
        in_specs=[pl.BlockSpec(memory_space=pltpu.SMEM)] + [vm] * (n - 1) + [anyspec] * len(extra),
        out_specs=(anyspec,) + ((vm,) if send_pipe else ()),
        scratch_shapes=scratch,
        input_output_aliases={} if first else {n: 0},
        compiler_params=pltpu.CompilerParams(collective_id=20 + tick, has_side_effects=True,
                                             vmem_limit_bytes=48 * 1024 * 1024),
    )(*operands, *extra)


def vmem_call(kernel, out_shapes, n_in, smem_first=True):
    in_specs = [pl.BlockSpec(memory_space=pltpu.SMEM)] + [pl.BlockSpec(memory_space=pltpu.VMEM)] * (n_in - 1)
    return pl.pallas_call(
        kernel,
        out_shape=out_shapes,
        in_specs=in_specs,
        out_specs=tuple(pl.BlockSpec(memory_space=pltpu.VMEM) for _ in out_shapes),
        compiler_params=pltpu.CompilerParams(vmem_limit_bytes=48 * 1024 * 1024),
    )


def whole_kernel(parts, sections, hs_ref, x_hbm, cot_hbm, osnd_ref, orcv_ref, orcvt_ref, osndt_ref,
                 orcvl_ref, ws_hbm, wr_hbm, wm_hbm, wn_hbm, wa_hbm, g_ref,
                 out_ref, grad_ref,
                 xbuf, cotbuf, wbuf,
                 hbuf, fpbuf, fnbuf, stage_n, stage_p, abuf, ubuf, cbuf, p32, hg, snbuf, spbuf,
                 fsend, frecv, bsend, brecv, lsem):
    micro, own, latent = xbuf.shape
    block = fpbuf.shape[1]
    span = block
    loads = [pltpu.make_async_copy(x_hbm, xbuf, lsem.at[0])]
    for i, w in enumerate((ws_hbm, wr_hbm, wm_hbm, wn_hbm, wa_hbm)):
        loads.append(pltpu.make_async_copy(w, wbuf.at[i], lsem.at[1 + i]))
    loads.append(pltpu.make_async_copy(cot_hbm, cotbuf, lsem.at[6]))
    for copy in loads:
        copy.start()
    d = lax.axis_index("dom")
    p = lax.axis_index("pipe")
    pipe_next = (d, lax.rem(p + 1, sections))
    pipe_prev = (d, lax.rem(p - 1 + sections, sections))
    dom_next = (lax.rem(d + 1, parts), p)
    dom_prev = (lax.rem(d - 1 + parts, parts), p)
    barrier = pltpu.get_barrier_semaphore()
    for nb in (pipe_prev, pipe_next, dom_prev, dom_next):
        pl.semaphore_signal(barrier, 1, device_id=nb, device_id_type=MESH_ID)
    pl.semaphore_wait(barrier, 4)
    hs0 = hs_ref[0]
    hs1 = hs_ref[1]
    has_prev = p > 0
    has_next = p < sections - 1
    gain = g_ref[...]
    ws, wr, wm, wn, wa = (wbuf.at[i] for i in range(5))

    def remote(src, dst, sems, idx, target):
        send_sem, recv_sem = sems
        return pltpu.make_async_remote_copy(
            src_ref=src, dst_ref=dst, send_sem=send_sem.at[idx], recv_sem=recv_sem.at[idx],
            device_id=target, device_id_type=MESH_ID)

    loads[0].wait()
    fwd_pipe = []
    fwd_halo = []
    for m in range(micro):
        pipe_in = remote(out_ref.at[m], hbuf.at[m], (fsend, frecv), m, pipe_next)
        pl.when(has_prev)(pipe_in.wait_recv)

        @pl.when(p == 0)
        def _():
            hbuf[m] = xbuf[m]

        h = hbuf[m]
        sel_n = h[0:block]
        sel_p = h[0:block]
        for b in range(1, own // block):
            piece = h[b * block:(b + 1) * block]
            sel_n = jnp.where(hs0 == b, piece, sel_n)
            sel_p = jnp.where(hs1 == b, piece, sel_p)
        stage_n[m] = sel_n
        stage_p[m] = sel_p
        pair = [remote(stage_n.at[m], fpbuf.at[m], (fsend, frecv), micro + 2 * m, dom_next),
                remote(stage_p.at[m], fnbuf.at[m], (fsend, frecv), micro + 2 * m + 1, dom_prev)]
        for copy in pair:
            copy.start()
        if m == 0:
            for copy in loads[1:6]:
                copy.wait()
        osnd = osnd_ref[...]
        own_gather = mm(osnd[:, :own], h)
        recv_rows = mm(orcv_ref[...], h).astype(BF16)
        recv_part = mm(recv_rows, wr[...])
        node_part = mm(h, wn[...])
        for copy in pair:
            copy.wait_recv()
        fwd_halo.extend(pair)
        gathered = (own_gather + mm(osnd[:, own:own + span], fpbuf[m])
                    + mm(osnd[:, own + span:], fnbuf[m])).astype(BF16)
        send_part = mm(gathered, ws[...]).astype(BF16).astype(F32)
        pre = send_part + recv_part
        abuf[m] = pre
        edge_hidden = (pre * sigmoid(pre)).astype(BF16)
        messages = mm(edge_hidden, wm[...])
        agg = split_sum(orcvt_ref[...], messages).astype(BF16)
        node_pre = node_part + mm(agg, wa[...])
        ubuf[m] = node_pre
        act = node_pre * sigmoid(node_pre)
        mean = jnp.mean(act, axis=-1, keepdims=True)
        cen = act - mean
        var = jnp.mean(cen * cen, axis=-1, keepdims=True)
        unit = cen * lax.rsqrt(var + EPSILON)
        out_ref[m] = (h.astype(F32) + unit * gain).astype(BF16)
        pl.when(has_next)(pipe_in.start)
        fwd_pipe.append(pipe_in)

    loads[6].wait()
    bwd_pipe = []
    bwd_halo = []
    for m in range(micro):
        pipe_in = remote(grad_ref.at[m], cbuf.at[m], (bsend, brecv), m, pipe_prev)
        pl.when(has_next)(pipe_in.wait_recv)

        @pl.when(p == sections - 1)
        def _():
            cbuf[m] = cotbuf[m]

        c = cbuf[m].astype(F32)
        node_pre = ubuf[m]
        sig_u = sigmoid(node_pre)
        act = node_pre * sig_u
        mean = jnp.mean(act, axis=-1, keepdims=True)
        cen = act - mean
        var = jnp.mean(cen * cen, axis=-1, keepdims=True)
        rs = lax.rsqrt(var + EPSILON)
        unit = cen * rs
        gu = c * gain
        gact = rs * (gu - jnp.mean(gu, axis=-1, keepdims=True)
                     - unit * jnp.mean(gu * unit, axis=-1, keepdims=True))
        du = (gact * (sig_u * (1.0 + node_pre * (1.0 - sig_u)))).astype(BF16)
        dagg = mm_t(du, wa[...]).astype(BF16)
        gmsg = mm(orcvl_ref[...], dagg).astype(BF16)
        pre = abuf[m]
        sig_a = sigmoid(pre)
        dedge = (mm_t(gmsg, wm[...]) * (sig_a * (1.0 + pre * (1.0 - sig_a)))).astype(BF16)
        send_x = mm_t(dedge, ws[...])
        osndt = osndt_ref[...]
        hg[m] = split_sum(osndt[own:], send_x).astype(BF16)
        pair = [remote(hg.at[m, pl.ds(0, block)], snbuf.at[m], (bsend, brecv), micro + 2 * m, dom_prev),
                remote(hg.at[m, pl.ds(block, block)], spbuf.at[m], (bsend, brecv), micro + 2 * m + 1,
                       dom_next)]
        for copy in pair:
            copy.start()
        rows = c + mm_t(du, wn[...])
        rows = rows + split_sum(orcvt_ref[...], mm_t(dedge, wr[...]))
        p32[m] = rows + split_sum(osndt[:own], send_x)
        for copy in pair:
            copy.wait_recv()
        bwd_halo.extend(pair)
        sn = snbuf[m].astype(F32)
        sp = spbuf[m].astype(F32)
        for b in range(own // block):
            piece = p32[m, b * block:(b + 1) * block]
            piece = piece + jnp.where(hs0 == b, sn, 0.0) + jnp.where(hs1 == b, sp, 0.0)
            grad_ref[m, b * block:(b + 1) * block] = piece.astype(grad_ref.dtype)
        pl.when(has_prev)(pipe_in.start)
        bwd_pipe.append(pipe_in)

    for copy in fwd_pipe:
        pl.when(has_next)(copy.wait_send)
    for copy in bwd_pipe:
        pl.when(has_prev)(copy.wait_send)
    for copy in fwd_halo + bwd_halo:
        copy.wait_send()


def whole(operands, span, parts, sections):
    x = operands[1]
    micro, own, latent = x.shape
    vm = pl.BlockSpec(memory_space=pltpu.VMEM)
    anyspec = pl.BlockSpec(memory_space=pltpu.HBM)
    bf = lambda rows: pltpu.VMEM((micro, rows, latent), BF16)
    f32 = pltpu.VMEM((micro, own, latent), F32)
    in_specs = [pl.BlockSpec(memory_space=pltpu.SMEM), anyspec, anyspec] + [vm] * 5 + [anyspec] * 5 + [vm]
    return pl.pallas_call(
        functools.partial(whole_kernel, parts, sections),
        out_shape=(jax.ShapeDtypeStruct((micro, own, latent), BF16),
                   jax.ShapeDtypeStruct((micro, own, latent), BF16)),
        in_specs=in_specs,
        out_specs=(vm, vm),
        scratch_shapes=[bf(own), bf(own), pltpu.VMEM((5, latent, latent), BF16),
                        bf(own), bf(span), bf(span), bf(span), bf(span), f32, f32, bf(own), f32,
                        bf(2 * span), bf(span), bf(span),
                        pltpu.SemaphoreType.DMA((3 * micro,)), pltpu.SemaphoreType.DMA((3 * micro,)),
                        pltpu.SemaphoreType.DMA((3 * micro,)), pltpu.SemaphoreType.DMA((3 * micro,)),
                        pltpu.SemaphoreType.DMA((7,))],
        compiler_params=pltpu.CompilerParams(collective_id=0, has_side_effects=True,
                                             vmem_limit_bytes=67043328),
    )(*operands)


def shards(inputs, cotangent, w_send, w_recv, w_message, w_node, w_aggregate, gains,
           edge_send, edge_recv, edge_count, halo_send):
    sections = lax.axis_size("pipe")
    parts = lax.axis_size("dom")
    p_idx = lax.axis_index("pipe")
    micro, own, latent = inputs.shape
    block = edge_send.shape[1]
    span = halo_send.shape[2] * block
    ext_rows = own + 2 * span
    weights = (w_send[0], w_recv[0], w_message[0], w_node[0], w_aggregate[0])
    gain = gains[0].reshape(1, latent)
    hs = halo_send[0].reshape(-1).astype(jnp.int32)

    snd = edge_send.reshape(-1)
    rcv = edge_recv.reshape(-1)
    live = (jnp.arange(block)[None, :] < edge_count[:, None]).reshape(-1)
    osnd = (snd[:, None] == jnp.arange(ext_rows)[None, :]).astype(BF16)
    orcv_b = rcv[:, None] == jnp.arange(own)[None, :]
    orcv = orcv_b.astype(BF16)
    orcvl_b = orcv_b & live[:, None]
    orcvl = orcvl_b.astype(BF16)
    orcvt = orcvl_b.T.astype(BF16)
    osndt = osnd.T

    def blocks_of(x):
        shaped = x.reshape(micro, own // block, block, latent)
        nxt = jnp.take(shaped, hs[0], axis=1)
        prv = jnp.take(shaped, hs[1], axis=1)
        return nxt, prv

    S, D = sections, parts

    def perm_pipe(shift):
        return [(i, (i + shift) % S) for i in range(S)]

    def perm_both(dshift, pshift):
        return [(d * S + p, ((d + dshift) % D) * S + (p + pshift) % S)
                for d in range(D) for p in range(S)]

    both = ("dom", "pipe")

    fwd = vmem_call(
        fwd_kernel,
        (jax.ShapeDtypeStruct((micro, own, latent), BF16),
         jax.ShapeDtypeStruct((micro, own, latent), F32),
         jax.ShapeDtypeStruct((micro, own, latent), F32)),
        13)

    out_rec, grad_rec = whole(
        (hs, inputs, cotangent, osnd, orcv, orcvt, osndt, orcvl, *weights, gain), span, D, S)
    return (out_rec[None], grad_rec[None])


def solution(mesh):
    in_specs = (
        P(None, "dom", None),
        P(None, "dom", None),
        P("pipe", None, None),
        P("pipe", None, None),
        P("pipe", None, None),
        P("pipe", None, None),
        P("pipe", None, None),
        P("pipe", None),
        P("dom", None),
        P("dom", None),
        P("dom"),
        P("dom", None, None),
    )
    out_specs = (P("pipe", None, "dom", None), P("pipe", None, "dom", None))
    return jax.shard_map(shards, mesh=mesh, in_specs=in_specs, out_specs=out_specs, check_vma=False)
```

```python
import functools

import jax
import jax.numpy as jnp
from jax import lax
from jax.experimental import pallas as pl
from jax.experimental.pallas import tpu as pltpu
from jax.sharding import PartitionSpec as P

EPSILON = 1e-05
F32 = jnp.float32
BF16 = jnp.bfloat16


def mm(x, w):
    return jnp.dot(x, w, preferred_element_type=F32)


def mm_t(x, w):
    return lax.dot_general(x, w, (((1,), (1,)), ((), ())), preferred_element_type=F32)


def sigmoid(v):
    return 1.0 / (1.0 + jnp.exp(-v))


def split_sum(onehot, values):
    hi = values.astype(BF16)
    lo = (values - hi.astype(F32)).astype(BF16)
    return mm(onehot, hi) + mm(onehot, lo)


def fwd_micro(m, hs_ref, h_ref, fp_ref, fn_ref, osnd_ref, orcv_ref, orcvt_ref,
              ws_ref, wr_ref, wm_ref, wn_ref, wa_ref, g_ref, out_ref, a_ref, u_ref):
    own = h_ref.shape[1]
    span = fp_ref.shape[1]
    osnd = osnd_ref[...]
    h = h_ref[m]
    gathered = (mm(osnd[:, :own], h) + mm(osnd[:, own:own + span], fp_ref[m])
                + mm(osnd[:, own + span:], fn_ref[m])).astype(BF16)
    send_part = mm(gathered, ws_ref[...]).astype(BF16).astype(F32)
    recv_rows = mm(orcv_ref[...], h).astype(BF16)
    pre = send_part + mm(recv_rows, wr_ref[...])
    a_ref[m] = pre
    edge_hidden = (pre * sigmoid(pre)).astype(BF16)
    messages = mm(edge_hidden, wm_ref[...])
    agg = split_sum(orcvt_ref[...], messages).astype(BF16)
    node_pre = mm(h, wn_ref[...]) + mm(agg, wa_ref[...])
    u_ref[m] = node_pre
    act = node_pre * sigmoid(node_pre)
    mean = jnp.mean(act, axis=-1, keepdims=True)
    cen = act - mean
    var = jnp.mean(cen * cen, axis=-1, keepdims=True)
    unit = cen * lax.rsqrt(var + EPSILON)
    out_ref[m] = (h.astype(F32) + unit * g_ref[...]).astype(BF16)


def fwd_kernel(*refs):
    for m in range(refs[1].shape[0]):
        fwd_micro(m, *refs)


def bwd_micro(m, pin_ref, a_ref, u_ref, osndt_ref, orcvl_ref, orcvt_ref,
              ws_ref, wr_ref, wm_ref, wn_ref, wa_ref, g_ref, p32_ref, hg_ref):
    own = pin_ref.shape[1]
    gain = g_ref[...]
    c = pin_ref[m].astype(F32)
    node_pre = u_ref[m]
    sig_u = sigmoid(node_pre)
    act = node_pre * sig_u
    mean = jnp.mean(act, axis=-1, keepdims=True)
    cen = act - mean
    var = jnp.mean(cen * cen, axis=-1, keepdims=True)
    rs = lax.rsqrt(var + EPSILON)
    unit = cen * rs
    gu = c * gain
    gact = rs * (gu - jnp.mean(gu, axis=-1, keepdims=True)
                 - unit * jnp.mean(gu * unit, axis=-1, keepdims=True))
    du = (gact * (sig_u * (1.0 + node_pre * (1.0 - sig_u)))).astype(BF16)
    dagg = mm_t(du, wa_ref[...]).astype(BF16)
    rows = c + mm_t(du, wn_ref[...])
    gmsg = mm(orcvl_ref[...], dagg).astype(BF16)
    pre = a_ref[m]
    sig_a = sigmoid(pre)
    dedge = (mm_t(gmsg, wm_ref[...]) * (sig_a * (1.0 + pre * (1.0 - sig_a)))).astype(BF16)
    rows = rows + split_sum(orcvt_ref[...], mm_t(dedge, wr_ref[...]))
    send_rows = split_sum(osndt_ref[...], mm_t(dedge, ws_ref[...]))
    p32_ref[m] = rows + send_rows[:own]
    hg_ref[m] = send_rows[own:].astype(BF16)


MESH_ID = pl.DeviceIdType.MESH


def comm_kernel(sends, n_in, parts, sections, *refs):
    ins = refs[:n_in]
    outs = refs[n_in:n_in + len(sends)]
    send_sem, recv_sem = refs[n_in + len(sends):]
    d = lax.axis_index("dom")
    p = lax.axis_index("pipe")
    barrier = pltpu.get_barrier_semaphore()
    for _, _, _, dd, dp in sends:
        src = (lax.rem(d - dd + parts, parts), lax.rem(p - dp + sections, sections))
        pl.semaphore_signal(barrier, 1, device_id=src, device_id_type=MESH_ID)
    pl.semaphore_wait(barrier, len(sends))
    copies = []
    for i, (k, start, rows, dd, dp) in enumerate(sends):
        dst = (lax.rem(d + dd + parts, parts), lax.rem(p + dp + sections, sections))
        source = ins[k] if start is None else ins[k].at[:, pl.ds(start, rows)]
        copy = pltpu.make_async_remote_copy(
            src_ref=source, dst_ref=outs[i], send_sem=send_sem.at[i], recv_sem=recv_sem.at[i],
            device_id=dst, device_id_type=MESH_ID)
        copy.start()
        copies.append(copy)
    for copy in copies:
        copy.wait()


def exchange(sends, payloads, parts, sections, cid):
    out_shapes = []
    for k, start, rows, _, _ in sends:
        shape = payloads[k].shape
        if start is not None:
            shape = (shape[0], rows) + shape[2:]
        out_shapes.append(jax.ShapeDtypeStruct(shape, payloads[k].dtype))
    n = len(sends)
    return pl.pallas_call(
        functools.partial(comm_kernel, tuple(sends), len(payloads), parts, sections),
        out_shape=tuple(out_shapes),
        in_specs=[pl.BlockSpec(memory_space=pl.ANY)] * len(payloads),
        out_specs=tuple(pl.BlockSpec(memory_space=pl.ANY) for _ in sends),
        scratch_shapes=[pltpu.SemaphoreType.DMA((n,)), pltpu.SemaphoreType.DMA((n,))],
        compiler_params=pltpu.CompilerParams(collective_id=cid, has_side_effects=True),
    )(*payloads)


def record_copies(pairs, sem, active):
    def run():
        copies = [pltpu.make_async_copy(buf, rec, sem.at[i]) for i, (buf, rec) in enumerate(pairs)]
        for copy in copies:
            copy.start()
        for copy in copies:
            copy.wait()
    if active is None:
        run()
    else:
        pl.when(active)(run)


def fwd_tick_kernel(parts, sections, tick, hs_ref, h_ref, fp_ref, fn_ref, osnd_ref, orcv_ref, orcvt_ref,
                    ws_ref, wr_ref, wm_ref, wn_ref, wa_ref, g_ref, *refs):
    if tick > 0:
        refs = refs[3:]
    (orec, arec, urec, hn_ref, fpn_ref, fnn_ref, obuf, abuf, ubuf,
     hbuf, fpbuf, fnbuf, stage_n, stage_p, send_sem, recv_sem, rec_sem) = refs
    micro, own, _ = h_ref.shape
    block = fp_ref.shape[1]
    d = lax.axis_index("dom")
    p = lax.axis_index("pipe")
    pipe_next = (d, lax.rem(p + 1, sections))
    pipe_prev = (d, lax.rem(p - 1 + sections, sections))
    dom_next = (lax.rem(d + 1, parts), p)
    dom_prev = (lax.rem(d - 1 + parts, parts), p)
    barrier = pltpu.get_barrier_semaphore()
    for src in (pipe_prev, dom_prev, dom_next):
        pl.semaphore_signal(barrier, 1, device_id=src, device_id_type=MESH_ID)
    compute_refs = (hs_ref, h_ref, fp_ref, fn_ref, osnd_ref, orcv_ref, orcvt_ref,
                    ws_ref, wr_ref, wm_ref, wn_ref, wa_ref, g_ref, obuf, abuf, ubuf)
    pipe_copies = []
    for m in range(micro):
        fwd_micro(m, *compute_refs)
        if m == 0:
            pl.semaphore_wait(barrier, 3)
        copy = pltpu.make_async_remote_copy(
            src_ref=obuf.at[m], dst_ref=hbuf.at[m], send_sem=send_sem.at[0, m],
            recv_sem=recv_sem.at[0, m], device_id=pipe_next, device_id_type=MESH_ID)
        copy.start()
        pipe_copies.append(copy)
    record_copies(((obuf, orec), (abuf, arec), (ubuf, urec)), rec_sem,
                  None if tick == 0 else p == tick)
    hs0 = hs_ref[0]
    hs1 = hs_ref[1]
    halo_copies = []
    for m in range(micro):
        pipe_copies[m].wait_recv()
        h = hbuf[m]
        sel_n = h[0:block]
        sel_p = h[0:block]
        for b in range(1, own // block):
            piece = h[b * block:(b + 1) * block]
            sel_n = jnp.where(hs0 == b, piece, sel_n)
            sel_p = jnp.where(hs1 == b, piece, sel_p)
        stage_n[m] = sel_n
        stage_p[m] = sel_p
        for j, (stage, buf, dst) in enumerate(((stage_n, fpbuf, dom_next), (stage_p, fnbuf, dom_prev))):
            copy = pltpu.make_async_remote_copy(
                src_ref=stage.at[m], dst_ref=buf.at[m], send_sem=send_sem.at[1 + j, m],
                recv_sem=recv_sem.at[1 + j, m], device_id=dst, device_id_type=MESH_ID)
            copy.start()
            halo_copies.append(copy)
    for copy in pipe_copies:
        copy.wait_send()
    for copy in halo_copies:
        copy.wait()
    hn_ref[...] = hbuf[...]
    fpn_ref[...] = fpbuf[...]
    fnn_ref[...] = fnbuf[...]


def fwd_tick(operands, records, tick, span, parts, sections):
    h = operands[1]
    micro, own, latent = h.shape
    vm = pl.BlockSpec(memory_space=pltpu.VMEM)
    anyspec = pl.BlockSpec(memory_space=pl.ANY)
    bf = lambda rows: jax.ShapeDtypeStruct((micro, rows, latent), BF16)
    f32 = jax.ShapeDtypeStruct((micro, own, latent), F32)
    n = len(operands)
    extra = () if tick == 0 else tuple(records)
    return pl.pallas_call(
        functools.partial(fwd_tick_kernel, parts, sections, tick),
        out_shape=(bf(own), f32, f32, bf(own), bf(span), bf(span)),
        in_specs=[pl.BlockSpec(memory_space=pltpu.SMEM)] + [vm] * (n - 1) + [anyspec] * len(extra),
        out_specs=(anyspec, anyspec, anyspec, vm, vm, vm),
        scratch_shapes=[pltpu.VMEM((micro, own, latent), BF16),
                        pltpu.VMEM((micro, own, latent), F32),
                        pltpu.VMEM((micro, own, latent), F32),
                        pltpu.VMEM((micro, own, latent), BF16),
                        pltpu.VMEM((micro, span, latent), BF16),
                        pltpu.VMEM((micro, span, latent), BF16),
                        pltpu.VMEM((micro, span, latent), BF16),
                        pltpu.VMEM((micro, span, latent), BF16),
                        pltpu.SemaphoreType.DMA((3, micro)),
                        pltpu.SemaphoreType.DMA((3, micro)),
                        pltpu.SemaphoreType.DMA((3,))],
        input_output_aliases={} if tick == 0 else {n: 0, n + 1: 1, n + 2: 2},
        compiler_params=pltpu.CompilerParams(collective_id=10 + tick,
                                             has_side_effects=True,
                                             vmem_limit_bytes=48 * 1024 * 1024),
    )(*operands, *extra)


def fwd_last_kernel(tick, hs_ref, h_ref, fp_ref, fn_ref, osnd_ref, orcv_ref, orcvt_ref,
                    ws_ref, wr_ref, wm_ref, wn_ref, wa_ref, g_ref, orec_in, arec_in, urec_in,
                    orec, arec, urec, obuf, abuf, ubuf, rec_sem):
    compute_refs = (hs_ref, h_ref, fp_ref, fn_ref, osnd_ref, orcv_ref, orcvt_ref,
                    ws_ref, wr_ref, wm_ref, wn_ref, wa_ref, g_ref, obuf, abuf, ubuf)
    for m in range(h_ref.shape[0]):
        fwd_micro(m, *compute_refs)
    record_copies(((obuf, orec), (abuf, arec), (ubuf, urec)), rec_sem,
                  lax.axis_index("pipe") == tick)


def fwd_last(operands, records, tick):
    h = operands[1]
    micro, own, latent = h.shape
    vm = pl.BlockSpec(memory_space=pltpu.VMEM)
    anyspec = pl.BlockSpec(memory_space=pl.ANY)
    n = len(operands)
    return pl.pallas_call(
        functools.partial(fwd_last_kernel, tick),
        out_shape=tuple(jax.ShapeDtypeStruct(r.shape, r.dtype) for r in records),
        in_specs=[pl.BlockSpec(memory_space=pltpu.SMEM)] + [vm] * (n - 1) + [anyspec] * 3,
        out_specs=(anyspec, anyspec, anyspec),
        scratch_shapes=[pltpu.VMEM((micro, own, latent), BF16),
                        pltpu.VMEM((micro, own, latent), F32),
                        pltpu.VMEM((micro, own, latent), F32),
                        pltpu.SemaphoreType.DMA((3,))],
        input_output_aliases={n: 0, n + 1: 1, n + 2: 2},
        compiler_params=pltpu.CompilerParams(vmem_limit_bytes=48 * 1024 * 1024),
    )(*operands, *records)


def bwd_tick_kernel(parts, sections, tick, first, hs_ref, pin_ref, a_ref, u_ref, osndt_ref, orcvl_ref,
                    orcvt_ref, ws_ref, wr_ref, wm_ref, wn_ref, wa_ref, g_ref, *refs):
    send_pipe = tick > 0
    if not first:
        refs = refs[1:]
    if send_pipe:
        grec, pinn_ref, p32, hg, snbuf, spbuf, gbuf, pinbuf, send_sem, recv_sem, rec_sem = refs
    else:
        grec, p32, hg, snbuf, spbuf, gbuf, send_sem, recv_sem, rec_sem = refs
    micro, own, _ = pin_ref.shape
    block = snbuf.shape[1]
    d = lax.axis_index("dom")
    p = lax.axis_index("pipe")
    pipe_prev = (d, lax.rem(p - 1 + sections, sections))
    pipe_next = (d, lax.rem(p + 1, sections))
    dom_next = (lax.rem(d + 1, parts), p)
    dom_prev = (lax.rem(d - 1 + parts, parts), p)
    barrier = pltpu.get_barrier_semaphore()
    sources = [dom_next, dom_prev] + ([pipe_next] if send_pipe else [])
    for src in sources:
        pl.semaphore_signal(barrier, 1, device_id=src, device_id_type=MESH_ID)
    compute_refs = (pin_ref, a_ref, u_ref, osndt_ref, orcvl_ref, orcvt_ref,
                    ws_ref, wr_ref, wm_ref, wn_ref, wa_ref, g_ref, p32, hg)
    halo_copies = []
    for m in range(micro):
        bwd_micro(m, *compute_refs)
        if m == 0:
            pl.semaphore_wait(barrier, len(sources))
        pair = []
        for j, (lo, buf, dst) in enumerate(((0, snbuf, dom_prev), (block, spbuf, dom_next))):
            copy = pltpu.make_async_remote_copy(
                src_ref=hg.at[m, pl.ds(lo, block)], dst_ref=buf.at[m],
                send_sem=send_sem.at[j, m], recv_sem=recv_sem.at[j, m],
                device_id=dst, device_id_type=MESH_ID)
            copy.start()
            pair.append(copy)
        halo_copies.append(pair)
    hs0 = hs_ref[0]
    hs1 = hs_ref[1]
    pipe_copies = []
    for m in range(micro):
        for copy in halo_copies[m]:
            copy.wait_recv()
        sn = snbuf[m].astype(F32)
        sp = spbuf[m].astype(F32)
        for b in range(own // block):
            piece = p32[m, b * block:(b + 1) * block]
            piece = piece + jnp.where(hs0 == b, sn, 0.0) + jnp.where(hs1 == b, sp, 0.0)
            gbuf[m, b * block:(b + 1) * block] = piece.astype(gbuf.dtype)
        if send_pipe:
            copy = pltpu.make_async_remote_copy(
                src_ref=gbuf.at[m], dst_ref=pinbuf.at[m], send_sem=send_sem.at[2, m],
                recv_sem=recv_sem.at[2, m], device_id=pipe_prev, device_id_type=MESH_ID)
            copy.start()
            pipe_copies.append(copy)
    record_copies(((gbuf, grec),), rec_sem, None if first else p == tick)
    for pair in halo_copies:
        for copy in pair:
            copy.wait_send()
    for copy in pipe_copies:
        copy.wait()
    if send_pipe:
        pinn_ref[...] = pinbuf[...]


def bwd_tick(operands, grad_rec, tick, span, parts, sections):
    pin = operands[1]
    micro, own, latent = pin.shape
    send_pipe = tick > 0
    first = grad_rec is None
    vm = pl.BlockSpec(memory_space=pltpu.VMEM)
    anyspec = pl.BlockSpec(memory_space=pl.ANY)
    grad = jax.ShapeDtypeStruct((micro, own, latent), BF16)
    scratch = [pltpu.VMEM((micro, own, latent), F32), pltpu.VMEM((micro, 2 * span, latent), BF16),
               pltpu.VMEM((micro, span, latent), BF16), pltpu.VMEM((micro, span, latent), BF16),
               pltpu.VMEM((micro, own, latent), BF16)]
    if send_pipe:
        scratch.append(pltpu.VMEM((micro, own, latent), BF16))
    scratch += [pltpu.SemaphoreType.DMA((3, micro)), pltpu.SemaphoreType.DMA((3, micro)),
                pltpu.SemaphoreType.DMA((1,))]
    outs = (grad, grad) if send_pipe else (grad,)
    n = len(operands)
    extra = () if first else (grad_rec,)
    return pl.pallas_call(
        functools.partial(bwd_tick_kernel, parts, sections, tick, first),
        out_shape=outs,
        in_specs=[pl.BlockSpec(memory_space=pltpu.SMEM)] + [vm] * (n - 1) + [anyspec] * len(extra),
        out_specs=(anyspec,) + ((vm,) if send_pipe else ()),
        scratch_shapes=scratch,
        input_output_aliases={} if first else {n: 0},
        compiler_params=pltpu.CompilerParams(collective_id=20 + tick, has_side_effects=True,
                                             vmem_limit_bytes=48 * 1024 * 1024),
    )(*operands, *extra)


def vmem_call(kernel, out_shapes, n_in, smem_first=True):
    in_specs = [pl.BlockSpec(memory_space=pltpu.SMEM)] + [pl.BlockSpec(memory_space=pltpu.VMEM)] * (n_in - 1)
    return pl.pallas_call(
        kernel,
        out_shape=out_shapes,
        in_specs=in_specs,
        out_specs=tuple(pl.BlockSpec(memory_space=pltpu.VMEM) for _ in out_shapes),
        compiler_params=pltpu.CompilerParams(vmem_limit_bytes=48 * 1024 * 1024),
    )


def whole_kernel(parts, sections, hs_ref, cnt_ref, x_hbm, cot_hbm, esnd_ref, ercv_ref,
                 ws_hbm, wr_hbm, wm_hbm, wn_hbm, wa_hbm, g_ref,
                 out_ref, grad_ref,
                 xbuf, cotbuf, wbuf, osnd_ref, orcv_ref, orcvt_ref, osndt_ref, orcvl_ref,
                 hbuf, fpbuf, fnbuf, stage_n, stage_p, abuf, ubuf, cbuf, p32, hg, snbuf, spbuf,
                 fsend, frecv, bsend, brecv, lsem):
    micro, own, latent = xbuf.shape
    block = fpbuf.shape[1]
    span = block
    loads = [pltpu.make_async_copy(x_hbm, xbuf, lsem.at[0])]
    for i, w in enumerate((ws_hbm, wr_hbm, wm_hbm, wn_hbm, wa_hbm)):
        loads.append(pltpu.make_async_copy(w, wbuf.at[i], lsem.at[1 + i]))
    loads.append(pltpu.make_async_copy(cot_hbm, cotbuf, lsem.at[6]))
    for copy in loads:
        copy.start()
    edges = osnd_ref.shape[0]
    ext_rows = osnd_ref.shape[1]
    own_rows = orcv_ref.shape[1]
    es = esnd_ref[...]
    er = ercv_ref[...]
    snd = jnp.concatenate([es[i:i + 1] for i in range(es.shape[0])], axis=1)
    rcv = jnp.concatenate([er[i:i + 1] for i in range(er.shape[0])], axis=1)
    lane = lax.broadcasted_iota(jnp.int32, (1, edges), 1)
    per_block = es.shape[1]
    live = lane < 0
    for i in range(es.shape[0]):
        live = live | ((lane >= i * per_block) & (lane < i * per_block + cnt_ref[i]))
    sndt = lax.broadcasted_iota(jnp.int32, (ext_rows, edges), 0) == snd
    rcvt = lax.broadcasted_iota(jnp.int32, (own_rows, edges), 0) == rcv
    osndt_f = sndt.astype(F32)
    rcvt_f = rcvt.astype(F32)
    rcvlt_f = (rcvt & live).astype(F32)
    osndt_ref[...] = osndt_f.astype(BF16)
    orcvt_ref[...] = rcvlt_f.astype(BF16)
    osnd_ref[...] = osndt_f.T.astype(BF16)
    orcv_ref[...] = rcvt_f.T.astype(BF16)
    orcvl_ref[...] = rcvlt_f.T.astype(BF16)
    d = lax.axis_index("dom")
    p = lax.axis_index("pipe")
    pipe_next = (d, lax.rem(p + 1, sections))
    pipe_prev = (d, lax.rem(p - 1 + sections, sections))
    dom_next = (lax.rem(d + 1, parts), p)
    dom_prev = (lax.rem(d - 1 + parts, parts), p)
    barrier = pltpu.get_barrier_semaphore()
    for nb in (pipe_prev, pipe_next, dom_prev, dom_next):
        pl.semaphore_signal(barrier, 1, device_id=nb, device_id_type=MESH_ID)
    pl.semaphore_wait(barrier, 4)
    hs0 = hs_ref[0]
    hs1 = hs_ref[1]
    has_prev = p > 0
    has_next = p < sections - 1
    gain = g_ref[...]
    ws, wr, wm, wn, wa = (wbuf.at[i] for i in range(5))

    def remote(src, dst, sems, idx, target):
        send_sem, recv_sem = sems
        return pltpu.make_async_remote_copy(
            src_ref=src, dst_ref=dst, send_sem=send_sem.at[idx], recv_sem=recv_sem.at[idx],
            device_id=target, device_id_type=MESH_ID)

    loads[0].wait()
    fwd_pipe = []
    fwd_halo = []
    for m in range(micro):
        pipe_in = remote(out_ref.at[m], hbuf.at[m], (fsend, frecv), m, pipe_next)
        pl.when(has_prev)(pipe_in.wait_recv)

        @pl.when(p == 0)
        def _():
            hbuf[m] = xbuf[m]

        h = hbuf[m]
        sel_n = h[0:block]
        sel_p = h[0:block]
        for b in range(1, own // block):
            piece = h[b * block:(b + 1) * block]
            sel_n = jnp.where(hs0 == b, piece, sel_n)
            sel_p = jnp.where(hs1 == b, piece, sel_p)
        stage_n[m] = sel_n
        stage_p[m] = sel_p
        pair = [remote(stage_n.at[m], fpbuf.at[m], (fsend, frecv), micro + 2 * m, dom_next),
                remote(stage_p.at[m], fnbuf.at[m], (fsend, frecv), micro + 2 * m + 1, dom_prev)]
        for copy in pair:
            copy.start()
        if m == 0:
            for copy in loads[1:6]:
                copy.wait()
        osnd = osnd_ref[...]
        own_gather = mm(osnd[:, :own], h)
        recv_rows = mm(orcv_ref[...], h).astype(BF16)
        recv_part = mm(recv_rows, wr[...])
        node_part = mm(h, wn[...])
        for copy in pair:
            copy.wait_recv()
        fwd_halo.extend(pair)
        gathered = (own_gather + mm(osnd[:, own:own + span], fpbuf[m])
                    + mm(osnd[:, own + span:], fnbuf[m])).astype(BF16)
        send_part = mm(gathered, ws[...]).astype(BF16).astype(F32)
        pre = send_part + recv_part
        abuf[m] = pre
        edge_hidden = (pre * sigmoid(pre)).astype(BF16)
        messages = mm(edge_hidden, wm[...])
        agg = split_sum(orcvt_ref[...], messages).astype(BF16)
        node_pre = node_part + mm(agg, wa[...])
        ubuf[m] = node_pre
        act = node_pre * sigmoid(node_pre)
        mean = jnp.mean(act, axis=-1, keepdims=True)
        cen = act - mean
        var = jnp.mean(cen * cen, axis=-1, keepdims=True)
        unit = cen * lax.rsqrt(var + EPSILON)
        out_ref[m] = (h.astype(F32) + unit * gain).astype(BF16)
        pl.when(has_next)(pipe_in.start)
        fwd_pipe.append(pipe_in)

    loads[6].wait()
    bwd_pipe = []
    bwd_halo = []
    for m in range(micro):
        pipe_in = remote(grad_ref.at[m], cbuf.at[m], (bsend, brecv), m, pipe_prev)
        pl.when(has_next)(pipe_in.wait_recv)

        @pl.when(p == sections - 1)
        def _():
            cbuf[m] = cotbuf[m]

        c = cbuf[m].astype(F32)
        node_pre = ubuf[m]
        sig_u = sigmoid(node_pre)
        act = node_pre * sig_u
        mean = jnp.mean(act, axis=-1, keepdims=True)
        cen = act - mean
        var = jnp.mean(cen * cen, axis=-1, keepdims=True)
        rs = lax.rsqrt(var + EPSILON)
        unit = cen * rs
        gu = c * gain
        gact = rs * (gu - jnp.mean(gu, axis=-1, keepdims=True)
                     - unit * jnp.mean(gu * unit, axis=-1, keepdims=True))
        du = (gact * (sig_u * (1.0 + node_pre * (1.0 - sig_u)))).astype(BF16)
        dagg = mm_t(du, wa[...]).astype(BF16)
        gmsg = mm(orcvl_ref[...], dagg).astype(BF16)
        pre = abuf[m]
        sig_a = sigmoid(pre)
        dedge = (mm_t(gmsg, wm[...]) * (sig_a * (1.0 + pre * (1.0 - sig_a)))).astype(BF16)
        send_x = mm_t(dedge, ws[...])
        osndt = osndt_ref[...]
        hg[m] = split_sum(osndt[own:], send_x).astype(BF16)
        pair = [remote(hg.at[m, pl.ds(0, block)], snbuf.at[m], (bsend, brecv), micro + 2 * m, dom_prev),
                remote(hg.at[m, pl.ds(block, block)], spbuf.at[m], (bsend, brecv), micro + 2 * m + 1,
                       dom_next)]
        for copy in pair:
            copy.start()
        rows = c + mm_t(du, wn[...])
        rows = rows + split_sum(orcvt_ref[...], mm_t(dedge, wr[...]))
        p32[m] = rows + split_sum(osndt[:own], send_x)
        for copy in pair:
            copy.wait_recv()
        bwd_halo.extend(pair)
        sn = snbuf[m].astype(F32)
        sp = spbuf[m].astype(F32)
        for b in range(own // block):
            piece = p32[m, b * block:(b + 1) * block]
            piece = piece + jnp.where(hs0 == b, sn, 0.0) + jnp.where(hs1 == b, sp, 0.0)
            grad_ref[m, b * block:(b + 1) * block] = piece.astype(grad_ref.dtype)
        pl.when(has_prev)(pipe_in.start)
        bwd_pipe.append(pipe_in)

    for copy in fwd_pipe:
        pl.when(has_next)(copy.wait_send)
    for copy in bwd_pipe:
        pl.when(has_prev)(copy.wait_send)
    for copy in fwd_halo + bwd_halo:
        copy.wait_send()


def whole(operands, span, parts, sections):
    x = operands[2]
    micro, own, latent = x.shape
    vm = pl.BlockSpec(memory_space=pltpu.VMEM)
    anyspec = pl.BlockSpec(memory_space=pltpu.HBM)
    bf = lambda rows: pltpu.VMEM((micro, rows, latent), BF16)
    f32 = pltpu.VMEM((micro, own, latent), F32)
    smem = pl.BlockSpec(memory_space=pltpu.SMEM)
    in_specs = [smem, smem, anyspec, anyspec, vm, vm] + [anyspec] * 5 + [vm]
    edges = operands[4].size
    ext_rows = own + 2 * span
    return pl.pallas_call(
        functools.partial(whole_kernel, parts, sections),
        out_shape=(jax.ShapeDtypeStruct((micro, own, latent), BF16),
                   jax.ShapeDtypeStruct((micro, own, latent), BF16)),
        in_specs=in_specs,
        out_specs=(vm, vm),
        scratch_shapes=[bf(own), bf(own), pltpu.VMEM((5, latent, latent), BF16),
                        pltpu.VMEM((edges, ext_rows), BF16), pltpu.VMEM((edges, own), BF16),
                        pltpu.VMEM((own, edges), BF16), pltpu.VMEM((ext_rows, edges), BF16),
                        pltpu.VMEM((edges, own), BF16),
                        bf(own), bf(span), bf(span), bf(span), bf(span), f32, f32, bf(own), f32,
                        bf(2 * span), bf(span), bf(span),
                        pltpu.SemaphoreType.DMA((3 * micro,)), pltpu.SemaphoreType.DMA((3 * micro,)),
                        pltpu.SemaphoreType.DMA((3 * micro,)), pltpu.SemaphoreType.DMA((3 * micro,)),
                        pltpu.SemaphoreType.DMA((7,))],
        compiler_params=pltpu.CompilerParams(collective_id=0, has_side_effects=True,
                                             vmem_limit_bytes=67043328),
    )(*operands)


def shards(inputs, cotangent, w_send, w_recv, w_message, w_node, w_aggregate, gains,
           edge_send, edge_recv, edge_count, halo_send):
    sections = lax.axis_size("pipe")
    parts = lax.axis_size("dom")
    p_idx = lax.axis_index("pipe")
    micro, own, latent = inputs.shape
    block = edge_send.shape[1]
    span = halo_send.shape[2] * block
    ext_rows = own + 2 * span
    weights = (w_send[0], w_recv[0], w_message[0], w_node[0], w_aggregate[0])
    gain = gains[0].reshape(1, latent)
    hs = halo_send[0].reshape(-1).astype(jnp.int32)

    def blocks_of(x):
        shaped = x.reshape(micro, own // block, block, latent)
        nxt = jnp.take(shaped, hs[0], axis=1)
        prv = jnp.take(shaped, hs[1], axis=1)
        return nxt, prv

    S, D = sections, parts

    def perm_pipe(shift):
        return [(i, (i + shift) % S) for i in range(S)]

    def perm_both(dshift, pshift):
        return [(d * S + p, ((d + dshift) % D) * S + (p + pshift) % S)
                for d in range(D) for p in range(S)]

    both = ("dom", "pipe")

    fwd = vmem_call(
        fwd_kernel,
        (jax.ShapeDtypeStruct((micro, own, latent), BF16),
         jax.ShapeDtypeStruct((micro, own, latent), F32),
         jax.ShapeDtypeStruct((micro, own, latent), F32)),
        13)

    out_rec, grad_rec = whole(
        (hs, edge_count.astype(jnp.int32), inputs, cotangent, edge_send.astype(jnp.int32),
         edge_recv.astype(jnp.int32), *weights, gain), span, D, S)
    return (out_rec[None], grad_rec[None])


def solution(mesh):
    in_specs = (
        P(None, "dom", None),
        P(None, "dom", None),
        P("pipe", None, None),
        P("pipe", None, None),
        P("pipe", None, None),
        P("pipe", None, None),
        P("pipe", None, None),
        P("pipe", None),
        P("dom", None),
        P("dom", None),
        P("dom"),
        P("dom", None, None),
    )
    out_specs = (P("pipe", None, "dom", None), P("pipe", None, "dom", None))
    return jax.shard_map(shards, mesh=mesh, in_specs=in_specs, out_specs=out_specs, check_vma=False)
```

```python
import functools

import jax
import jax.numpy as jnp
from jax import lax
from jax.experimental import pallas as pl
from jax.experimental.pallas import tpu as pltpu
from jax.sharding import PartitionSpec as P

EPSILON = 1e-05
F32 = jnp.float32
BF16 = jnp.bfloat16


def mm(x, w):
    return jnp.dot(x, w, preferred_element_type=F32)


def mm_t(x, w):
    return lax.dot_general(x, w, (((1,), (1,)), ((), ())), preferred_element_type=F32)


def sigmoid(v):
    return 1.0 / (1.0 + jnp.exp(-v))


def split_sum(onehot, values):
    hi = values.astype(BF16)
    lo = (values - hi.astype(F32)).astype(BF16)
    return mm(onehot, hi) + mm(onehot, lo)


def fwd_micro(m, hs_ref, h_ref, fp_ref, fn_ref, osnd_ref, orcv_ref, orcvt_ref,
              ws_ref, wr_ref, wm_ref, wn_ref, wa_ref, g_ref, out_ref, a_ref, u_ref):
    own = h_ref.shape[1]
    span = fp_ref.shape[1]
    osnd = osnd_ref[...]
    h = h_ref[m]
    gathered = (mm(osnd[:, :own], h) + mm(osnd[:, own:own + span], fp_ref[m])
                + mm(osnd[:, own + span:], fn_ref[m])).astype(BF16)
    send_part = mm(gathered, ws_ref[...]).astype(BF16).astype(F32)
    recv_rows = mm(orcv_ref[...], h).astype(BF16)
    pre = send_part + mm(recv_rows, wr_ref[...])
    a_ref[m] = pre
    edge_hidden = (pre * sigmoid(pre)).astype(BF16)
    messages = mm(edge_hidden, wm_ref[...])
    agg = split_sum(orcvt_ref[...], messages).astype(BF16)
    node_pre = mm(h, wn_ref[...]) + mm(agg, wa_ref[...])
    u_ref[m] = node_pre
    act = node_pre * sigmoid(node_pre)
    mean = jnp.mean(act, axis=-1, keepdims=True)
    cen = act - mean
    var = jnp.mean(cen * cen, axis=-1, keepdims=True)
    unit = cen * lax.rsqrt(var + EPSILON)
    out_ref[m] = (h.astype(F32) + unit * g_ref[...]).astype(BF16)


def fwd_kernel(*refs):
    for m in range(refs[1].shape[0]):
        fwd_micro(m, *refs)


def bwd_micro(m, pin_ref, a_ref, u_ref, osndt_ref, orcvl_ref, orcvt_ref,
              ws_ref, wr_ref, wm_ref, wn_ref, wa_ref, g_ref, p32_ref, hg_ref):
    own = pin_ref.shape[1]
    gain = g_ref[...]
    c = pin_ref[m].astype(F32)
    node_pre = u_ref[m]
    sig_u = sigmoid(node_pre)
    act = node_pre * sig_u
    mean = jnp.mean(act, axis=-1, keepdims=True)
    cen = act - mean
    var = jnp.mean(cen * cen, axis=-1, keepdims=True)
    rs = lax.rsqrt(var + EPSILON)
    unit = cen * rs
    gu = c * gain
    gact = rs * (gu - jnp.mean(gu, axis=-1, keepdims=True)
                 - unit * jnp.mean(gu * unit, axis=-1, keepdims=True))
    du = (gact * (sig_u * (1.0 + node_pre * (1.0 - sig_u)))).astype(BF16)
    dagg = mm_t(du, wa_ref[...]).astype(BF16)
    rows = c + mm_t(du, wn_ref[...])
    gmsg = mm(orcvl_ref[...], dagg).astype(BF16)
    pre = a_ref[m]
    sig_a = sigmoid(pre)
    dedge = (mm_t(gmsg, wm_ref[...]) * (sig_a * (1.0 + pre * (1.0 - sig_a)))).astype(BF16)
    rows = rows + split_sum(orcvt_ref[...], mm_t(dedge, wr_ref[...]))
    send_rows = split_sum(osndt_ref[...], mm_t(dedge, ws_ref[...]))
    p32_ref[m] = rows + send_rows[:own]
    hg_ref[m] = send_rows[own:].astype(BF16)


MESH_ID = pl.DeviceIdType.MESH


def comm_kernel(sends, n_in, parts, sections, *refs):
    ins = refs[:n_in]
    outs = refs[n_in:n_in + len(sends)]
    send_sem, recv_sem = refs[n_in + len(sends):]
    d = lax.axis_index("dom")
    p = lax.axis_index("pipe")
    barrier = pltpu.get_barrier_semaphore()
    for _, _, _, dd, dp in sends:
        src = (lax.rem(d - dd + parts, parts), lax.rem(p - dp + sections, sections))
        pl.semaphore_signal(barrier, 1, device_id=src, device_id_type=MESH_ID)
    pl.semaphore_wait(barrier, len(sends))
    copies = []
    for i, (k, start, rows, dd, dp) in enumerate(sends):
        dst = (lax.rem(d + dd + parts, parts), lax.rem(p + dp + sections, sections))
        source = ins[k] if start is None else ins[k].at[:, pl.ds(start, rows)]
        copy = pltpu.make_async_remote_copy(
            src_ref=source, dst_ref=outs[i], send_sem=send_sem.at[i], recv_sem=recv_sem.at[i],
            device_id=dst, device_id_type=MESH_ID)
        copy.start()
        copies.append(copy)
    for copy in copies:
        copy.wait()


def exchange(sends, payloads, parts, sections, cid):
    out_shapes = []
    for k, start, rows, _, _ in sends:
        shape = payloads[k].shape
        if start is not None:
            shape = (shape[0], rows) + shape[2:]
        out_shapes.append(jax.ShapeDtypeStruct(shape, payloads[k].dtype))
    n = len(sends)
    return pl.pallas_call(
        functools.partial(comm_kernel, tuple(sends), len(payloads), parts, sections),
        out_shape=tuple(out_shapes),
        in_specs=[pl.BlockSpec(memory_space=pl.ANY)] * len(payloads),
        out_specs=tuple(pl.BlockSpec(memory_space=pl.ANY) for _ in sends),
        scratch_shapes=[pltpu.SemaphoreType.DMA((n,)), pltpu.SemaphoreType.DMA((n,))],
        compiler_params=pltpu.CompilerParams(collective_id=cid, has_side_effects=True),
    )(*payloads)


def record_copies(pairs, sem, active):
    def run():
        copies = [pltpu.make_async_copy(buf, rec, sem.at[i]) for i, (buf, rec) in enumerate(pairs)]
        for copy in copies:
            copy.start()
        for copy in copies:
            copy.wait()
    if active is None:
        run()
    else:
        pl.when(active)(run)


def fwd_tick_kernel(parts, sections, tick, hs_ref, h_ref, fp_ref, fn_ref, osnd_ref, orcv_ref, orcvt_ref,
                    ws_ref, wr_ref, wm_ref, wn_ref, wa_ref, g_ref, *refs):
    if tick > 0:
        refs = refs[3:]
    (orec, arec, urec, hn_ref, fpn_ref, fnn_ref, obuf, abuf, ubuf,
     hbuf, fpbuf, fnbuf, stage_n, stage_p, send_sem, recv_sem, rec_sem) = refs
    micro, own, _ = h_ref.shape
    block = fp_ref.shape[1]
    d = lax.axis_index("dom")
    p = lax.axis_index("pipe")
    pipe_next = (d, lax.rem(p + 1, sections))
    pipe_prev = (d, lax.rem(p - 1 + sections, sections))
    dom_next = (lax.rem(d + 1, parts), p)
    dom_prev = (lax.rem(d - 1 + parts, parts), p)
    barrier = pltpu.get_barrier_semaphore()
    for src in (pipe_prev, dom_prev, dom_next):
        pl.semaphore_signal(barrier, 1, device_id=src, device_id_type=MESH_ID)
    compute_refs = (hs_ref, h_ref, fp_ref, fn_ref, osnd_ref, orcv_ref, orcvt_ref,
                    ws_ref, wr_ref, wm_ref, wn_ref, wa_ref, g_ref, obuf, abuf, ubuf)
    pipe_copies = []
    for m in range(micro):
        fwd_micro(m, *compute_refs)
        if m == 0:
            pl.semaphore_wait(barrier, 3)
        copy = pltpu.make_async_remote_copy(
            src_ref=obuf.at[m], dst_ref=hbuf.at[m], send_sem=send_sem.at[0, m],
            recv_sem=recv_sem.at[0, m], device_id=pipe_next, device_id_type=MESH_ID)
        copy.start()
        pipe_copies.append(copy)
    record_copies(((obuf, orec), (abuf, arec), (ubuf, urec)), rec_sem,
                  None if tick == 0 else p == tick)
    hs0 = hs_ref[0]
    hs1 = hs_ref[1]
    halo_copies = []
    for m in range(micro):
        pipe_copies[m].wait_recv()
        h = hbuf[m]
        sel_n = h[0:block]
        sel_p = h[0:block]
        for b in range(1, own // block):
            piece = h[b * block:(b + 1) * block]
            sel_n = jnp.where(hs0 == b, piece, sel_n)
            sel_p = jnp.where(hs1 == b, piece, sel_p)
        stage_n[m] = sel_n
        stage_p[m] = sel_p
        for j, (stage, buf, dst) in enumerate(((stage_n, fpbuf, dom_next), (stage_p, fnbuf, dom_prev))):
            copy = pltpu.make_async_remote_copy(
                src_ref=stage.at[m], dst_ref=buf.at[m], send_sem=send_sem.at[1 + j, m],
                recv_sem=recv_sem.at[1 + j, m], device_id=dst, device_id_type=MESH_ID)
            copy.start()
            halo_copies.append(copy)
    for copy in pipe_copies:
        copy.wait_send()
    for copy in halo_copies:
        copy.wait()
    hn_ref[...] = hbuf[...]
    fpn_ref[...] = fpbuf[...]
    fnn_ref[...] = fnbuf[...]


def fwd_tick(operands, records, tick, span, parts, sections):
    h = operands[1]
    micro, own, latent = h.shape
    vm = pl.BlockSpec(memory_space=pltpu.VMEM)
    anyspec = pl.BlockSpec(memory_space=pl.ANY)
    bf = lambda rows: jax.ShapeDtypeStruct((micro, rows, latent), BF16)
    f32 = jax.ShapeDtypeStruct((micro, own, latent), F32)
    n = len(operands)
    extra = () if tick == 0 else tuple(records)
    return pl.pallas_call(
        functools.partial(fwd_tick_kernel, parts, sections, tick),
        out_shape=(bf(own), f32, f32, bf(own), bf(span), bf(span)),
        in_specs=[pl.BlockSpec(memory_space=pltpu.SMEM)] + [vm] * (n - 1) + [anyspec] * len(extra),
        out_specs=(anyspec, anyspec, anyspec, vm, vm, vm),
        scratch_shapes=[pltpu.VMEM((micro, own, latent), BF16),
                        pltpu.VMEM((micro, own, latent), F32),
                        pltpu.VMEM((micro, own, latent), F32),
                        pltpu.VMEM((micro, own, latent), BF16),
                        pltpu.VMEM((micro, span, latent), BF16),
                        pltpu.VMEM((micro, span, latent), BF16),
                        pltpu.VMEM((micro, span, latent), BF16),
                        pltpu.VMEM((micro, span, latent), BF16),
                        pltpu.SemaphoreType.DMA((3, micro)),
                        pltpu.SemaphoreType.DMA((3, micro)),
                        pltpu.SemaphoreType.DMA((3,))],
        input_output_aliases={} if tick == 0 else {n: 0, n + 1: 1, n + 2: 2},
        compiler_params=pltpu.CompilerParams(collective_id=10 + tick,
                                             has_side_effects=True,
                                             vmem_limit_bytes=48 * 1024 * 1024),
    )(*operands, *extra)


def fwd_last_kernel(tick, hs_ref, h_ref, fp_ref, fn_ref, osnd_ref, orcv_ref, orcvt_ref,
                    ws_ref, wr_ref, wm_ref, wn_ref, wa_ref, g_ref, orec_in, arec_in, urec_in,
                    orec, arec, urec, obuf, abuf, ubuf, rec_sem):
    compute_refs = (hs_ref, h_ref, fp_ref, fn_ref, osnd_ref, orcv_ref, orcvt_ref,
                    ws_ref, wr_ref, wm_ref, wn_ref, wa_ref, g_ref, obuf, abuf, ubuf)
    for m in range(h_ref.shape[0]):
        fwd_micro(m, *compute_refs)
    record_copies(((obuf, orec), (abuf, arec), (ubuf, urec)), rec_sem,
                  lax.axis_index("pipe") == tick)


def fwd_last(operands, records, tick):
    h = operands[1]
    micro, own, latent = h.shape
    vm = pl.BlockSpec(memory_space=pltpu.VMEM)
    anyspec = pl.BlockSpec(memory_space=pl.ANY)
    n = len(operands)
    return pl.pallas_call(
        functools.partial(fwd_last_kernel, tick),
        out_shape=tuple(jax.ShapeDtypeStruct(r.shape, r.dtype) for r in records),
        in_specs=[pl.BlockSpec(memory_space=pltpu.SMEM)] + [vm] * (n - 1) + [anyspec] * 3,
        out_specs=(anyspec, anyspec, anyspec),
        scratch_shapes=[pltpu.VMEM((micro, own, latent), BF16),
                        pltpu.VMEM((micro, own, latent), F32),
                        pltpu.VMEM((micro, own, latent), F32),
                        pltpu.SemaphoreType.DMA((3,))],
        input_output_aliases={n: 0, n + 1: 1, n + 2: 2},
        compiler_params=pltpu.CompilerParams(vmem_limit_bytes=48 * 1024 * 1024),
    )(*operands, *records)


def bwd_tick_kernel(parts, sections, tick, first, hs_ref, pin_ref, a_ref, u_ref, osndt_ref, orcvl_ref,
                    orcvt_ref, ws_ref, wr_ref, wm_ref, wn_ref, wa_ref, g_ref, *refs):
    send_pipe = tick > 0
    if not first:
        refs = refs[1:]
    if send_pipe:
        grec, pinn_ref, p32, hg, snbuf, spbuf, gbuf, pinbuf, send_sem, recv_sem, rec_sem = refs
    else:
        grec, p32, hg, snbuf, spbuf, gbuf, send_sem, recv_sem, rec_sem = refs
    micro, own, _ = pin_ref.shape
    block = snbuf.shape[1]
    d = lax.axis_index("dom")
    p = lax.axis_index("pipe")
    pipe_prev = (d, lax.rem(p - 1 + sections, sections))
    pipe_next = (d, lax.rem(p + 1, sections))
    dom_next = (lax.rem(d + 1, parts), p)
    dom_prev = (lax.rem(d - 1 + parts, parts), p)
    barrier = pltpu.get_barrier_semaphore()
    sources = [dom_next, dom_prev] + ([pipe_next] if send_pipe else [])
    for src in sources:
        pl.semaphore_signal(barrier, 1, device_id=src, device_id_type=MESH_ID)
    compute_refs = (pin_ref, a_ref, u_ref, osndt_ref, orcvl_ref, orcvt_ref,
                    ws_ref, wr_ref, wm_ref, wn_ref, wa_ref, g_ref, p32, hg)
    halo_copies = []
    for m in range(micro):
        bwd_micro(m, *compute_refs)
        if m == 0:
            pl.semaphore_wait(barrier, len(sources))
        pair = []
        for j, (lo, buf, dst) in enumerate(((0, snbuf, dom_prev), (block, spbuf, dom_next))):
            copy = pltpu.make_async_remote_copy(
                src_ref=hg.at[m, pl.ds(lo, block)], dst_ref=buf.at[m],
                send_sem=send_sem.at[j, m], recv_sem=recv_sem.at[j, m],
                device_id=dst, device_id_type=MESH_ID)
            copy.start()
            pair.append(copy)
        halo_copies.append(pair)
    hs0 = hs_ref[0]
    hs1 = hs_ref[1]
    pipe_copies = []
    for m in range(micro):
        for copy in halo_copies[m]:
            copy.wait_recv()
        sn = snbuf[m].astype(F32)
        sp = spbuf[m].astype(F32)
        for b in range(own // block):
            piece = p32[m, b * block:(b + 1) * block]
            piece = piece + jnp.where(hs0 == b, sn, 0.0) + jnp.where(hs1 == b, sp, 0.0)
            gbuf[m, b * block:(b + 1) * block] = piece.astype(gbuf.dtype)
        if send_pipe:
            copy = pltpu.make_async_remote_copy(
                src_ref=gbuf.at[m], dst_ref=pinbuf.at[m], send_sem=send_sem.at[2, m],
                recv_sem=recv_sem.at[2, m], device_id=pipe_prev, device_id_type=MESH_ID)
            copy.start()
            pipe_copies.append(copy)
    record_copies(((gbuf, grec),), rec_sem, None if first else p == tick)
    for pair in halo_copies:
        for copy in pair:
            copy.wait_send()
    for copy in pipe_copies:
        copy.wait()
    if send_pipe:
        pinn_ref[...] = pinbuf[...]


def bwd_tick(operands, grad_rec, tick, span, parts, sections):
    pin = operands[1]
    micro, own, latent = pin.shape
    send_pipe = tick > 0
    first = grad_rec is None
    vm = pl.BlockSpec(memory_space=pltpu.VMEM)
    anyspec = pl.BlockSpec(memory_space=pl.ANY)
    grad = jax.ShapeDtypeStruct((micro, own, latent), BF16)
    scratch = [pltpu.VMEM((micro, own, latent), F32), pltpu.VMEM((micro, 2 * span, latent), BF16),
               pltpu.VMEM((micro, span, latent), BF16), pltpu.VMEM((micro, span, latent), BF16),
               pltpu.VMEM((micro, own, latent), BF16)]
    if send_pipe:
        scratch.append(pltpu.VMEM((micro, own, latent), BF16))
    scratch += [pltpu.SemaphoreType.DMA((3, micro)), pltpu.SemaphoreType.DMA((3, micro)),
                pltpu.SemaphoreType.DMA((1,))]
    outs = (grad, grad) if send_pipe else (grad,)
    n = len(operands)
    extra = () if first else (grad_rec,)
    return pl.pallas_call(
        functools.partial(bwd_tick_kernel, parts, sections, tick, first),
        out_shape=outs,
        in_specs=[pl.BlockSpec(memory_space=pltpu.SMEM)] + [vm] * (n - 1) + [anyspec] * len(extra),
        out_specs=(anyspec,) + ((vm,) if send_pipe else ()),
        scratch_shapes=scratch,
        input_output_aliases={} if first else {n: 0},
        compiler_params=pltpu.CompilerParams(collective_id=20 + tick, has_side_effects=True,
                                             vmem_limit_bytes=48 * 1024 * 1024),
    )(*operands, *extra)


def vmem_call(kernel, out_shapes, n_in, smem_first=True):
    in_specs = [pl.BlockSpec(memory_space=pltpu.SMEM)] + [pl.BlockSpec(memory_space=pltpu.VMEM)] * (n_in - 1)
    return pl.pallas_call(
        kernel,
        out_shape=out_shapes,
        in_specs=in_specs,
        out_specs=tuple(pl.BlockSpec(memory_space=pltpu.VMEM) for _ in out_shapes),
        compiler_params=pltpu.CompilerParams(vmem_limit_bytes=48 * 1024 * 1024),
    )


def whole_kernel(parts, sections, hs_ref, cnt_ref, x_hbm, cot_hbm, esnd_ref, ercv_ref,
                 ws_hbm, wr_hbm, wm_hbm, wn_hbm, wa_hbm, g_ref,
                 out_ref, grad_ref,
                 xbuf, cotbuf, wbuf, osnd_ref, orcv_ref, orcvt_ref, osndt_ref, orcvl_ref,
                 hbuf, fpbuf, fnbuf, stage_n, stage_p, abuf, ubuf, cbuf, p32, hg, snbuf, spbuf,
                 fsend, frecv, bsend, brecv, lsem):
    micro, own, latent = xbuf.shape
    block = fpbuf.shape[1]
    span = block
    loads = [pltpu.make_async_copy(x_hbm, xbuf, lsem.at[0])]
    for i, w in enumerate((ws_hbm, wr_hbm, wm_hbm, wn_hbm, wa_hbm)):
        loads.append(pltpu.make_async_copy(w, wbuf.at[i], lsem.at[1 + i]))
    loads.append(pltpu.make_async_copy(cot_hbm, cotbuf, lsem.at[6]))
    for copy in loads:
        copy.start()
    edges = osnd_ref.shape[0]
    ext_rows = osnd_ref.shape[1]
    own_rows = orcv_ref.shape[1]
    es = esnd_ref[...]
    er = ercv_ref[...]
    snd = jnp.concatenate([es[i:i + 1] for i in range(es.shape[0])], axis=1)
    rcv = jnp.concatenate([er[i:i + 1] for i in range(er.shape[0])], axis=1)
    lane = lax.broadcasted_iota(jnp.int32, (1, edges), 1)
    per_block = es.shape[1]
    live = lane < 0
    for i in range(es.shape[0]):
        live = live | ((lane >= i * per_block) & (lane < i * per_block + cnt_ref[i]))
    sndt = lax.broadcasted_iota(jnp.int32, (ext_rows, edges), 0) == snd
    rcvt = lax.broadcasted_iota(jnp.int32, (own_rows, edges), 0) == rcv
    osndt_f = sndt.astype(F32)
    rcvt_f = rcvt.astype(F32)
    rcvlt_f = (rcvt & live).astype(F32)
    osndt_ref[...] = osndt_f.astype(BF16)
    orcvt_ref[...] = rcvlt_f.astype(BF16)
    osnd_ref[...] = osndt_f.T.astype(BF16)
    orcv_ref[...] = rcvt_f.T.astype(BF16)
    orcvl_ref[...] = rcvlt_f.T.astype(BF16)
    d = lax.axis_index("dom")
    p = lax.axis_index("pipe")
    pipe_next = (d, lax.rem(p + 1, sections))
    pipe_prev = (d, lax.rem(p - 1 + sections, sections))
    dom_next = (lax.rem(d + 1, parts), p)
    dom_prev = (lax.rem(d - 1 + parts, parts), p)
    barrier = pltpu.get_barrier_semaphore()
    for nb in (pipe_prev, pipe_next, dom_prev, dom_next):
        pl.semaphore_signal(barrier, 1, device_id=nb, device_id_type=MESH_ID)
    pl.semaphore_wait(barrier, 4)
    hs0 = hs_ref[0]
    hs1 = hs_ref[1]
    has_prev = p > 0
    has_next = p < sections - 1
    gain = g_ref[...]
    ws, wr, wm, wn, wa = (wbuf.at[i] for i in range(5))

    def remote(src, dst, sems, idx, target):
        send_sem, recv_sem = sems
        return pltpu.make_async_remote_copy(
            src_ref=src, dst_ref=dst, send_sem=send_sem.at[idx], recv_sem=recv_sem.at[idx],
            device_id=target, device_id_type=MESH_ID)

    loads[0].wait()
    fwd_pipe = []
    fwd_halo = []

    def fwd_step(m):
        pipe_in = remote(out_ref.at[m], hbuf.at[m], (fsend, frecv), m, pipe_next)
        pl.when(has_prev)(pipe_in.wait_recv)

        @pl.when(p == 0)
        def _():
            hbuf[m] = xbuf[m]

        h = hbuf[m]
        sel_n = h[0:block]
        sel_p = h[0:block]
        for b in range(1, own // block):
            piece = h[b * block:(b + 1) * block]
            sel_n = jnp.where(hs0 == b, piece, sel_n)
            sel_p = jnp.where(hs1 == b, piece, sel_p)
        stage_n[m] = sel_n
        stage_p[m] = sel_p
        pair = [remote(stage_n.at[m], fpbuf.at[m], (fsend, frecv), micro + 2 * m, dom_next),
                remote(stage_p.at[m], fnbuf.at[m], (fsend, frecv), micro + 2 * m + 1, dom_prev)]
        for copy in pair:
            copy.start()
        if m == 0:
            for copy in loads[1:6]:
                copy.wait()
        osnd = osnd_ref[...]
        own_gather = mm(osnd[:, :own], h)
        recv_rows = mm(orcv_ref[...], h).astype(BF16)
        recv_part = mm(recv_rows, wr[...])
        node_part = mm(h, wn[...])
        for copy in pair:
            copy.wait_recv()
        fwd_halo.extend(pair)
        gathered = (own_gather + mm(osnd[:, own:own + span], fpbuf[m])
                    + mm(osnd[:, own + span:], fnbuf[m])).astype(BF16)
        send_part = mm(gathered, ws[...]).astype(BF16).astype(F32)
        pre = send_part + recv_part
        abuf[m] = pre
        edge_hidden = (pre * sigmoid(pre)).astype(BF16)
        messages = mm(edge_hidden, wm[...])
        agg = split_sum(orcvt_ref[...], messages).astype(BF16)
        node_pre = node_part + mm(agg, wa[...])
        ubuf[m] = node_pre
        act = node_pre * sigmoid(node_pre)
        mean = jnp.mean(act, axis=-1, keepdims=True)
        cen = act - mean
        var = jnp.mean(cen * cen, axis=-1, keepdims=True)
        unit = cen * lax.rsqrt(var + EPSILON)
        out_ref[m] = (h.astype(F32) + unit * gain).astype(BF16)
        pl.when(has_next)(pipe_in.start)
        fwd_pipe.append(pipe_in)


    def bwd_step(m):
        d = lax.axis_index("dom")
        p = lax.axis_index("pipe")
        pipe_prev = (d, lax.rem(p - 1 + sections, sections))
        pipe_next = (d, lax.rem(p + 1, sections))
        dom_next = (lax.rem(d + 1, parts), p)
        dom_prev = (lax.rem(d - 1 + parts, parts), p)
        has_prev = p > 0
        has_next = p < sections - 1
        hs0 = hs_ref[0]
        hs1 = hs_ref[1]
        gain = g_ref[...]
        pipe_in = remote(grad_ref.at[m], cbuf.at[m], (bsend, brecv), m, pipe_prev)
        pl.when(has_next)(pipe_in.wait_recv)

        @pl.when(p == sections - 1)
        def _():
            cbuf[m] = cotbuf[m]

        c = cbuf[m].astype(F32)
        node_pre = ubuf[m]
        sig_u = sigmoid(node_pre)
        act = node_pre * sig_u
        mean = jnp.mean(act, axis=-1, keepdims=True)
        cen = act - mean
        var = jnp.mean(cen * cen, axis=-1, keepdims=True)
        rs = lax.rsqrt(var + EPSILON)
        unit = cen * rs
        gu = c * gain
        gact = rs * (gu - jnp.mean(gu, axis=-1, keepdims=True)
                     - unit * jnp.mean(gu * unit, axis=-1, keepdims=True))
        du = (gact * (sig_u * (1.0 + node_pre * (1.0 - sig_u)))).astype(BF16)
        dagg = mm_t(du, wa[...]).astype(BF16)
        gmsg = mm(orcvl_ref[...], dagg).astype(BF16)
        pre = abuf[m]
        sig_a = sigmoid(pre)
        dedge = (mm_t(gmsg, wm[...]) * (sig_a * (1.0 + pre * (1.0 - sig_a)))).astype(BF16)
        send_x = mm_t(dedge, ws[...])
        osndt = osndt_ref[...]
        hg[m] = split_sum(osndt[own:], send_x).astype(BF16)
        pair = [remote(hg.at[m, pl.ds(0, block)], snbuf.at[m], (bsend, brecv), micro + 2 * m, dom_prev),
                remote(hg.at[m, pl.ds(block, block)], spbuf.at[m], (bsend, brecv), micro + 2 * m + 1,
                       dom_next)]
        for copy in pair:
            copy.start()
        rows = c + mm_t(du, wn[...])
        rows = rows + split_sum(orcvt_ref[...], mm_t(dedge, wr[...]))
        p32[m] = rows + split_sum(osndt[:own], send_x)
        for copy in pair:
            copy.wait_recv()
        sn = snbuf[m].astype(F32)
        sp = spbuf[m].astype(F32)
        for b in range(own // block):
            piece = p32[m, b * block:(b + 1) * block]
            piece = piece + jnp.where(hs0 == b, sn, 0.0) + jnp.where(hs1 == b, sp, 0.0)
            grad_ref[m, b * block:(b + 1) * block] = piece.astype(grad_ref.dtype)
        pl.when(has_prev)(pipe_in.start)


    last = p == sections - 1
    fwd_step(0)
    loads[6].wait()
    pl.when(last)(functools.partial(bwd_step, 0))
    for m in range(1, micro):
        fwd_step(m)
    pl.when(jnp.logical_not(last))(functools.partial(bwd_step, 0))
    for m in range(1, micro):
        bwd_step(m)

    for copy in fwd_pipe:
        pl.when(has_next)(copy.wait_send)
    for m in range(micro):
        done = remote(grad_ref.at[m], cbuf.at[m], (bsend, brecv), m, pipe_prev)
        pl.when(has_prev)(done.wait_send)
        fwd_halo.append(remote(hg.at[m, pl.ds(0, block)], snbuf.at[m], (bsend, brecv), micro + 2 * m,
                               dom_prev))
        fwd_halo.append(remote(hg.at[m, pl.ds(block, block)], spbuf.at[m], (bsend, brecv),
                               micro + 2 * m + 1, dom_next))
    for copy in fwd_halo:
        copy.wait_send()


def whole(operands, span, parts, sections):
    x = operands[2]
    micro, own, latent = x.shape
    vm = pl.BlockSpec(memory_space=pltpu.VMEM)
    anyspec = pl.BlockSpec(memory_space=pltpu.HBM)
    bf = lambda rows: pltpu.VMEM((micro, rows, latent), BF16)
    f32 = pltpu.VMEM((micro, own, latent), F32)
    smem = pl.BlockSpec(memory_space=pltpu.SMEM)
    in_specs = [smem, smem, anyspec, anyspec, vm, vm] + [anyspec] * 5 + [vm]
    edges = operands[4].size
    ext_rows = own + 2 * span
    return pl.pallas_call(
        functools.partial(whole_kernel, parts, sections),
        out_shape=(jax.ShapeDtypeStruct((micro, own, latent), BF16),
                   jax.ShapeDtypeStruct((micro, own, latent), BF16)),
        in_specs=in_specs,
        out_specs=(vm, vm),
        scratch_shapes=[bf(own), bf(own), pltpu.VMEM((5, latent, latent), BF16),
                        pltpu.VMEM((edges, ext_rows), BF16), pltpu.VMEM((edges, own), BF16),
                        pltpu.VMEM((own, edges), BF16), pltpu.VMEM((ext_rows, edges), BF16),
                        pltpu.VMEM((edges, own), BF16),
                        bf(own), bf(span), bf(span), bf(span), bf(span), f32, f32, bf(own), f32,
                        bf(2 * span), bf(span), bf(span),
                        pltpu.SemaphoreType.DMA((3 * micro,)), pltpu.SemaphoreType.DMA((3 * micro,)),
                        pltpu.SemaphoreType.DMA((3 * micro,)), pltpu.SemaphoreType.DMA((3 * micro,)),
                        pltpu.SemaphoreType.DMA((7,))],
        compiler_params=pltpu.CompilerParams(collective_id=0, has_side_effects=True,
                                             vmem_limit_bytes=67043328),
    )(*operands)


def shards(inputs, cotangent, w_send, w_recv, w_message, w_node, w_aggregate, gains,
           edge_send, edge_recv, edge_count, halo_send):
    sections = lax.axis_size("pipe")
    parts = lax.axis_size("dom")
    p_idx = lax.axis_index("pipe")
    micro, own, latent = inputs.shape
    block = edge_send.shape[1]
    span = halo_send.shape[2] * block
    ext_rows = own + 2 * span
    weights = (w_send[0], w_recv[0], w_message[0], w_node[0], w_aggregate[0])
    gain = gains[0].reshape(1, latent)
    hs = halo_send[0].reshape(-1).astype(jnp.int32)

    def blocks_of(x):
        shaped = x.reshape(micro, own // block, block, latent)
        nxt = jnp.take(shaped, hs[0], axis=1)
        prv = jnp.take(shaped, hs[1], axis=1)
        return nxt, prv

    S, D = sections, parts

    def perm_pipe(shift):
        return [(i, (i + shift) % S) for i in range(S)]

    def perm_both(dshift, pshift):
        return [(d * S + p, ((d + dshift) % D) * S + (p + pshift) % S)
                for d in range(D) for p in range(S)]

    both = ("dom", "pipe")

    fwd = vmem_call(
        fwd_kernel,
        (jax.ShapeDtypeStruct((micro, own, latent), BF16),
         jax.ShapeDtypeStruct((micro, own, latent), F32),
         jax.ShapeDtypeStruct((micro, own, latent), F32)),
        13)

    out_rec, grad_rec = whole(
        (hs, edge_count.astype(jnp.int32), inputs, cotangent, edge_send.astype(jnp.int32),
         edge_recv.astype(jnp.int32), *weights, gain), span, D, S)
    return (out_rec[None], grad_rec[None])


def solution(mesh):
    in_specs = (
        P(None, "dom", None),
        P(None, "dom", None),
        P("pipe", None, None),
        P("pipe", None, None),
        P("pipe", None, None),
        P("pipe", None, None),
        P("pipe", None, None),
        P("pipe", None),
        P("dom", None),
        P("dom", None),
        P("dom"),
        P("dom", None, None),
    )
    out_specs = (P("pipe", None, "dom", None), P("pipe", None, "dom", None))
    return jax.shard_map(shards, mesh=mesh, in_specs=in_specs, out_specs=out_specs, check_vma=False)
```

```python
import functools

import jax
import jax.numpy as jnp
from jax import lax
from jax.experimental import pallas as pl
from jax.experimental.pallas import tpu as pltpu
from jax.sharding import PartitionSpec as P

EPSILON = 1e-05
F32 = jnp.float32
BF16 = jnp.bfloat16


def mm(x, w):
    return jnp.dot(x, w, preferred_element_type=F32)


def mm_t(x, w):
    return lax.dot_general(x, w, (((1,), (1,)), ((), ())), preferred_element_type=F32)


def sigmoid(v):
    return 1.0 / (1.0 + jnp.exp(-v))


def split_sum(onehot, values):
    hi = values.astype(BF16)
    lo = (values - hi.astype(F32)).astype(BF16)
    return mm(onehot, hi) + mm(onehot, lo)


def fwd_micro(m, hs_ref, h_ref, fp_ref, fn_ref, osnd_ref, orcv_ref, orcvt_ref,
              ws_ref, wr_ref, wm_ref, wn_ref, wa_ref, g_ref, out_ref, a_ref, u_ref):
    own = h_ref.shape[1]
    span = fp_ref.shape[1]
    osnd = osnd_ref[...]
    h = h_ref[m]
    gathered = (mm(osnd[:, :own], h) + mm(osnd[:, own:own + span], fp_ref[m])
                + mm(osnd[:, own + span:], fn_ref[m])).astype(BF16)
    send_part = mm(gathered, ws_ref[...]).astype(BF16).astype(F32)
    recv_rows = mm(orcv_ref[...], h).astype(BF16)
    pre = send_part + mm(recv_rows, wr_ref[...])
    a_ref[m] = pre
    edge_hidden = (pre * sigmoid(pre)).astype(BF16)
    messages = mm(edge_hidden, wm_ref[...])
    agg = split_sum(orcvt_ref[...], messages).astype(BF16)
    node_pre = mm(h, wn_ref[...]) + mm(agg, wa_ref[...])
    u_ref[m] = node_pre
    act = node_pre * sigmoid(node_pre)
    mean = jnp.mean(act, axis=-1, keepdims=True)
    cen = act - mean
    var = jnp.mean(cen * cen, axis=-1, keepdims=True)
    unit = cen * lax.rsqrt(var + EPSILON)
    out_ref[m] = (h.astype(F32) + unit * g_ref[...]).astype(BF16)


def fwd_kernel(*refs):
    for m in range(refs[1].shape[0]):
        fwd_micro(m, *refs)


def bwd_micro(m, pin_ref, a_ref, u_ref, osndt_ref, orcvl_ref, orcvt_ref,
              ws_ref, wr_ref, wm_ref, wn_ref, wa_ref, g_ref, p32_ref, hg_ref):
    own = pin_ref.shape[1]
    gain = g_ref[...]
    c = pin_ref[m].astype(F32)
    node_pre = u_ref[m]
    sig_u = sigmoid(node_pre)
    act = node_pre * sig_u
    mean = jnp.mean(act, axis=-1, keepdims=True)
    cen = act - mean
    var = jnp.mean(cen * cen, axis=-1, keepdims=True)
    rs = lax.rsqrt(var + EPSILON)
    unit = cen * rs
    gu = c * gain
    gact = rs * (gu - jnp.mean(gu, axis=-1, keepdims=True)
                 - unit * jnp.mean(gu * unit, axis=-1, keepdims=True))
    du = (gact * (sig_u * (1.0 + node_pre * (1.0 - sig_u)))).astype(BF16)
    dagg = mm_t(du, wa_ref[...]).astype(BF16)
    rows = c + mm_t(du, wn_ref[...])
    gmsg = mm(orcvl_ref[...], dagg).astype(BF16)
    pre = a_ref[m]
    sig_a = sigmoid(pre)
    dedge = (mm_t(gmsg, wm_ref[...]) * (sig_a * (1.0 + pre * (1.0 - sig_a)))).astype(BF16)
    rows = rows + split_sum(orcvt_ref[...], mm_t(dedge, wr_ref[...]))
    send_rows = split_sum(osndt_ref[...], mm_t(dedge, ws_ref[...]))
    p32_ref[m] = rows + send_rows[:own]
    hg_ref[m] = send_rows[own:].astype(BF16)


MESH_ID = pl.DeviceIdType.MESH


def comm_kernel(sends, n_in, parts, sections, *refs):
    ins = refs[:n_in]
    outs = refs[n_in:n_in + len(sends)]
    send_sem, recv_sem = refs[n_in + len(sends):]
    d = lax.axis_index("dom")
    p = lax.axis_index("pipe")
    barrier = pltpu.get_barrier_semaphore()
    for _, _, _, dd, dp in sends:
        src = (lax.rem(d - dd + parts, parts), lax.rem(p - dp + sections, sections))
        pl.semaphore_signal(barrier, 1, device_id=src, device_id_type=MESH_ID)
    pl.semaphore_wait(barrier, len(sends))
    copies = []
    for i, (k, start, rows, dd, dp) in enumerate(sends):
        dst = (lax.rem(d + dd + parts, parts), lax.rem(p + dp + sections, sections))
        source = ins[k] if start is None else ins[k].at[:, pl.ds(start, rows)]
        copy = pltpu.make_async_remote_copy(
            src_ref=source, dst_ref=outs[i], send_sem=send_sem.at[i], recv_sem=recv_sem.at[i],
            device_id=dst, device_id_type=MESH_ID)
        copy.start()
        copies.append(copy)
    for copy in copies:
        copy.wait()


def exchange(sends, payloads, parts, sections, cid):
    out_shapes = []
    for k, start, rows, _, _ in sends:
        shape = payloads[k].shape
        if start is not None:
            shape = (shape[0], rows) + shape[2:]
        out_shapes.append(jax.ShapeDtypeStruct(shape, payloads[k].dtype))
    n = len(sends)
    return pl.pallas_call(
        functools.partial(comm_kernel, tuple(sends), len(payloads), parts, sections),
        out_shape=tuple(out_shapes),
        in_specs=[pl.BlockSpec(memory_space=pl.ANY)] * len(payloads),
        out_specs=tuple(pl.BlockSpec(memory_space=pl.ANY) for _ in sends),
        scratch_shapes=[pltpu.SemaphoreType.DMA((n,)), pltpu.SemaphoreType.DMA((n,))],
        compiler_params=pltpu.CompilerParams(collective_id=cid, has_side_effects=True),
    )(*payloads)


def record_copies(pairs, sem, active):
    def run():
        copies = [pltpu.make_async_copy(buf, rec, sem.at[i]) for i, (buf, rec) in enumerate(pairs)]
        for copy in copies:
            copy.start()
        for copy in copies:
            copy.wait()
    if active is None:
        run()
    else:
        pl.when(active)(run)


def fwd_tick_kernel(parts, sections, tick, hs_ref, h_ref, fp_ref, fn_ref, osnd_ref, orcv_ref, orcvt_ref,
                    ws_ref, wr_ref, wm_ref, wn_ref, wa_ref, g_ref, *refs):
    if tick > 0:
        refs = refs[3:]
    (orec, arec, urec, hn_ref, fpn_ref, fnn_ref, obuf, abuf, ubuf,
     hbuf, fpbuf, fnbuf, stage_n, stage_p, send_sem, recv_sem, rec_sem) = refs
    micro, own, _ = h_ref.shape
    block = fp_ref.shape[1]
    d = lax.axis_index("dom")
    p = lax.axis_index("pipe")
    pipe_next = (d, lax.rem(p + 1, sections))
    pipe_prev = (d, lax.rem(p - 1 + sections, sections))
    dom_next = (lax.rem(d + 1, parts), p)
    dom_prev = (lax.rem(d - 1 + parts, parts), p)
    barrier = pltpu.get_barrier_semaphore()
    for src in (pipe_prev, dom_prev, dom_next):
        pl.semaphore_signal(barrier, 1, device_id=src, device_id_type=MESH_ID)
    compute_refs = (hs_ref, h_ref, fp_ref, fn_ref, osnd_ref, orcv_ref, orcvt_ref,
                    ws_ref, wr_ref, wm_ref, wn_ref, wa_ref, g_ref, obuf, abuf, ubuf)
    pipe_copies = []
    for m in range(micro):
        fwd_micro(m, *compute_refs)
        if m == 0:
            pl.semaphore_wait(barrier, 3)
        copy = pltpu.make_async_remote_copy(
            src_ref=obuf.at[m], dst_ref=hbuf.at[m], send_sem=send_sem.at[0, m],
            recv_sem=recv_sem.at[0, m], device_id=pipe_next, device_id_type=MESH_ID)
        copy.start()
        pipe_copies.append(copy)
    record_copies(((obuf, orec), (abuf, arec), (ubuf, urec)), rec_sem,
                  None if tick == 0 else p == tick)
    hs0 = hs_ref[0]
    hs1 = hs_ref[1]
    halo_copies = []
    for m in range(micro):
        pipe_copies[m].wait_recv()
        h = hbuf[m]
        sel_n = h[0:block]
        sel_p = h[0:block]
        for b in range(1, own // block):
            piece = h[b * block:(b + 1) * block]
            sel_n = jnp.where(hs0 == b, piece, sel_n)
            sel_p = jnp.where(hs1 == b, piece, sel_p)
        stage_n[m] = sel_n
        stage_p[m] = sel_p
        for j, (stage, buf, dst) in enumerate(((stage_n, fpbuf, dom_next), (stage_p, fnbuf, dom_prev))):
            copy = pltpu.make_async_remote_copy(
                src_ref=stage.at[m], dst_ref=buf.at[m], send_sem=send_sem.at[1 + j, m],
                recv_sem=recv_sem.at[1 + j, m], device_id=dst, device_id_type=MESH_ID)
            copy.start()
            halo_copies.append(copy)
    for copy in pipe_copies:
        copy.wait_send()
    for copy in halo_copies:
        copy.wait()
    hn_ref[...] = hbuf[...]
    fpn_ref[...] = fpbuf[...]
    fnn_ref[...] = fnbuf[...]


def fwd_tick(operands, records, tick, span, parts, sections):
    h = operands[1]
    micro, own, latent = h.shape
    vm = pl.BlockSpec(memory_space=pltpu.VMEM)
    anyspec = pl.BlockSpec(memory_space=pl.ANY)
    bf = lambda rows: jax.ShapeDtypeStruct((micro, rows, latent), BF16)
    f32 = jax.ShapeDtypeStruct((micro, own, latent), F32)
    n = len(operands)
    extra = () if tick == 0 else tuple(records)
    return pl.pallas_call(
        functools.partial(fwd_tick_kernel, parts, sections, tick),
        out_shape=(bf(own), f32, f32, bf(own), bf(span), bf(span)),
        in_specs=[pl.BlockSpec(memory_space=pltpu.SMEM)] + [vm] * (n - 1) + [anyspec] * len(extra),
        out_specs=(anyspec, anyspec, anyspec, vm, vm, vm),
        scratch_shapes=[pltpu.VMEM((micro, own, latent), BF16),
                        pltpu.VMEM((micro, own, latent), F32),
                        pltpu.VMEM((micro, own, latent), F32),
                        pltpu.VMEM((micro, own, latent), BF16),
                        pltpu.VMEM((micro, span, latent), BF16),
                        pltpu.VMEM((micro, span, latent), BF16),
                        pltpu.VMEM((micro, span, latent), BF16),
                        pltpu.VMEM((micro, span, latent), BF16),
                        pltpu.SemaphoreType.DMA((3, micro)),
                        pltpu.SemaphoreType.DMA((3, micro)),
                        pltpu.SemaphoreType.DMA((3,))],
        input_output_aliases={} if tick == 0 else {n: 0, n + 1: 1, n + 2: 2},
        compiler_params=pltpu.CompilerParams(collective_id=10 + tick,
                                             has_side_effects=True,
                                             vmem_limit_bytes=48 * 1024 * 1024),
    )(*operands, *extra)


def fwd_last_kernel(tick, hs_ref, h_ref, fp_ref, fn_ref, osnd_ref, orcv_ref, orcvt_ref,
                    ws_ref, wr_ref, wm_ref, wn_ref, wa_ref, g_ref, orec_in, arec_in, urec_in,
                    orec, arec, urec, obuf, abuf, ubuf, rec_sem):
    compute_refs = (hs_ref, h_ref, fp_ref, fn_ref, osnd_ref, orcv_ref, orcvt_ref,
                    ws_ref, wr_ref, wm_ref, wn_ref, wa_ref, g_ref, obuf, abuf, ubuf)
    for m in range(h_ref.shape[0]):
        fwd_micro(m, *compute_refs)
    record_copies(((obuf, orec), (abuf, arec), (ubuf, urec)), rec_sem,
                  lax.axis_index("pipe") == tick)


def fwd_last(operands, records, tick):
    h = operands[1]
    micro, own, latent = h.shape
    vm = pl.BlockSpec(memory_space=pltpu.VMEM)
    anyspec = pl.BlockSpec(memory_space=pl.ANY)
    n = len(operands)
    return pl.pallas_call(
        functools.partial(fwd_last_kernel, tick),
        out_shape=tuple(jax.ShapeDtypeStruct(r.shape, r.dtype) for r in records),
        in_specs=[pl.BlockSpec(memory_space=pltpu.SMEM)] + [vm] * (n - 1) + [anyspec] * 3,
        out_specs=(anyspec, anyspec, anyspec),
        scratch_shapes=[pltpu.VMEM((micro, own, latent), BF16),
                        pltpu.VMEM((micro, own, latent), F32),
                        pltpu.VMEM((micro, own, latent), F32),
                        pltpu.SemaphoreType.DMA((3,))],
        input_output_aliases={n: 0, n + 1: 1, n + 2: 2},
        compiler_params=pltpu.CompilerParams(vmem_limit_bytes=48 * 1024 * 1024),
    )(*operands, *records)


def bwd_tick_kernel(parts, sections, tick, first, hs_ref, pin_ref, a_ref, u_ref, osndt_ref, orcvl_ref,
                    orcvt_ref, ws_ref, wr_ref, wm_ref, wn_ref, wa_ref, g_ref, *refs):
    send_pipe = tick > 0
    if not first:
        refs = refs[1:]
    if send_pipe:
        grec, pinn_ref, p32, hg, snbuf, spbuf, gbuf, pinbuf, send_sem, recv_sem, rec_sem = refs
    else:
        grec, p32, hg, snbuf, spbuf, gbuf, send_sem, recv_sem, rec_sem = refs
    micro, own, _ = pin_ref.shape
    block = snbuf.shape[1]
    d = lax.axis_index("dom")
    p = lax.axis_index("pipe")
    pipe_prev = (d, lax.rem(p - 1 + sections, sections))
    pipe_next = (d, lax.rem(p + 1, sections))
    dom_next = (lax.rem(d + 1, parts), p)
    dom_prev = (lax.rem(d - 1 + parts, parts), p)
    barrier = pltpu.get_barrier_semaphore()
    sources = [dom_next, dom_prev] + ([pipe_next] if send_pipe else [])
    for src in sources:
        pl.semaphore_signal(barrier, 1, device_id=src, device_id_type=MESH_ID)
    compute_refs = (pin_ref, a_ref, u_ref, osndt_ref, orcvl_ref, orcvt_ref,
                    ws_ref, wr_ref, wm_ref, wn_ref, wa_ref, g_ref, p32, hg)
    halo_copies = []
    for m in range(micro):
        bwd_micro(m, *compute_refs)
        if m == 0:
            pl.semaphore_wait(barrier, len(sources))
        pair = []
        for j, (lo, buf, dst) in enumerate(((0, snbuf, dom_prev), (block, spbuf, dom_next))):
            copy = pltpu.make_async_remote_copy(
                src_ref=hg.at[m, pl.ds(lo, block)], dst_ref=buf.at[m],
                send_sem=send_sem.at[j, m], recv_sem=recv_sem.at[j, m],
                device_id=dst, device_id_type=MESH_ID)
            copy.start()
            pair.append(copy)
        halo_copies.append(pair)
    hs0 = hs_ref[0]
    hs1 = hs_ref[1]
    pipe_copies = []
    for m in range(micro):
        for copy in halo_copies[m]:
            copy.wait_recv()
        sn = snbuf[m].astype(F32)
        sp = spbuf[m].astype(F32)
        for b in range(own // block):
            piece = p32[m, b * block:(b + 1) * block]
            piece = piece + jnp.where(hs0 == b, sn, 0.0) + jnp.where(hs1 == b, sp, 0.0)
            gbuf[m, b * block:(b + 1) * block] = piece.astype(gbuf.dtype)
        if send_pipe:
            copy = pltpu.make_async_remote_copy(
                src_ref=gbuf.at[m], dst_ref=pinbuf.at[m], send_sem=send_sem.at[2, m],
                recv_sem=recv_sem.at[2, m], device_id=pipe_prev, device_id_type=MESH_ID)
            copy.start()
            pipe_copies.append(copy)
    record_copies(((gbuf, grec),), rec_sem, None if first else p == tick)
    for pair in halo_copies:
        for copy in pair:
            copy.wait_send()
    for copy in pipe_copies:
        copy.wait()
    if send_pipe:
        pinn_ref[...] = pinbuf[...]


def bwd_tick(operands, grad_rec, tick, span, parts, sections):
    pin = operands[1]
    micro, own, latent = pin.shape
    send_pipe = tick > 0
    first = grad_rec is None
    vm = pl.BlockSpec(memory_space=pltpu.VMEM)
    anyspec = pl.BlockSpec(memory_space=pl.ANY)
    grad = jax.ShapeDtypeStruct((micro, own, latent), BF16)
    scratch = [pltpu.VMEM((micro, own, latent), F32), pltpu.VMEM((micro, 2 * span, latent), BF16),
               pltpu.VMEM((micro, span, latent), BF16), pltpu.VMEM((micro, span, latent), BF16),
               pltpu.VMEM((micro, own, latent), BF16)]
    if send_pipe:
        scratch.append(pltpu.VMEM((micro, own, latent), BF16))
    scratch += [pltpu.SemaphoreType.DMA((3, micro)), pltpu.SemaphoreType.DMA((3, micro)),
                pltpu.SemaphoreType.DMA((1,))]
    outs = (grad, grad) if send_pipe else (grad,)
    n = len(operands)
    extra = () if first else (grad_rec,)
    return pl.pallas_call(
        functools.partial(bwd_tick_kernel, parts, sections, tick, first),
        out_shape=outs,
        in_specs=[pl.BlockSpec(memory_space=pltpu.SMEM)] + [vm] * (n - 1) + [anyspec] * len(extra),
        out_specs=(anyspec,) + ((vm,) if send_pipe else ()),
        scratch_shapes=scratch,
        input_output_aliases={} if first else {n: 0},
        compiler_params=pltpu.CompilerParams(collective_id=20 + tick, has_side_effects=True,
                                             vmem_limit_bytes=48 * 1024 * 1024),
    )(*operands, *extra)


def vmem_call(kernel, out_shapes, n_in, smem_first=True):
    in_specs = [pl.BlockSpec(memory_space=pltpu.SMEM)] + [pl.BlockSpec(memory_space=pltpu.VMEM)] * (n_in - 1)
    return pl.pallas_call(
        kernel,
        out_shape=out_shapes,
        in_specs=in_specs,
        out_specs=tuple(pl.BlockSpec(memory_space=pltpu.VMEM) for _ in out_shapes),
        compiler_params=pltpu.CompilerParams(vmem_limit_bytes=48 * 1024 * 1024),
    )


def whole_kernel(parts, sections, hs_ref, cnt_ref, x_hbm, cot_hbm, esnd_ref, ercv_ref,
                 ws_hbm, wr_hbm, wm_hbm, wn_hbm, wa_hbm, g_ref,
                 out_ref, grad_ref,
                 xbuf, cotbuf, wbuf, osnd_ref, orcv_ref, orcvt_ref, osndt_ref, orcvl_ref,
                 hbuf, fpbuf, fnbuf, stage_n, stage_p, abuf, ubuf, cbuf, p32, hg, snbuf, spbuf,
                 fsend, frecv, bsend, brecv, lsem):
    micro, own, latent = xbuf.shape
    block = fpbuf.shape[1]
    span = block
    loads = [pltpu.make_async_copy(x_hbm, xbuf, lsem.at[0])]
    for i, w in enumerate((ws_hbm, wr_hbm, wm_hbm, wn_hbm, wa_hbm)):
        loads.append(pltpu.make_async_copy(w, wbuf.at[i], lsem.at[1 + i]))
    loads.append(pltpu.make_async_copy(cot_hbm, cotbuf, lsem.at[6]))
    for copy in loads:
        copy.start()
    edges = osnd_ref.shape[0]
    ext_rows = osnd_ref.shape[1]
    own_rows = orcv_ref.shape[1]
    es = esnd_ref[...]
    er = ercv_ref[...]
    snd = jnp.concatenate([es[i:i + 1] for i in range(es.shape[0])], axis=1)
    rcv = jnp.concatenate([er[i:i + 1] for i in range(er.shape[0])], axis=1)
    lane = lax.broadcasted_iota(jnp.int32, (1, edges), 1)
    per_block = es.shape[1]
    live = lane < 0
    for i in range(es.shape[0]):
        live = live | ((lane >= i * per_block) & (lane < i * per_block + cnt_ref[i]))
    sndt = lax.broadcasted_iota(jnp.int32, (ext_rows, edges), 0) == snd
    rcvt = lax.broadcasted_iota(jnp.int32, (own_rows, edges), 0) == rcv
    osndt_f = sndt.astype(F32)
    rcvt_f = rcvt.astype(F32)
    rcvlt_f = (rcvt & live).astype(F32)
    osndt_ref[...] = osndt_f.astype(BF16)
    orcvt_ref[...] = rcvlt_f.astype(BF16)
    osnd_ref[...] = osndt_f.T.astype(BF16)
    orcv_ref[...] = rcvt_f.T.astype(BF16)
    orcvl_ref[...] = rcvlt_f.T.astype(BF16)
    d = lax.axis_index("dom")
    p = lax.axis_index("pipe")
    pipe_next = (d, lax.rem(p + 1, sections))
    pipe_prev = (d, lax.rem(p - 1 + sections, sections))
    dom_next = (lax.rem(d + 1, parts), p)
    dom_prev = (lax.rem(d - 1 + parts, parts), p)
    barrier = pltpu.get_barrier_semaphore()
    for nb in (pipe_prev, pipe_next, dom_prev, dom_next):
        pl.semaphore_signal(barrier, 1, device_id=nb, device_id_type=MESH_ID)
    pl.semaphore_wait(barrier, 4)
    hs0 = hs_ref[0]
    hs1 = hs_ref[1]
    has_prev = p > 0
    has_next = p < sections - 1
    gain = g_ref[...]
    ws, wr, wm, wn, wa = (wbuf.at[i] for i in range(5))

    def remote(src, dst, sems, idx, target):
        send_sem, recv_sem = sems
        return pltpu.make_async_remote_copy(
            src_ref=src, dst_ref=dst, send_sem=send_sem.at[idx], recv_sem=recv_sem.at[idx],
            device_id=target, device_id_type=MESH_ID)

    loads[0].wait()
    fwd_pipe = []
    fwd_halo = []
    for m in range(micro):
        half = own // 2
        pipe_in = [remote(out_ref.at[m, pl.ds(k * half, half)], hbuf.at[m, pl.ds(k * half, half)],
                          (fsend, frecv), 6 * micro + 2 * m + k, pipe_next) for k in range(2)]
        for piece_copy in pipe_in:
            pl.when(has_prev)(piece_copy.wait_recv)

        @pl.when(p == 0)
        def _():
            hbuf[m] = xbuf[m]

        h = hbuf[m]
        sel_n = h[0:block]
        sel_p = h[0:block]
        for b in range(1, own // block):
            piece = h[b * block:(b + 1) * block]
            sel_n = jnp.where(hs0 == b, piece, sel_n)
            sel_p = jnp.where(hs1 == b, piece, sel_p)
        stage_n[m] = sel_n
        stage_p[m] = sel_p
        pair = [remote(stage_n.at[m], fpbuf.at[m], (fsend, frecv), micro + 2 * m, dom_next),
                remote(stage_p.at[m], fnbuf.at[m], (fsend, frecv), micro + 2 * m + 1, dom_prev)]
        for copy in pair:
            copy.start()
        if m == 0:
            for copy in loads[1:6]:
                copy.wait()
        osnd = osnd_ref[...]
        own_gather = mm(osnd[:, :own], h)
        recv_rows = mm(orcv_ref[...], h).astype(BF16)
        recv_part = mm(recv_rows, wr[...])
        node_part = mm(h, wn[...])
        for copy in pair:
            copy.wait_recv()
        fwd_halo.extend(pair)
        gathered = (own_gather + mm(osnd[:, own:own + span], fpbuf[m])
                    + mm(osnd[:, own + span:], fnbuf[m])).astype(BF16)
        send_part = mm(gathered, ws[...]).astype(BF16).astype(F32)
        pre = send_part + recv_part
        abuf[m] = pre
        edge_hidden = (pre * sigmoid(pre)).astype(BF16)
        messages = mm(edge_hidden, wm[...])
        agg = split_sum(orcvt_ref[...], messages).astype(BF16)
        node_pre = node_part + mm(agg, wa[...])
        ubuf[m] = node_pre
        act = node_pre * sigmoid(node_pre)
        mean = jnp.mean(act, axis=-1, keepdims=True)
        cen = act - mean
        var = jnp.mean(cen * cen, axis=-1, keepdims=True)
        unit = cen * lax.rsqrt(var + EPSILON)
        out_ref[m] = (h.astype(F32) + unit * gain).astype(BF16)
        for piece_copy in pipe_in:
            pl.when(has_next)(piece_copy.start)
        fwd_pipe.extend(pipe_in)

    loads[6].wait()
    bwd_pipe = []
    bwd_halo = []
    for m in range(micro):
        half = own // 2
        pipe_in = [remote(grad_ref.at[m, pl.ds(k * half, half)], cbuf.at[m, pl.ds(k * half, half)],
                          (bsend, brecv), 6 * micro + 2 * m + k, pipe_prev) for k in range(2)]
        for piece_copy in pipe_in:
            pl.when(has_next)(piece_copy.wait_recv)

        @pl.when(p == sections - 1)
        def _():
            cbuf[m] = cotbuf[m]

        c = cbuf[m].astype(F32)
        node_pre = ubuf[m]
        sig_u = sigmoid(node_pre)
        act = node_pre * sig_u
        mean = jnp.mean(act, axis=-1, keepdims=True)
        cen = act - mean
        var = jnp.mean(cen * cen, axis=-1, keepdims=True)
        rs = lax.rsqrt(var + EPSILON)
        unit = cen * rs
        gu = c * gain
        gact = rs * (gu - jnp.mean(gu, axis=-1, keepdims=True)
                     - unit * jnp.mean(gu * unit, axis=-1, keepdims=True))
        du = (gact * (sig_u * (1.0 + node_pre * (1.0 - sig_u)))).astype(BF16)
        dagg = mm_t(du, wa[...]).astype(BF16)
        gmsg = mm(orcvl_ref[...], dagg).astype(BF16)
        pre = abuf[m]
        sig_a = sigmoid(pre)
        dedge = (mm_t(gmsg, wm[...]) * (sig_a * (1.0 + pre * (1.0 - sig_a)))).astype(BF16)
        send_x = mm_t(dedge, ws[...])
        osndt = osndt_ref[...]
        hg[m] = split_sum(osndt[own:], send_x).astype(BF16)
        pair = [remote(hg.at[m, pl.ds(0, block)], snbuf.at[m], (bsend, brecv), micro + 2 * m, dom_prev),
                remote(hg.at[m, pl.ds(block, block)], spbuf.at[m], (bsend, brecv), micro + 2 * m + 1,
                       dom_next)]
        for copy in pair:
            copy.start()
        rows = c + mm_t(du, wn[...])
        rows = rows + split_sum(orcvt_ref[...], mm_t(dedge, wr[...]))
        p32[m] = rows + split_sum(osndt[:own], send_x)
        for copy in pair:
            copy.wait_recv()
        bwd_halo.extend(pair)
        sn = snbuf[m].astype(F32)
        sp = spbuf[m].astype(F32)
        for b in range(own // block):
            piece = p32[m, b * block:(b + 1) * block]
            piece = piece + jnp.where(hs0 == b, sn, 0.0) + jnp.where(hs1 == b, sp, 0.0)
            grad_ref[m, b * block:(b + 1) * block] = piece.astype(grad_ref.dtype)
        for piece_copy in pipe_in:
            pl.when(has_prev)(piece_copy.start)
        bwd_pipe.extend(pipe_in)

    for copy in fwd_pipe:
        pl.when(has_next)(copy.wait_send)
    for copy in bwd_pipe:
        pl.when(has_prev)(copy.wait_send)
    for copy in fwd_halo + bwd_halo:
        copy.wait_send()


def whole(operands, span, parts, sections):
    x = operands[2]
    micro, own, latent = x.shape
    vm = pl.BlockSpec(memory_space=pltpu.VMEM)
    anyspec = pl.BlockSpec(memory_space=pltpu.HBM)
    bf = lambda rows: pltpu.VMEM((micro, rows, latent), BF16)
    f32 = pltpu.VMEM((micro, own, latent), F32)
    smem = pl.BlockSpec(memory_space=pltpu.SMEM)
    in_specs = [smem, smem, anyspec, anyspec, vm, vm] + [anyspec] * 5 + [vm]
    edges = operands[4].size
    ext_rows = own + 2 * span
    return pl.pallas_call(
        functools.partial(whole_kernel, parts, sections),
        out_shape=(jax.ShapeDtypeStruct((micro, own, latent), BF16),
                   jax.ShapeDtypeStruct((micro, own, latent), BF16)),
        in_specs=in_specs,
        out_specs=(vm, vm),
        scratch_shapes=[bf(own), bf(own), pltpu.VMEM((5, latent, latent), BF16),
                        pltpu.VMEM((edges, ext_rows), BF16), pltpu.VMEM((edges, own), BF16),
                        pltpu.VMEM((own, edges), BF16), pltpu.VMEM((ext_rows, edges), BF16),
                        pltpu.VMEM((edges, own), BF16),
                        bf(own), bf(span), bf(span), bf(span), bf(span), f32, f32, bf(own), f32,
                        bf(2 * span), bf(span), bf(span),
                        pltpu.SemaphoreType.DMA((8 * micro,)), pltpu.SemaphoreType.DMA((8 * micro,)),
                        pltpu.SemaphoreType.DMA((8 * micro,)), pltpu.SemaphoreType.DMA((8 * micro,)),
                        pltpu.SemaphoreType.DMA((7,))],
        compiler_params=pltpu.CompilerParams(collective_id=0, has_side_effects=True,
                                             vmem_limit_bytes=67043328),
    )(*operands)


def shards(inputs, cotangent, w_send, w_recv, w_message, w_node, w_aggregate, gains,
           edge_send, edge_recv, edge_count, halo_send):
    sections = lax.axis_size("pipe")
    parts = lax.axis_size("dom")
    p_idx = lax.axis_index("pipe")
    micro, own, latent = inputs.shape
    block = edge_send.shape[1]
    span = halo_send.shape[2] * block
    ext_rows = own + 2 * span
    weights = (w_send[0], w_recv[0], w_message[0], w_node[0], w_aggregate[0])
    gain = gains[0].reshape(1, latent)
    hs = halo_send[0].reshape(-1).astype(jnp.int32)

    def blocks_of(x):
        shaped = x.reshape(micro, own // block, block, latent)
        nxt = jnp.take(shaped, hs[0], axis=1)
        prv = jnp.take(shaped, hs[1], axis=1)
        return nxt, prv

    S, D = sections, parts

    def perm_pipe(shift):
        return [(i, (i + shift) % S) for i in range(S)]

    def perm_both(dshift, pshift):
        return [(d * S + p, ((d + dshift) % D) * S + (p + pshift) % S)
                for d in range(D) for p in range(S)]

    both = ("dom", "pipe")

    fwd = vmem_call(
        fwd_kernel,
        (jax.ShapeDtypeStruct((micro, own, latent), BF16),
         jax.ShapeDtypeStruct((micro, own, latent), F32),
         jax.ShapeDtypeStruct((micro, own, latent), F32)),
        13)

    out_rec, grad_rec = whole(
        (hs, edge_count.astype(jnp.int32), inputs, cotangent, edge_send.astype(jnp.int32),
         edge_recv.astype(jnp.int32), *weights, gain), span, D, S)
    return (out_rec[None], grad_rec[None])


def solution(mesh):
    in_specs = (
        P(None, "dom", None),
        P(None, "dom", None),
        P("pipe", None, None),
        P("pipe", None, None),
        P("pipe", None, None),
        P("pipe", None, None),
        P("pipe", None, None),
        P("pipe", None),
        P("dom", None),
        P("dom", None),
        P("dom"),
        P("dom", None, None),
    )
    out_specs = (P("pipe", None, "dom", None), P("pipe", None, "dom", None))
    return jax.shard_map(shards, mesh=mesh, in_specs=in_specs, out_specs=out_specs, check_vma=False)
```

```python
import functools

import jax
import jax.numpy as jnp
from jax import lax
from jax.experimental import pallas as pl
from jax.experimental.pallas import tpu as pltpu
from jax.sharding import PartitionSpec as P

EPSILON = 1e-05
F32 = jnp.float32
BF16 = jnp.bfloat16


def mm(x, w):
    return jnp.dot(x, w, preferred_element_type=F32)


def mm_t(x, w):
    return lax.dot_general(x, w, (((1,), (1,)), ((), ())), preferred_element_type=F32)


def sigmoid(v):
    return 1.0 / (1.0 + jnp.exp(-v))


def split_sum(onehot, values):
    hi = values.astype(BF16)
    lo = (values - hi.astype(F32)).astype(BF16)
    return mm(onehot, hi) + mm(onehot, lo)


def fwd_micro(m, hs_ref, h_ref, fp_ref, fn_ref, osnd_ref, orcv_ref, orcvt_ref,
              ws_ref, wr_ref, wm_ref, wn_ref, wa_ref, g_ref, out_ref, a_ref, u_ref):
    own = h_ref.shape[1]
    span = fp_ref.shape[1]
    osnd = osnd_ref[...]
    h = h_ref[m]
    gathered = (mm(osnd[:, :own], h) + mm(osnd[:, own:own + span], fp_ref[m])
                + mm(osnd[:, own + span:], fn_ref[m])).astype(BF16)
    send_part = mm(gathered, ws_ref[...]).astype(BF16).astype(F32)
    recv_rows = mm(orcv_ref[...], h).astype(BF16)
    pre = send_part + mm(recv_rows, wr_ref[...])
    a_ref[m] = pre
    edge_hidden = (pre * sigmoid(pre)).astype(BF16)
    messages = mm(edge_hidden, wm_ref[...])
    agg = split_sum(orcvt_ref[...], messages).astype(BF16)
    node_pre = mm(h, wn_ref[...]) + mm(agg, wa_ref[...])
    u_ref[m] = node_pre
    act = node_pre * sigmoid(node_pre)
    mean = jnp.mean(act, axis=-1, keepdims=True)
    cen = act - mean
    var = jnp.mean(cen * cen, axis=-1, keepdims=True)
    unit = cen * lax.rsqrt(var + EPSILON)
    out_ref[m] = (h.astype(F32) + unit * g_ref[...]).astype(BF16)


def fwd_kernel(*refs):
    for m in range(refs[1].shape[0]):
        fwd_micro(m, *refs)


def bwd_micro(m, pin_ref, a_ref, u_ref, osndt_ref, orcvl_ref, orcvt_ref,
              ws_ref, wr_ref, wm_ref, wn_ref, wa_ref, g_ref, p32_ref, hg_ref):
    own = pin_ref.shape[1]
    gain = g_ref[...]
    c = pin_ref[m].astype(F32)
    node_pre = u_ref[m]
    sig_u = sigmoid(node_pre)
    act = node_pre * sig_u
    mean = jnp.mean(act, axis=-1, keepdims=True)
    cen = act - mean
    var = jnp.mean(cen * cen, axis=-1, keepdims=True)
    rs = lax.rsqrt(var + EPSILON)
    unit = cen * rs
    gu = c * gain
    gact = rs * (gu - jnp.mean(gu, axis=-1, keepdims=True)
                 - unit * jnp.mean(gu * unit, axis=-1, keepdims=True))
    du = (gact * (sig_u * (1.0 + node_pre * (1.0 - sig_u)))).astype(BF16)
    dagg = mm_t(du, wa_ref[...]).astype(BF16)
    rows = c + mm_t(du, wn_ref[...])
    gmsg = mm(orcvl_ref[...], dagg).astype(BF16)
    pre = a_ref[m]
    sig_a = sigmoid(pre)
    dedge = (mm_t(gmsg, wm_ref[...]) * (sig_a * (1.0 + pre * (1.0 - sig_a)))).astype(BF16)
    rows = rows + split_sum(orcvt_ref[...], mm_t(dedge, wr_ref[...]))
    send_rows = split_sum(osndt_ref[...], mm_t(dedge, ws_ref[...]))
    p32_ref[m] = rows + send_rows[:own]
    hg_ref[m] = send_rows[own:].astype(BF16)


MESH_ID = pl.DeviceIdType.MESH


def comm_kernel(sends, n_in, parts, sections, *refs):
    ins = refs[:n_in]
    outs = refs[n_in:n_in + len(sends)]
    send_sem, recv_sem = refs[n_in + len(sends):]
    d = lax.axis_index("dom")
    p = lax.axis_index("pipe")
    barrier = pltpu.get_barrier_semaphore()
    for _, _, _, dd, dp in sends:
        src = (lax.rem(d - dd + parts, parts), lax.rem(p - dp + sections, sections))
        pl.semaphore_signal(barrier, 1, device_id=src, device_id_type=MESH_ID)
    pl.semaphore_wait(barrier, len(sends))
    copies = []
    for i, (k, start, rows, dd, dp) in enumerate(sends):
        dst = (lax.rem(d + dd + parts, parts), lax.rem(p + dp + sections, sections))
        source = ins[k] if start is None else ins[k].at[:, pl.ds(start, rows)]
        copy = pltpu.make_async_remote_copy(
            src_ref=source, dst_ref=outs[i], send_sem=send_sem.at[i], recv_sem=recv_sem.at[i],
            device_id=dst, device_id_type=MESH_ID)
        copy.start()
        copies.append(copy)
    for copy in copies:
        copy.wait()


def exchange(sends, payloads, parts, sections, cid):
    out_shapes = []
    for k, start, rows, _, _ in sends:
        shape = payloads[k].shape
        if start is not None:
            shape = (shape[0], rows) + shape[2:]
        out_shapes.append(jax.ShapeDtypeStruct(shape, payloads[k].dtype))
    n = len(sends)
    return pl.pallas_call(
        functools.partial(comm_kernel, tuple(sends), len(payloads), parts, sections),
        out_shape=tuple(out_shapes),
        in_specs=[pl.BlockSpec(memory_space=pl.ANY)] * len(payloads),
        out_specs=tuple(pl.BlockSpec(memory_space=pl.ANY) for _ in sends),
        scratch_shapes=[pltpu.SemaphoreType.DMA((n,)), pltpu.SemaphoreType.DMA((n,))],
        compiler_params=pltpu.CompilerParams(collective_id=cid, has_side_effects=True),
    )(*payloads)


def record_copies(pairs, sem, active):
    def run():
        copies = [pltpu.make_async_copy(buf, rec, sem.at[i]) for i, (buf, rec) in enumerate(pairs)]
        for copy in copies:
            copy.start()
        for copy in copies:
            copy.wait()
    if active is None:
        run()
    else:
        pl.when(active)(run)


def fwd_tick_kernel(parts, sections, tick, hs_ref, h_ref, fp_ref, fn_ref, osnd_ref, orcv_ref, orcvt_ref,
                    ws_ref, wr_ref, wm_ref, wn_ref, wa_ref, g_ref, *refs):
    if tick > 0:
        refs = refs[3:]
    (orec, arec, urec, hn_ref, fpn_ref, fnn_ref, obuf, abuf, ubuf,
     hbuf, fpbuf, fnbuf, stage_n, stage_p, send_sem, recv_sem, rec_sem) = refs
    micro, own, _ = h_ref.shape
    block = fp_ref.shape[1]
    d = lax.axis_index("dom")
    p = lax.axis_index("pipe")
    pipe_next = (d, lax.rem(p + 1, sections))
    pipe_prev = (d, lax.rem(p - 1 + sections, sections))
    dom_next = (lax.rem(d + 1, parts), p)
    dom_prev = (lax.rem(d - 1 + parts, parts), p)
    barrier = pltpu.get_barrier_semaphore()
    for src in (pipe_prev, dom_prev, dom_next):
        pl.semaphore_signal(barrier, 1, device_id=src, device_id_type=MESH_ID)
    compute_refs = (hs_ref, h_ref, fp_ref, fn_ref, osnd_ref, orcv_ref, orcvt_ref,
                    ws_ref, wr_ref, wm_ref, wn_ref, wa_ref, g_ref, obuf, abuf, ubuf)
    pipe_copies = []
    for m in range(micro):
        fwd_micro(m, *compute_refs)
        if m == 0:
            pl.semaphore_wait(barrier, 3)
        copy = pltpu.make_async_remote_copy(
            src_ref=obuf.at[m], dst_ref=hbuf.at[m], send_sem=send_sem.at[0, m],
            recv_sem=recv_sem.at[0, m], device_id=pipe_next, device_id_type=MESH_ID)
        copy.start()
        pipe_copies.append(copy)
    record_copies(((obuf, orec), (abuf, arec), (ubuf, urec)), rec_sem,
                  None if tick == 0 else p == tick)
    hs0 = hs_ref[0]
    hs1 = hs_ref[1]
    halo_copies = []
    for m in range(micro):
        pipe_copies[m].wait_recv()
        h = hbuf[m]
        sel_n = h[0:block]
        sel_p = h[0:block]
        for b in range(1, own // block):
            piece = h[b * block:(b + 1) * block]
            sel_n = jnp.where(hs0 == b, piece, sel_n)
            sel_p = jnp.where(hs1 == b, piece, sel_p)
        stage_n[m] = sel_n
        stage_p[m] = sel_p
        for j, (stage, buf, dst) in enumerate(((stage_n, fpbuf, dom_next), (stage_p, fnbuf, dom_prev))):
            copy = pltpu.make_async_remote_copy(
                src_ref=stage.at[m], dst_ref=buf.at[m], send_sem=send_sem.at[1 + j, m],
                recv_sem=recv_sem.at[1 + j, m], device_id=dst, device_id_type=MESH_ID)
            copy.start()
            halo_copies.append(copy)
    for copy in pipe_copies:
        copy.wait_send()
    for copy in halo_copies:
        copy.wait()
    hn_ref[...] = hbuf[...]
    fpn_ref[...] = fpbuf[...]
    fnn_ref[...] = fnbuf[...]


def fwd_tick(operands, records, tick, span, parts, sections):
    h = operands[1]
    micro, own, latent = h.shape
    vm = pl.BlockSpec(memory_space=pltpu.VMEM)
    anyspec = pl.BlockSpec(memory_space=pl.ANY)
    bf = lambda rows: jax.ShapeDtypeStruct((micro, rows, latent), BF16)
    f32 = jax.ShapeDtypeStruct((micro, own, latent), F32)
    n = len(operands)
    extra = () if tick == 0 else tuple(records)
    return pl.pallas_call(
        functools.partial(fwd_tick_kernel, parts, sections, tick),
        out_shape=(bf(own), f32, f32, bf(own), bf(span), bf(span)),
        in_specs=[pl.BlockSpec(memory_space=pltpu.SMEM)] + [vm] * (n - 1) + [anyspec] * len(extra),
        out_specs=(anyspec, anyspec, anyspec, vm, vm, vm),
        scratch_shapes=[pltpu.VMEM((micro, own, latent), BF16),
                        pltpu.VMEM((micro, own, latent), F32),
                        pltpu.VMEM((micro, own, latent), F32),
                        pltpu.VMEM((micro, own, latent), BF16),
                        pltpu.VMEM((micro, span, latent), BF16),
                        pltpu.VMEM((micro, span, latent), BF16),
                        pltpu.VMEM((micro, span, latent), BF16),
                        pltpu.VMEM((micro, span, latent), BF16),
                        pltpu.SemaphoreType.DMA((3, micro)),
                        pltpu.SemaphoreType.DMA((3, micro)),
                        pltpu.SemaphoreType.DMA((3,))],
        input_output_aliases={} if tick == 0 else {n: 0, n + 1: 1, n + 2: 2},
        compiler_params=pltpu.CompilerParams(collective_id=10 + tick,
                                             has_side_effects=True,
                                             vmem_limit_bytes=48 * 1024 * 1024),
    )(*operands, *extra)


def fwd_last_kernel(tick, hs_ref, h_ref, fp_ref, fn_ref, osnd_ref, orcv_ref, orcvt_ref,
                    ws_ref, wr_ref, wm_ref, wn_ref, wa_ref, g_ref, orec_in, arec_in, urec_in,
                    orec, arec, urec, obuf, abuf, ubuf, rec_sem):
    compute_refs = (hs_ref, h_ref, fp_ref, fn_ref, osnd_ref, orcv_ref, orcvt_ref,
                    ws_ref, wr_ref, wm_ref, wn_ref, wa_ref, g_ref, obuf, abuf, ubuf)
    for m in range(h_ref.shape[0]):
        fwd_micro(m, *compute_refs)
    record_copies(((obuf, orec), (abuf, arec), (ubuf, urec)), rec_sem,
                  lax.axis_index("pipe") == tick)


def fwd_last(operands, records, tick):
    h = operands[1]
    micro, own, latent = h.shape
    vm = pl.BlockSpec(memory_space=pltpu.VMEM)
    anyspec = pl.BlockSpec(memory_space=pl.ANY)
    n = len(operands)
    return pl.pallas_call(
        functools.partial(fwd_last_kernel, tick),
        out_shape=tuple(jax.ShapeDtypeStruct(r.shape, r.dtype) for r in records),
        in_specs=[pl.BlockSpec(memory_space=pltpu.SMEM)] + [vm] * (n - 1) + [anyspec] * 3,
        out_specs=(anyspec, anyspec, anyspec),
        scratch_shapes=[pltpu.VMEM((micro, own, latent), BF16),
                        pltpu.VMEM((micro, own, latent), F32),
                        pltpu.VMEM((micro, own, latent), F32),
                        pltpu.SemaphoreType.DMA((3,))],
        input_output_aliases={n: 0, n + 1: 1, n + 2: 2},
        compiler_params=pltpu.CompilerParams(vmem_limit_bytes=48 * 1024 * 1024),
    )(*operands, *records)


def bwd_tick_kernel(parts, sections, tick, first, hs_ref, pin_ref, a_ref, u_ref, osndt_ref, orcvl_ref,
                    orcvt_ref, ws_ref, wr_ref, wm_ref, wn_ref, wa_ref, g_ref, *refs):
    send_pipe = tick > 0
    if not first:
        refs = refs[1:]
    if send_pipe:
        grec, pinn_ref, p32, hg, snbuf, spbuf, gbuf, pinbuf, send_sem, recv_sem, rec_sem = refs
    else:
        grec, p32, hg, snbuf, spbuf, gbuf, send_sem, recv_sem, rec_sem = refs
    micro, own, _ = pin_ref.shape
    block = snbuf.shape[1]
    d = lax.axis_index("dom")
    p = lax.axis_index("pipe")
    pipe_prev = (d, lax.rem(p - 1 + sections, sections))
    pipe_next = (d, lax.rem(p + 1, sections))
    dom_next = (lax.rem(d + 1, parts), p)
    dom_prev = (lax.rem(d - 1 + parts, parts), p)
    barrier = pltpu.get_barrier_semaphore()
    sources = [dom_next, dom_prev] + ([pipe_next] if send_pipe else [])
    for src in sources:
        pl.semaphore_signal(barrier, 1, device_id=src, device_id_type=MESH_ID)
    compute_refs = (pin_ref, a_ref, u_ref, osndt_ref, orcvl_ref, orcvt_ref,
                    ws_ref, wr_ref, wm_ref, wn_ref, wa_ref, g_ref, p32, hg)
    halo_copies = []
    for m in range(micro):
        bwd_micro(m, *compute_refs)
        if m == 0:
            pl.semaphore_wait(barrier, len(sources))
        pair = []
        for j, (lo, buf, dst) in enumerate(((0, snbuf, dom_prev), (block, spbuf, dom_next))):
            copy = pltpu.make_async_remote_copy(
                src_ref=hg.at[m, pl.ds(lo, block)], dst_ref=buf.at[m],
                send_sem=send_sem.at[j, m], recv_sem=recv_sem.at[j, m],
                device_id=dst, device_id_type=MESH_ID)
            copy.start()
            pair.append(copy)
        halo_copies.append(pair)
    hs0 = hs_ref[0]
    hs1 = hs_ref[1]
    pipe_copies = []
    for m in range(micro):
        for copy in halo_copies[m]:
            copy.wait_recv()
        sn = snbuf[m].astype(F32)
        sp = spbuf[m].astype(F32)
        for b in range(own // block):
            piece = p32[m, b * block:(b + 1) * block]
            piece = piece + jnp.where(hs0 == b, sn, 0.0) + jnp.where(hs1 == b, sp, 0.0)
            gbuf[m, b * block:(b + 1) * block] = piece.astype(gbuf.dtype)
        if send_pipe:
            copy = pltpu.make_async_remote_copy(
                src_ref=gbuf.at[m], dst_ref=pinbuf.at[m], send_sem=send_sem.at[2, m],
                recv_sem=recv_sem.at[2, m], device_id=pipe_prev, device_id_type=MESH_ID)
            copy.start()
            pipe_copies.append(copy)
    record_copies(((gbuf, grec),), rec_sem, None if first else p == tick)
    for pair in halo_copies:
        for copy in pair:
            copy.wait_send()
    for copy in pipe_copies:
        copy.wait()
    if send_pipe:
        pinn_ref[...] = pinbuf[...]


def bwd_tick(operands, grad_rec, tick, span, parts, sections):
    pin = operands[1]
    micro, own, latent = pin.shape
    send_pipe = tick > 0
    first = grad_rec is None
    vm = pl.BlockSpec(memory_space=pltpu.VMEM)
    anyspec = pl.BlockSpec(memory_space=pl.ANY)
    grad = jax.ShapeDtypeStruct((micro, own, latent), BF16)
    scratch = [pltpu.VMEM((micro, own, latent), F32), pltpu.VMEM((micro, 2 * span, latent), BF16),
               pltpu.VMEM((micro, span, latent), BF16), pltpu.VMEM((micro, span, latent), BF16),
               pltpu.VMEM((micro, own, latent), BF16)]
    if send_pipe:
        scratch.append(pltpu.VMEM((micro, own, latent), BF16))
    scratch += [pltpu.SemaphoreType.DMA((3, micro)), pltpu.SemaphoreType.DMA((3, micro)),
                pltpu.SemaphoreType.DMA((1,))]
    outs = (grad, grad) if send_pipe else (grad,)
    n = len(operands)
    extra = () if first else (grad_rec,)
    return pl.pallas_call(
        functools.partial(bwd_tick_kernel, parts, sections, tick, first),
        out_shape=outs,
        in_specs=[pl.BlockSpec(memory_space=pltpu.SMEM)] + [vm] * (n - 1) + [anyspec] * len(extra),
        out_specs=(anyspec,) + ((vm,) if send_pipe else ()),
        scratch_shapes=scratch,
        input_output_aliases={} if first else {n: 0},
        compiler_params=pltpu.CompilerParams(collective_id=20 + tick, has_side_effects=True,
                                             vmem_limit_bytes=48 * 1024 * 1024),
    )(*operands, *extra)


def vmem_call(kernel, out_shapes, n_in, smem_first=True):
    in_specs = [pl.BlockSpec(memory_space=pltpu.SMEM)] + [pl.BlockSpec(memory_space=pltpu.VMEM)] * (n_in - 1)
    return pl.pallas_call(
        kernel,
        out_shape=out_shapes,
        in_specs=in_specs,
        out_specs=tuple(pl.BlockSpec(memory_space=pltpu.VMEM) for _ in out_shapes),
        compiler_params=pltpu.CompilerParams(vmem_limit_bytes=48 * 1024 * 1024),
    )


def whole_kernel(parts, sections, hs_ref, cnt_ref, x_hbm, cot_hbm, esnd_ref, ercv_ref,
                 ws_hbm, wr_hbm, wm_hbm, wn_hbm, wa_hbm, g_ref,
                 out_ref, grad_ref,
                 xbuf, cotbuf, wbuf, osnd_ref, orcv_ref, orcvt_ref, osndt_ref, orcvl_ref,
                 hbuf, fpbuf, fnbuf, stage_n, stage_p, abuf, ubuf, cbuf, p32, hg, snbuf, spbuf,
                 fsend, frecv, bsend, brecv, lsem):
    micro, own, latent = xbuf.shape
    block = fpbuf.shape[1]
    span = block
    loads = [pltpu.make_async_copy(x_hbm, xbuf, lsem.at[0])]
    for i, w in enumerate((ws_hbm, wr_hbm, wm_hbm, wn_hbm, wa_hbm)):
        loads.append(pltpu.make_async_copy(w, wbuf.at[i], lsem.at[1 + i]))
    loads.append(pltpu.make_async_copy(cot_hbm, cotbuf, lsem.at[6]))
    for copy in loads:
        copy.start()
    edges = osnd_ref.shape[0]
    ext_rows = osnd_ref.shape[1]
    own_rows = orcv_ref.shape[1]
    es = esnd_ref[...]
    er = ercv_ref[...]
    snd = jnp.concatenate([es[i:i + 1] for i in range(es.shape[0])], axis=1)
    rcv = jnp.concatenate([er[i:i + 1] for i in range(er.shape[0])], axis=1)
    lane = lax.broadcasted_iota(jnp.int32, (1, edges), 1)
    per_block = es.shape[1]
    live = lane < 0
    for i in range(es.shape[0]):
        live = live | ((lane >= i * per_block) & (lane < i * per_block + cnt_ref[i]))
    sndt = lax.broadcasted_iota(jnp.int32, (ext_rows, edges), 0) == snd
    rcvt = lax.broadcasted_iota(jnp.int32, (own_rows, edges), 0) == rcv
    osndt_f = sndt.astype(F32)
    rcvt_f = rcvt.astype(F32)
    rcvlt_f = (rcvt & live).astype(F32)
    osndt_ref[...] = osndt_f.astype(BF16)
    orcvt_ref[...] = rcvlt_f.astype(BF16)
    osnd_ref[...] = osndt_f.T.astype(BF16)
    orcv_ref[...] = rcvt_f.T.astype(BF16)
    orcvl_ref[...] = rcvlt_f.T.astype(BF16)
    d = lax.axis_index("dom")
    p = lax.axis_index("pipe")
    pipe_next = (d, lax.rem(p + 1, sections))
    pipe_prev = (d, lax.rem(p - 1 + sections, sections))
    dom_next = (lax.rem(d + 1, parts), p)
    dom_prev = (lax.rem(d - 1 + parts, parts), p)
    barrier = pltpu.get_barrier_semaphore()
    for nb in (pipe_prev, pipe_next, dom_prev, dom_next):
        pl.semaphore_signal(barrier, 1, device_id=nb, device_id_type=MESH_ID)
    pl.semaphore_wait(barrier, 4)
    hs0 = hs_ref[0]
    hs1 = hs_ref[1]
    has_prev = p > 0
    has_next = p < sections - 1
    gain = g_ref[...]
    ws, wr, wm, wn, wa = (wbuf.at[i] for i in range(5))

    def remote(src, dst, sems, idx, target):
        send_sem, recv_sem = sems
        return pltpu.make_async_remote_copy(
            src_ref=src, dst_ref=dst, send_sem=send_sem.at[idx], recv_sem=recv_sem.at[idx],
            device_id=target, device_id_type=MESH_ID)

    loads[0].wait()
    fwd_pipe = []
    fwd_halo = []
    for m in range(micro):
        pipe_in = remote(out_ref.at[m], hbuf.at[m], (fsend, frecv), m, pipe_next)
        pl.when(has_prev)(pipe_in.wait_recv)

        @pl.when(p == 0)
        def _():
            hbuf[m] = xbuf[m]

        h = hbuf[m]
        sel_n = h[0:block]
        sel_p = h[0:block]
        for b in range(1, own // block):
            piece = h[b * block:(b + 1) * block]
            sel_n = jnp.where(hs0 == b, piece, sel_n)
            sel_p = jnp.where(hs1 == b, piece, sel_p)
        stage_n[m] = sel_n
        stage_p[m] = sel_p
        pair = [remote(stage_n.at[m], fpbuf.at[m], (fsend, frecv), micro + 2 * m, dom_next),
                remote(stage_p.at[m], fnbuf.at[m], (fsend, frecv), micro + 2 * m + 1, dom_prev)]
        for copy in pair:
            copy.start()
        if m == 0:
            for copy in loads[1:6]:
                copy.wait()
        osnd = osnd_ref[...]
        own_gather = mm(osnd[:, :own], h)
        recv_rows = mm(orcv_ref[...], h).astype(BF16)
        recv_part = mm(recv_rows, wr[...])
        node_part = mm(h, wn[...])
        for copy in pair:
            copy.wait_recv()
        fwd_halo.extend(pair)
        gathered = (own_gather + mm(osnd[:, own:own + span], fpbuf[m])
                    + mm(osnd[:, own + span:], fnbuf[m])).astype(BF16)
        send_part = mm(gathered, ws[...]).astype(BF16).astype(F32)
        pre = send_part + recv_part
        abuf[m] = pre
        edge_hidden = (pre * sigmoid(pre)).astype(BF16)
        messages = mm(edge_hidden, wm[...])
        agg = split_sum(orcvt_ref[...], messages).astype(BF16)
        node_pre = node_part + mm(agg, wa[...])
        ubuf[m] = node_pre
        act = node_pre * sigmoid(node_pre)
        mean = jnp.mean(act, axis=-1, keepdims=True)
        cen = act - mean
        var = jnp.mean(cen * cen, axis=-1, keepdims=True)
        unit = cen * lax.rsqrt(var + EPSILON)
        out_ref[m] = (h.astype(F32) + unit * gain).astype(BF16)
        if fwd_pipe:
            pl.when(has_next)(fwd_pipe[-1].wait_send)
        pl.when(has_next)(pipe_in.start)
        fwd_pipe.append(pipe_in)

    loads[6].wait()
    bwd_pipe = []
    bwd_halo = []
    for m in range(micro):
        pipe_in = remote(grad_ref.at[m], cbuf.at[m], (bsend, brecv), m, pipe_prev)
        pl.when(has_next)(pipe_in.wait_recv)

        @pl.when(p == sections - 1)
        def _():
            cbuf[m] = cotbuf[m]

        c = cbuf[m].astype(F32)
        node_pre = ubuf[m]
        sig_u = sigmoid(node_pre)
        act = node_pre * sig_u
        mean = jnp.mean(act, axis=-1, keepdims=True)
        cen = act - mean
        var = jnp.mean(cen * cen, axis=-1, keepdims=True)
        rs = lax.rsqrt(var + EPSILON)
        unit = cen * rs
        gu = c * gain
        gact = rs * (gu - jnp.mean(gu, axis=-1, keepdims=True)
                     - unit * jnp.mean(gu * unit, axis=-1, keepdims=True))
        du = (gact * (sig_u * (1.0 + node_pre * (1.0 - sig_u)))).astype(BF16)
        dagg = mm_t(du, wa[...]).astype(BF16)
        gmsg = mm(orcvl_ref[...], dagg).astype(BF16)
        pre = abuf[m]
        sig_a = sigmoid(pre)
        dedge = (mm_t(gmsg, wm[...]) * (sig_a * (1.0 + pre * (1.0 - sig_a)))).astype(BF16)
        send_x = mm_t(dedge, ws[...])
        osndt = osndt_ref[...]
        hg[m] = split_sum(osndt[own:], send_x).astype(BF16)
        pair = [remote(hg.at[m, pl.ds(0, block)], snbuf.at[m], (bsend, brecv), micro + 2 * m, dom_prev),
                remote(hg.at[m, pl.ds(block, block)], spbuf.at[m], (bsend, brecv), micro + 2 * m + 1,
                       dom_next)]
        for copy in pair:
            copy.start()
        rows = c + mm_t(du, wn[...])
        rows = rows + split_sum(orcvt_ref[...], mm_t(dedge, wr[...]))
        p32[m] = rows + split_sum(osndt[:own], send_x)
        for copy in pair:
            copy.wait_recv()
        bwd_halo.extend(pair)
        sn = snbuf[m].astype(F32)
        sp = spbuf[m].astype(F32)
        for b in range(own // block):
            piece = p32[m, b * block:(b + 1) * block]
            piece = piece + jnp.where(hs0 == b, sn, 0.0) + jnp.where(hs1 == b, sp, 0.0)
            grad_ref[m, b * block:(b + 1) * block] = piece.astype(grad_ref.dtype)
        if bwd_pipe:
            pl.when(has_prev)(bwd_pipe[-1].wait_send)
        pl.when(has_prev)(pipe_in.start)
        bwd_pipe.append(pipe_in)

    pl.when(has_next)(fwd_pipe[-1].wait_send)
    pl.when(has_prev)(bwd_pipe[-1].wait_send)
    for copy in fwd_halo + bwd_halo:
        copy.wait_send()


def whole(operands, span, parts, sections):
    x = operands[2]
    micro, own, latent = x.shape
    vm = pl.BlockSpec(memory_space=pltpu.VMEM)
    anyspec = pl.BlockSpec(memory_space=pltpu.HBM)
    bf = lambda rows: pltpu.VMEM((micro, rows, latent), BF16)
    f32 = pltpu.VMEM((micro, own, latent), F32)
    smem = pl.BlockSpec(memory_space=pltpu.SMEM)
    in_specs = [smem, smem, anyspec, anyspec, vm, vm] + [anyspec] * 5 + [vm]
    edges = operands[4].size
    ext_rows = own + 2 * span
    return pl.pallas_call(
        functools.partial(whole_kernel, parts, sections),
        out_shape=(jax.ShapeDtypeStruct((micro, own, latent), BF16),
                   jax.ShapeDtypeStruct((micro, own, latent), BF16)),
        in_specs=in_specs,
        out_specs=(vm, vm),
        scratch_shapes=[bf(own), bf(own), pltpu.VMEM((5, latent, latent), BF16),
                        pltpu.VMEM((edges, ext_rows), BF16), pltpu.VMEM((edges, own), BF16),
                        pltpu.VMEM((own, edges), BF16), pltpu.VMEM((ext_rows, edges), BF16),
                        pltpu.VMEM((edges, own), BF16),
                        bf(own), bf(span), bf(span), bf(span), bf(span), f32, f32, bf(own), f32,
                        bf(2 * span), bf(span), bf(span),
                        pltpu.SemaphoreType.DMA((3 * micro,)), pltpu.SemaphoreType.DMA((3 * micro,)),
                        pltpu.SemaphoreType.DMA((3 * micro,)), pltpu.SemaphoreType.DMA((3 * micro,)),
                        pltpu.SemaphoreType.DMA((7,))],
        compiler_params=pltpu.CompilerParams(collective_id=0, has_side_effects=True,
                                             vmem_limit_bytes=67043328),
    )(*operands)


def shards(inputs, cotangent, w_send, w_recv, w_message, w_node, w_aggregate, gains,
           edge_send, edge_recv, edge_count, halo_send):
    sections = lax.axis_size("pipe")
    parts = lax.axis_size("dom")
    p_idx = lax.axis_index("pipe")
    micro, own, latent = inputs.shape
    block = edge_send.shape[1]
    span = halo_send.shape[2] * block
    ext_rows = own + 2 * span
    weights = (w_send[0], w_recv[0], w_message[0], w_node[0], w_aggregate[0])
    gain = gains[0].reshape(1, latent)
    hs = halo_send[0].reshape(-1).astype(jnp.int32)

    def blocks_of(x):
        shaped = x.reshape(micro, own // block, block, latent)
        nxt = jnp.take(shaped, hs[0], axis=1)
        prv = jnp.take(shaped, hs[1], axis=1)
        return nxt, prv

    S, D = sections, parts

    def perm_pipe(shift):
        return [(i, (i + shift) % S) for i in range(S)]

    def perm_both(dshift, pshift):
        return [(d * S + p, ((d + dshift) % D) * S + (p + pshift) % S)
                for d in range(D) for p in range(S)]

    both = ("dom", "pipe")

    fwd = vmem_call(
        fwd_kernel,
        (jax.ShapeDtypeStruct((micro, own, latent), BF16),
         jax.ShapeDtypeStruct((micro, own, latent), F32),
         jax.ShapeDtypeStruct((micro, own, latent), F32)),
        13)

    out_rec, grad_rec = whole(
        (hs, edge_count.astype(jnp.int32), inputs, cotangent, edge_send.astype(jnp.int32),
         edge_recv.astype(jnp.int32), *weights, gain), span, D, S)
    return (out_rec[None], grad_rec[None])


def solution(mesh):
    in_specs = (
        P(None, "dom", None),
        P(None, "dom", None),
        P("pipe", None, None),
        P("pipe", None, None),
        P("pipe", None, None),
        P("pipe", None, None),
        P("pipe", None, None),
        P("pipe", None),
        P("dom", None),
        P("dom", None),
        P("dom"),
        P("dom", None, None),
    )
    out_specs = (P("pipe", None, "dom", None), P("pipe", None, "dom", None))
    return jax.shard_map(shards, mesh=mesh, in_specs=in_specs, out_specs=out_specs, check_vma=False)
```

```python
import functools

import jax
import jax.numpy as jnp
from jax import lax
from jax.experimental import pallas as pl
from jax.experimental.pallas import tpu as pltpu
from jax.sharding import PartitionSpec as P

EPSILON = 1e-05
F32 = jnp.float32
BF16 = jnp.bfloat16


def mm(x, w):
    return jnp.dot(x, w, preferred_element_type=F32)


def mm_t(x, w):
    return lax.dot_general(x, w, (((1,), (1,)), ((), ())), preferred_element_type=F32)


def sigmoid(v):
    return 1.0 / (1.0 + jnp.exp(-v))


def split_sum(onehot, values):
    hi = values.astype(BF16)
    lo = (values - hi.astype(F32)).astype(BF16)
    return mm(onehot, hi) + mm(onehot, lo)


def fwd_micro(m, hs_ref, h_ref, fp_ref, fn_ref, osnd_ref, orcv_ref, orcvt_ref,
              ws_ref, wr_ref, wm_ref, wn_ref, wa_ref, g_ref, out_ref, a_ref, u_ref):
    own = h_ref.shape[1]
    span = fp_ref.shape[1]
    osnd = osnd_ref[...]
    h = h_ref[m]
    gathered = (mm(osnd[:, :own], h) + mm(osnd[:, own:own + span], fp_ref[m])
                + mm(osnd[:, own + span:], fn_ref[m])).astype(BF16)
    send_part = mm(gathered, ws_ref[...]).astype(BF16).astype(F32)
    recv_rows = mm(orcv_ref[...], h).astype(BF16)
    pre = send_part + mm(recv_rows, wr_ref[...])
    a_ref[m] = pre
    edge_hidden = (pre * sigmoid(pre)).astype(BF16)
    messages = mm(edge_hidden, wm_ref[...])
    agg = split_sum(orcvt_ref[...], messages).astype(BF16)
    node_pre = mm(h, wn_ref[...]) + mm(agg, wa_ref[...])
    u_ref[m] = node_pre
    act = node_pre * sigmoid(node_pre)
    mean = jnp.mean(act, axis=-1, keepdims=True)
    cen = act - mean
    var = jnp.mean(cen * cen, axis=-1, keepdims=True)
    unit = cen * lax.rsqrt(var + EPSILON)
    out_ref[m] = (h.astype(F32) + unit * g_ref[...]).astype(BF16)


def fwd_kernel(*refs):
    for m in range(refs[1].shape[0]):
        fwd_micro(m, *refs)


def bwd_micro(m, pin_ref, a_ref, u_ref, osndt_ref, orcvl_ref, orcvt_ref,
              ws_ref, wr_ref, wm_ref, wn_ref, wa_ref, g_ref, p32_ref, hg_ref):
    own = pin_ref.shape[1]
    gain = g_ref[...]
    c = pin_ref[m].astype(F32)
    node_pre = u_ref[m]
    sig_u = sigmoid(node_pre)
    act = node_pre * sig_u
    mean = jnp.mean(act, axis=-1, keepdims=True)
    cen = act - mean
    var = jnp.mean(cen * cen, axis=-1, keepdims=True)
    rs = lax.rsqrt(var + EPSILON)
    unit = cen * rs
    gu = c * gain
    gact = rs * (gu - jnp.mean(gu, axis=-1, keepdims=True)
                 - unit * jnp.mean(gu * unit, axis=-1, keepdims=True))
    du = (gact * (sig_u * (1.0 + node_pre * (1.0 - sig_u)))).astype(BF16)
    dagg = mm_t(du, wa_ref[...]).astype(BF16)
    rows = c + mm_t(du, wn_ref[...])
    gmsg = mm(orcvl_ref[...], dagg).astype(BF16)
    pre = a_ref[m]
    sig_a = sigmoid(pre)
    dedge = (mm_t(gmsg, wm_ref[...]) * (sig_a * (1.0 + pre * (1.0 - sig_a)))).astype(BF16)
    rows = rows + split_sum(orcvt_ref[...], mm_t(dedge, wr_ref[...]))
    send_rows = split_sum(osndt_ref[...], mm_t(dedge, ws_ref[...]))
    p32_ref[m] = rows + send_rows[:own]
    hg_ref[m] = send_rows[own:].astype(BF16)


MESH_ID = pl.DeviceIdType.MESH


def comm_kernel(sends, n_in, parts, sections, *refs):
    ins = refs[:n_in]
    outs = refs[n_in:n_in + len(sends)]
    send_sem, recv_sem = refs[n_in + len(sends):]
    d = lax.axis_index("dom")
    p = lax.axis_index("pipe")
    barrier = pltpu.get_barrier_semaphore()
    for _, _, _, dd, dp in sends:
        src = (lax.rem(d - dd + parts, parts), lax.rem(p - dp + sections, sections))
        pl.semaphore_signal(barrier, 1, device_id=src, device_id_type=MESH_ID)
    pl.semaphore_wait(barrier, len(sends))
    copies = []
    for i, (k, start, rows, dd, dp) in enumerate(sends):
        dst = (lax.rem(d + dd + parts, parts), lax.rem(p + dp + sections, sections))
        source = ins[k] if start is None else ins[k].at[:, pl.ds(start, rows)]
        copy = pltpu.make_async_remote_copy(
            src_ref=source, dst_ref=outs[i], send_sem=send_sem.at[i], recv_sem=recv_sem.at[i],
            device_id=dst, device_id_type=MESH_ID)
        copy.start()
        copies.append(copy)
    for copy in copies:
        copy.wait()


def exchange(sends, payloads, parts, sections, cid):
    out_shapes = []
    for k, start, rows, _, _ in sends:
        shape = payloads[k].shape
        if start is not None:
            shape = (shape[0], rows) + shape[2:]
        out_shapes.append(jax.ShapeDtypeStruct(shape, payloads[k].dtype))
    n = len(sends)
    return pl.pallas_call(
        functools.partial(comm_kernel, tuple(sends), len(payloads), parts, sections),
        out_shape=tuple(out_shapes),
        in_specs=[pl.BlockSpec(memory_space=pl.ANY)] * len(payloads),
        out_specs=tuple(pl.BlockSpec(memory_space=pl.ANY) for _ in sends),
        scratch_shapes=[pltpu.SemaphoreType.DMA((n,)), pltpu.SemaphoreType.DMA((n,))],
        compiler_params=pltpu.CompilerParams(collective_id=cid, has_side_effects=True),
    )(*payloads)


def record_copies(pairs, sem, active):
    def run():
        copies = [pltpu.make_async_copy(buf, rec, sem.at[i]) for i, (buf, rec) in enumerate(pairs)]
        for copy in copies:
            copy.start()
        for copy in copies:
            copy.wait()
    if active is None:
        run()
    else:
        pl.when(active)(run)


def fwd_tick_kernel(parts, sections, tick, hs_ref, h_ref, fp_ref, fn_ref, osnd_ref, orcv_ref, orcvt_ref,
                    ws_ref, wr_ref, wm_ref, wn_ref, wa_ref, g_ref, *refs):
    if tick > 0:
        refs = refs[3:]
    (orec, arec, urec, hn_ref, fpn_ref, fnn_ref, obuf, abuf, ubuf,
     hbuf, fpbuf, fnbuf, stage_n, stage_p, send_sem, recv_sem, rec_sem) = refs
    micro, own, _ = h_ref.shape
    block = fp_ref.shape[1]
    d = lax.axis_index("dom")
    p = lax.axis_index("pipe")
    pipe_next = (d, lax.rem(p + 1, sections))
    pipe_prev = (d, lax.rem(p - 1 + sections, sections))
    dom_next = (lax.rem(d + 1, parts), p)
    dom_prev = (lax.rem(d - 1 + parts, parts), p)
    barrier = pltpu.get_barrier_semaphore()
    for src in (pipe_prev, dom_prev, dom_next):
        pl.semaphore_signal(barrier, 1, device_id=src, device_id_type=MESH_ID)
    compute_refs = (hs_ref, h_ref, fp_ref, fn_ref, osnd_ref, orcv_ref, orcvt_ref,
                    ws_ref, wr_ref, wm_ref, wn_ref, wa_ref, g_ref, obuf, abuf, ubuf)
    pipe_copies = []
    for m in range(micro):
        fwd_micro(m, *compute_refs)
        if m == 0:
            pl.semaphore_wait(barrier, 3)
        copy = pltpu.make_async_remote_copy(
            src_ref=obuf.at[m], dst_ref=hbuf.at[m], send_sem=send_sem.at[0, m],
            recv_sem=recv_sem.at[0, m], device_id=pipe_next, device_id_type=MESH_ID)
        copy.start()
        pipe_copies.append(copy)
    record_copies(((obuf, orec), (abuf, arec), (ubuf, urec)), rec_sem,
                  None if tick == 0 else p == tick)
    hs0 = hs_ref[0]
    hs1 = hs_ref[1]
    halo_copies = []
    for m in range(micro):
        pipe_copies[m].wait_recv()
        h = hbuf[m]
        sel_n = h[0:block]
        sel_p = h[0:block]
        for b in range(1, own // block):
            piece = h[b * block:(b + 1) * block]
            sel_n = jnp.where(hs0 == b, piece, sel_n)
            sel_p = jnp.where(hs1 == b, piece, sel_p)
        stage_n[m] = sel_n
        stage_p[m] = sel_p
        for j, (stage, buf, dst) in enumerate(((stage_n, fpbuf, dom_next), (stage_p, fnbuf, dom_prev))):
            copy = pltpu.make_async_remote_copy(
                src_ref=stage.at[m], dst_ref=buf.at[m], send_sem=send_sem.at[1 + j, m],
                recv_sem=recv_sem.at[1 + j, m], device_id=dst, device_id_type=MESH_ID)
            copy.start()
            halo_copies.append(copy)
    for copy in pipe_copies:
        copy.wait_send()
    for copy in halo_copies:
        copy.wait()
    hn_ref[...] = hbuf[...]
    fpn_ref[...] = fpbuf[...]
    fnn_ref[...] = fnbuf[...]


def fwd_tick(operands, records, tick, span, parts, sections):
    h = operands[1]
    micro, own, latent = h.shape
    vm = pl.BlockSpec(memory_space=pltpu.VMEM)
    anyspec = pl.BlockSpec(memory_space=pl.ANY)
    bf = lambda rows: jax.ShapeDtypeStruct((micro, rows, latent), BF16)
    f32 = jax.ShapeDtypeStruct((micro, own, latent), F32)
    n = len(operands)
    extra = () if tick == 0 else tuple(records)
    return pl.pallas_call(
        functools.partial(fwd_tick_kernel, parts, sections, tick),
        out_shape=(bf(own), f32, f32, bf(own), bf(span), bf(span)),
        in_specs=[pl.BlockSpec(memory_space=pltpu.SMEM)] + [vm] * (n - 1) + [anyspec] * len(extra),
        out_specs=(anyspec, anyspec, anyspec, vm, vm, vm),
        scratch_shapes=[pltpu.VMEM((micro, own, latent), BF16),
                        pltpu.VMEM((micro, own, latent), F32),
                        pltpu.VMEM((micro, own, latent), F32),
                        pltpu.VMEM((micro, own, latent), BF16),
                        pltpu.VMEM((micro, span, latent), BF16),
                        pltpu.VMEM((micro, span, latent), BF16),
                        pltpu.VMEM((micro, span, latent), BF16),
                        pltpu.VMEM((micro, span, latent), BF16),
                        pltpu.SemaphoreType.DMA((3, micro)),
                        pltpu.SemaphoreType.DMA((3, micro)),
                        pltpu.SemaphoreType.DMA((3,))],
        input_output_aliases={} if tick == 0 else {n: 0, n + 1: 1, n + 2: 2},
        compiler_params=pltpu.CompilerParams(collective_id=10 + tick,
                                             has_side_effects=True,
                                             vmem_limit_bytes=48 * 1024 * 1024),
    )(*operands, *extra)


def fwd_last_kernel(tick, hs_ref, h_ref, fp_ref, fn_ref, osnd_ref, orcv_ref, orcvt_ref,
                    ws_ref, wr_ref, wm_ref, wn_ref, wa_ref, g_ref, orec_in, arec_in, urec_in,
                    orec, arec, urec, obuf, abuf, ubuf, rec_sem):
    compute_refs = (hs_ref, h_ref, fp_ref, fn_ref, osnd_ref, orcv_ref, orcvt_ref,
                    ws_ref, wr_ref, wm_ref, wn_ref, wa_ref, g_ref, obuf, abuf, ubuf)
    for m in range(h_ref.shape[0]):
        fwd_micro(m, *compute_refs)
    record_copies(((obuf, orec), (abuf, arec), (ubuf, urec)), rec_sem,
                  lax.axis_index("pipe") == tick)


def fwd_last(operands, records, tick):
    h = operands[1]
    micro, own, latent = h.shape
    vm = pl.BlockSpec(memory_space=pltpu.VMEM)
    anyspec = pl.BlockSpec(memory_space=pl.ANY)
    n = len(operands)
    return pl.pallas_call(
        functools.partial(fwd_last_kernel, tick),
        out_shape=tuple(jax.ShapeDtypeStruct(r.shape, r.dtype) for r in records),
        in_specs=[pl.BlockSpec(memory_space=pltpu.SMEM)] + [vm] * (n - 1) + [anyspec] * 3,
        out_specs=(anyspec, anyspec, anyspec),
        scratch_shapes=[pltpu.VMEM((micro, own, latent), BF16),
                        pltpu.VMEM((micro, own, latent), F32),
                        pltpu.VMEM((micro, own, latent), F32),
                        pltpu.SemaphoreType.DMA((3,))],
        input_output_aliases={n: 0, n + 1: 1, n + 2: 2},
        compiler_params=pltpu.CompilerParams(vmem_limit_bytes=48 * 1024 * 1024),
    )(*operands, *records)


def bwd_tick_kernel(parts, sections, tick, first, hs_ref, pin_ref, a_ref, u_ref, osndt_ref, orcvl_ref,
                    orcvt_ref, ws_ref, wr_ref, wm_ref, wn_ref, wa_ref, g_ref, *refs):
    send_pipe = tick > 0
    if not first:
        refs = refs[1:]
    if send_pipe:
        grec, pinn_ref, p32, hg, snbuf, spbuf, gbuf, pinbuf, send_sem, recv_sem, rec_sem = refs
    else:
        grec, p32, hg, snbuf, spbuf, gbuf, send_sem, recv_sem, rec_sem = refs
    micro, own, _ = pin_ref.shape
    block = snbuf.shape[1]
    d = lax.axis_index("dom")
    p = lax.axis_index("pipe")
    pipe_prev = (d, lax.rem(p - 1 + sections, sections))
    pipe_next = (d, lax.rem(p + 1, sections))
    dom_next = (lax.rem(d + 1, parts), p)
    dom_prev = (lax.rem(d - 1 + parts, parts), p)
    barrier = pltpu.get_barrier_semaphore()
    sources = [dom_next, dom_prev] + ([pipe_next] if send_pipe else [])
    for src in sources:
        pl.semaphore_signal(barrier, 1, device_id=src, device_id_type=MESH_ID)
    compute_refs = (pin_ref, a_ref, u_ref, osndt_ref, orcvl_ref, orcvt_ref,
                    ws_ref, wr_ref, wm_ref, wn_ref, wa_ref, g_ref, p32, hg)
    halo_copies = []
    for m in range(micro):
        bwd_micro(m, *compute_refs)
        if m == 0:
            pl.semaphore_wait(barrier, len(sources))
        pair = []
        for j, (lo, buf, dst) in enumerate(((0, snbuf, dom_prev), (block, spbuf, dom_next))):
            copy = pltpu.make_async_remote_copy(
                src_ref=hg.at[m, pl.ds(lo, block)], dst_ref=buf.at[m],
                send_sem=send_sem.at[j, m], recv_sem=recv_sem.at[j, m],
                device_id=dst, device_id_type=MESH_ID)
            copy.start()
            pair.append(copy)
        halo_copies.append(pair)
    hs0 = hs_ref[0]
    hs1 = hs_ref[1]
    pipe_copies = []
    for m in range(micro):
        for copy in halo_copies[m]:
            copy.wait_recv()
        sn = snbuf[m].astype(F32)
        sp = spbuf[m].astype(F32)
        for b in range(own // block):
            piece = p32[m, b * block:(b + 1) * block]
            piece = piece + jnp.where(hs0 == b, sn, 0.0) + jnp.where(hs1 == b, sp, 0.0)
            gbuf[m, b * block:(b + 1) * block] = piece.astype(gbuf.dtype)
        if send_pipe:
            copy = pltpu.make_async_remote_copy(
                src_ref=gbuf.at[m], dst_ref=pinbuf.at[m], send_sem=send_sem.at[2, m],
                recv_sem=recv_sem.at[2, m], device_id=pipe_prev, device_id_type=MESH_ID)
            copy.start()
            pipe_copies.append(copy)
    record_copies(((gbuf, grec),), rec_sem, None if first else p == tick)
    for pair in halo_copies:
        for copy in pair:
            copy.wait_send()
    for copy in pipe_copies:
        copy.wait()
    if send_pipe:
        pinn_ref[...] = pinbuf[...]


def bwd_tick(operands, grad_rec, tick, span, parts, sections):
    pin = operands[1]
    micro, own, latent = pin.shape
    send_pipe = tick > 0
    first = grad_rec is None
    vm = pl.BlockSpec(memory_space=pltpu.VMEM)
    anyspec = pl.BlockSpec(memory_space=pl.ANY)
    grad = jax.ShapeDtypeStruct((micro, own, latent), BF16)
    scratch = [pltpu.VMEM((micro, own, latent), F32), pltpu.VMEM((micro, 2 * span, latent), BF16),
               pltpu.VMEM((micro, span, latent), BF16), pltpu.VMEM((micro, span, latent), BF16),
               pltpu.VMEM((micro, own, latent), BF16)]
    if send_pipe:
        scratch.append(pltpu.VMEM((micro, own, latent), BF16))
    scratch += [pltpu.SemaphoreType.DMA((3, micro)), pltpu.SemaphoreType.DMA((3, micro)),
                pltpu.SemaphoreType.DMA((1,))]
    outs = (grad, grad) if send_pipe else (grad,)
    n = len(operands)
    extra = () if first else (grad_rec,)
    return pl.pallas_call(
        functools.partial(bwd_tick_kernel, parts, sections, tick, first),
        out_shape=outs,
        in_specs=[pl.BlockSpec(memory_space=pltpu.SMEM)] + [vm] * (n - 1) + [anyspec] * len(extra),
        out_specs=(anyspec,) + ((vm,) if send_pipe else ()),
        scratch_shapes=scratch,
        input_output_aliases={} if first else {n: 0},
        compiler_params=pltpu.CompilerParams(collective_id=20 + tick, has_side_effects=True,
                                             vmem_limit_bytes=48 * 1024 * 1024),
    )(*operands, *extra)


def vmem_call(kernel, out_shapes, n_in, smem_first=True):
    in_specs = [pl.BlockSpec(memory_space=pltpu.SMEM)] + [pl.BlockSpec(memory_space=pltpu.VMEM)] * (n_in - 1)
    return pl.pallas_call(
        kernel,
        out_shape=out_shapes,
        in_specs=in_specs,
        out_specs=tuple(pl.BlockSpec(memory_space=pltpu.VMEM) for _ in out_shapes),
        compiler_params=pltpu.CompilerParams(vmem_limit_bytes=48 * 1024 * 1024),
    )


def whole_kernel(parts, sections, hs_ref, cnt_ref, x_hbm, cot_hbm, esnd_ref, ercv_ref,
                 ws_hbm, wr_hbm, wm_hbm, wn_hbm, wa_hbm, g_ref,
                 out_ref, grad_ref,
                 xbuf, cotbuf, wbuf, osnd_ref, orcv_ref, orcvt_ref, osndt_ref, orcvl_ref,
                 hbuf, fpbuf, fnbuf, stage_n, stage_p, abuf, ubuf, cbuf, p32, hg, snbuf, spbuf,
                 unitbuf, rsbuf,
                 fsend, frecv, bsend, brecv, lsem):
    micro, own, latent = xbuf.shape
    block = fpbuf.shape[1]
    span = block
    loads = [pltpu.make_async_copy(x_hbm, xbuf, lsem.at[0])]
    for i, w in enumerate((ws_hbm, wr_hbm, wm_hbm, wn_hbm, wa_hbm)):
        loads.append(pltpu.make_async_copy(w, wbuf.at[i], lsem.at[1 + i]))
    loads.append(pltpu.make_async_copy(cot_hbm, cotbuf, lsem.at[6]))
    for copy in loads:
        copy.start()
    edges = osnd_ref.shape[0]
    ext_rows = osnd_ref.shape[1]
    own_rows = orcv_ref.shape[1]
    es = esnd_ref[...]
    er = ercv_ref[...]
    snd = jnp.concatenate([es[i:i + 1] for i in range(es.shape[0])], axis=1)
    rcv = jnp.concatenate([er[i:i + 1] for i in range(er.shape[0])], axis=1)
    lane = lax.broadcasted_iota(jnp.int32, (1, edges), 1)
    per_block = es.shape[1]
    live = lane < 0
    for i in range(es.shape[0]):
        live = live | ((lane >= i * per_block) & (lane < i * per_block + cnt_ref[i]))
    sndt = lax.broadcasted_iota(jnp.int32, (ext_rows, edges), 0) == snd
    rcvt = lax.broadcasted_iota(jnp.int32, (own_rows, edges), 0) == rcv
    osndt_f = sndt.astype(F32)
    rcvt_f = rcvt.astype(F32)
    rcvlt_f = (rcvt & live).astype(F32)
    osndt_ref[...] = osndt_f.astype(BF16)
    orcvt_ref[...] = rcvlt_f.astype(BF16)
    osnd_ref[...] = osndt_f.T.astype(BF16)
    orcv_ref[...] = rcvt_f.T.astype(BF16)
    orcvl_ref[...] = rcvlt_f.T.astype(BF16)
    d = lax.axis_index("dom")
    p = lax.axis_index("pipe")
    pipe_next = (d, lax.rem(p + 1, sections))
    pipe_prev = (d, lax.rem(p - 1 + sections, sections))
    dom_next = (lax.rem(d + 1, parts), p)
    dom_prev = (lax.rem(d - 1 + parts, parts), p)
    barrier = pltpu.get_barrier_semaphore()
    for nb in (pipe_prev, pipe_next, dom_prev, dom_next):
        pl.semaphore_signal(barrier, 1, device_id=nb, device_id_type=MESH_ID)
    pl.semaphore_wait(barrier, 4)
    hs0 = hs_ref[0]
    hs1 = hs_ref[1]
    has_prev = p > 0
    has_next = p < sections - 1
    gain = g_ref[...]
    ws, wr, wm, wn, wa = (wbuf.at[i] for i in range(5))

    def remote(src, dst, sems, idx, target):
        send_sem, recv_sem = sems
        return pltpu.make_async_remote_copy(
            src_ref=src, dst_ref=dst, send_sem=send_sem.at[idx], recv_sem=recv_sem.at[idx],
            device_id=target, device_id_type=MESH_ID)

    loads[0].wait()
    fwd_pipe = []
    fwd_halo = []
    for m in range(micro):
        pipe_in = remote(out_ref.at[m], hbuf.at[m], (fsend, frecv), m, pipe_next)
        pl.when(has_prev)(pipe_in.wait_recv)

        @pl.when(p == 0)
        def _():
            hbuf[m] = xbuf[m]

        h = hbuf[m]
        sel_n = h[0:block]
        sel_p = h[0:block]
        for b in range(1, own // block):
            piece = h[b * block:(b + 1) * block]
            sel_n = jnp.where(hs0 == b, piece, sel_n)
            sel_p = jnp.where(hs1 == b, piece, sel_p)
        stage_n[m] = sel_n
        stage_p[m] = sel_p
        pair = [remote(stage_n.at[m], fpbuf.at[m], (fsend, frecv), micro + 2 * m, dom_next),
                remote(stage_p.at[m], fnbuf.at[m], (fsend, frecv), micro + 2 * m + 1, dom_prev)]
        for copy in pair:
            copy.start()
        if m == 0:
            for copy in loads[1:6]:
                copy.wait()
        osnd = osnd_ref[...]
        own_gather = mm(osnd[:, :own], h)
        recv_rows = mm(orcv_ref[...], h).astype(BF16)
        recv_part = mm(recv_rows, wr[...])
        node_part = mm(h, wn[...])
        for copy in pair:
            copy.wait_recv()
        fwd_halo.extend(pair)
        gathered = (own_gather + mm(osnd[:, own:own + span], fpbuf[m])
                    + mm(osnd[:, own + span:], fnbuf[m])).astype(BF16)
        send_part = mm(gathered, ws[...]).astype(BF16).astype(F32)
        pre = send_part + recv_part
        sig_a = sigmoid(pre)
        edge_hidden = (pre * sig_a).astype(BF16)
        messages = mm(edge_hidden, wm[...])
        agg = split_sum(orcvt_ref[...], messages).astype(BF16)
        node_pre = node_part + mm(agg, wa[...])
        sig_u = sigmoid(node_pre)
        act = node_pre * sig_u
        mean = jnp.mean(act, axis=-1, keepdims=True)
        cen = act - mean
        var = jnp.mean(cen * cen, axis=-1, keepdims=True)
        rs = lax.rsqrt(var + EPSILON)
        unit = cen * rs
        out_ref[m] = (h.astype(F32) + unit * gain).astype(BF16)
        pl.when(has_next)(pipe_in.start)
        fwd_pipe.append(pipe_in)
        unitbuf[m] = unit
        rsbuf[m] = jnp.broadcast_to(rs, rsbuf.shape[1:])
        ubuf[m] = sig_u * (1.0 + node_pre * (1.0 - sig_u))
        abuf[m] = sig_a * (1.0 + pre * (1.0 - sig_a))

    loads[6].wait()
    bwd_pipe = []
    bwd_halo = []
    for m in range(micro):
        pipe_in = remote(grad_ref.at[m], cbuf.at[m], (bsend, brecv), m, pipe_prev)
        pl.when(has_next)(pipe_in.wait_recv)

        @pl.when(p == sections - 1)
        def _():
            cbuf[m] = cotbuf[m]

        c = cbuf[m].astype(F32)
        unit = unitbuf[m]
        rs = rsbuf[m][:, 0:1]
        gu = c * gain
        gact = rs * (gu - jnp.mean(gu, axis=-1, keepdims=True)
                     - unit * jnp.mean(gu * unit, axis=-1, keepdims=True))
        du = (gact * ubuf[m]).astype(BF16)
        dagg = mm_t(du, wa[...]).astype(BF16)
        gmsg = mm(orcvl_ref[...], dagg).astype(BF16)
        dedge = (mm_t(gmsg, wm[...]) * abuf[m]).astype(BF16)
        send_x = mm_t(dedge, ws[...])
        osndt = osndt_ref[...]
        hg[m] = split_sum(osndt[own:], send_x).astype(BF16)
        pair = [remote(hg.at[m, pl.ds(0, block)], snbuf.at[m], (bsend, brecv), micro + 2 * m, dom_prev),
                remote(hg.at[m, pl.ds(block, block)], spbuf.at[m], (bsend, brecv), micro + 2 * m + 1,
                       dom_next)]
        for copy in pair:
            copy.start()
        rows = c + mm_t(du, wn[...])
        rows = rows + split_sum(orcvt_ref[...], mm_t(dedge, wr[...]))
        p32[m] = rows + split_sum(osndt[:own], send_x)
        for copy in pair:
            copy.wait_recv()
        bwd_halo.extend(pair)
        sn = snbuf[m].astype(F32)
        sp = spbuf[m].astype(F32)
        for b in range(own // block):
            piece = p32[m, b * block:(b + 1) * block]
            piece = piece + jnp.where(hs0 == b, sn, 0.0) + jnp.where(hs1 == b, sp, 0.0)
            grad_ref[m, b * block:(b + 1) * block] = piece.astype(grad_ref.dtype)
        pl.when(has_prev)(pipe_in.start)
        bwd_pipe.append(pipe_in)

    for copy in fwd_pipe:
        pl.when(has_next)(copy.wait_send)
    for copy in bwd_pipe:
        pl.when(has_prev)(copy.wait_send)
    for copy in fwd_halo + bwd_halo:
        copy.wait_send()


def whole(operands, span, parts, sections):
    x = operands[2]
    micro, own, latent = x.shape
    vm = pl.BlockSpec(memory_space=pltpu.VMEM)
    anyspec = pl.BlockSpec(memory_space=pltpu.HBM)
    bf = lambda rows: pltpu.VMEM((micro, rows, latent), BF16)
    f32 = pltpu.VMEM((micro, own, latent), F32)
    smem = pl.BlockSpec(memory_space=pltpu.SMEM)
    in_specs = [smem, smem, anyspec, anyspec, vm, vm] + [anyspec] * 5 + [vm]
    edges = operands[4].size
    ext_rows = own + 2 * span
    return pl.pallas_call(
        functools.partial(whole_kernel, parts, sections),
        out_shape=(jax.ShapeDtypeStruct((micro, own, latent), BF16),
                   jax.ShapeDtypeStruct((micro, own, latent), BF16)),
        in_specs=in_specs,
        out_specs=(vm, vm),
        scratch_shapes=[bf(own), bf(own), pltpu.VMEM((5, latent, latent), BF16),
                        pltpu.VMEM((edges, ext_rows), BF16), pltpu.VMEM((edges, own), BF16),
                        pltpu.VMEM((own, edges), BF16), pltpu.VMEM((ext_rows, edges), BF16),
                        pltpu.VMEM((edges, own), BF16),
                        bf(own), bf(span), bf(span), bf(span), bf(span), f32, f32, bf(own), f32,
                        bf(2 * span), bf(span), bf(span), f32, pltpu.VMEM((micro, own, 128), F32),
                        pltpu.SemaphoreType.DMA((3 * micro,)), pltpu.SemaphoreType.DMA((3 * micro,)),
                        pltpu.SemaphoreType.DMA((3 * micro,)), pltpu.SemaphoreType.DMA((3 * micro,)),
                        pltpu.SemaphoreType.DMA((7,))],
        compiler_params=pltpu.CompilerParams(collective_id=0, has_side_effects=True,
                                             vmem_limit_bytes=67043328),
    )(*operands)


def shards(inputs, cotangent, w_send, w_recv, w_message, w_node, w_aggregate, gains,
           edge_send, edge_recv, edge_count, halo_send):
    sections = lax.axis_size("pipe")
    parts = lax.axis_size("dom")
    p_idx = lax.axis_index("pipe")
    micro, own, latent = inputs.shape
    block = edge_send.shape[1]
    span = halo_send.shape[2] * block
    ext_rows = own + 2 * span
    weights = (w_send[0], w_recv[0], w_message[0], w_node[0], w_aggregate[0])
    gain = gains[0].reshape(1, latent)
    hs = halo_send[0].reshape(-1).astype(jnp.int32)

    def blocks_of(x):
        shaped = x.reshape(micro, own // block, block, latent)
        nxt = jnp.take(shaped, hs[0], axis=1)
        prv = jnp.take(shaped, hs[1], axis=1)
        return nxt, prv

    S, D = sections, parts

    def perm_pipe(shift):
        return [(i, (i + shift) % S) for i in range(S)]

    def perm_both(dshift, pshift):
        return [(d * S + p, ((d + dshift) % D) * S + (p + pshift) % S)
                for d in range(D) for p in range(S)]

    both = ("dom", "pipe")

    fwd = vmem_call(
        fwd_kernel,
        (jax.ShapeDtypeStruct((micro, own, latent), BF16),
         jax.ShapeDtypeStruct((micro, own, latent), F32),
         jax.ShapeDtypeStruct((micro, own, latent), F32)),
        13)

    out_rec, grad_rec = whole(
        (hs, edge_count.astype(jnp.int32), inputs, cotangent, edge_send.astype(jnp.int32),
         edge_recv.astype(jnp.int32), *weights, gain), span, D, S)
    return (out_rec[None], grad_rec[None])


def solution(mesh):
    in_specs = (
        P(None, "dom", None),
        P(None, "dom", None),
        P("pipe", None, None),
        P("pipe", None, None),
        P("pipe", None, None),
        P("pipe", None, None),
        P("pipe", None, None),
        P("pipe", None),
        P("dom", None),
        P("dom", None),
        P("dom"),
        P("dom", None, None),
    )
    out_specs = (P("pipe", None, "dom", None), P("pipe", None, "dom", None))
    return jax.shard_map(shards, mesh=mesh, in_specs=in_specs, out_specs=out_specs, check_vma=False)
```

```python
import functools

import jax
import jax.numpy as jnp
from jax import lax
from jax.experimental import pallas as pl
from jax.experimental.pallas import tpu as pltpu
from jax.sharding import PartitionSpec as P

EPSILON = 1e-05
F32 = jnp.float32
BF16 = jnp.bfloat16


def mm(x, w):
    return jnp.dot(x, w, preferred_element_type=F32)


def mm_t(x, w):
    return lax.dot_general(x, w, (((1,), (1,)), ((), ())), preferred_element_type=F32)


def sigmoid(v):
    return 0.5 * (1.0 + jnp.tanh(0.5 * v))


def split_sum(onehot, values):
    hi = values.astype(BF16)
    lo = (values - hi.astype(F32)).astype(BF16)
    return mm(onehot, hi) + mm(onehot, lo)


def fwd_micro(m, hs_ref, h_ref, fp_ref, fn_ref, osnd_ref, orcv_ref, orcvt_ref,
              ws_ref, wr_ref, wm_ref, wn_ref, wa_ref, g_ref, out_ref, a_ref, u_ref):
    own = h_ref.shape[1]
    span = fp_ref.shape[1]
    osnd = osnd_ref[...]
    h = h_ref[m]
    gathered = (mm(osnd[:, :own], h) + mm(osnd[:, own:own + span], fp_ref[m])
                + mm(osnd[:, own + span:], fn_ref[m])).astype(BF16)
    send_part = mm(gathered, ws_ref[...]).astype(BF16).astype(F32)
    recv_rows = mm(orcv_ref[...], h).astype(BF16)
    pre = send_part + mm(recv_rows, wr_ref[...])
    a_ref[m] = pre
    edge_hidden = (pre * sigmoid(pre)).astype(BF16)
    messages = mm(edge_hidden, wm_ref[...])
    agg = split_sum(orcvt_ref[...], messages).astype(BF16)
    node_pre = mm(h, wn_ref[...]) + mm(agg, wa_ref[...])
    u_ref[m] = node_pre
    act = node_pre * sigmoid(node_pre)
    mean = jnp.mean(act, axis=-1, keepdims=True)
    cen = act - mean
    var = jnp.mean(cen * cen, axis=-1, keepdims=True)
    unit = cen * lax.rsqrt(var + EPSILON)
    out_ref[m] = (h.astype(F32) + unit * g_ref[...]).astype(BF16)


def fwd_kernel(*refs):
    for m in range(refs[1].shape[0]):
        fwd_micro(m, *refs)


def bwd_micro(m, pin_ref, a_ref, u_ref, osndt_ref, orcvl_ref, orcvt_ref,
              ws_ref, wr_ref, wm_ref, wn_ref, wa_ref, g_ref, p32_ref, hg_ref):
    own = pin_ref.shape[1]
    gain = g_ref[...]
    c = pin_ref[m].astype(F32)
    node_pre = u_ref[m]
    sig_u = sigmoid(node_pre)
    act = node_pre * sig_u
    mean = jnp.mean(act, axis=-1, keepdims=True)
    cen = act - mean
    var = jnp.mean(cen * cen, axis=-1, keepdims=True)
    rs = lax.rsqrt(var + EPSILON)
    unit = cen * rs
    gu = c * gain
    gact = rs * (gu - jnp.mean(gu, axis=-1, keepdims=True)
                 - unit * jnp.mean(gu * unit, axis=-1, keepdims=True))
    du = (gact * (sig_u * (1.0 + node_pre * (1.0 - sig_u)))).astype(BF16)
    dagg = mm_t(du, wa_ref[...]).astype(BF16)
    rows = c + mm_t(du, wn_ref[...])
    gmsg = mm(orcvl_ref[...], dagg).astype(BF16)
    pre = a_ref[m]
    sig_a = sigmoid(pre)
    dedge = (mm_t(gmsg, wm_ref[...]) * (sig_a * (1.0 + pre * (1.0 - sig_a)))).astype(BF16)
    rows = rows + split_sum(orcvt_ref[...], mm_t(dedge, wr_ref[...]))
    send_rows = split_sum(osndt_ref[...], mm_t(dedge, ws_ref[...]))
    p32_ref[m] = rows + send_rows[:own]
    hg_ref[m] = send_rows[own:].astype(BF16)


MESH_ID = pl.DeviceIdType.MESH


def comm_kernel(sends, n_in, parts, sections, *refs):
    ins = refs[:n_in]
    outs = refs[n_in:n_in + len(sends)]
    send_sem, recv_sem = refs[n_in + len(sends):]
    d = lax.axis_index("dom")
    p = lax.axis_index("pipe")
    barrier = pltpu.get_barrier_semaphore()
    for _, _, _, dd, dp in sends:
        src = (lax.rem(d - dd + parts, parts), lax.rem(p - dp + sections, sections))
        pl.semaphore_signal(barrier, 1, device_id=src, device_id_type=MESH_ID)
    pl.semaphore_wait(barrier, len(sends))
    copies = []
    for i, (k, start, rows, dd, dp) in enumerate(sends):
        dst = (lax.rem(d + dd + parts, parts), lax.rem(p + dp + sections, sections))
        source = ins[k] if start is None else ins[k].at[:, pl.ds(start, rows)]
        copy = pltpu.make_async_remote_copy(
            src_ref=source, dst_ref=outs[i], send_sem=send_sem.at[i], recv_sem=recv_sem.at[i],
            device_id=dst, device_id_type=MESH_ID)
        copy.start()
        copies.append(copy)
    for copy in copies:
        copy.wait()


def exchange(sends, payloads, parts, sections, cid):
    out_shapes = []
    for k, start, rows, _, _ in sends:
        shape = payloads[k].shape
        if start is not None:
            shape = (shape[0], rows) + shape[2:]
        out_shapes.append(jax.ShapeDtypeStruct(shape, payloads[k].dtype))
    n = len(sends)
    return pl.pallas_call(
        functools.partial(comm_kernel, tuple(sends), len(payloads), parts, sections),
        out_shape=tuple(out_shapes),
        in_specs=[pl.BlockSpec(memory_space=pl.ANY)] * len(payloads),
        out_specs=tuple(pl.BlockSpec(memory_space=pl.ANY) for _ in sends),
        scratch_shapes=[pltpu.SemaphoreType.DMA((n,)), pltpu.SemaphoreType.DMA((n,))],
        compiler_params=pltpu.CompilerParams(collective_id=cid, has_side_effects=True),
    )(*payloads)


def record_copies(pairs, sem, active):
    def run():
        copies = [pltpu.make_async_copy(buf, rec, sem.at[i]) for i, (buf, rec) in enumerate(pairs)]
        for copy in copies:
            copy.start()
        for copy in copies:
            copy.wait()
    if active is None:
        run()
    else:
        pl.when(active)(run)


def fwd_tick_kernel(parts, sections, tick, hs_ref, h_ref, fp_ref, fn_ref, osnd_ref, orcv_ref, orcvt_ref,
                    ws_ref, wr_ref, wm_ref, wn_ref, wa_ref, g_ref, *refs):
    if tick > 0:
        refs = refs[3:]
    (orec, arec, urec, hn_ref, fpn_ref, fnn_ref, obuf, abuf, ubuf,
     hbuf, fpbuf, fnbuf, stage_n, stage_p, send_sem, recv_sem, rec_sem) = refs
    micro, own, _ = h_ref.shape
    block = fp_ref.shape[1]
    d = lax.axis_index("dom")
    p = lax.axis_index("pipe")
    pipe_next = (d, lax.rem(p + 1, sections))
    pipe_prev = (d, lax.rem(p - 1 + sections, sections))
    dom_next = (lax.rem(d + 1, parts), p)
    dom_prev = (lax.rem(d - 1 + parts, parts), p)
    barrier = pltpu.get_barrier_semaphore()
    for src in (pipe_prev, dom_prev, dom_next):
        pl.semaphore_signal(barrier, 1, device_id=src, device_id_type=MESH_ID)
    compute_refs = (hs_ref, h_ref, fp_ref, fn_ref, osnd_ref, orcv_ref, orcvt_ref,
                    ws_ref, wr_ref, wm_ref, wn_ref, wa_ref, g_ref, obuf, abuf, ubuf)
    pipe_copies = []
    for m in range(micro):
        fwd_micro(m, *compute_refs)
        if m == 0:
            pl.semaphore_wait(barrier, 3)
        copy = pltpu.make_async_remote_copy(
            src_ref=obuf.at[m], dst_ref=hbuf.at[m], send_sem=send_sem.at[0, m],
            recv_sem=recv_sem.at[0, m], device_id=pipe_next, device_id_type=MESH_ID)
        copy.start()
        pipe_copies.append(copy)
    record_copies(((obuf, orec), (abuf, arec), (ubuf, urec)), rec_sem,
                  None if tick == 0 else p == tick)
    hs0 = hs_ref[0]
    hs1 = hs_ref[1]
    halo_copies = []
    for m in range(micro):
        pipe_copies[m].wait_recv()
        h = hbuf[m]
        sel_n = h[0:block]
        sel_p = h[0:block]
        for b in range(1, own // block):
            piece = h[b * block:(b + 1) * block]
            sel_n = jnp.where(hs0 == b, piece, sel_n)
            sel_p = jnp.where(hs1 == b, piece, sel_p)
        stage_n[m] = sel_n
        stage_p[m] = sel_p
        for j, (stage, buf, dst) in enumerate(((stage_n, fpbuf, dom_next), (stage_p, fnbuf, dom_prev))):
            copy = pltpu.make_async_remote_copy(
                src_ref=stage.at[m], dst_ref=buf.at[m], send_sem=send_sem.at[1 + j, m],
                recv_sem=recv_sem.at[1 + j, m], device_id=dst, device_id_type=MESH_ID)
            copy.start()
            halo_copies.append(copy)
    for copy in pipe_copies:
        copy.wait_send()
    for copy in halo_copies:
        copy.wait()
    hn_ref[...] = hbuf[...]
    fpn_ref[...] = fpbuf[...]
    fnn_ref[...] = fnbuf[...]


def fwd_tick(operands, records, tick, span, parts, sections):
    h = operands[1]
    micro, own, latent = h.shape
    vm = pl.BlockSpec(memory_space=pltpu.VMEM)
    anyspec = pl.BlockSpec(memory_space=pl.ANY)
    bf = lambda rows: jax.ShapeDtypeStruct((micro, rows, latent), BF16)
    f32 = jax.ShapeDtypeStruct((micro, own, latent), F32)
    n = len(operands)
    extra = () if tick == 0 else tuple(records)
    return pl.pallas_call(
        functools.partial(fwd_tick_kernel, parts, sections, tick),
        out_shape=(bf(own), f32, f32, bf(own), bf(span), bf(span)),
        in_specs=[pl.BlockSpec(memory_space=pltpu.SMEM)] + [vm] * (n - 1) + [anyspec] * len(extra),
        out_specs=(anyspec, anyspec, anyspec, vm, vm, vm),
        scratch_shapes=[pltpu.VMEM((micro, own, latent), BF16),
                        pltpu.VMEM((micro, own, latent), F32),
                        pltpu.VMEM((micro, own, latent), F32),
                        pltpu.VMEM((micro, own, latent), BF16),
                        pltpu.VMEM((micro, span, latent), BF16),
                        pltpu.VMEM((micro, span, latent), BF16),
                        pltpu.VMEM((micro, span, latent), BF16),
                        pltpu.VMEM((micro, span, latent), BF16),
                        pltpu.SemaphoreType.DMA((3, micro)),
                        pltpu.SemaphoreType.DMA((3, micro)),
                        pltpu.SemaphoreType.DMA((3,))],
        input_output_aliases={} if tick == 0 else {n: 0, n + 1: 1, n + 2: 2},
        compiler_params=pltpu.CompilerParams(collective_id=10 + tick,
                                             has_side_effects=True,
                                             vmem_limit_bytes=48 * 1024 * 1024),
    )(*operands, *extra)


def fwd_last_kernel(tick, hs_ref, h_ref, fp_ref, fn_ref, osnd_ref, orcv_ref, orcvt_ref,
                    ws_ref, wr_ref, wm_ref, wn_ref, wa_ref, g_ref, orec_in, arec_in, urec_in,
                    orec, arec, urec, obuf, abuf, ubuf, rec_sem):
    compute_refs = (hs_ref, h_ref, fp_ref, fn_ref, osnd_ref, orcv_ref, orcvt_ref,
                    ws_ref, wr_ref, wm_ref, wn_ref, wa_ref, g_ref, obuf, abuf, ubuf)
    for m in range(h_ref.shape[0]):
        fwd_micro(m, *compute_refs)
    record_copies(((obuf, orec), (abuf, arec), (ubuf, urec)), rec_sem,
                  lax.axis_index("pipe") == tick)


def fwd_last(operands, records, tick):
    h = operands[1]
    micro, own, latent = h.shape
    vm = pl.BlockSpec(memory_space=pltpu.VMEM)
    anyspec = pl.BlockSpec(memory_space=pl.ANY)
    n = len(operands)
    return pl.pallas_call(
        functools.partial(fwd_last_kernel, tick),
        out_shape=tuple(jax.ShapeDtypeStruct(r.shape, r.dtype) for r in records),
        in_specs=[pl.BlockSpec(memory_space=pltpu.SMEM)] + [vm] * (n - 1) + [anyspec] * 3,
        out_specs=(anyspec, anyspec, anyspec),
        scratch_shapes=[pltpu.VMEM((micro, own, latent), BF16),
                        pltpu.VMEM((micro, own, latent), F32),
                        pltpu.VMEM((micro, own, latent), F32),
                        pltpu.SemaphoreType.DMA((3,))],
        input_output_aliases={n: 0, n + 1: 1, n + 2: 2},
        compiler_params=pltpu.CompilerParams(vmem_limit_bytes=48 * 1024 * 1024),
    )(*operands, *records)


def bwd_tick_kernel(parts, sections, tick, first, hs_ref, pin_ref, a_ref, u_ref, osndt_ref, orcvl_ref,
                    orcvt_ref, ws_ref, wr_ref, wm_ref, wn_ref, wa_ref, g_ref, *refs):
    send_pipe = tick > 0
    if not first:
        refs = refs[1:]
    if send_pipe:
        grec, pinn_ref, p32, hg, snbuf, spbuf, gbuf, pinbuf, send_sem, recv_sem, rec_sem = refs
    else:
        grec, p32, hg, snbuf, spbuf, gbuf, send_sem, recv_sem, rec_sem = refs
    micro, own, _ = pin_ref.shape
    block = snbuf.shape[1]
    d = lax.axis_index("dom")
    p = lax.axis_index("pipe")
    pipe_prev = (d, lax.rem(p - 1 + sections, sections))
    pipe_next = (d, lax.rem(p + 1, sections))
    dom_next = (lax.rem(d + 1, parts), p)
    dom_prev = (lax.rem(d - 1 + parts, parts), p)
    barrier = pltpu.get_barrier_semaphore()
    sources = [dom_next, dom_prev] + ([pipe_next] if send_pipe else [])
    for src in sources:
        pl.semaphore_signal(barrier, 1, device_id=src, device_id_type=MESH_ID)
    compute_refs = (pin_ref, a_ref, u_ref, osndt_ref, orcvl_ref, orcvt_ref,
                    ws_ref, wr_ref, wm_ref, wn_ref, wa_ref, g_ref, p32, hg)
    halo_copies = []
    for m in range(micro):
        bwd_micro(m, *compute_refs)
        if m == 0:
            pl.semaphore_wait(barrier, len(sources))
        pair = []
        for j, (lo, buf, dst) in enumerate(((0, snbuf, dom_prev), (block, spbuf, dom_next))):
            copy = pltpu.make_async_remote_copy(
                src_ref=hg.at[m, pl.ds(lo, block)], dst_ref=buf.at[m],
                send_sem=send_sem.at[j, m], recv_sem=recv_sem.at[j, m],
                device_id=dst, device_id_type=MESH_ID)
            copy.start()
            pair.append(copy)
        halo_copies.append(pair)
    hs0 = hs_ref[0]
    hs1 = hs_ref[1]
    pipe_copies = []
    for m in range(micro):
        for copy in halo_copies[m]:
            copy.wait_recv()
        sn = snbuf[m].astype(F32)
        sp = spbuf[m].astype(F32)
        for b in range(own // block):
            piece = p32[m, b * block:(b + 1) * block]
            piece = piece + jnp.where(hs0 == b, sn, 0.0) + jnp.where(hs1 == b, sp, 0.0)
            gbuf[m, b * block:(b + 1) * block] = piece.astype(gbuf.dtype)
        if send_pipe:
            copy = pltpu.make_async_remote_copy(
                src_ref=gbuf.at[m], dst_ref=pinbuf.at[m], send_sem=send_sem.at[2, m],
                recv_sem=recv_sem.at[2, m], device_id=pipe_prev, device_id_type=MESH_ID)
            copy.start()
            pipe_copies.append(copy)
    record_copies(((gbuf, grec),), rec_sem, None if first else p == tick)
    for pair in halo_copies:
        for copy in pair:
            copy.wait_send()
    for copy in pipe_copies:
        copy.wait()
    if send_pipe:
        pinn_ref[...] = pinbuf[...]


def bwd_tick(operands, grad_rec, tick, span, parts, sections):
    pin = operands[1]
    micro, own, latent = pin.shape
    send_pipe = tick > 0
    first = grad_rec is None
    vm = pl.BlockSpec(memory_space=pltpu.VMEM)
    anyspec = pl.BlockSpec(memory_space=pl.ANY)
    grad = jax.ShapeDtypeStruct((micro, own, latent), BF16)
    scratch = [pltpu.VMEM((micro, own, latent), F32), pltpu.VMEM((micro, 2 * span, latent), BF16),
               pltpu.VMEM((micro, span, latent), BF16), pltpu.VMEM((micro, span, latent), BF16),
               pltpu.VMEM((micro, own, latent), BF16)]
    if send_pipe:
        scratch.append(pltpu.VMEM((micro, own, latent), BF16))
    scratch += [pltpu.SemaphoreType.DMA((3, micro)), pltpu.SemaphoreType.DMA((3, micro)),
                pltpu.SemaphoreType.DMA((1,))]
    outs = (grad, grad) if send_pipe else (grad,)
    n = len(operands)
    extra = () if first else (grad_rec,)
    return pl.pallas_call(
        functools.partial(bwd_tick_kernel, parts, sections, tick, first),
        out_shape=outs,
        in_specs=[pl.BlockSpec(memory_space=pltpu.SMEM)] + [vm] * (n - 1) + [anyspec] * len(extra),
        out_specs=(anyspec,) + ((vm,) if send_pipe else ()),
        scratch_shapes=scratch,
        input_output_aliases={} if first else {n: 0},
        compiler_params=pltpu.CompilerParams(collective_id=20 + tick, has_side_effects=True,
                                             vmem_limit_bytes=48 * 1024 * 1024),
    )(*operands, *extra)


def vmem_call(kernel, out_shapes, n_in, smem_first=True):
    in_specs = [pl.BlockSpec(memory_space=pltpu.SMEM)] + [pl.BlockSpec(memory_space=pltpu.VMEM)] * (n_in - 1)
    return pl.pallas_call(
        kernel,
        out_shape=out_shapes,
        in_specs=in_specs,
        out_specs=tuple(pl.BlockSpec(memory_space=pltpu.VMEM) for _ in out_shapes),
        compiler_params=pltpu.CompilerParams(vmem_limit_bytes=48 * 1024 * 1024),
    )


def whole_kernel(parts, sections, hs_ref, cnt_ref, x_hbm, cot_hbm, esnd_ref, ercv_ref,
                 ws_hbm, wr_hbm, wm_hbm, wn_hbm, wa_hbm, g_ref,
                 out_ref, grad_ref,
                 xbuf, cotbuf, wbuf, osnd_ref, orcv_ref, orcvt_ref, osndt_ref, orcvl_ref,
                 hbuf, fpbuf, fnbuf, stage_n, stage_p, abuf, ubuf, cbuf, p32, hg, snbuf, spbuf,
                 unitbuf, rsbuf,
                 fsend, frecv, bsend, brecv, lsem):
    micro, own, latent = xbuf.shape
    block = fpbuf.shape[1]
    span = block
    loads = [pltpu.make_async_copy(x_hbm, xbuf, lsem.at[0])]
    for i, w in enumerate((ws_hbm, wr_hbm, wm_hbm, wn_hbm, wa_hbm)):
        loads.append(pltpu.make_async_copy(w, wbuf.at[i], lsem.at[1 + i]))
    loads.append(pltpu.make_async_copy(cot_hbm, cotbuf, lsem.at[6]))
    for copy in loads:
        copy.start()
    edges = osnd_ref.shape[0]
    ext_rows = osnd_ref.shape[1]
    own_rows = orcv_ref.shape[1]
    es = esnd_ref[...]
    er = ercv_ref[...]
    snd = jnp.concatenate([es[i:i + 1] for i in range(es.shape[0])], axis=1)
    rcv = jnp.concatenate([er[i:i + 1] for i in range(er.shape[0])], axis=1)
    lane = lax.broadcasted_iota(jnp.int32, (1, edges), 1)
    per_block = es.shape[1]
    live = lane < 0
    for i in range(es.shape[0]):
        live = live | ((lane >= i * per_block) & (lane < i * per_block + cnt_ref[i]))
    sndt = lax.broadcasted_iota(jnp.int32, (ext_rows, edges), 0) == snd
    rcvt = lax.broadcasted_iota(jnp.int32, (own_rows, edges), 0) == rcv
    osndt_f = sndt.astype(F32)
    rcvt_f = rcvt.astype(F32)
    rcvlt_f = (rcvt & live).astype(F32)
    osndt_ref[...] = osndt_f.astype(BF16)
    orcvt_ref[...] = rcvlt_f.astype(BF16)
    osnd_ref[...] = osndt_f.T.astype(BF16)
    orcv_ref[...] = rcvt_f.T.astype(BF16)
    orcvl_ref[...] = rcvlt_f.T.astype(BF16)
    d = lax.axis_index("dom")
    p = lax.axis_index("pipe")
    pipe_next = (d, lax.rem(p + 1, sections))
    pipe_prev = (d, lax.rem(p - 1 + sections, sections))
    dom_next = (lax.rem(d + 1, parts), p)
    dom_prev = (lax.rem(d - 1 + parts, parts), p)
    barrier = pltpu.get_barrier_semaphore()
    for nb in (pipe_prev, pipe_next, dom_prev, dom_next):
        pl.semaphore_signal(barrier, 1, device_id=nb, device_id_type=MESH_ID)
    pl.semaphore_wait(barrier, 4)
    hs0 = hs_ref[0]
    hs1 = hs_ref[1]
    has_prev = p > 0
    has_next = p < sections - 1
    gain = g_ref[...]
    ws, wr, wm, wn, wa = (wbuf.at[i] for i in range(5))

    def remote(src, dst, sems, idx, target):
        send_sem, recv_sem = sems
        return pltpu.make_async_remote_copy(
            src_ref=src, dst_ref=dst, send_sem=send_sem.at[idx], recv_sem=recv_sem.at[idx],
            device_id=target, device_id_type=MESH_ID)

    loads[0].wait()
    fwd_pipe = []
    fwd_halo = []
    for m in range(micro):
        pipe_in = remote(out_ref.at[m], hbuf.at[m], (fsend, frecv), m, pipe_next)
        pl.when(has_prev)(pipe_in.wait_recv)

        @pl.when(p == 0)
        def _():
            hbuf[m] = xbuf[m]

        h = hbuf[m]
        sel_n = h[0:block]
        sel_p = h[0:block]
        for b in range(1, own // block):
            piece = h[b * block:(b + 1) * block]
            sel_n = jnp.where(hs0 == b, piece, sel_n)
            sel_p = jnp.where(hs1 == b, piece, sel_p)
        stage_n[m] = sel_n
        stage_p[m] = sel_p
        pair = [remote(stage_n.at[m], fpbuf.at[m], (fsend, frecv), micro + 2 * m, dom_next),
                remote(stage_p.at[m], fnbuf.at[m], (fsend, frecv), micro + 2 * m + 1, dom_prev)]
        for copy in pair:
            copy.start()
        if m == 0:
            for copy in loads[1:6]:
                copy.wait()
        osnd = osnd_ref[...]
        own_gather = mm(osnd[:, :own], h)
        recv_rows = mm(orcv_ref[...], h).astype(BF16)
        recv_part = mm(recv_rows, wr[...])
        node_part = mm(h, wn[...])
        for copy in pair:
            copy.wait_recv()
        fwd_halo.extend(pair)
        gathered = (own_gather + mm(osnd[:, own:own + span], fpbuf[m])
                    + mm(osnd[:, own + span:], fnbuf[m])).astype(BF16)
        send_part = mm(gathered, ws[...]).astype(BF16).astype(F32)
        pre = send_part + recv_part
        sig_a = sigmoid(pre)
        edge_hidden = (pre * sig_a).astype(BF16)
        messages = mm(edge_hidden, wm[...])
        agg = split_sum(orcvt_ref[...], messages).astype(BF16)
        node_pre = node_part + mm(agg, wa[...])
        sig_u = sigmoid(node_pre)
        act = node_pre * sig_u
        mean = jnp.mean(act, axis=-1, keepdims=True)
        cen = act - mean
        var = jnp.mean(cen * cen, axis=-1, keepdims=True)
        rs = lax.rsqrt(var + EPSILON)
        unit = cen * rs
        out_ref[m] = (h.astype(F32) + unit * gain).astype(BF16)
        pl.when(has_next)(pipe_in.start)
        fwd_pipe.append(pipe_in)
        unitbuf[m] = unit
        rsbuf[m] = jnp.broadcast_to(rs, rsbuf.shape[1:])
        ubuf[m] = sig_u * (1.0 + node_pre * (1.0 - sig_u))
        abuf[m] = sig_a * (1.0 + pre * (1.0 - sig_a))

    loads[6].wait()
    bwd_pipe = []
    bwd_halo = []
    for m in range(micro):
        pipe_in = remote(grad_ref.at[m], cbuf.at[m], (bsend, brecv), m, pipe_prev)
        pl.when(has_next)(pipe_in.wait_recv)

        @pl.when(p == sections - 1)
        def _():
            cbuf[m] = cotbuf[m]

        c = cbuf[m].astype(F32)
        unit = unitbuf[m]
        rs = rsbuf[m][:, 0:1]
        gu = c * gain
        gact = rs * (gu - jnp.mean(gu, axis=-1, keepdims=True)
                     - unit * jnp.mean(gu * unit, axis=-1, keepdims=True))
        du = (gact * ubuf[m]).astype(BF16)
        dagg = mm_t(du, wa[...]).astype(BF16)
        gmsg = mm(orcvl_ref[...], dagg).astype(BF16)
        dedge = (mm_t(gmsg, wm[...]) * abuf[m]).astype(BF16)
        send_x = mm_t(dedge, ws[...])
        osndt = osndt_ref[...]
        hg[m] = split_sum(osndt[own:], send_x).astype(BF16)
        pair = [remote(hg.at[m, pl.ds(0, block)], snbuf.at[m], (bsend, brecv), micro + 2 * m, dom_prev),
                remote(hg.at[m, pl.ds(block, block)], spbuf.at[m], (bsend, brecv), micro + 2 * m + 1,
                       dom_next)]
        for copy in pair:
            copy.start()
        rows = c + mm_t(du, wn[...])
        rows = rows + split_sum(orcvt_ref[...], mm_t(dedge, wr[...]))
        p32[m] = rows + split_sum(osndt[:own], send_x)
        for copy in pair:
            copy.wait_recv()
        bwd_halo.extend(pair)
        sn = snbuf[m].astype(F32)
        sp = spbuf[m].astype(F32)
        for b in range(own // block):
            piece = p32[m, b * block:(b + 1) * block]
            piece = piece + jnp.where(hs0 == b, sn, 0.0) + jnp.where(hs1 == b, sp, 0.0)
            grad_ref[m, b * block:(b + 1) * block] = piece.astype(grad_ref.dtype)
        pl.when(has_prev)(pipe_in.start)
        bwd_pipe.append(pipe_in)

    for copy in fwd_pipe:
        pl.when(has_next)(copy.wait_send)
    for copy in bwd_pipe:
        pl.when(has_prev)(copy.wait_send)
    for copy in fwd_halo + bwd_halo:
        copy.wait_send()


def whole(operands, span, parts, sections):
    x = operands[2]
    micro, own, latent = x.shape
    vm = pl.BlockSpec(memory_space=pltpu.VMEM)
    anyspec = pl.BlockSpec(memory_space=pltpu.HBM)
    bf = lambda rows: pltpu.VMEM((micro, rows, latent), BF16)
    f32 = pltpu.VMEM((micro, own, latent), F32)
    smem = pl.BlockSpec(memory_space=pltpu.SMEM)
    in_specs = [smem, smem, anyspec, anyspec, vm, vm] + [anyspec] * 5 + [vm]
    edges = operands[4].size
    ext_rows = own + 2 * span
    return pl.pallas_call(
        functools.partial(whole_kernel, parts, sections),
        out_shape=(jax.ShapeDtypeStruct((micro, own, latent), BF16),
                   jax.ShapeDtypeStruct((micro, own, latent), BF16)),
        in_specs=in_specs,
        out_specs=(vm, vm),
        scratch_shapes=[bf(own), bf(own), pltpu.VMEM((5, latent, latent), BF16),
                        pltpu.VMEM((edges, ext_rows), BF16), pltpu.VMEM((edges, own), BF16),
                        pltpu.VMEM((own, edges), BF16), pltpu.VMEM((ext_rows, edges), BF16),
                        pltpu.VMEM((edges, own), BF16),
                        bf(own), bf(span), bf(span), bf(span), bf(span), f32, f32, bf(own), f32,
                        bf(2 * span), bf(span), bf(span), f32, pltpu.VMEM((micro, own, 128), F32),
                        pltpu.SemaphoreType.DMA((3 * micro,)), pltpu.SemaphoreType.DMA((3 * micro,)),
                        pltpu.SemaphoreType.DMA((3 * micro,)), pltpu.SemaphoreType.DMA((3 * micro,)),
                        pltpu.SemaphoreType.DMA((7,))],
        compiler_params=pltpu.CompilerParams(collective_id=0, has_side_effects=True,
                                             vmem_limit_bytes=67043328),
    )(*operands)


def shards(inputs, cotangent, w_send, w_recv, w_message, w_node, w_aggregate, gains,
           edge_send, edge_recv, edge_count, halo_send):
    sections = lax.axis_size("pipe")
    parts = lax.axis_size("dom")
    p_idx = lax.axis_index("pipe")
    micro, own, latent = inputs.shape
    block = edge_send.shape[1]
    span = halo_send.shape[2] * block
    ext_rows = own + 2 * span
    weights = (w_send[0], w_recv[0], w_message[0], w_node[0], w_aggregate[0])
    gain = gains[0].reshape(1, latent)
    hs = halo_send[0].reshape(-1).astype(jnp.int32)

    def blocks_of(x):
        shaped = x.reshape(micro, own // block, block, latent)
        nxt = jnp.take(shaped, hs[0], axis=1)
        prv = jnp.take(shaped, hs[1], axis=1)
        return nxt, prv

    S, D = sections, parts

    def perm_pipe(shift):
        return [(i, (i + shift) % S) for i in range(S)]

    def perm_both(dshift, pshift):
        return [(d * S + p, ((d + dshift) % D) * S + (p + pshift) % S)
                for d in range(D) for p in range(S)]

    both = ("dom", "pipe")

    fwd = vmem_call(
        fwd_kernel,
        (jax.ShapeDtypeStruct((micro, own, latent), BF16),
         jax.ShapeDtypeStruct((micro, own, latent), F32),
         jax.ShapeDtypeStruct((micro, own, latent), F32)),
        13)

    out_rec, grad_rec = whole(
        (hs, edge_count.astype(jnp.int32), inputs, cotangent, edge_send.astype(jnp.int32),
         edge_recv.astype(jnp.int32), *weights, gain), span, D, S)
    return (out_rec[None], grad_rec[None])


def solution(mesh):
    in_specs = (
        P(None, "dom", None),
        P(None, "dom", None),
        P("pipe", None, None),
        P("pipe", None, None),
        P("pipe", None, None),
        P("pipe", None, None),
        P("pipe", None, None),
        P("pipe", None),
        P("dom", None),
        P("dom", None),
        P("dom"),
        P("dom", None, None),
    )
    out_specs = (P("pipe", None, "dom", None), P("pipe", None, "dom", None))
    return jax.shard_map(shards, mesh=mesh, in_specs=in_specs, out_specs=out_specs, check_vma=False)
```

```python
import functools

import jax
import jax.numpy as jnp
from jax import lax
from jax.experimental import pallas as pl
from jax.experimental.pallas import tpu as pltpu
from jax.sharding import PartitionSpec as P

EPSILON = 1e-05
F32 = jnp.float32
BF16 = jnp.bfloat16


def mm(x, w):
    return jnp.dot(x, w, preferred_element_type=F32)


def mm_t(x, w):
    return lax.dot_general(x, w, (((1,), (1,)), ((), ())), preferred_element_type=F32)


def sigmoid(v):
    return 1.0 / (1.0 + jnp.exp(-v))


def split_sum(onehot, values):
    hi = values.astype(BF16)
    lo = (values - hi.astype(F32)).astype(BF16)
    return mm(onehot, hi) + mm(onehot, lo)


def fwd_micro(m, hs_ref, h_ref, fp_ref, fn_ref, osnd_ref, orcv_ref, orcvt_ref,
              ws_ref, wr_ref, wm_ref, wn_ref, wa_ref, g_ref, out_ref, a_ref, u_ref):
    own = h_ref.shape[1]
    span = fp_ref.shape[1]
    osnd = osnd_ref[...]
    h = h_ref[m]
    gathered = (mm(osnd[:, :own], h) + mm(osnd[:, own:own + span], fp_ref[m])
                + mm(osnd[:, own + span:], fn_ref[m])).astype(BF16)
    send_part = mm(gathered, ws_ref[...]).astype(BF16).astype(F32)
    recv_rows = mm(orcv_ref[...], h).astype(BF16)
    pre = send_part + mm(recv_rows, wr_ref[...])
    a_ref[m] = pre
    edge_hidden = (pre * sigmoid(pre)).astype(BF16)
    messages = mm(edge_hidden, wm_ref[...])
    agg = split_sum(orcvt_ref[...], messages).astype(BF16)
    node_pre = mm(h, wn_ref[...]) + mm(agg, wa_ref[...])
    u_ref[m] = node_pre
    act = node_pre * sigmoid(node_pre)
    mean = jnp.mean(act, axis=-1, keepdims=True)
    cen = act - mean
    var = jnp.mean(cen * cen, axis=-1, keepdims=True)
    unit = cen * lax.rsqrt(var + EPSILON)
    out_ref[m] = (h.astype(F32) + unit * g_ref[...]).astype(BF16)


def fwd_kernel(*refs):
    for m in range(refs[1].shape[0]):
        fwd_micro(m, *refs)


def bwd_micro(m, pin_ref, a_ref, u_ref, osndt_ref, orcvl_ref, orcvt_ref,
              ws_ref, wr_ref, wm_ref, wn_ref, wa_ref, g_ref, p32_ref, hg_ref):
    own = pin_ref.shape[1]
    gain = g_ref[...]
    c = pin_ref[m].astype(F32)
    node_pre = u_ref[m]
    sig_u = sigmoid(node_pre)
    act = node_pre * sig_u
    mean = jnp.mean(act, axis=-1, keepdims=True)
    cen = act - mean
    var = jnp.mean(cen * cen, axis=-1, keepdims=True)
    rs = lax.rsqrt(var + EPSILON)
    unit = cen * rs
    gu = c * gain
    gact = rs * (gu - jnp.mean(gu, axis=-1, keepdims=True)
                 - unit * jnp.mean(gu * unit, axis=-1, keepdims=True))
    du = (gact * (sig_u * (1.0 + node_pre * (1.0 - sig_u)))).astype(BF16)
    dagg = mm_t(du, wa_ref[...]).astype(BF16)
    rows = c + mm_t(du, wn_ref[...])
    gmsg = mm(orcvl_ref[...], dagg).astype(BF16)
    pre = a_ref[m]
    sig_a = sigmoid(pre)
    dedge = (mm_t(gmsg, wm_ref[...]) * (sig_a * (1.0 + pre * (1.0 - sig_a)))).astype(BF16)
    rows = rows + split_sum(orcvt_ref[...], mm_t(dedge, wr_ref[...]))
    send_rows = split_sum(osndt_ref[...], mm_t(dedge, ws_ref[...]))
    p32_ref[m] = rows + send_rows[:own]
    hg_ref[m] = send_rows[own:].astype(BF16)


MESH_ID = pl.DeviceIdType.MESH


def comm_kernel(sends, n_in, parts, sections, *refs):
    ins = refs[:n_in]
    outs = refs[n_in:n_in + len(sends)]
    send_sem, recv_sem = refs[n_in + len(sends):]
    d = lax.axis_index("dom")
    p = lax.axis_index("pipe")
    barrier = pltpu.get_barrier_semaphore()
    for _, _, _, dd, dp in sends:
        src = (lax.rem(d - dd + parts, parts), lax.rem(p - dp + sections, sections))
        pl.semaphore_signal(barrier, 1, device_id=src, device_id_type=MESH_ID)
    pl.semaphore_wait(barrier, len(sends))
    copies = []
    for i, (k, start, rows, dd, dp) in enumerate(sends):
        dst = (lax.rem(d + dd + parts, parts), lax.rem(p + dp + sections, sections))
        source = ins[k] if start is None else ins[k].at[:, pl.ds(start, rows)]
        copy = pltpu.make_async_remote_copy(
            src_ref=source, dst_ref=outs[i], send_sem=send_sem.at[i], recv_sem=recv_sem.at[i],
            device_id=dst, device_id_type=MESH_ID)
        copy.start()
        copies.append(copy)
    for copy in copies:
        copy.wait()


def exchange(sends, payloads, parts, sections, cid):
    out_shapes = []
    for k, start, rows, _, _ in sends:
        shape = payloads[k].shape
        if start is not None:
            shape = (shape[0], rows) + shape[2:]
        out_shapes.append(jax.ShapeDtypeStruct(shape, payloads[k].dtype))
    n = len(sends)
    return pl.pallas_call(
        functools.partial(comm_kernel, tuple(sends), len(payloads), parts, sections),
        out_shape=tuple(out_shapes),
        in_specs=[pl.BlockSpec(memory_space=pl.ANY)] * len(payloads),
        out_specs=tuple(pl.BlockSpec(memory_space=pl.ANY) for _ in sends),
        scratch_shapes=[pltpu.SemaphoreType.DMA((n,)), pltpu.SemaphoreType.DMA((n,))],
        compiler_params=pltpu.CompilerParams(collective_id=cid, has_side_effects=True),
    )(*payloads)


def record_copies(pairs, sem, active):
    def run():
        copies = [pltpu.make_async_copy(buf, rec, sem.at[i]) for i, (buf, rec) in enumerate(pairs)]
        for copy in copies:
            copy.start()
        for copy in copies:
            copy.wait()
    if active is None:
        run()
    else:
        pl.when(active)(run)


def fwd_tick_kernel(parts, sections, tick, hs_ref, h_ref, fp_ref, fn_ref, osnd_ref, orcv_ref, orcvt_ref,
                    ws_ref, wr_ref, wm_ref, wn_ref, wa_ref, g_ref, *refs):
    if tick > 0:
        refs = refs[3:]
    (orec, arec, urec, hn_ref, fpn_ref, fnn_ref, obuf, abuf, ubuf,
     hbuf, fpbuf, fnbuf, stage_n, stage_p, send_sem, recv_sem, rec_sem) = refs
    micro, own, _ = h_ref.shape
    block = fp_ref.shape[1]
    d = lax.axis_index("dom")
    p = lax.axis_index("pipe")
    pipe_next = (d, lax.rem(p + 1, sections))
    pipe_prev = (d, lax.rem(p - 1 + sections, sections))
    dom_next = (lax.rem(d + 1, parts), p)
    dom_prev = (lax.rem(d - 1 + parts, parts), p)
    barrier = pltpu.get_barrier_semaphore()
    for src in (pipe_prev, dom_prev, dom_next):
        pl.semaphore_signal(barrier, 1, device_id=src, device_id_type=MESH_ID)
    compute_refs = (hs_ref, h_ref, fp_ref, fn_ref, osnd_ref, orcv_ref, orcvt_ref,
                    ws_ref, wr_ref, wm_ref, wn_ref, wa_ref, g_ref, obuf, abuf, ubuf)
    pipe_copies = []
    for m in range(micro):
        fwd_micro(m, *compute_refs)
        if m == 0:
            pl.semaphore_wait(barrier, 3)
        copy = pltpu.make_async_remote_copy(
            src_ref=obuf.at[m], dst_ref=hbuf.at[m], send_sem=send_sem.at[0, m],
            recv_sem=recv_sem.at[0, m], device_id=pipe_next, device_id_type=MESH_ID)
        copy.start()
        pipe_copies.append(copy)
    record_copies(((obuf, orec), (abuf, arec), (ubuf, urec)), rec_sem,
                  None if tick == 0 else p == tick)
    hs0 = hs_ref[0]
    hs1 = hs_ref[1]
    halo_copies = []
    for m in range(micro):
        pipe_copies[m].wait_recv()
        h = hbuf[m]
        sel_n = h[0:block]
        sel_p = h[0:block]
        for b in range(1, own // block):
            piece = h[b * block:(b + 1) * block]
            sel_n = jnp.where(hs0 == b, piece, sel_n)
            sel_p = jnp.where(hs1 == b, piece, sel_p)
        stage_n[m] = sel_n
        stage_p[m] = sel_p
        for j, (stage, buf, dst) in enumerate(((stage_n, fpbuf, dom_next), (stage_p, fnbuf, dom_prev))):
            copy = pltpu.make_async_remote_copy(
                src_ref=stage.at[m], dst_ref=buf.at[m], send_sem=send_sem.at[1 + j, m],
                recv_sem=recv_sem.at[1 + j, m], device_id=dst, device_id_type=MESH_ID)
            copy.start()
            halo_copies.append(copy)
    for copy in pipe_copies:
        copy.wait_send()
    for copy in halo_copies:
        copy.wait()
    hn_ref[...] = hbuf[...]
    fpn_ref[...] = fpbuf[...]
    fnn_ref[...] = fnbuf[...]


def fwd_tick(operands, records, tick, span, parts, sections):
    h = operands[1]
    micro, own, latent = h.shape
    vm = pl.BlockSpec(memory_space=pltpu.VMEM)
    anyspec = pl.BlockSpec(memory_space=pl.ANY)
    bf = lambda rows: jax.ShapeDtypeStruct((micro, rows, latent), BF16)
    f32 = jax.ShapeDtypeStruct((micro, own, latent), F32)
    n = len(operands)
    extra = () if tick == 0 else tuple(records)
    return pl.pallas_call(
        functools.partial(fwd_tick_kernel, parts, sections, tick),
        out_shape=(bf(own), f32, f32, bf(own), bf(span), bf(span)),
        in_specs=[pl.BlockSpec(memory_space=pltpu.SMEM)] + [vm] * (n - 1) + [anyspec] * len(extra),
        out_specs=(anyspec, anyspec, anyspec, vm, vm, vm),
        scratch_shapes=[pltpu.VMEM((micro, own, latent), BF16),
                        pltpu.VMEM((micro, own, latent), F32),
                        pltpu.VMEM((micro, own, latent), F32),
                        pltpu.VMEM((micro, own, latent), BF16),
                        pltpu.VMEM((micro, span, latent), BF16),
                        pltpu.VMEM((micro, span, latent), BF16),
                        pltpu.VMEM((micro, span, latent), BF16),
                        pltpu.VMEM((micro, span, latent), BF16),
                        pltpu.SemaphoreType.DMA((3, micro)),
                        pltpu.SemaphoreType.DMA((3, micro)),
                        pltpu.SemaphoreType.DMA((3,))],
        input_output_aliases={} if tick == 0 else {n: 0, n + 1: 1, n + 2: 2},
        compiler_params=pltpu.CompilerParams(collective_id=10 + tick,
                                             has_side_effects=True,
                                             vmem_limit_bytes=48 * 1024 * 1024),
    )(*operands, *extra)


def fwd_last_kernel(tick, hs_ref, h_ref, fp_ref, fn_ref, osnd_ref, orcv_ref, orcvt_ref,
                    ws_ref, wr_ref, wm_ref, wn_ref, wa_ref, g_ref, orec_in, arec_in, urec_in,
                    orec, arec, urec, obuf, abuf, ubuf, rec_sem):
    compute_refs = (hs_ref, h_ref, fp_ref, fn_ref, osnd_ref, orcv_ref, orcvt_ref,
                    ws_ref, wr_ref, wm_ref, wn_ref, wa_ref, g_ref, obuf, abuf, ubuf)
    for m in range(h_ref.shape[0]):
        fwd_micro(m, *compute_refs)
    record_copies(((obuf, orec), (abuf, arec), (ubuf, urec)), rec_sem,
                  lax.axis_index("pipe") == tick)


def fwd_last(operands, records, tick):
    h = operands[1]
    micro, own, latent = h.shape
    vm = pl.BlockSpec(memory_space=pltpu.VMEM)
    anyspec = pl.BlockSpec(memory_space=pl.ANY)
    n = len(operands)
    return pl.pallas_call(
        functools.partial(fwd_last_kernel, tick),
        out_shape=tuple(jax.ShapeDtypeStruct(r.shape, r.dtype) for r in records),
        in_specs=[pl.BlockSpec(memory_space=pltpu.SMEM)] + [vm] * (n - 1) + [anyspec] * 3,
        out_specs=(anyspec, anyspec, anyspec),
        scratch_shapes=[pltpu.VMEM((micro, own, latent), BF16),
                        pltpu.VMEM((micro, own, latent), F32),
                        pltpu.VMEM((micro, own, latent), F32),
                        pltpu.SemaphoreType.DMA((3,))],
        input_output_aliases={n: 0, n + 1: 1, n + 2: 2},
        compiler_params=pltpu.CompilerParams(vmem_limit_bytes=48 * 1024 * 1024),
    )(*operands, *records)


def bwd_tick_kernel(parts, sections, tick, first, hs_ref, pin_ref, a_ref, u_ref, osndt_ref, orcvl_ref,
                    orcvt_ref, ws_ref, wr_ref, wm_ref, wn_ref, wa_ref, g_ref, *refs):
    send_pipe = tick > 0
    if not first:
        refs = refs[1:]
    if send_pipe:
        grec, pinn_ref, p32, hg, snbuf, spbuf, gbuf, pinbuf, send_sem, recv_sem, rec_sem = refs
    else:
        grec, p32, hg, snbuf, spbuf, gbuf, send_sem, recv_sem, rec_sem = refs
    micro, own, _ = pin_ref.shape
    block = snbuf.shape[1]
    d = lax.axis_index("dom")
    p = lax.axis_index("pipe")
    pipe_prev = (d, lax.rem(p - 1 + sections, sections))
    pipe_next = (d, lax.rem(p + 1, sections))
    dom_next = (lax.rem(d + 1, parts), p)
    dom_prev = (lax.rem(d - 1 + parts, parts), p)
    barrier = pltpu.get_barrier_semaphore()
    sources = [dom_next, dom_prev] + ([pipe_next] if send_pipe else [])
    for src in sources:
        pl.semaphore_signal(barrier, 1, device_id=src, device_id_type=MESH_ID)
    compute_refs = (pin_ref, a_ref, u_ref, osndt_ref, orcvl_ref, orcvt_ref,
                    ws_ref, wr_ref, wm_ref, wn_ref, wa_ref, g_ref, p32, hg)
    halo_copies = []
    for m in range(micro):
        bwd_micro(m, *compute_refs)
        if m == 0:
            pl.semaphore_wait(barrier, len(sources))
        pair = []
        for j, (lo, buf, dst) in enumerate(((0, snbuf, dom_prev), (block, spbuf, dom_next))):
            copy = pltpu.make_async_remote_copy(
                src_ref=hg.at[m, pl.ds(lo, block)], dst_ref=buf.at[m],
                send_sem=send_sem.at[j, m], recv_sem=recv_sem.at[j, m],
                device_id=dst, device_id_type=MESH_ID)
            copy.start()
            pair.append(copy)
        halo_copies.append(pair)
    hs0 = hs_ref[0]
    hs1 = hs_ref[1]
    pipe_copies = []
    for m in range(micro):
        for copy in halo_copies[m]:
            copy.wait_recv()
        sn = snbuf[m].astype(F32)
        sp = spbuf[m].astype(F32)
        for b in range(own // block):
            piece = p32[m, b * block:(b + 1) * block]
            piece = piece + jnp.where(hs0 == b, sn, 0.0) + jnp.where(hs1 == b, sp, 0.0)
            gbuf[m, b * block:(b + 1) * block] = piece.astype(gbuf.dtype)
        if send_pipe:
            copy = pltpu.make_async_remote_copy(
                src_ref=gbuf.at[m], dst_ref=pinbuf.at[m], send_sem=send_sem.at[2, m],
                recv_sem=recv_sem.at[2, m], device_id=pipe_prev, device_id_type=MESH_ID)
            copy.start()
            pipe_copies.append(copy)
    record_copies(((gbuf, grec),), rec_sem, None if first else p == tick)
    for pair in halo_copies:
        for copy in pair:
            copy.wait_send()
    for copy in pipe_copies:
        copy.wait()
    if send_pipe:
        pinn_ref[...] = pinbuf[...]


def bwd_tick(operands, grad_rec, tick, span, parts, sections):
    pin = operands[1]
    micro, own, latent = pin.shape
    send_pipe = tick > 0
    first = grad_rec is None
    vm = pl.BlockSpec(memory_space=pltpu.VMEM)
    anyspec = pl.BlockSpec(memory_space=pl.ANY)
    grad = jax.ShapeDtypeStruct((micro, own, latent), BF16)
    scratch = [pltpu.VMEM((micro, own, latent), F32), pltpu.VMEM((micro, 2 * span, latent), BF16),
               pltpu.VMEM((micro, span, latent), BF16), pltpu.VMEM((micro, span, latent), BF16),
               pltpu.VMEM((micro, own, latent), BF16)]
    if send_pipe:
        scratch.append(pltpu.VMEM((micro, own, latent), BF16))
    scratch += [pltpu.SemaphoreType.DMA((3, micro)), pltpu.SemaphoreType.DMA((3, micro)),
                pltpu.SemaphoreType.DMA((1,))]
    outs = (grad, grad) if send_pipe else (grad,)
    n = len(operands)
    extra = () if first else (grad_rec,)
    return pl.pallas_call(
        functools.partial(bwd_tick_kernel, parts, sections, tick, first),
        out_shape=outs,
        in_specs=[pl.BlockSpec(memory_space=pltpu.SMEM)] + [vm] * (n - 1) + [anyspec] * len(extra),
        out_specs=(anyspec,) + ((vm,) if send_pipe else ()),
        scratch_shapes=scratch,
        input_output_aliases={} if first else {n: 0},
        compiler_params=pltpu.CompilerParams(collective_id=20 + tick, has_side_effects=True,
                                             vmem_limit_bytes=48 * 1024 * 1024),
    )(*operands, *extra)


def vmem_call(kernel, out_shapes, n_in, smem_first=True):
    in_specs = [pl.BlockSpec(memory_space=pltpu.SMEM)] + [pl.BlockSpec(memory_space=pltpu.VMEM)] * (n_in - 1)
    return pl.pallas_call(
        kernel,
        out_shape=out_shapes,
        in_specs=in_specs,
        out_specs=tuple(pl.BlockSpec(memory_space=pltpu.VMEM) for _ in out_shapes),
        compiler_params=pltpu.CompilerParams(vmem_limit_bytes=48 * 1024 * 1024),
    )


def whole_kernel(parts, sections, hs_ref, cnt_ref, x_hbm, cot_hbm, esnd_ref, ercv_ref,
                 ws_hbm, wr_hbm, wm_hbm, wn_hbm, wa_hbm, g_ref,
                 out_ref, grad_ref,
                 xbuf, cotbuf, wbuf, osnd_ref, orcv_ref, orcvt_ref, osndt_ref, orcvl_ref,
                 hbuf, fpbuf, fnbuf, stage_n, stage_p, abuf, ubuf, cbuf, p32, hg, snbuf, spbuf,
                 unitbuf, rsbuf,
                 fsend, frecv, bsend, brecv, lsem):
    micro, own, latent = xbuf.shape
    block = fpbuf.shape[1]
    span = block
    loads = [pltpu.make_async_copy(x_hbm, xbuf, lsem.at[0])]
    for i, w in enumerate((ws_hbm, wr_hbm, wm_hbm, wn_hbm, wa_hbm)):
        loads.append(pltpu.make_async_copy(w, wbuf.at[i], lsem.at[1 + i]))
    loads.append(pltpu.make_async_copy(cot_hbm, cotbuf, lsem.at[6]))
    for copy in loads:
        copy.start()
    d = lax.axis_index("dom")
    p = lax.axis_index("pipe")
    pipe_next = (d, lax.rem(p + 1, sections))
    pipe_prev = (d, lax.rem(p - 1 + sections, sections))
    dom_next = (lax.rem(d + 1, parts), p)
    dom_prev = (lax.rem(d - 1 + parts, parts), p)
    barrier = pltpu.get_barrier_semaphore()
    for nb in (pipe_prev, pipe_next, dom_prev, dom_next):
        pl.semaphore_signal(barrier, 1, device_id=nb, device_id_type=MESH_ID)
    pl.semaphore_wait(barrier, 4)
    hs0 = hs_ref[0]
    hs1 = hs_ref[1]
    has_prev = p > 0
    has_next = p < sections - 1
    gain = g_ref[...]
    ws, wr, wm, wn, wa = (wbuf.at[i] for i in range(5))

    def remote(src, dst, sems, idx, target):
        send_sem, recv_sem = sems
        return pltpu.make_async_remote_copy(
            src_ref=src, dst_ref=dst, send_sem=send_sem.at[idx], recv_sem=recv_sem.at[idx],
            device_id=target, device_id_type=MESH_ID)

    def build_onehots():
        edges = osnd_ref.shape[0]
        ext_rows = osnd_ref.shape[1]
        own_rows = orcv_ref.shape[1]
        es = esnd_ref[...]
        er = ercv_ref[...]
        snd = jnp.concatenate([es[i:i + 1] for i in range(es.shape[0])], axis=1)
        rcv = jnp.concatenate([er[i:i + 1] for i in range(er.shape[0])], axis=1)
        lane = lax.broadcasted_iota(jnp.int32, (1, edges), 1)
        per_block = es.shape[1]
        live = lane < 0
        for i in range(es.shape[0]):
            live = live | ((lane >= i * per_block) & (lane < i * per_block + cnt_ref[i]))
        sndt = lax.broadcasted_iota(jnp.int32, (ext_rows, edges), 0) == snd
        rcvt = lax.broadcasted_iota(jnp.int32, (own_rows, edges), 0) == rcv
        osndt_f = sndt.astype(F32)
        rcvt_f = rcvt.astype(F32)
        rcvlt_f = (rcvt & live).astype(F32)
        osndt_ref[...] = osndt_f.astype(BF16)
        orcvt_ref[...] = rcvlt_f.astype(BF16)
        osnd_ref[...] = osndt_f.T.astype(BF16)
        orcv_ref[...] = rcvt_f.T.astype(BF16)
        orcvl_ref[...] = rcvlt_f.T.astype(BF16)

    loads[0].wait()
    fwd_pipe = []
    fwd_halo = []
    for m in range(micro):
        pipe_in = remote(out_ref.at[m], hbuf.at[m], (fsend, frecv), m, pipe_next)
        pl.when(has_prev)(pipe_in.wait_recv)

        @pl.when(p == 0)
        def _():
            hbuf[m] = xbuf[m]

        h = hbuf[m]
        sel_n = h[0:block]
        sel_p = h[0:block]
        for b in range(1, own // block):
            piece = h[b * block:(b + 1) * block]
            sel_n = jnp.where(hs0 == b, piece, sel_n)
            sel_p = jnp.where(hs1 == b, piece, sel_p)
        stage_n[m] = sel_n
        stage_p[m] = sel_p
        pair = [remote(stage_n.at[m], fpbuf.at[m], (fsend, frecv), micro + 2 * m, dom_next),
                remote(stage_p.at[m], fnbuf.at[m], (fsend, frecv), micro + 2 * m + 1, dom_prev)]
        for copy in pair:
            copy.start()
        if m == 0:
            build_onehots()
            for copy in loads[1:6]:
                copy.wait()
        osnd = osnd_ref[...]
        own_gather = mm(osnd[:, :own], h)
        recv_rows = mm(orcv_ref[...], h).astype(BF16)
        recv_part = mm(recv_rows, wr[...])
        node_part = mm(h, wn[...])
        for copy in pair:
            copy.wait_recv()
        fwd_halo.extend(pair)
        gathered = (own_gather + mm(osnd[:, own:own + span], fpbuf[m])
                    + mm(osnd[:, own + span:], fnbuf[m])).astype(BF16)
        send_part = mm(gathered, ws[...]).astype(BF16).astype(F32)
        pre = send_part + recv_part
        sig_a = sigmoid(pre)
        edge_hidden = (pre * sig_a).astype(BF16)
        messages = mm(edge_hidden, wm[...])
        agg = split_sum(orcvt_ref[...], messages).astype(BF16)
        node_pre = node_part + mm(agg, wa[...])
        sig_u = sigmoid(node_pre)
        act = node_pre * sig_u
        mean = jnp.mean(act, axis=-1, keepdims=True)
        cen = act - mean
        var = jnp.mean(cen * cen, axis=-1, keepdims=True)
        rs = lax.rsqrt(var + EPSILON)
        unit = cen * rs
        out_ref[m] = (h.astype(F32) + unit * gain).astype(BF16)
        pl.when(has_next)(pipe_in.start)
        fwd_pipe.append(pipe_in)
        unitbuf[m] = unit
        rsbuf[m] = jnp.broadcast_to(rs, rsbuf.shape[1:])
        ubuf[m] = sig_u * (1.0 + node_pre * (1.0 - sig_u))
        abuf[m] = sig_a * (1.0 + pre * (1.0 - sig_a))

    loads[6].wait()
    bwd_pipe = []
    bwd_halo = []
    for m in range(micro):
        pipe_in = remote(grad_ref.at[m], cbuf.at[m], (bsend, brecv), m, pipe_prev)
        pl.when(has_next)(pipe_in.wait_recv)

        @pl.when(p == sections - 1)
        def _():
            cbuf[m] = cotbuf[m]

        c = cbuf[m].astype(F32)
        unit = unitbuf[m]
        rs = rsbuf[m][:, 0:1]
        gu = c * gain
        gact = rs * (gu - jnp.mean(gu, axis=-1, keepdims=True)
                     - unit * jnp.mean(gu * unit, axis=-1, keepdims=True))
        du = (gact * ubuf[m]).astype(BF16)
        dagg = mm_t(du, wa[...]).astype(BF16)
        gmsg = mm(orcvl_ref[...], dagg).astype(BF16)
        dedge = (mm_t(gmsg, wm[...]) * abuf[m]).astype(BF16)
        send_x = mm_t(dedge, ws[...])
        osndt = osndt_ref[...]
        hg[m] = split_sum(osndt[own:], send_x).astype(BF16)
        pair = [remote(hg.at[m, pl.ds(0, block)], snbuf.at[m], (bsend, brecv), micro + 2 * m, dom_prev),
                remote(hg.at[m, pl.ds(block, block)], spbuf.at[m], (bsend, brecv), micro + 2 * m + 1,
                       dom_next)]
        for copy in pair:
            copy.start()
        rows = c + mm_t(du, wn[...])
        rows = rows + split_sum(orcvt_ref[...], mm_t(dedge, wr[...]))
        p32[m] = rows + split_sum(osndt[:own], send_x)
        for copy in pair:
            copy.wait_recv()
        bwd_halo.extend(pair)
        sn = snbuf[m].astype(F32)
        sp = spbuf[m].astype(F32)
        for b in range(own // block):
            piece = p32[m, b * block:(b + 1) * block]
            piece = piece + jnp.where(hs0 == b, sn, 0.0) + jnp.where(hs1 == b, sp, 0.0)
            grad_ref[m, b * block:(b + 1) * block] = piece.astype(grad_ref.dtype)
        pl.when(has_prev)(pipe_in.start)
        bwd_pipe.append(pipe_in)

    for copy in fwd_pipe:
        pl.when(has_next)(copy.wait_send)
    for copy in bwd_pipe:
        pl.when(has_prev)(copy.wait_send)
    for copy in fwd_halo + bwd_halo:
        copy.wait_send()


def whole(operands, span, parts, sections):
    x = operands[2]
    micro, own, latent = x.shape
    vm = pl.BlockSpec(memory_space=pltpu.VMEM)
    anyspec = pl.BlockSpec(memory_space=pltpu.HBM)
    bf = lambda rows: pltpu.VMEM((micro, rows, latent), BF16)
    f32 = pltpu.VMEM((micro, own, latent), F32)
    smem = pl.BlockSpec(memory_space=pltpu.SMEM)
    in_specs = [smem, smem, anyspec, anyspec, vm, vm] + [anyspec] * 5 + [vm]
    edges = operands[4].size
    ext_rows = own + 2 * span
    return pl.pallas_call(
        functools.partial(whole_kernel, parts, sections),
        out_shape=(jax.ShapeDtypeStruct((micro, own, latent), BF16),
                   jax.ShapeDtypeStruct((micro, own, latent), BF16)),
        in_specs=in_specs,
        out_specs=(vm, vm),
        scratch_shapes=[bf(own), bf(own), pltpu.VMEM((5, latent, latent), BF16),
                        pltpu.VMEM((edges, ext_rows), BF16), pltpu.VMEM((edges, own), BF16),
                        pltpu.VMEM((own, edges), BF16), pltpu.VMEM((ext_rows, edges), BF16),
                        pltpu.VMEM((edges, own), BF16),
                        bf(own), bf(span), bf(span), bf(span), bf(span), f32, f32, bf(own), f32,
                        bf(2 * span), bf(span), bf(span), f32, pltpu.VMEM((micro, own, 128), F32),
                        pltpu.SemaphoreType.DMA((3 * micro,)), pltpu.SemaphoreType.DMA((3 * micro,)),
                        pltpu.SemaphoreType.DMA((3 * micro,)), pltpu.SemaphoreType.DMA((3 * micro,)),
                        pltpu.SemaphoreType.DMA((7,))],
        compiler_params=pltpu.CompilerParams(collective_id=0, has_side_effects=True,
                                             vmem_limit_bytes=67043328),
    )(*operands)


def shards(inputs, cotangent, w_send, w_recv, w_message, w_node, w_aggregate, gains,
           edge_send, edge_recv, edge_count, halo_send):
    sections = lax.axis_size("pipe")
    parts = lax.axis_size("dom")
    p_idx = lax.axis_index("pipe")
    micro, own, latent = inputs.shape
    block = edge_send.shape[1]
    span = halo_send.shape[2] * block
    ext_rows = own + 2 * span
    weights = (w_send[0], w_recv[0], w_message[0], w_node[0], w_aggregate[0])
    gain = gains[0].reshape(1, latent)
    hs = halo_send[0].reshape(-1).astype(jnp.int32)

    def blocks_of(x):
        shaped = x.reshape(micro, own // block, block, latent)
        nxt = jnp.take(shaped, hs[0], axis=1)
        prv = jnp.take(shaped, hs[1], axis=1)
        return nxt, prv

    S, D = sections, parts

    def perm_pipe(shift):
        return [(i, (i + shift) % S) for i in range(S)]

    def perm_both(dshift, pshift):
        return [(d * S + p, ((d + dshift) % D) * S + (p + pshift) % S)
                for d in range(D) for p in range(S)]

    both = ("dom", "pipe")

    fwd = vmem_call(
        fwd_kernel,
        (jax.ShapeDtypeStruct((micro, own, latent), BF16),
         jax.ShapeDtypeStruct((micro, own, latent), F32),
         jax.ShapeDtypeStruct((micro, own, latent), F32)),
        13)

    out_rec, grad_rec = whole(
        (hs, edge_count.astype(jnp.int32), inputs, cotangent, edge_send.astype(jnp.int32),
         edge_recv.astype(jnp.int32), *weights, gain), span, D, S)
    return (out_rec[None], grad_rec[None])


def solution(mesh):
    in_specs = (
        P(None, "dom", None),
        P(None, "dom", None),
        P("pipe", None, None),
        P("pipe", None, None),
        P("pipe", None, None),
        P("pipe", None, None),
        P("pipe", None, None),
        P("pipe", None),
        P("dom", None),
        P("dom", None),
        P("dom"),
        P("dom", None, None),
    )
    out_specs = (P("pipe", None, "dom", None), P("pipe", None, "dom", None))
    return jax.shard_map(shards, mesh=mesh, in_specs=in_specs, out_specs=out_specs, check_vma=False)
```

```python
import functools

import jax
import jax.numpy as jnp
from jax import lax
from jax.experimental import pallas as pl
from jax.experimental.pallas import tpu as pltpu
from jax.sharding import PartitionSpec as P

EPSILON = 1e-05
F32 = jnp.float32
BF16 = jnp.bfloat16


def mm(x, w):
    return jnp.dot(x, w, preferred_element_type=F32)


def mm_t(x, w):
    return lax.dot_general(x, w, (((1,), (1,)), ((), ())), preferred_element_type=F32)


def sigmoid(v):
    return 1.0 / (1.0 + jnp.exp(-v))


def split_sum(onehot, values):
    hi = values.astype(BF16)
    lo = (values - hi.astype(F32)).astype(BF16)
    return mm(onehot, hi) + mm(onehot, lo)


def fwd_micro(m, hs_ref, h_ref, fp_ref, fn_ref, osnd_ref, orcv_ref, orcvt_ref,
              ws_ref, wr_ref, wm_ref, wn_ref, wa_ref, g_ref, out_ref, a_ref, u_ref):
    own = h_ref.shape[1]
    span = fp_ref.shape[1]
    osnd = osnd_ref[...]
    h = h_ref[m]
    gathered = (mm(osnd[:, :own], h) + mm(osnd[:, own:own + span], fp_ref[m])
                + mm(osnd[:, own + span:], fn_ref[m])).astype(BF16)
    send_part = mm(gathered, ws_ref[...]).astype(BF16).astype(F32)
    recv_rows = mm(orcv_ref[...], h).astype(BF16)
    pre = send_part + mm(recv_rows, wr_ref[...])
    a_ref[m] = pre
    edge_hidden = (pre * sigmoid(pre)).astype(BF16)
    messages = mm(edge_hidden, wm_ref[...])
    agg = split_sum(orcvt_ref[...], messages).astype(BF16)
    node_pre = mm(h, wn_ref[...]) + mm(agg, wa_ref[...])
    u_ref[m] = node_pre
    act = node_pre * sigmoid(node_pre)
    mean = jnp.mean(act, axis=-1, keepdims=True)
    cen = act - mean
    var = jnp.mean(cen * cen, axis=-1, keepdims=True)
    unit = cen * lax.rsqrt(var + EPSILON)
    out_ref[m] = (h.astype(F32) + unit * g_ref[...]).astype(BF16)


def fwd_kernel(*refs):
    for m in range(refs[1].shape[0]):
        fwd_micro(m, *refs)


def bwd_micro(m, pin_ref, a_ref, u_ref, osndt_ref, orcvl_ref, orcvt_ref,
              ws_ref, wr_ref, wm_ref, wn_ref, wa_ref, g_ref, p32_ref, hg_ref):
    own = pin_ref.shape[1]
    gain = g_ref[...]
    c = pin_ref[m].astype(F32)
    node_pre = u_ref[m]
    sig_u = sigmoid(node_pre)
    act = node_pre * sig_u
    mean = jnp.mean(act, axis=-1, keepdims=True)
    cen = act - mean
    var = jnp.mean(cen * cen, axis=-1, keepdims=True)
    rs = lax.rsqrt(var + EPSILON)
    unit = cen * rs
    gu = c * gain
    gact = rs * (gu - jnp.mean(gu, axis=-1, keepdims=True)
                 - unit * jnp.mean(gu * unit, axis=-1, keepdims=True))
    du = (gact * (sig_u * (1.0 + node_pre * (1.0 - sig_u)))).astype(BF16)
    dagg = mm_t(du, wa_ref[...]).astype(BF16)
    rows = c + mm_t(du, wn_ref[...])
    gmsg = mm(orcvl_ref[...], dagg).astype(BF16)
    pre = a_ref[m]
    sig_a = sigmoid(pre)
    dedge = (mm_t(gmsg, wm_ref[...]) * (sig_a * (1.0 + pre * (1.0 - sig_a)))).astype(BF16)
    rows = rows + split_sum(orcvt_ref[...], mm_t(dedge, wr_ref[...]))
    send_rows = split_sum(osndt_ref[...], mm_t(dedge, ws_ref[...]))
    p32_ref[m] = rows + send_rows[:own]
    hg_ref[m] = send_rows[own:].astype(BF16)


MESH_ID = pl.DeviceIdType.MESH


def comm_kernel(sends, n_in, parts, sections, *refs):
    ins = refs[:n_in]
    outs = refs[n_in:n_in + len(sends)]
    send_sem, recv_sem = refs[n_in + len(sends):]
    d = lax.axis_index("dom")
    p = lax.axis_index("pipe")
    barrier = pltpu.get_barrier_semaphore()
    for _, _, _, dd, dp in sends:
        src = (lax.rem(d - dd + parts, parts), lax.rem(p - dp + sections, sections))
        pl.semaphore_signal(barrier, 1, device_id=src, device_id_type=MESH_ID)
    pl.semaphore_wait(barrier, len(sends))
    copies = []
    for i, (k, start, rows, dd, dp) in enumerate(sends):
        dst = (lax.rem(d + dd + parts, parts), lax.rem(p + dp + sections, sections))
        source = ins[k] if start is None else ins[k].at[:, pl.ds(start, rows)]
        copy = pltpu.make_async_remote_copy(
            src_ref=source, dst_ref=outs[i], send_sem=send_sem.at[i], recv_sem=recv_sem.at[i],
            device_id=dst, device_id_type=MESH_ID)
        copy.start()
        copies.append(copy)
    for copy in copies:
        copy.wait()


def exchange(sends, payloads, parts, sections, cid):
    out_shapes = []
    for k, start, rows, _, _ in sends:
        shape = payloads[k].shape
        if start is not None:
            shape = (shape[0], rows) + shape[2:]
        out_shapes.append(jax.ShapeDtypeStruct(shape, payloads[k].dtype))
    n = len(sends)
    return pl.pallas_call(
        functools.partial(comm_kernel, tuple(sends), len(payloads), parts, sections),
        out_shape=tuple(out_shapes),
        in_specs=[pl.BlockSpec(memory_space=pl.ANY)] * len(payloads),
        out_specs=tuple(pl.BlockSpec(memory_space=pl.ANY) for _ in sends),
        scratch_shapes=[pltpu.SemaphoreType.DMA((n,)), pltpu.SemaphoreType.DMA((n,))],
        compiler_params=pltpu.CompilerParams(collective_id=cid, has_side_effects=True),
    )(*payloads)


def record_copies(pairs, sem, active):
    def run():
        copies = [pltpu.make_async_copy(buf, rec, sem.at[i]) for i, (buf, rec) in enumerate(pairs)]
        for copy in copies:
            copy.start()
        for copy in copies:
            copy.wait()
    if active is None:
        run()
    else:
        pl.when(active)(run)


def fwd_tick_kernel(parts, sections, tick, hs_ref, h_ref, fp_ref, fn_ref, osnd_ref, orcv_ref, orcvt_ref,
                    ws_ref, wr_ref, wm_ref, wn_ref, wa_ref, g_ref, *refs):
    if tick > 0:
        refs = refs[3:]
    (orec, arec, urec, hn_ref, fpn_ref, fnn_ref, obuf, abuf, ubuf,
     hbuf, fpbuf, fnbuf, stage_n, stage_p, send_sem, recv_sem, rec_sem) = refs
    micro, own, _ = h_ref.shape
    block = fp_ref.shape[1]
    d = lax.axis_index("dom")
    p = lax.axis_index("pipe")
    pipe_next = (d, lax.rem(p + 1, sections))
    pipe_prev = (d, lax.rem(p - 1 + sections, sections))
    dom_next = (lax.rem(d + 1, parts), p)
    dom_prev = (lax.rem(d - 1 + parts, parts), p)
    barrier = pltpu.get_barrier_semaphore()
    for src in (pipe_prev, dom_prev, dom_next):
        pl.semaphore_signal(barrier, 1, device_id=src, device_id_type=MESH_ID)
    compute_refs = (hs_ref, h_ref, fp_ref, fn_ref, osnd_ref, orcv_ref, orcvt_ref,
                    ws_ref, wr_ref, wm_ref, wn_ref, wa_ref, g_ref, obuf, abuf, ubuf)
    pipe_copies = []
    for m in range(micro):
        fwd_micro(m, *compute_refs)
        if m == 0:
            pl.semaphore_wait(barrier, 3)
        copy = pltpu.make_async_remote_copy(
            src_ref=obuf.at[m], dst_ref=hbuf.at[m], send_sem=send_sem.at[0, m],
            recv_sem=recv_sem.at[0, m], device_id=pipe_next, device_id_type=MESH_ID)
        copy.start()
        pipe_copies.append(copy)
    record_copies(((obuf, orec), (abuf, arec), (ubuf, urec)), rec_sem,
                  None if tick == 0 else p == tick)
    hs0 = hs_ref[0]
    hs1 = hs_ref[1]
    halo_copies = []
    for m in range(micro):
        pipe_copies[m].wait_recv()
        h = hbuf[m]
        sel_n = h[0:block]
        sel_p = h[0:block]
        for b in range(1, own // block):
            piece = h[b * block:(b + 1) * block]
            sel_n = jnp.where(hs0 == b, piece, sel_n)
            sel_p = jnp.where(hs1 == b, piece, sel_p)
        stage_n[m] = sel_n
        stage_p[m] = sel_p
        for j, (stage, buf, dst) in enumerate(((stage_n, fpbuf, dom_next), (stage_p, fnbuf, dom_prev))):
            copy = pltpu.make_async_remote_copy(
                src_ref=stage.at[m], dst_ref=buf.at[m], send_sem=send_sem.at[1 + j, m],
                recv_sem=recv_sem.at[1 + j, m], device_id=dst, device_id_type=MESH_ID)
            copy.start()
            halo_copies.append(copy)
    for copy in pipe_copies:
        copy.wait_send()
    for copy in halo_copies:
        copy.wait()
    hn_ref[...] = hbuf[...]
    fpn_ref[...] = fpbuf[...]
    fnn_ref[...] = fnbuf[...]


def fwd_tick(operands, records, tick, span, parts, sections):
    h = operands[1]
    micro, own, latent = h.shape
    vm = pl.BlockSpec(memory_space=pltpu.VMEM)
    anyspec = pl.BlockSpec(memory_space=pl.ANY)
    bf = lambda rows: jax.ShapeDtypeStruct((micro, rows, latent), BF16)
    f32 = jax.ShapeDtypeStruct((micro, own, latent), F32)
    n = len(operands)
    extra = () if tick == 0 else tuple(records)
    return pl.pallas_call(
        functools.partial(fwd_tick_kernel, parts, sections, tick),
        out_shape=(bf(own), f32, f32, bf(own), bf(span), bf(span)),
        in_specs=[pl.BlockSpec(memory_space=pltpu.SMEM)] + [vm] * (n - 1) + [anyspec] * len(extra),
        out_specs=(anyspec, anyspec, anyspec, vm, vm, vm),
        scratch_shapes=[pltpu.VMEM((micro, own, latent), BF16),
                        pltpu.VMEM((micro, own, latent), F32),
                        pltpu.VMEM((micro, own, latent), F32),
                        pltpu.VMEM((micro, own, latent), BF16),
                        pltpu.VMEM((micro, span, latent), BF16),
                        pltpu.VMEM((micro, span, latent), BF16),
                        pltpu.VMEM((micro, span, latent), BF16),
                        pltpu.VMEM((micro, span, latent), BF16),
                        pltpu.SemaphoreType.DMA((3, micro)),
                        pltpu.SemaphoreType.DMA((3, micro)),
                        pltpu.SemaphoreType.DMA((3,))],
        input_output_aliases={} if tick == 0 else {n: 0, n + 1: 1, n + 2: 2},
        compiler_params=pltpu.CompilerParams(collective_id=10 + tick,
                                             has_side_effects=True,
                                             vmem_limit_bytes=48 * 1024 * 1024),
    )(*operands, *extra)


def fwd_last_kernel(tick, hs_ref, h_ref, fp_ref, fn_ref, osnd_ref, orcv_ref, orcvt_ref,
                    ws_ref, wr_ref, wm_ref, wn_ref, wa_ref, g_ref, orec_in, arec_in, urec_in,
                    orec, arec, urec, obuf, abuf, ubuf, rec_sem):
    compute_refs = (hs_ref, h_ref, fp_ref, fn_ref, osnd_ref, orcv_ref, orcvt_ref,
                    ws_ref, wr_ref, wm_ref, wn_ref, wa_ref, g_ref, obuf, abuf, ubuf)
    for m in range(h_ref.shape[0]):
        fwd_micro(m, *compute_refs)
    record_copies(((obuf, orec), (abuf, arec), (ubuf, urec)), rec_sem,
                  lax.axis_index("pipe") == tick)


def fwd_last(operands, records, tick):
    h = operands[1]
    micro, own, latent = h.shape
    vm = pl.BlockSpec(memory_space=pltpu.VMEM)
    anyspec = pl.BlockSpec(memory_space=pl.ANY)
    n = len(operands)
    return pl.pallas_call(
        functools.partial(fwd_last_kernel, tick),
        out_shape=tuple(jax.ShapeDtypeStruct(r.shape, r.dtype) for r in records),
        in_specs=[pl.BlockSpec(memory_space=pltpu.SMEM)] + [vm] * (n - 1) + [anyspec] * 3,
        out_specs=(anyspec, anyspec, anyspec),
        scratch_shapes=[pltpu.VMEM((micro, own, latent), BF16),
                        pltpu.VMEM((micro, own, latent), F32),
                        pltpu.VMEM((micro, own, latent), F32),
                        pltpu.SemaphoreType.DMA((3,))],
        input_output_aliases={n: 0, n + 1: 1, n + 2: 2},
        compiler_params=pltpu.CompilerParams(vmem_limit_bytes=48 * 1024 * 1024),
    )(*operands, *records)


def bwd_tick_kernel(parts, sections, tick, first, hs_ref, pin_ref, a_ref, u_ref, osndt_ref, orcvl_ref,
                    orcvt_ref, ws_ref, wr_ref, wm_ref, wn_ref, wa_ref, g_ref, *refs):
    send_pipe = tick > 0
    if not first:
        refs = refs[1:]
    if send_pipe:
        grec, pinn_ref, p32, hg, snbuf, spbuf, gbuf, pinbuf, send_sem, recv_sem, rec_sem = refs
    else:
        grec, p32, hg, snbuf, spbuf, gbuf, send_sem, recv_sem, rec_sem = refs
    micro, own, _ = pin_ref.shape
    block = snbuf.shape[1]
    d = lax.axis_index("dom")
    p = lax.axis_index("pipe")
    pipe_prev = (d, lax.rem(p - 1 + sections, sections))
    pipe_next = (d, lax.rem(p + 1, sections))
    dom_next = (lax.rem(d + 1, parts), p)
    dom_prev = (lax.rem(d - 1 + parts, parts), p)
    barrier = pltpu.get_barrier_semaphore()
    sources = [dom_next, dom_prev] + ([pipe_next] if send_pipe else [])
    for src in sources:
        pl.semaphore_signal(barrier, 1, device_id=src, device_id_type=MESH_ID)
    compute_refs = (pin_ref, a_ref, u_ref, osndt_ref, orcvl_ref, orcvt_ref,
                    ws_ref, wr_ref, wm_ref, wn_ref, wa_ref, g_ref, p32, hg)
    halo_copies = []
    for m in range(micro):
        bwd_micro(m, *compute_refs)
        if m == 0:
            pl.semaphore_wait(barrier, len(sources))
        pair = []
        for j, (lo, buf, dst) in enumerate(((0, snbuf, dom_prev), (block, spbuf, dom_next))):
            copy = pltpu.make_async_remote_copy(
                src_ref=hg.at[m, pl.ds(lo, block)], dst_ref=buf.at[m],
                send_sem=send_sem.at[j, m], recv_sem=recv_sem.at[j, m],
                device_id=dst, device_id_type=MESH_ID)
            copy.start()
            pair.append(copy)
        halo_copies.append(pair)
    hs0 = hs_ref[0]
    hs1 = hs_ref[1]
    pipe_copies = []
    for m in range(micro):
        for copy in halo_copies[m]:
            copy.wait_recv()
        sn = snbuf[m].astype(F32)
        sp = spbuf[m].astype(F32)
        for b in range(own // block):
            piece = p32[m, b * block:(b + 1) * block]
            piece = piece + jnp.where(hs0 == b, sn, 0.0) + jnp.where(hs1 == b, sp, 0.0)
            gbuf[m, b * block:(b + 1) * block] = piece.astype(gbuf.dtype)
        if send_pipe:
            copy = pltpu.make_async_remote_copy(
                src_ref=gbuf.at[m], dst_ref=pinbuf.at[m], send_sem=send_sem.at[2, m],
                recv_sem=recv_sem.at[2, m], device_id=pipe_prev, device_id_type=MESH_ID)
            copy.start()
            pipe_copies.append(copy)
    record_copies(((gbuf, grec),), rec_sem, None if first else p == tick)
    for pair in halo_copies:
        for copy in pair:
            copy.wait_send()
    for copy in pipe_copies:
        copy.wait()
    if send_pipe:
        pinn_ref[...] = pinbuf[...]


def bwd_tick(operands, grad_rec, tick, span, parts, sections):
    pin = operands[1]
    micro, own, latent = pin.shape
    send_pipe = tick > 0
    first = grad_rec is None
    vm = pl.BlockSpec(memory_space=pltpu.VMEM)
    anyspec = pl.BlockSpec(memory_space=pl.ANY)
    grad = jax.ShapeDtypeStruct((micro, own, latent), BF16)
    scratch = [pltpu.VMEM((micro, own, latent), F32), pltpu.VMEM((micro, 2 * span, latent), BF16),
               pltpu.VMEM((micro, span, latent), BF16), pltpu.VMEM((micro, span, latent), BF16),
               pltpu.VMEM((micro, own, latent), BF16)]
    if send_pipe:
        scratch.append(pltpu.VMEM((micro, own, latent), BF16))
    scratch += [pltpu.SemaphoreType.DMA((3, micro)), pltpu.SemaphoreType.DMA((3, micro)),
                pltpu.SemaphoreType.DMA((1,))]
    outs = (grad, grad) if send_pipe else (grad,)
    n = len(operands)
    extra = () if first else (grad_rec,)
    return pl.pallas_call(
        functools.partial(bwd_tick_kernel, parts, sections, tick, first),
        out_shape=outs,
        in_specs=[pl.BlockSpec(memory_space=pltpu.SMEM)] + [vm] * (n - 1) + [anyspec] * len(extra),
        out_specs=(anyspec,) + ((vm,) if send_pipe else ()),
        scratch_shapes=scratch,
        input_output_aliases={} if first else {n: 0},
        compiler_params=pltpu.CompilerParams(collective_id=20 + tick, has_side_effects=True,
                                             vmem_limit_bytes=48 * 1024 * 1024),
    )(*operands, *extra)


def vmem_call(kernel, out_shapes, n_in, smem_first=True):
    in_specs = [pl.BlockSpec(memory_space=pltpu.SMEM)] + [pl.BlockSpec(memory_space=pltpu.VMEM)] * (n_in - 1)
    return pl.pallas_call(
        kernel,
        out_shape=out_shapes,
        in_specs=in_specs,
        out_specs=tuple(pl.BlockSpec(memory_space=pltpu.VMEM) for _ in out_shapes),
        compiler_params=pltpu.CompilerParams(vmem_limit_bytes=48 * 1024 * 1024),
    )


def whole_kernel(parts, sections, hs_ref, cnt_ref, x_hbm, cot_hbm, esnd_ref, ercv_ref,
                 ws_hbm, wr_hbm, wm_hbm, wn_hbm, wa_hbm, g_ref,
                 out_ref, grad_ref,
                 xbuf, cotbuf, wbuf, osnd_ref, orcv_ref, orcvt_ref, osndt_ref, orcvl_ref,
                 hbuf, fpbuf, fnbuf, stage_n, stage_p, abuf, ubuf, cbuf, p32, hg, snbuf, spbuf,
                 unitbuf, rsbuf,
                 fsend, frecv, bsend, brecv, lsem):
    micro, own, latent = xbuf.shape
    block = fpbuf.shape[1]
    span = block
    loads = [pltpu.make_async_copy(x_hbm, xbuf, lsem.at[0])]
    for i, w in enumerate((ws_hbm, wr_hbm, wm_hbm, wn_hbm, wa_hbm)):
        loads.append(pltpu.make_async_copy(w, wbuf.at[i], lsem.at[1 + i]))
    loads.append(pltpu.make_async_copy(cot_hbm, cotbuf, lsem.at[6]))
    for copy in loads:
        copy.start()
    edges = osnd_ref.shape[0]
    ext_rows = osnd_ref.shape[1]
    own_rows = orcv_ref.shape[1]
    es = esnd_ref[...]
    er = ercv_ref[...]
    snd = jnp.concatenate([es[i:i + 1] for i in range(es.shape[0])], axis=1)
    rcv = jnp.concatenate([er[i:i + 1] for i in range(er.shape[0])], axis=1)
    lane = lax.broadcasted_iota(jnp.int32, (1, edges), 1)
    per_block = es.shape[1]
    live = lane < 0
    for i in range(es.shape[0]):
        live = live | ((lane >= i * per_block) & (lane < i * per_block + cnt_ref[i]))
    sndt = lax.broadcasted_iota(jnp.int32, (ext_rows, edges), 0) == snd
    rcvt = lax.broadcasted_iota(jnp.int32, (own_rows, edges), 0) == rcv
    osndt_f = sndt.astype(F32)
    rcvt_f = rcvt.astype(F32)
    rcvlt_f = (rcvt & live).astype(F32)
    osndt_ref[...] = osndt_f.astype(BF16)
    orcvt_ref[...] = rcvlt_f.astype(BF16)
    osnd_ref[...] = osndt_f.T.astype(BF16)
    orcv_ref[...] = rcvt_f.T.astype(BF16)
    orcvl_ref[...] = rcvlt_f.T.astype(BF16)
    d = lax.axis_index("dom")
    p = lax.axis_index("pipe")
    pipe_next = (d, lax.rem(p + 1, sections))
    pipe_prev = (d, lax.rem(p - 1 + sections, sections))
    dom_next = (lax.rem(d + 1, parts), p)
    dom_prev = (lax.rem(d - 1 + parts, parts), p)
    barrier = pltpu.get_barrier_semaphore()
    for nb in (pipe_prev, pipe_next, dom_prev, dom_next):
        pl.semaphore_signal(barrier, 1, device_id=nb, device_id_type=MESH_ID)
    pl.semaphore_wait(barrier, 4)
    hs0 = hs_ref[0]
    hs1 = hs_ref[1]
    has_prev = p > 0
    has_next = p < sections - 1
    gain = g_ref[...]
    ws, wr, wm, wn, wa = (wbuf.at[i] for i in range(5))

    def remote(src, dst, sems, idx, target):
        send_sem, recv_sem = sems
        return pltpu.make_async_remote_copy(
            src_ref=src, dst_ref=dst, send_sem=send_sem.at[idx], recv_sem=recv_sem.at[idx],
            device_id=target, device_id_type=MESH_ID)

    loads[0].wait()
    fwd_pipe = []
    fwd_halo = []
    for m in range(micro):
        pipe_in = remote(out_ref.at[m], hbuf.at[m], (fsend, frecv), m, pipe_next)
        pl.when(has_prev)(pipe_in.wait_recv)

        @pl.when(p == 0)
        def _():
            hbuf[m] = xbuf[m]

        h = hbuf[m]
        sel_n = h[0:block]
        sel_p = h[0:block]
        for b in range(1, own // block):
            piece = h[b * block:(b + 1) * block]
            sel_n = jnp.where(hs0 == b, piece, sel_n)
            sel_p = jnp.where(hs1 == b, piece, sel_p)
        stage_n[m] = sel_n
        stage_p[m] = sel_p
        pair = [remote(stage_n.at[m], fpbuf.at[m], (fsend, frecv), micro + 2 * m, dom_next),
                remote(stage_p.at[m], fnbuf.at[m], (fsend, frecv), micro + 2 * m + 1, dom_prev)]
        for copy in pair:
            copy.start()
        if m == 0:
            for copy in loads[1:6]:
                copy.wait()
        osnd = osnd_ref[...]
        own_gather = mm(osnd[:, :own], h)
        recv_rows = mm(orcv_ref[...], h).astype(BF16)
        recv_part = mm(recv_rows, wr[...])
        node_part = mm(h, wn[...])
        for copy in pair:
            copy.wait_recv()
        fwd_halo.extend(pair)
        gathered = (own_gather + mm(osnd[:, own:own + span], fpbuf[m])
                    + mm(osnd[:, own + span:], fnbuf[m])).astype(BF16)
        send_part = mm(gathered, ws[...]).astype(BF16).astype(F32)
        pre = send_part + recv_part
        sig_a = sigmoid(pre)
        edge_hidden = (pre * sig_a).astype(BF16)
        messages = mm(edge_hidden, wm[...])
        agg = mm(orcvt_ref[...], messages.astype(BF16)).astype(BF16)
        node_pre = node_part + mm(agg, wa[...])
        sig_u = sigmoid(node_pre)
        act = node_pre * sig_u
        mean = jnp.mean(act, axis=-1, keepdims=True)
        cen = act - mean
        var = jnp.mean(cen * cen, axis=-1, keepdims=True)
        rs = lax.rsqrt(var + EPSILON)
        unit = cen * rs
        out_ref[m] = (h.astype(F32) + unit * gain).astype(BF16)
        pl.when(has_next)(pipe_in.start)
        fwd_pipe.append(pipe_in)
        unitbuf[m] = unit
        rsbuf[m] = jnp.broadcast_to(rs, rsbuf.shape[1:])
        ubuf[m] = sig_u * (1.0 + node_pre * (1.0 - sig_u))
        abuf[m] = sig_a * (1.0 + pre * (1.0 - sig_a))

    loads[6].wait()
    bwd_pipe = []
    bwd_halo = []
    for m in range(micro):
        pipe_in = remote(grad_ref.at[m], cbuf.at[m], (bsend, brecv), m, pipe_prev)
        pl.when(has_next)(pipe_in.wait_recv)

        @pl.when(p == sections - 1)
        def _():
            cbuf[m] = cotbuf[m]

        c = cbuf[m].astype(F32)
        unit = unitbuf[m]
        rs = rsbuf[m][:, 0:1]
        gu = c * gain
        gact = rs * (gu - jnp.mean(gu, axis=-1, keepdims=True)
                     - unit * jnp.mean(gu * unit, axis=-1, keepdims=True))
        du = (gact * ubuf[m]).astype(BF16)
        dagg = mm_t(du, wa[...]).astype(BF16)
        gmsg = mm(orcvl_ref[...], dagg).astype(BF16)
        dedge = (mm_t(gmsg, wm[...]) * abuf[m]).astype(BF16)
        send_x = mm_t(dedge, ws[...])
        osndt = osndt_ref[...]
        hg[m] = mm(osndt[own:], send_x.astype(BF16)).astype(BF16)
        pair = [remote(hg.at[m, pl.ds(0, block)], snbuf.at[m], (bsend, brecv), micro + 2 * m, dom_prev),
                remote(hg.at[m, pl.ds(block, block)], spbuf.at[m], (bsend, brecv), micro + 2 * m + 1,
                       dom_next)]
        for copy in pair:
            copy.start()
        rows = c + mm_t(du, wn[...])
        rows = rows + split_sum(orcvt_ref[...], mm_t(dedge, wr[...]))
        p32[m] = rows + split_sum(osndt[:own], send_x)
        for copy in pair:
            copy.wait_recv()
        bwd_halo.extend(pair)
        sn = snbuf[m].astype(F32)
        sp = spbuf[m].astype(F32)
        for b in range(own // block):
            piece = p32[m, b * block:(b + 1) * block]
            piece = piece + jnp.where(hs0 == b, sn, 0.0) + jnp.where(hs1 == b, sp, 0.0)
            grad_ref[m, b * block:(b + 1) * block] = piece.astype(grad_ref.dtype)
        pl.when(has_prev)(pipe_in.start)
        bwd_pipe.append(pipe_in)

    for copy in fwd_pipe:
        pl.when(has_next)(copy.wait_send)
    for copy in bwd_pipe:
        pl.when(has_prev)(copy.wait_send)
    for copy in fwd_halo + bwd_halo:
        copy.wait_send()


def whole(operands, span, parts, sections):
    x = operands[2]
    micro, own, latent = x.shape
    vm = pl.BlockSpec(memory_space=pltpu.VMEM)
    anyspec = pl.BlockSpec(memory_space=pltpu.HBM)
    bf = lambda rows: pltpu.VMEM((micro, rows, latent), BF16)
    f32 = pltpu.VMEM((micro, own, latent), F32)
    smem = pl.BlockSpec(memory_space=pltpu.SMEM)
    in_specs = [smem, smem, anyspec, anyspec, vm, vm] + [anyspec] * 5 + [vm]
    edges = operands[4].size
    ext_rows = own + 2 * span
    return pl.pallas_call(
        functools.partial(whole_kernel, parts, sections),
        out_shape=(jax.ShapeDtypeStruct((micro, own, latent), BF16),
                   jax.ShapeDtypeStruct((micro, own, latent), BF16)),
        in_specs=in_specs,
        out_specs=(vm, vm),
        scratch_shapes=[bf(own), bf(own), pltpu.VMEM((5, latent, latent), BF16),
                        pltpu.VMEM((edges, ext_rows), BF16), pltpu.VMEM((edges, own), BF16),
                        pltpu.VMEM((own, edges), BF16), pltpu.VMEM((ext_rows, edges), BF16),
                        pltpu.VMEM((edges, own), BF16),
                        bf(own), bf(span), bf(span), bf(span), bf(span), f32, f32, bf(own), f32,
                        bf(2 * span), bf(span), bf(span), f32, pltpu.VMEM((micro, own, 128), F32),
                        pltpu.SemaphoreType.DMA((3 * micro,)), pltpu.SemaphoreType.DMA((3 * micro,)),
                        pltpu.SemaphoreType.DMA((3 * micro,)), pltpu.SemaphoreType.DMA((3 * micro,)),
                        pltpu.SemaphoreType.DMA((7,))],
        compiler_params=pltpu.CompilerParams(collective_id=0, has_side_effects=True,
                                             vmem_limit_bytes=67043328),
    )(*operands)


def shards(inputs, cotangent, w_send, w_recv, w_message, w_node, w_aggregate, gains,
           edge_send, edge_recv, edge_count, halo_send):
    sections = lax.axis_size("pipe")
    parts = lax.axis_size("dom")
    p_idx = lax.axis_index("pipe")
    micro, own, latent = inputs.shape
    block = edge_send.shape[1]
    span = halo_send.shape[2] * block
    ext_rows = own + 2 * span
    weights = (w_send[0], w_recv[0], w_message[0], w_node[0], w_aggregate[0])
    gain = gains[0].reshape(1, latent)
    hs = halo_send[0].reshape(-1).astype(jnp.int32)

    def blocks_of(x):
        shaped = x.reshape(micro, own // block, block, latent)
        nxt = jnp.take(shaped, hs[0], axis=1)
        prv = jnp.take(shaped, hs[1], axis=1)
        return nxt, prv

    S, D = sections, parts

    def perm_pipe(shift):
        return [(i, (i + shift) % S) for i in range(S)]

    def perm_both(dshift, pshift):
        return [(d * S + p, ((d + dshift) % D) * S + (p + pshift) % S)
                for d in range(D) for p in range(S)]

    both = ("dom", "pipe")

    fwd = vmem_call(
        fwd_kernel,
        (jax.ShapeDtypeStruct((micro, own, latent), BF16),
         jax.ShapeDtypeStruct((micro, own, latent), F32),
         jax.ShapeDtypeStruct((micro, own, latent), F32)),
        13)

    out_rec, grad_rec = whole(
        (hs, edge_count.astype(jnp.int32), inputs, cotangent, edge_send.astype(jnp.int32),
         edge_recv.astype(jnp.int32), *weights, gain), span, D, S)
    return (out_rec[None], grad_rec[None])


def solution(mesh):
    in_specs = (
        P(None, "dom", None),
        P(None, "dom", None),
        P("pipe", None, None),
        P("pipe", None, None),
        P("pipe", None, None),
        P("pipe", None, None),
        P("pipe", None, None),
        P("pipe", None),
        P("dom", None),
        P("dom", None),
        P("dom"),
        P("dom", None, None),
    )
    out_specs = (P("pipe", None, "dom", None), P("pipe", None, "dom", None))
    return jax.shard_map(shards, mesh=mesh, in_specs=in_specs, out_specs=out_specs, check_vma=False)
```

```python
import functools

import jax
import jax.numpy as jnp
from jax import lax
from jax.experimental import pallas as pl
from jax.experimental.pallas import tpu as pltpu
from jax.sharding import PartitionSpec as P

EPSILON = 1e-05
F32 = jnp.float32
BF16 = jnp.bfloat16


def mm(x, w):
    return jnp.dot(x, w, preferred_element_type=F32)


def mm_t(x, w):
    return lax.dot_general(x, w, (((1,), (1,)), ((), ())), preferred_element_type=F32)


def sigmoid(v):
    return 0.5 * (1.0 + jnp.tanh(0.5 * v))


def split_sum(onehot, values):
    hi = values.astype(BF16)
    lo = (values - hi.astype(F32)).astype(BF16)
    return mm(onehot, hi) + mm(onehot, lo)


def fwd_micro(m, hs_ref, h_ref, fp_ref, fn_ref, osnd_ref, orcv_ref, orcvt_ref,
              ws_ref, wr_ref, wm_ref, wn_ref, wa_ref, g_ref, out_ref, a_ref, u_ref):
    own = h_ref.shape[1]
    span = fp_ref.shape[1]
    osnd = osnd_ref[...]
    h = h_ref[m]
    gathered = (mm(osnd[:, :own], h) + mm(osnd[:, own:own + span], fp_ref[m])
                + mm(osnd[:, own + span:], fn_ref[m])).astype(BF16)
    send_part = mm(gathered, ws_ref[...]).astype(BF16).astype(F32)
    recv_rows = mm(orcv_ref[...], h).astype(BF16)
    pre = send_part + mm(recv_rows, wr_ref[...])
    a_ref[m] = pre
    edge_hidden = (pre * sigmoid(pre)).astype(BF16)
    messages = mm(edge_hidden, wm_ref[...])
    agg = split_sum(orcvt_ref[...], messages).astype(BF16)
    node_pre = mm(h, wn_ref[...]) + mm(agg, wa_ref[...])
    u_ref[m] = node_pre
    act = node_pre * sigmoid(node_pre)
    mean = jnp.mean(act, axis=-1, keepdims=True)
    cen = act - mean
    var = jnp.mean(cen * cen, axis=-1, keepdims=True)
    unit = cen * lax.rsqrt(var + EPSILON)
    out_ref[m] = (h.astype(F32) + unit * g_ref[...]).astype(BF16)


def fwd_kernel(*refs):
    for m in range(refs[1].shape[0]):
        fwd_micro(m, *refs)


def bwd_micro(m, pin_ref, a_ref, u_ref, osndt_ref, orcvl_ref, orcvt_ref,
              ws_ref, wr_ref, wm_ref, wn_ref, wa_ref, g_ref, p32_ref, hg_ref):
    own = pin_ref.shape[1]
    gain = g_ref[...]
    c = pin_ref[m].astype(F32)
    node_pre = u_ref[m]
    sig_u = sigmoid(node_pre)
    act = node_pre * sig_u
    mean = jnp.mean(act, axis=-1, keepdims=True)
    cen = act - mean
    var = jnp.mean(cen * cen, axis=-1, keepdims=True)
    rs = lax.rsqrt(var + EPSILON)
    unit = cen * rs
    gu = c * gain
    gact = rs * (gu - jnp.mean(gu, axis=-1, keepdims=True)
                 - unit * jnp.mean(gu * unit, axis=-1, keepdims=True))
    du = (gact * (sig_u * (1.0 + node_pre * (1.0 - sig_u)))).astype(BF16)
    dagg = mm_t(du, wa_ref[...]).astype(BF16)
    rows = c + mm_t(du, wn_ref[...])
    gmsg = mm(orcvl_ref[...], dagg).astype(BF16)
    pre = a_ref[m]
    sig_a = sigmoid(pre)
    dedge = (mm_t(gmsg, wm_ref[...]) * (sig_a * (1.0 + pre * (1.0 - sig_a)))).astype(BF16)
    rows = rows + split_sum(orcvt_ref[...], mm_t(dedge, wr_ref[...]))
    send_rows = split_sum(osndt_ref[...], mm_t(dedge, ws_ref[...]))
    p32_ref[m] = rows + send_rows[:own]
    hg_ref[m] = send_rows[own:].astype(BF16)


MESH_ID = pl.DeviceIdType.MESH


def comm_kernel(sends, n_in, parts, sections, *refs):
    ins = refs[:n_in]
    outs = refs[n_in:n_in + len(sends)]
    send_sem, recv_sem = refs[n_in + len(sends):]
    d = lax.axis_index("dom")
    p = lax.axis_index("pipe")
    barrier = pltpu.get_barrier_semaphore()
    for _, _, _, dd, dp in sends:
        src = (lax.rem(d - dd + parts, parts), lax.rem(p - dp + sections, sections))
        pl.semaphore_signal(barrier, 1, device_id=src, device_id_type=MESH_ID)
    pl.semaphore_wait(barrier, len(sends))
    copies = []
    for i, (k, start, rows, dd, dp) in enumerate(sends):
        dst = (lax.rem(d + dd + parts, parts), lax.rem(p + dp + sections, sections))
        source = ins[k] if start is None else ins[k].at[:, pl.ds(start, rows)]
        copy = pltpu.make_async_remote_copy(
            src_ref=source, dst_ref=outs[i], send_sem=send_sem.at[i], recv_sem=recv_sem.at[i],
            device_id=dst, device_id_type=MESH_ID)
        copy.start()
        copies.append(copy)
    for copy in copies:
        copy.wait()


def exchange(sends, payloads, parts, sections, cid):
    out_shapes = []
    for k, start, rows, _, _ in sends:
        shape = payloads[k].shape
        if start is not None:
            shape = (shape[0], rows) + shape[2:]
        out_shapes.append(jax.ShapeDtypeStruct(shape, payloads[k].dtype))
    n = len(sends)
    return pl.pallas_call(
        functools.partial(comm_kernel, tuple(sends), len(payloads), parts, sections),
        out_shape=tuple(out_shapes),
        in_specs=[pl.BlockSpec(memory_space=pl.ANY)] * len(payloads),
        out_specs=tuple(pl.BlockSpec(memory_space=pl.ANY) for _ in sends),
        scratch_shapes=[pltpu.SemaphoreType.DMA((n,)), pltpu.SemaphoreType.DMA((n,))],
        compiler_params=pltpu.CompilerParams(collective_id=cid, has_side_effects=True),
    )(*payloads)


def record_copies(pairs, sem, active):
    def run():
        copies = [pltpu.make_async_copy(buf, rec, sem.at[i]) for i, (buf, rec) in enumerate(pairs)]
        for copy in copies:
            copy.start()
        for copy in copies:
            copy.wait()
    if active is None:
        run()
    else:
        pl.when(active)(run)


def fwd_tick_kernel(parts, sections, tick, hs_ref, h_ref, fp_ref, fn_ref, osnd_ref, orcv_ref, orcvt_ref,
                    ws_ref, wr_ref, wm_ref, wn_ref, wa_ref, g_ref, *refs):
    if tick > 0:
        refs = refs[3:]
    (orec, arec, urec, hn_ref, fpn_ref, fnn_ref, obuf, abuf, ubuf,
     hbuf, fpbuf, fnbuf, stage_n, stage_p, send_sem, recv_sem, rec_sem) = refs
    micro, own, _ = h_ref.shape
    block = fp_ref.shape[1]
    d = lax.axis_index("dom")
    p = lax.axis_index("pipe")
    pipe_next = (d, lax.rem(p + 1, sections))
    pipe_prev = (d, lax.rem(p - 1 + sections, sections))
    dom_next = (lax.rem(d + 1, parts), p)
    dom_prev = (lax.rem(d - 1 + parts, parts), p)
    barrier = pltpu.get_barrier_semaphore()
    for src in (pipe_prev, dom_prev, dom_next):
        pl.semaphore_signal(barrier, 1, device_id=src, device_id_type=MESH_ID)
    compute_refs = (hs_ref, h_ref, fp_ref, fn_ref, osnd_ref, orcv_ref, orcvt_ref,
                    ws_ref, wr_ref, wm_ref, wn_ref, wa_ref, g_ref, obuf, abuf, ubuf)
    pipe_copies = []
    for m in range(micro):
        fwd_micro(m, *compute_refs)
        if m == 0:
            pl.semaphore_wait(barrier, 3)
        copy = pltpu.make_async_remote_copy(
            src_ref=obuf.at[m], dst_ref=hbuf.at[m], send_sem=send_sem.at[0, m],
            recv_sem=recv_sem.at[0, m], device_id=pipe_next, device_id_type=MESH_ID)
        copy.start()
        pipe_copies.append(copy)
    record_copies(((obuf, orec), (abuf, arec), (ubuf, urec)), rec_sem,
                  None if tick == 0 else p == tick)
    hs0 = hs_ref[0]
    hs1 = hs_ref[1]
    halo_copies = []
    for m in range(micro):
        pipe_copies[m].wait_recv()
        h = hbuf[m]
        sel_n = h[0:block]
        sel_p = h[0:block]
        for b in range(1, own // block):
            piece = h[b * block:(b + 1) * block]
            sel_n = jnp.where(hs0 == b, piece, sel_n)
            sel_p = jnp.where(hs1 == b, piece, sel_p)
        stage_n[m] = sel_n
        stage_p[m] = sel_p
        for j, (stage, buf, dst) in enumerate(((stage_n, fpbuf, dom_next), (stage_p, fnbuf, dom_prev))):
            copy = pltpu.make_async_remote_copy(
                src_ref=stage.at[m], dst_ref=buf.at[m], send_sem=send_sem.at[1 + j, m],
                recv_sem=recv_sem.at[1 + j, m], device_id=dst, device_id_type=MESH_ID)
            copy.start()
            halo_copies.append(copy)
    for copy in pipe_copies:
        copy.wait_send()
    for copy in halo_copies:
        copy.wait()
    hn_ref[...] = hbuf[...]
    fpn_ref[...] = fpbuf[...]
    fnn_ref[...] = fnbuf[...]


def fwd_tick(operands, records, tick, span, parts, sections):
    h = operands[1]
    micro, own, latent = h.shape
    vm = pl.BlockSpec(memory_space=pltpu.VMEM)
    anyspec = pl.BlockSpec(memory_space=pl.ANY)
    bf = lambda rows: jax.ShapeDtypeStruct((micro, rows, latent), BF16)
    f32 = jax.ShapeDtypeStruct((micro, own, latent), F32)
    n = len(operands)
    extra = () if tick == 0 else tuple(records)
    return pl.pallas_call(
        functools.partial(fwd_tick_kernel, parts, sections, tick),
        out_shape=(bf(own), f32, f32, bf(own), bf(span), bf(span)),
        in_specs=[pl.BlockSpec(memory_space=pltpu.SMEM)] + [vm] * (n - 1) + [anyspec] * len(extra),
        out_specs=(anyspec, anyspec, anyspec, vm, vm, vm),
        scratch_shapes=[pltpu.VMEM((micro, own, latent), BF16),
                        pltpu.VMEM((micro, own, latent), F32),
                        pltpu.VMEM((micro, own, latent), F32),
                        pltpu.VMEM((micro, own, latent), BF16),
                        pltpu.VMEM((micro, span, latent), BF16),
                        pltpu.VMEM((micro, span, latent), BF16),
                        pltpu.VMEM((micro, span, latent), BF16),
                        pltpu.VMEM((micro, span, latent), BF16),
                        pltpu.SemaphoreType.DMA((3, micro)),
                        pltpu.SemaphoreType.DMA((3, micro)),
                        pltpu.SemaphoreType.DMA((3,))],
        input_output_aliases={} if tick == 0 else {n: 0, n + 1: 1, n + 2: 2},
        compiler_params=pltpu.CompilerParams(collective_id=10 + tick,
                                             has_side_effects=True,
                                             vmem_limit_bytes=48 * 1024 * 1024),
    )(*operands, *extra)


def fwd_last_kernel(tick, hs_ref, h_ref, fp_ref, fn_ref, osnd_ref, orcv_ref, orcvt_ref,
                    ws_ref, wr_ref, wm_ref, wn_ref, wa_ref, g_ref, orec_in, arec_in, urec_in,
                    orec, arec, urec, obuf, abuf, ubuf, rec_sem):
    compute_refs = (hs_ref, h_ref, fp_ref, fn_ref, osnd_ref, orcv_ref, orcvt_ref,
                    ws_ref, wr_ref, wm_ref, wn_ref, wa_ref, g_ref, obuf, abuf, ubuf)
    for m in range(h_ref.shape[0]):
        fwd_micro(m, *compute_refs)
    record_copies(((obuf, orec), (abuf, arec), (ubuf, urec)), rec_sem,
                  lax.axis_index("pipe") == tick)


def fwd_last(operands, records, tick):
    h = operands[1]
    micro, own, latent = h.shape
    vm = pl.BlockSpec(memory_space=pltpu.VMEM)
    anyspec = pl.BlockSpec(memory_space=pl.ANY)
    n = len(operands)
    return pl.pallas_call(
        functools.partial(fwd_last_kernel, tick),
        out_shape=tuple(jax.ShapeDtypeStruct(r.shape, r.dtype) for r in records),
        in_specs=[pl.BlockSpec(memory_space=pltpu.SMEM)] + [vm] * (n - 1) + [anyspec] * 3,
        out_specs=(anyspec, anyspec, anyspec),
        scratch_shapes=[pltpu.VMEM((micro, own, latent), BF16),
                        pltpu.VMEM((micro, own, latent), F32),
                        pltpu.VMEM((micro, own, latent), F32),
                        pltpu.SemaphoreType.DMA((3,))],
        input_output_aliases={n: 0, n + 1: 1, n + 2: 2},
        compiler_params=pltpu.CompilerParams(vmem_limit_bytes=48 * 1024 * 1024),
    )(*operands, *records)


def bwd_tick_kernel(parts, sections, tick, first, hs_ref, pin_ref, a_ref, u_ref, osndt_ref, orcvl_ref,
                    orcvt_ref, ws_ref, wr_ref, wm_ref, wn_ref, wa_ref, g_ref, *refs):
    send_pipe = tick > 0
    if not first:
        refs = refs[1:]
    if send_pipe:
        grec, pinn_ref, p32, hg, snbuf, spbuf, gbuf, pinbuf, send_sem, recv_sem, rec_sem = refs
    else:
        grec, p32, hg, snbuf, spbuf, gbuf, send_sem, recv_sem, rec_sem = refs
    micro, own, _ = pin_ref.shape
    block = snbuf.shape[1]
    d = lax.axis_index("dom")
    p = lax.axis_index("pipe")
    pipe_prev = (d, lax.rem(p - 1 + sections, sections))
    pipe_next = (d, lax.rem(p + 1, sections))
    dom_next = (lax.rem(d + 1, parts), p)
    dom_prev = (lax.rem(d - 1 + parts, parts), p)
    barrier = pltpu.get_barrier_semaphore()
    sources = [dom_next, dom_prev] + ([pipe_next] if send_pipe else [])
    for src in sources:
        pl.semaphore_signal(barrier, 1, device_id=src, device_id_type=MESH_ID)
    compute_refs = (pin_ref, a_ref, u_ref, osndt_ref, orcvl_ref, orcvt_ref,
                    ws_ref, wr_ref, wm_ref, wn_ref, wa_ref, g_ref, p32, hg)
    halo_copies = []
    for m in range(micro):
        bwd_micro(m, *compute_refs)
        if m == 0:
            pl.semaphore_wait(barrier, len(sources))
        pair = []
        for j, (lo, buf, dst) in enumerate(((0, snbuf, dom_prev), (block, spbuf, dom_next))):
            copy = pltpu.make_async_remote_copy(
                src_ref=hg.at[m, pl.ds(lo, block)], dst_ref=buf.at[m],
                send_sem=send_sem.at[j, m], recv_sem=recv_sem.at[j, m],
                device_id=dst, device_id_type=MESH_ID)
            copy.start()
            pair.append(copy)
        halo_copies.append(pair)
    hs0 = hs_ref[0]
    hs1 = hs_ref[1]
    pipe_copies = []
    for m in range(micro):
        for copy in halo_copies[m]:
            copy.wait_recv()
        sn = snbuf[m].astype(F32)
        sp = spbuf[m].astype(F32)
        for b in range(own // block):
            piece = p32[m, b * block:(b + 1) * block]
            piece = piece + jnp.where(hs0 == b, sn, 0.0) + jnp.where(hs1 == b, sp, 0.0)
            gbuf[m, b * block:(b + 1) * block] = piece.astype(gbuf.dtype)
        if send_pipe:
            copy = pltpu.make_async_remote_copy(
                src_ref=gbuf.at[m], dst_ref=pinbuf.at[m], send_sem=send_sem.at[2, m],
                recv_sem=recv_sem.at[2, m], device_id=pipe_prev, device_id_type=MESH_ID)
            copy.start()
            pipe_copies.append(copy)
    record_copies(((gbuf, grec),), rec_sem, None if first else p == tick)
    for pair in halo_copies:
        for copy in pair:
            copy.wait_send()
    for copy in pipe_copies:
        copy.wait()
    if send_pipe:
        pinn_ref[...] = pinbuf[...]


def bwd_tick(operands, grad_rec, tick, span, parts, sections):
    pin = operands[1]
    micro, own, latent = pin.shape
    send_pipe = tick > 0
    first = grad_rec is None
    vm = pl.BlockSpec(memory_space=pltpu.VMEM)
    anyspec = pl.BlockSpec(memory_space=pl.ANY)
    grad = jax.ShapeDtypeStruct((micro, own, latent), BF16)
    scratch = [pltpu.VMEM((micro, own, latent), F32), pltpu.VMEM((micro, 2 * span, latent), BF16),
               pltpu.VMEM((micro, span, latent), BF16), pltpu.VMEM((micro, span, latent), BF16),
               pltpu.VMEM((micro, own, latent), BF16)]
    if send_pipe:
        scratch.append(pltpu.VMEM((micro, own, latent), BF16))
    scratch += [pltpu.SemaphoreType.DMA((3, micro)), pltpu.SemaphoreType.DMA((3, micro)),
                pltpu.SemaphoreType.DMA((1,))]
    outs = (grad, grad) if send_pipe else (grad,)
    n = len(operands)
    extra = () if first else (grad_rec,)
    return pl.pallas_call(
        functools.partial(bwd_tick_kernel, parts, sections, tick, first),
        out_shape=outs,
        in_specs=[pl.BlockSpec(memory_space=pltpu.SMEM)] + [vm] * (n - 1) + [anyspec] * len(extra),
        out_specs=(anyspec,) + ((vm,) if send_pipe else ()),
        scratch_shapes=scratch,
        input_output_aliases={} if first else {n: 0},
        compiler_params=pltpu.CompilerParams(collective_id=20 + tick, has_side_effects=True,
                                             vmem_limit_bytes=48 * 1024 * 1024),
    )(*operands, *extra)


def vmem_call(kernel, out_shapes, n_in, smem_first=True):
    in_specs = [pl.BlockSpec(memory_space=pltpu.SMEM)] + [pl.BlockSpec(memory_space=pltpu.VMEM)] * (n_in - 1)
    return pl.pallas_call(
        kernel,
        out_shape=out_shapes,
        in_specs=in_specs,
        out_specs=tuple(pl.BlockSpec(memory_space=pltpu.VMEM) for _ in out_shapes),
        compiler_params=pltpu.CompilerParams(vmem_limit_bytes=48 * 1024 * 1024),
    )


def whole_kernel(parts, sections, hs_ref, cnt_ref, x_hbm, cot_hbm, esnd_ref, ercv_ref,
                 ws_hbm, wr_hbm, wm_hbm, wn_hbm, wa_hbm, g_ref,
                 out_ref, grad_ref,
                 xbuf, cotbuf, wbuf, osnd_ref, orcv_ref, orcvt_ref, osndt_ref, orcvl_ref,
                 hbuf, fpbuf, fnbuf, stage_n, stage_p, abuf, ubuf, cbuf, p32, hg, snbuf, spbuf,
                 unitbuf, rsbuf,
                 fsend, frecv, bsend, brecv, lsem):
    micro, own, latent = xbuf.shape
    block = fpbuf.shape[1]
    span = block
    loads = [pltpu.make_async_copy(x_hbm, xbuf, lsem.at[0])]
    for i, w in enumerate((ws_hbm, wr_hbm, wm_hbm, wn_hbm, wa_hbm)):
        loads.append(pltpu.make_async_copy(w, wbuf.at[i], lsem.at[1 + i]))
    loads.append(pltpu.make_async_copy(cot_hbm, cotbuf, lsem.at[6]))
    for copy in loads:
        copy.start()
    edges = osnd_ref.shape[0]
    ext_rows = osnd_ref.shape[1]
    own_rows = orcv_ref.shape[1]
    es = esnd_ref[...]
    er = ercv_ref[...]
    snd = jnp.concatenate([es[i:i + 1] for i in range(es.shape[0])], axis=1)
    rcv = jnp.concatenate([er[i:i + 1] for i in range(er.shape[0])], axis=1)
    lane = lax.broadcasted_iota(jnp.int32, (1, edges), 1)
    per_block = es.shape[1]
    live = lane < 0
    for i in range(es.shape[0]):
        live = live | ((lane >= i * per_block) & (lane < i * per_block + cnt_ref[i]))
    sndt = lax.broadcasted_iota(jnp.int32, (ext_rows, edges), 0) == snd
    rcvt = lax.broadcasted_iota(jnp.int32, (own_rows, edges), 0) == rcv
    osndt_f = sndt.astype(F32)
    rcvt_f = rcvt.astype(F32)
    rcvlt_f = (rcvt & live).astype(F32)
    osndt_ref[...] = osndt_f.astype(BF16)
    orcvt_ref[...] = rcvlt_f.astype(BF16)
    osnd_ref[...] = osndt_f.T.astype(BF16)
    orcv_ref[...] = rcvt_f.T.astype(BF16)
    orcvl_ref[...] = rcvlt_f.T.astype(BF16)
    d = lax.axis_index("dom")
    p = lax.axis_index("pipe")
    pipe_next = (d, lax.rem(p + 1, sections))
    pipe_prev = (d, lax.rem(p - 1 + sections, sections))
    dom_next = (lax.rem(d + 1, parts), p)
    dom_prev = (lax.rem(d - 1 + parts, parts), p)
    barrier = pltpu.get_barrier_semaphore()
    for nb in (pipe_prev, pipe_next, dom_prev, dom_next):
        pl.semaphore_signal(barrier, 1, device_id=nb, device_id_type=MESH_ID)
    pl.semaphore_wait(barrier, 4)
    hs0 = hs_ref[0]
    hs1 = hs_ref[1]
    has_prev = p > 0
    has_next = p < sections - 1
    gain = g_ref[...]
    ws, wr, wm, wn, wa = (wbuf.at[i] for i in range(5))

    def remote(src, dst, sems, idx, target):
        send_sem, recv_sem = sems
        return pltpu.make_async_remote_copy(
            src_ref=src, dst_ref=dst, send_sem=send_sem.at[idx], recv_sem=recv_sem.at[idx],
            device_id=target, device_id_type=MESH_ID)

    loads[0].wait()
    fwd_pipe = []
    fwd_halo = []
    for m in range(micro):
        pipe_in = remote(out_ref.at[m], hbuf.at[m], (fsend, frecv), m, pipe_next)
        pl.when(has_prev)(pipe_in.wait_recv)

        @pl.when(p == 0)
        def _():
            hbuf[m] = xbuf[m]

        h = hbuf[m]
        sel_n = h[0:block]
        sel_p = h[0:block]
        for b in range(1, own // block):
            piece = h[b * block:(b + 1) * block]
            sel_n = jnp.where(hs0 == b, piece, sel_n)
            sel_p = jnp.where(hs1 == b, piece, sel_p)
        stage_n[m] = sel_n
        stage_p[m] = sel_p
        pair = [remote(stage_n.at[m], fpbuf.at[m], (fsend, frecv), micro + 2 * m, dom_next),
                remote(stage_p.at[m], fnbuf.at[m], (fsend, frecv), micro + 2 * m + 1, dom_prev)]
        for copy in pair:
            copy.start()
        if m == 0:
            for copy in loads[1:6]:
                copy.wait()
        osnd = osnd_ref[...]
        own_gather = mm(osnd[:, :own], h)
        recv_rows = mm(orcv_ref[...], h).astype(BF16)
        recv_part = mm(recv_rows, wr[...])
        node_part = mm(h, wn[...])
        for copy in pair:
            copy.wait_recv()
        fwd_halo.extend(pair)
        gathered = (own_gather + mm(osnd[:, own:own + span], fpbuf[m])
                    + mm(osnd[:, own + span:], fnbuf[m])).astype(BF16)
        send_part = mm(gathered, ws[...]).astype(BF16).astype(F32)
        pre = send_part + recv_part
        sig_a = sigmoid(pre)
        edge_hidden = (pre * sig_a).astype(BF16)
        messages = mm(edge_hidden, wm[...])
        agg = mm(orcvt_ref[...], messages.astype(BF16)).astype(BF16)
        node_pre = node_part + mm(agg, wa[...])
        sig_u = sigmoid(node_pre)
        act = node_pre * sig_u
        mean = jnp.mean(act, axis=-1, keepdims=True)
        cen = act - mean
        var = jnp.mean(cen * cen, axis=-1, keepdims=True)
        rs = lax.rsqrt(var + EPSILON)
        unit = cen * rs
        out_ref[m] = (h.astype(F32) + unit * gain).astype(BF16)
        pl.when(has_next)(pipe_in.start)
        fwd_pipe.append(pipe_in)
        unitbuf[m] = unit
        rsbuf[m] = jnp.broadcast_to(rs, rsbuf.shape[1:])
        ubuf[m] = sig_u * (1.0 + node_pre * (1.0 - sig_u))
        abuf[m] = sig_a * (1.0 + pre * (1.0 - sig_a))

    loads[6].wait()
    bwd_pipe = []
    bwd_halo = []
    for m in range(micro):
        pipe_in = remote(grad_ref.at[m], cbuf.at[m], (bsend, brecv), m, pipe_prev)
        pl.when(has_next)(pipe_in.wait_recv)

        @pl.when(p == sections - 1)
        def _():
            cbuf[m] = cotbuf[m]

        c = cbuf[m].astype(F32)
        unit = unitbuf[m]
        rs = rsbuf[m][:, 0:1]
        gu = c * gain
        gact = rs * (gu - jnp.mean(gu, axis=-1, keepdims=True)
                     - unit * jnp.mean(gu * unit, axis=-1, keepdims=True))
        du = (gact * ubuf[m]).astype(BF16)
        dagg = mm_t(du, wa[...]).astype(BF16)
        gmsg = mm(orcvl_ref[...], dagg).astype(BF16)
        dedge = (mm_t(gmsg, wm[...]) * abuf[m]).astype(BF16)
        send_x = mm_t(dedge, ws[...])
        osndt = osndt_ref[...]
        hg[m] = mm(osndt[own:], send_x.astype(BF16)).astype(BF16)
        pair = [remote(hg.at[m, pl.ds(0, block)], snbuf.at[m], (bsend, brecv), micro + 2 * m, dom_prev),
                remote(hg.at[m, pl.ds(block, block)], spbuf.at[m], (bsend, brecv), micro + 2 * m + 1,
                       dom_next)]
        for copy in pair:
            copy.start()
        rows = c + mm_t(du, wn[...])
        rows = rows + split_sum(orcvt_ref[...], mm_t(dedge, wr[...]))
        p32[m] = rows + split_sum(osndt[:own], send_x)
        for copy in pair:
            copy.wait_recv()
        bwd_halo.extend(pair)
        sn = snbuf[m].astype(F32)
        sp = spbuf[m].astype(F32)
        for b in range(own // block):
            piece = p32[m, b * block:(b + 1) * block]
            piece = piece + jnp.where(hs0 == b, sn, 0.0) + jnp.where(hs1 == b, sp, 0.0)
            grad_ref[m, b * block:(b + 1) * block] = piece.astype(grad_ref.dtype)
        pl.when(has_prev)(pipe_in.start)
        bwd_pipe.append(pipe_in)

    for copy in fwd_pipe:
        pl.when(has_next)(copy.wait_send)
    for copy in bwd_pipe:
        pl.when(has_prev)(copy.wait_send)
    for copy in fwd_halo + bwd_halo:
        copy.wait_send()


def whole(operands, span, parts, sections):
    x = operands[2]
    micro, own, latent = x.shape
    vm = pl.BlockSpec(memory_space=pltpu.VMEM)
    anyspec = pl.BlockSpec(memory_space=pltpu.HBM)
    bf = lambda rows: pltpu.VMEM((micro, rows, latent), BF16)
    f32 = pltpu.VMEM((micro, own, latent), F32)
    smem = pl.BlockSpec(memory_space=pltpu.SMEM)
    in_specs = [smem, smem, anyspec, anyspec, vm, vm] + [anyspec] * 5 + [vm]
    edges = operands[4].size
    ext_rows = own + 2 * span
    return pl.pallas_call(
        functools.partial(whole_kernel, parts, sections),
        out_shape=(jax.ShapeDtypeStruct((micro, own, latent), BF16),
                   jax.ShapeDtypeStruct((micro, own, latent), BF16)),
        in_specs=in_specs,
        out_specs=(vm, vm),
        scratch_shapes=[bf(own), bf(own), pltpu.VMEM((5, latent, latent), BF16),
                        pltpu.VMEM((edges, ext_rows), BF16), pltpu.VMEM((edges, own), BF16),
                        pltpu.VMEM((own, edges), BF16), pltpu.VMEM((ext_rows, edges), BF16),
                        pltpu.VMEM((edges, own), BF16),
                        bf(own), bf(span), bf(span), bf(span), bf(span), f32, f32, bf(own), f32,
                        bf(2 * span), bf(span), bf(span), f32, pltpu.VMEM((micro, own, 128), F32),
                        pltpu.SemaphoreType.DMA((3 * micro,)), pltpu.SemaphoreType.DMA((3 * micro,)),
                        pltpu.SemaphoreType.DMA((3 * micro,)), pltpu.SemaphoreType.DMA((3 * micro,)),
                        pltpu.SemaphoreType.DMA((7,))],
        compiler_params=pltpu.CompilerParams(collective_id=0, has_side_effects=True,
                                             vmem_limit_bytes=67043328),
    )(*operands)


def shards(inputs, cotangent, w_send, w_recv, w_message, w_node, w_aggregate, gains,
           edge_send, edge_recv, edge_count, halo_send):
    sections = lax.axis_size("pipe")
    parts = lax.axis_size("dom")
    p_idx = lax.axis_index("pipe")
    micro, own, latent = inputs.shape
    block = edge_send.shape[1]
    span = halo_send.shape[2] * block
    ext_rows = own + 2 * span
    weights = (w_send[0], w_recv[0], w_message[0], w_node[0], w_aggregate[0])
    gain = gains[0].reshape(1, latent)
    hs = halo_send[0].reshape(-1).astype(jnp.int32)

    def blocks_of(x):
        shaped = x.reshape(micro, own // block, block, latent)
        nxt = jnp.take(shaped, hs[0], axis=1)
        prv = jnp.take(shaped, hs[1], axis=1)
        return nxt, prv

    S, D = sections, parts

    def perm_pipe(shift):
        return [(i, (i + shift) % S) for i in range(S)]

    def perm_both(dshift, pshift):
        return [(d * S + p, ((d + dshift) % D) * S + (p + pshift) % S)
                for d in range(D) for p in range(S)]

    both = ("dom", "pipe")

    fwd = vmem_call(
        fwd_kernel,
        (jax.ShapeDtypeStruct((micro, own, latent), BF16),
         jax.ShapeDtypeStruct((micro, own, latent), F32),
         jax.ShapeDtypeStruct((micro, own, latent), F32)),
        13)

    out_rec, grad_rec = whole(
        (hs, edge_count.astype(jnp.int32), inputs, cotangent, edge_send.astype(jnp.int32),
         edge_recv.astype(jnp.int32), *weights, gain), span, D, S)
    return (out_rec[None], grad_rec[None])


def solution(mesh):
    in_specs = (
        P(None, "dom", None),
        P(None, "dom", None),
        P("pipe", None, None),
        P("pipe", None, None),
        P("pipe", None, None),
        P("pipe", None, None),
        P("pipe", None, None),
        P("pipe", None),
        P("dom", None),
        P("dom", None),
        P("dom"),
        P("dom", None, None),
    )
    out_specs = (P("pipe", None, "dom", None), P("pipe", None, "dom", None))
    return jax.shard_map(shards, mesh=mesh, in_specs=in_specs, out_specs=out_specs, check_vma=False)
```
